32 devices in a mesh: groups: 2 (over y), space: 4 (over z), batch: 4 (over x, core).
Axes of the slice: x: 2, y: 2, z: 4, core: 2. Of those that a mesh axis runs over, the one named last changes fastest.
Arguments:
- fields: bfloat16 [8, 32, 64, 128], P(('groups', 'batch'), 'space'), parts along dimension 0, may hold values from -36 to 36
- land: int32 [32, 64], P('space'), may hold values 0 or 1
- conv_in: bfloat16 [9, 128, 128], replicated, may hold values from -0.1875 to 0.1875
- conv_out: bfloat16 [9, 128, 128], replicated, may hold values from -0.1875 to 0.1875
- batchnorm_gain: float32 [128], replicated, may hold values from 0.25 to 1.75
- batchnorm_offset: float32 [128], replicated, may hold values from -3 to 3
- target_grad: bfloat16 [8, 32, 64, 128], P(('groups', 'batch'), 'space'), parts along dimension 0, may hold values from -6 to 6
Outputs:
- output: bfloat16 [8, 32, 64, 128], P(('groups', 'batch'), 'space'), parts along dimension 0
- grad_in: float32 [18, 128, 128], P('groups', None, 'batch'), parts along dimension 0
- grad_out: float32 [18, 128, 128], P('groups', None, 'batch'), parts along dimension 0
- gain_gradient: float32 [256], P('groups'), parts along dimension 0
- offset_gradient: float32 [256], P('groups'), parts along dimension 0
The draws below stay inside these ranges and needn't reach their ends.
There are 2 independent parts, one for each index of `groups`. The reference program is written for one: setup_inputs(seed, part) draws one part's arguments, and reference() takes and returns one part's arrays. A program takes and returns all parts, laid end to end along the dimension named above; an argument that names none is the same for every part. Nothing has to cross between parts.
All inputs are finite; a program needn't handle non-finite values. No bound on the sum of `land` on one device may be relied on, other than what follows from the above.
Results may differ from the reference program's by a relative error of at most 0.025.
Values may be sent and summed in bfloat16 or wider, within the bound.
No kernel may reach another device: no remote copies, remote signals or barrier semaphores. Data moves between devices by JAX's collectives and lax.ppermute only.
A program may use at most 64 MiB of HBM per device.

```python
import jax
import jax.numpy as jnp
from jax import lax

CH = 128
LAT = 64
NX = 32
SAMPLES = 4


def draw_fields(key, part):
    first_key, second_key = jax.random.split(key, 2)
    shape = (SAMPLES, NX, LAT, CH)
    longitude = jnp.arange(NX, dtype=jnp.float32)[None, :, None, None]
    sample_pos = jnp.arange(SAMPLES, dtype=jnp.float32)[:, None, None, None]
    rough = jnp.exp(jax.random.uniform(second_key, (SAMPLES, NX, LAT, 1), jnp.float32, -0.8, 0.8))
    scales = (0.5 + 1.5 * longitude / NX) * (0.5 + 1.5 * sample_pos / SAMPLES) * rough
    base = jax.random.truncated_normal(first_key, -4.0, 4.0, shape, jnp.float32)
    return (base * scales).astype(jnp.bfloat16)


def with_ends(values, own_key, smallest, largest):
    place = [jax.random.randint(jax.random.fold_in(own_key, axis), (), 0, length) for axis, length in enumerate(values.shape)]
    widest = values.shape.index(max(values.shape))
    next_to = place[:widest] + [(place[widest] + 1) % values.shape[widest]] + place[widest + 1:]
    return values.at[tuple(place)].set(smallest).at[tuple(next_to)].set(largest)


def with_spikes(values, rng, source, target, blocks, factor):
    owner, partner = [(jnp.arange(values.shape[axis_at]) // (values.shape[axis_at] // blocks)).reshape([-1 if axis == axis_at else 1 for axis in range(values.ndim)]) for axis_at in (source, target)]
    chosen = jax.random.permutation(rng, blocks)[partner]
    strong = (owner == chosen) | (owner == (partner + blocks // 2) % blocks)
    return jnp.where(strong, factor * values, values)


def block_levels(key, shape, shards, least, largest):
    gain = 1.0
    for axis_at, parts in shards:
        steps = jax.random.uniform(jax.random.fold_in(jax.random.fold_in(key, 6), axis_at), (parts,), jnp.float32, least / len(shards), largest / len(shards))
        gain = gain * jnp.repeat(jnp.exp(steps), shape[axis_at] // parts).reshape((-1,) + (1,) * (len(shape) - 1 - axis_at))
    return gain


def centred(key, extent, deviation, most, cuts=(), held_as=jnp.bfloat16):
    values = jax.random.normal(key, extent, jnp.float32) * deviation
    if len(cuts) > 0:
        values = block_levels(key, extent, cuts, -0.22, 0.18) * values
    return jnp.clip(values, min=-most, max=most).astype(held_as)


def gaussian_with(key, extent, scale, limit, pieces, heavy, kind=jnp.bfloat16):
    drawn = scale * jax.random.normal(key, extent, jnp.float32)
    if pieces:
        drawn = drawn * block_levels(key, extent, pieces, -0.22, 0.18)
    return jnp.clip(with_spikes(drawn, jax.random.fold_in(key, 3), *heavy), -limit, limit).astype(kind)


def setup_inputs(seed: int = 0, part: int = 0) -> dict:
    splits = jax.random.split(jax.random.key(seed), 8)
    part_splits = jax.random.split(jax.random.fold_in(splits[7], part), 8)
    return {
        "fields": draw_fields(jax.random.fold_in(jax.random.fold_in(splits[7], part), 71), part),
        "land": with_ends((jax.random.randint(splits[1], (NX, LAT), 0, 4) < 3).astype(jnp.int32), jax.random.fold_in(splits[1], 1), 0, 1),
        "conv_in": centred(splits[2], (9, CH, CH), (9 * CH) ** -0.5, 0.1875),
        "conv_out": centred(splits[3], (9, CH, CH), (9 * CH) ** -0.5, 0.1875),
        "batchnorm_gain": jnp.clip(1.0 + 0.15 * jax.random.normal(splits[4], (CH,), jnp.float32), 0.25, 1.75),
        "batchnorm_offset": centred(splits[5], (CH,), 0.5, 3.0, (), jnp.float32),
        "target_grad": gaussian_with(part_splits[6], (SAMPLES, NX, LAT, CH), 1.0, 6.0, ((0, 4), (1, 4)), (0, 3, 4, 2.0)),
    }


def pad_field(field):
    ghost = jnp.flip(field[:, :, -1:, :], axis=1)
    south = jnp.zeros_like(field[:, :, :1, :])
    extended = jnp.concatenate([south, field, ghost], axis=2)
    return jnp.concatenate([extended[:, -1:], extended, extended[:, :1]], axis=1)

def convolve(padded, weights, lon, lat):
    chans = padded.shape[3]
    total = jnp.zeros((padded.shape[0] * lon * lat, weights.shape[2]), jnp.float32)
    for tap in range(9):
        first, second = (tap // 3, tap % 3)
        piece = padded[:, first:first + lon, second:second + lat, :].reshape(-1, chans)
        total = total + jnp.dot(piece, weights[tap], preferred_element_type=jnp.float32)
    return total.reshape(padded.shape[0], lon, lat, weights.shape[2])

def adjoint_conv(padded, weights, lon, lat):
    chans = padded.shape[3]
    ghost_row = padded[:, :, lat + 1, :]
    cleared = padded.at[:, :, lat + 1, :].set(jnp.zeros_like(ghost_row))
    total = jnp.zeros((padded.shape[0] * lon * lat, weights.shape[1]), jnp.float32)
    for tap in range(9):
        first, second = (tap // 3, tap % 3)
        piece = cleared[:, 2 - first:2 - first + lon, 2 - second:2 - second + lat, :].reshape(-1, chans)
        total = total + jnp.dot(piece, weights[tap].T, preferred_element_type=jnp.float32)
    total = total.reshape(padded.shape[0], lon, lat, weights.shape[1])
    extra = jnp.zeros((padded.shape[0] * lon, weights.shape[1]), jnp.float32)
    for first in range(3):
        piece = ghost_row[:, first:first + lon, :].reshape(-1, chans)
        extra = extra + jnp.dot(piece, weights[3 * first + 2].T, preferred_element_type=jnp.float32)
    extra = extra.reshape(padded.shape[0], lon, weights.shape[1])
    return total.at[:, :, lat - 1, :].add(extra)

def tap_grads(padded, grad, lon, lat):
    chans = padded.shape[3]
    flat = grad.reshape(-1, grad.shape[3])
    result = []
    for tap in range(9):
        first, second = (tap // 3, tap % 3)
        piece = padded[:, first:first + lon, second:second + lat, :].reshape(-1, chans)
        result.append(lax.dot_general(piece, flat, (((0,), (0,)), ((), ())), preferred_element_type=jnp.float32))
    return jnp.stack(result, axis=0)

def gelu_value(value):
    inner = 0.7978845608 * (value + 0.044715 * value * value * value)
    return 0.5 * value * (1.0 + jnp.tanh(inner))

def gelu_slope(value):
    inner = 0.7978845608 * (value + 0.044715 * value * value * value)
    hyper = jnp.tanh(inner)
    return 0.5 * (1.0 + hyper) + 0.5 * value * (1.0 - hyper * hyper) * 0.7978845608 * (1.0 + 3.0 * 0.044715 * value * value)

def reference(fields, land, conv_in, conv_out, batchnorm_gain, batchnorm_offset, target_grad):
    lon, lat = (fields.shape[1], fields.shape[2])
    ocean_mask = land.astype(jnp.float32)[None, :, :, None]
    masked = fields * ocean_mask.astype(jnp.bfloat16)
    padded_in = pad_field(masked)
    first = convolve(padded_in, conv_in, lon, lat).astype(jnp.bfloat16)
    first_features = first.astype(jnp.float32)
    element_count = jnp.sum(land.astype(jnp.float32)) * fields.shape[0]
    channel_mean = lax.optimization_barrier(jnp.sum(first_features * ocean_mask, axis=(0, 1, 2))) / element_count
    var = lax.optimization_barrier(jnp.sum(first_features * first_features * ocean_mask, axis=(0, 1, 2))) / element_count - channel_mean * channel_mean
    inverse_deviation = lax.rsqrt(var + 1e-05)
    normalized_input = (first_features - channel_mean) * inverse_deviation
    preactivation = batchnorm_gain * normalized_input + batchnorm_offset
    act = (gelu_value(preactivation) * ocean_mask).astype(jnp.bfloat16)
    padded_act = pad_field(act)
    output = (convolve(padded_act, conv_out, lon, lat) * ocean_mask).astype(jnp.bfloat16)
    dout = (target_grad.astype(jnp.float32) * ocean_mask * lax.rsqrt(element_count)).astype(jnp.bfloat16)
    grad_out = tap_grads(padded_act, dout, lon, lat)
    dact = adjoint_conv(pad_field(dout), conv_out, lon, lat)
    preactivation_gradient = dact * ocean_mask * gelu_slope(preactivation)
    offset_gradient = lax.optimization_barrier(jnp.sum(preactivation_gradient, axis=(0, 1, 2)))
    gain_gradient = lax.optimization_barrier(jnp.sum(preactivation_gradient * normalized_input, axis=(0, 1, 2)))
    first_layer_gradient = (ocean_mask * batchnorm_gain * inverse_deviation * (preactivation_gradient - (offset_gradient + normalized_input * gain_gradient) / element_count)).astype(jnp.bfloat16)
    grad_in = tap_grads(padded_in, first_layer_gradient, lon, lat)
    return (output, grad_in, grad_out, gain_gradient, offset_gradient)
```

```python
import functools

import jax
import jax.numpy as jnp
from jax import lax
from jax.experimental import pallas as pl
from jax.experimental.pallas import tpu as pltpu
from jax.sharding import PartitionSpec as P

F32 = jnp.float32
BF16 = jnp.bfloat16
VMEM = pl.BlockSpec(memory_space=pltpu.VMEM)


def call(body, outs, scratch=(), flops=0, nbytes=0, name=None):
    return pl.pallas_call(
        body,
        out_shape=outs,
        in_specs=None,
        out_specs=jax.tree.map(lambda _: VMEM, outs),
        scratch_shapes=scratch,
        cost_estimate=pl.CostEstimate(flops=flops, bytes_accessed=nbytes, transcendentals=0),
        name=name,
    )


def run(body, outs, args, scratch=(), flops=0, name=None):
    nbytes = sum(a.size * a.dtype.itemsize for a in args)
    nbytes += sum(o.size * o.dtype.itemsize for o in outs)
    return pl.pallas_call(
        body,
        out_shape=list(outs),
        in_specs=[VMEM] * len(args),
        out_specs=[VMEM] * len(outs),
        scratch_shapes=list(scratch),
        cost_estimate=pl.CostEstimate(flops=flops, bytes_accessed=nbytes, transcendentals=0),
        name=name,
    )(*args)


def sds(shape, dtype):
    return jax.ShapeDtypeStruct(shape, dtype)


def dot(a, b):
    return jnp.dot(a, b, preferred_element_type=F32)


def column_mask(land_ref, lon, lat, chans):
    rows = lax.broadcasted_iota(jnp.int32, (lat, lat), 0)
    cols = lax.broadcasted_iota(jnp.int32, (lat, lat), 1)
    out = []
    for i in range(lon):
        line = jnp.broadcast_to(land_ref[i : i + 1, :].astype(F32), (lat, lat))
        col = jnp.sum(jnp.where(rows == cols, line, 0.0), axis=1, keepdims=True)
        out.append(jnp.broadcast_to(col, (lat, chans)))
    return out


def pack_kernel(lon, lat, chans, join, f_ref, t_ref, land_ref, e_ref, o_ref, p_ref):
    even = lax.rem(lax.axis_index("space"), 2) == 0
    mask = column_mask(land_ref, lon, lat, chans)

    def edge(cols_f, col):
        parts = [f_ref[0, i].astype(F32) * mask[i] for i in cols_f]
        parts += [t_ref[0, col].astype(F32) * mask[col], mask[col]]
        return jnp.concatenate(parts, axis=0).astype(BF16)

    west = edge((0, 1), 0)
    east = edge((lon - 2, lon - 1), lon - 1)
    n = west.shape[0]
    e_ref[...] = jnp.where(even, east, west)
    o_ref[0:n, :] = jnp.where(even, west, east)
    rows = []
    for j in (lat - 2, lat - 1):
        rows += [f_ref[0, i].astype(F32)[j : j + 1] * mask[i][j : j + 1] for i in range(lon)]
    rows += [t_ref[0, i].astype(F32)[lat - 1 : lat] * mask[i][lat - 1 : lat] for i in range(lon)]
    rows += [mask[i][lat - 1 : lat] for i in range(lon)]
    polar = jnp.concatenate(rows, axis=0).astype(BF16)
    p_ref[...] = polar
    if join:
        o_ref[n:, :] = polar


def shift_rows(x, step, fill):
    rows = lax.broadcasted_iota(jnp.int32, x.shape, 0)
    n = x.shape[0]
    moved = pltpu.roll(x, (-step) % n, 0)
    return jnp.where(rows == (n - 1 if step > 0 else 0), fill, moved)


def conv_kernel(
    lon, lat, chans, moff,
    f_ref, t_ref, land_ref, re_ref, ro_ref, rm_ref, r1_ref, r2_ref, own_ref, w_ref,
    first_ref, mask_ref, stat_ref, ss_ref, tt_ref, tx_ref,
):
    even = lax.rem(lax.axis_index("space"), 2) == 0
    mask = column_mask(land_ref, lon, lat, chans)
    recv_e = re_ref[...].astype(F32)
    recv_o = ro_ref[0 : recv_e.shape[0], :].astype(F32)
    west = jnp.where(even, recv_o, recv_e)
    east = jnp.where(even, recv_e, recv_o)
    polar_m = rm_ref[moff : moff + 4 * lon, :].astype(F32)
    if r1_ref is r2_ref:
        other = r1_ref[...].astype(F32)
        own = own_ref[...].astype(F32)
        polar_1 = jnp.where(even, other, own)
        polar_2 = jnp.where(even, own, other)
    else:
        polar_1 = r1_ref[...].astype(F32)
        polar_2 = r2_ref[...].astype(F32)

    def ghost(kind, cols):
        line = jnp.concatenate([p[kind * lon : (kind + 1) * lon] for p in (polar_1, polar_m, polar_2)], axis=0)
        picks = [2 * lon - 1 - i for i in cols]
        return jnp.concatenate([line[k : k + 1] for k in picks], axis=0)

    zero = jnp.zeros((1, chans), F32)
    wide = list(range(-2, lon + 2))
    near = list(range(-1, lon + 1))
    g62, g63 = ghost(0, wide), ghost(1, wide)
    gt, gm = ghost(2, near), ghost(3, near)
    cols = [west[0:lat], west[lat : 2 * lat]]
    cols += [f_ref[0, i].astype(F32) * mask[i] for i in range(lon)]
    cols += [east[0:lat], east[lat : 2 * lat]]
    top = []
    for k, x in enumerate(cols):
        ss_ref[k, :, 0:chans] = shift_rows(x, -1, zero).astype(BF16)
        ss_ref[k, :, chans : 2 * chans] = x.astype(BF16)
        ss_ref[k, :, 2 * chans :] = shift_rows(x, 1, g63[k : k + 1]).astype(BF16)
        top.append(x[lat - 1 : lat])
    top = jnp.concatenate(top, axis=0)
    fold = jnp.concatenate([g62, g63, top], axis=1)
    total = None
    n = lon + 2
    pad = jnp.zeros((16 - n, 3 * chans), F32)
    for a in (-1, 0, 1):
        ghost_rows = jnp.concatenate([fold[1 - a : 1 - a + n], pad], axis=0).astype(BF16)
        piece = jnp.concatenate([ss_ref[a + 1 : a + 1 + n].reshape(n * lat, 3 * chans), ghost_rows], axis=0)
        part = dot(piece, w_ref[3 * (a + 1) : 3 * (a + 2)].reshape(3 * chans, chans))
        total = part if total is None else total + part
    first = total.astype(BF16)
    first_ref[...] = first
    own_first = first[lat : lat + lon * lat].astype(F32)
    own_mask = jnp.concatenate(mask, axis=0)
    kept = own_first * own_mask
    sums = jnp.sum(kept, axis=0, keepdims=True)
    squares = jnp.sum(kept * own_first, axis=0, keepdims=True)
    count = jnp.sum(own_mask, axis=0, keepdims=True)
    stat_ref[...] = jnp.concatenate([sums, squares, count, jnp.zeros((5, chans), F32)], axis=0)
    mask_ref[...] = jnp.concatenate(
        [west[3 * lat :], own_mask, east[3 * lat :], gm, jnp.zeros((16 - n, chans), F32)], axis=0
    ).astype(BF16)
    tcols = [west[2 * lat : 3 * lat]]
    tcols += [t_ref[0, i].astype(F32) * mask[i] for i in range(lon)]
    tcols += [east[2 * lat : 3 * lat]]
    for k, x in enumerate(tcols):
        tt_ref[k, :, 0:chans] = shift_rows(x, 1, zero).astype(BF16)
        tt_ref[k, :, chans : 2 * chans] = x.astype(BF16)
        tt_ref[k, :, 2 * chans :] = shift_rows(x, -1, zero).astype(BF16)
    tx_ref[...] = jnp.concatenate([gt, jnp.zeros((16 - n, chans), F32)], axis=0)


def adjoint_kernel(lon, lat, chans, tt_ref, tx_ref, wt_ref, dact_ref):
    gt = tx_ref[...]
    total = None
    for a in (-1, 0, 1):
        extra = jnp.concatenate([gt[1 + a : 1 + a + lon], jnp.zeros((16 - lon, chans), F32)], axis=0)
        extra = jnp.concatenate([jnp.zeros((16, 2 * chans), F32), extra], axis=1).astype(BF16)
        piece = jnp.concatenate([tt_ref[1 - a : 1 - a + lon].reshape(lon * lat, 3 * chans), extra], axis=0)
        part = dot(piece, wt_ref[a + 1])
        total = part if total is None else total + part
    rows = lax.broadcasted_iota(jnp.int32, (lat, chans), 0)
    for i in range(lon):
        add = total[lon * lat + i : lon * lat + i + 1]
        dact_ref[i * lat : (i + 1) * lat, :] = total[i * lat : (i + 1) * lat] + jnp.where(rows == lat - 1, add, 0.0)


def moments(stat_ref):
    count = stat_ref[2:3, :]
    mean = stat_ref[0:1, :] / count
    var = stat_ref[1:2, :] / count - mean * mean
    return count, mean, lax.rsqrt(var + 1e-05)


def act_kernel(lon, lat, chans, first_ref, mask_ref, stat_ref, gain_ref, offset_ref, dact_ref, gsum_ref, dpre_ref, aa_ref):
    count, mean, rstd = moments(stat_ref)
    gain, offset = gain_ref[...], offset_ref[...]

    def forward(lo, hi):
        xhat = (first_ref[lo:hi].astype(F32) - mean) * rstd
        u = gain * xhat + offset
        hyper = jnp.tanh(0.7978845608 * (u + 0.044715 * u * u * u))
        m = mask_ref[lo:hi].astype(F32)
        return xhat, u, hyper, m, 0.5 * u * (1.0 + hyper) * m

    n = lon + 2
    zero = jnp.zeros((1, chans), F32)
    ghost = forward(n * lat, n * lat + 16)[4]
    scale = lax.rsqrt(count)
    goff = jnp.zeros((1, chans), F32)
    ggain = jnp.zeros((1, chans), F32)
    for k in range(n):
        xhat, u, hyper, m, act = forward(k * lat, (k + 1) * lat)
        aa_ref[k, :, 0:chans] = shift_rows(act, -1, zero).astype(BF16)
        aa_ref[k, :, chans : 2 * chans] = act.astype(BF16)
        aa_ref[k, :, 2 * chans :] = shift_rows(act, 1, ghost[k : k + 1]).astype(BF16)
        if 0 < k <= lon:
            slope = 0.5 * (1.0 + hyper) + 0.5 * u * (1.0 - hyper * hyper) * 0.7978845608 * (
                1.0 + 3.0 * 0.044715 * u * u
            )
            rows = slice((k - 1) * lat, k * lat)
            dpre = dact_ref[rows] * scale * m * slope
            dpre_ref[rows] = dpre
            goff = goff + jnp.sum(dpre, axis=0, keepdims=True)
            ggain = ggain + jnp.sum(dpre * xhat, axis=0, keepdims=True)
    gsum_ref[...] = jnp.concatenate([goff, ggain, jnp.zeros((6, chans), F32)], axis=0)


def taps_t(grad, shifted_ref, base, lon, lat, chans):
    parts = []
    for a in (-1, 0, 1):
        piece = shifted_ref[base + a : base + a + lon].reshape(lon * lat, 3 * chans)
        parts.append(lax.dot_general(grad, piece, (((0,), (0,)), ((), ())), preferred_element_type=F32))
    return jnp.concatenate(parts, axis=1)


def out_kernel(lon, lat, chans, aa_ref, mask_ref, t_ref, stat_ref, w_ref, out_ref, grad_ref):
    total = None
    for a in (-1, 0, 1):
        piece = aa_ref[a + 1 : a + 1 + lon].reshape(lon * lat, 3 * chans)
        part = dot(piece, w_ref[3 * (a + 1) : 3 * (a + 2)].reshape(3 * chans, chans))
        total = part if total is None else total + part
    own_mask = mask_ref[lat : lat + lon * lat].astype(F32)
    out_ref[...] = (total * own_mask).astype(BF16).reshape(1, lon, lat, chans)
    scale = lax.rsqrt(stat_ref[2:3, :])
    dout = (t_ref[...].reshape(lon * lat, chans).astype(F32) * own_mask * scale).astype(BF16)
    grad_ref[...] = taps_t(dout, aa_ref, 1, lon, lat, chans).astype(BF16)


def in_kernel(lon, lat, chans, first_ref, mask_ref, stat_ref, gain_ref, dpre_ref, gsum_ref, ss_ref, grad_ref):
    count, mean, rstd = moments(stat_ref)
    goff, ggain = gsum_ref[0:1, :], gsum_ref[1:2, :]
    own = slice(lat, lat + lon * lat)
    xhat = (first_ref[own].astype(F32) - mean) * rstd
    dfirst = mask_ref[own].astype(F32) * (gain_ref[...] * rstd) * (dpre_ref[...] - (goff + xhat * ggain) / count)
    grad_ref[...] = taps_t(dfirst.astype(BF16), ss_ref, 2, lon, lat, chans).astype(BF16)


def last_kernel(chans, a_ref, b_ref, out_ref):
    total = a_ref[...].astype(F32) + b_ref[...].astype(F32)
    for t in range(9):
        out_ref[t] = total[:, t * chans : (t + 1) * chans].T


def xor_pairs(size, k):
    return [(i, i ^ k) for i in range(size)]


def all_sum(x, axis):
    size = lax.axis_size(axis)
    bit = 1
    while bit < size:
        other = lax.ppermute(x, axis, xor_pairs(size, bit))
        if 2 * bit < size:
            far = lax.ppermute(x, axis, xor_pairs(size, 2 * bit))
            both = lax.ppermute(x, axis, xor_pairs(size, 3 * bit))
            x = (x + other) + (far + both)
        else:
            x = x + other
        bit *= 4
    return x


def scatter_sum(x, axis):
    size = lax.axis_size(axis)
    me = lax.axis_index(axis)
    x = x.reshape(size, x.shape[0] // size, x.shape[1])
    bit = 1
    while bit < size:
        mine = (me // bit) % 2
        split = x.reshape(x.shape[0] // 2, 2, *x.shape[1:])
        keep = lax.dynamic_index_in_dim(split, mine, 1, keepdims=False)
        send = lax.dynamic_index_in_dim(split, 1 - mine, 1, keepdims=False)
        got = lax.ppermute(send, axis, xor_pairs(size, bit))
        x = (keep.astype(F32) + got.astype(F32)).astype(BF16)
        bit *= 2
    return x[0]


def space_sum(x, chans):
    size = lax.axis_size("space")
    bit = 1
    while 2 * bit < size:
        got = lax.ppermute(x, "space", xor_pairs(size, bit))
        x = (x.astype(F32) + got.astype(F32)).astype(BF16)
        bit *= 2
    got = lax.ppermute(x, "space", xor_pairs(size, bit))
    return run(functools.partial(last_kernel, chans), [sds((9, chans, x.shape[0]), F32)], [x, got], name="last")[0]


def body(fields, land, conv_in, conv_out, batchnorm_gain, batchnorm_offset, target_grad):
    lon, lat, chans = fields.shape[1:]
    tiles = lax.axis_size("space")
    sizes = (lon, lat, chans)
    cells = lon * lat
    gain, offset = batchnorm_gain[None, :], batchnorm_offset[None, :]
    n = lon + 2
    join = tiles == 4
    edge = 4 * lat
    pay_e, pay_o, polar = run(
        functools.partial(pack_kernel, *sizes, join),
        [sds((edge, chans), BF16), sds((edge + (4 * lon if join else 0), chans), BF16), sds((4 * lon, chans), BF16)],
        [fields, target_grad, land],
        name="pack",
    )
    mirror = [(i, tiles - 1 - i) for i in range(tiles)]
    got_o = lax.ppermute(pay_o, "space", [(i, (i - 1 if i % 2 == 0 else i + 1) % tiles) for i in range(tiles)])
    got_e = lax.ppermute(pay_e, "space", xor_pairs(tiles, 1))
    if join:
        got_x = lax.ppermute(polar, "space", xor_pairs(tiles, 2))
        poles = [got_o, got_x, got_x, polar]
    else:
        poles = [
            lax.ppermute(polar, "space", mirror),
            lax.ppermute(polar, "space", [(i, (tiles - 2 - i) % tiles) for i in range(tiles)]),
            lax.ppermute(polar, "space", [(i, (tiles - i) % tiles) for i in range(tiles)]),
            polar,
        ]

    def conv_body(*refs):
        refs = list(refs)
        if join:
            refs[7] = refs[6] = refs[6]
        conv_kernel(*sizes, edge if join else 0, *refs)

    rows = n * lat + 16
    first, mask, stat, ss, tt, tx = run(
        conv_body,
        [
            sds((rows, chans), BF16), sds((rows, chans), BF16), sds((8, chans), F32),
            sds((lon + 4, lat, 3 * chans), BF16), sds((n, lat, 3 * chans), BF16), sds((16, chans), F32),
        ],
        [fields, target_grad, land, got_e, got_o, *poles, conv_in],
        flops=2 * rows * 9 * chans * chans,
        name="conv",
    )
    wt = jnp.swapaxes(conv_out, 1, 2).reshape(3, 3 * chans, chans)
    stat = all_sum(all_sum(stat, "batch"), "space")
    dact = run(
        functools.partial(adjoint_kernel, *sizes),
        [sds((cells, chans), F32)],
        [tt, tx, wt],
        flops=2 * cells * 9 * chans * chans,
        name="adjoint",
    )[0]
    gsum, dpre, aa = run(
        functools.partial(act_kernel, *sizes),
        [sds((8, chans), F32), sds((cells, chans), F32), sds((n, lat, 3 * chans), BF16)],
        [first, mask, stat, gain, offset, dact],
        name="act",
    )
    gsum = all_sum(all_sum(gsum, "batch"), "space")
    output, part_out = run(
        functools.partial(out_kernel, *sizes),
        [sds((1, lon, lat, chans), BF16), sds((chans, 9 * chans), BF16)],
        [aa, mask, target_grad, stat, conv_out],
        flops=4 * cells * 9 * chans * chans,
        name="out",
    )
    grad_out = space_sum(scatter_sum(part_out, "batch"), chans)
    part_in = run(
        functools.partial(in_kernel, *sizes),
        [sds((chans, 9 * chans), BF16)],
        [first, mask, stat, gain, dpre, gsum, ss],
        flops=2 * cells * 9 * chans * chans,
        name="grad_in",
    )[0]
    grad_in = space_sum(scatter_sum(part_in, "batch"), chans)
    return (output, grad_in, grad_out, gsum[1], gsum[0])


def solution(mesh):
    in_specs = (
        P(("groups", "batch"), "space", None, None),
        P("space", None),
        P(),
        P(),
        P(),
        P(),
        P(("groups", "batch"), "space", None, None),
    )
    out_specs = (
        P(("groups", "batch"), "space", None, None),
        P("groups", None, "batch"),
        P("groups", None, "batch"),
        P("groups"),
        P("groups"),
    )
    return jax.shard_map(body, mesh=mesh, in_specs=in_specs, out_specs=out_specs, check_vma=False)
```

```python
import functools

import jax
import jax.numpy as jnp
from jax import lax
from jax.experimental import pallas as pl
from jax.experimental.pallas import tpu as pltpu
from jax.sharding import PartitionSpec as P

F32 = jnp.float32
BF16 = jnp.bfloat16
VMEM = pl.BlockSpec(memory_space=pltpu.VMEM)


def run(body, outs, args, scratch=(), flops=0, name=None):
    nbytes = sum(a.size * a.dtype.itemsize for a in args)
    nbytes += sum(o.size * o.dtype.itemsize for o in outs)
    return pl.pallas_call(
        body,
        out_shape=list(outs),
        in_specs=[VMEM] * len(args),
        out_specs=[VMEM] * len(outs),
        scratch_shapes=list(scratch),
        cost_estimate=pl.CostEstimate(flops=flops, bytes_accessed=nbytes, transcendentals=0),
        compiler_params=pltpu.CompilerParams(vmem_limit_bytes=24 << 20),
        name=name,
    )(*args)


def sds(shape, dtype):
    return jax.ShapeDtypeStruct(shape, dtype)


def dot(a, b):
    return jnp.dot(a, b, preferred_element_type=F32)


def column_mask(land_ref, lon, lat, chans):
    rows = lax.broadcasted_iota(jnp.int32, (lat, lat), 0)
    cols = lax.broadcasted_iota(jnp.int32, (lat, lat), 1)
    out = []
    for i in range(lon):
        line = jnp.broadcast_to(land_ref[i : i + 1, :].astype(F32), (lat, lat))
        col = jnp.sum(jnp.where(rows == cols, line, 0.0), axis=1, keepdims=True)
        out.append(jnp.broadcast_to(col, (lat, chans)))
    return out


def pack_kernel(lon, lat, chans, join, f_ref, t_ref, land_ref, e_ref, o_ref, p_ref):
    even = lax.rem(lax.axis_index("space"), 2) == 0
    mask = column_mask(land_ref, lon, lat, chans)

    def edge(cols_f, col):
        parts = [f_ref[0, i].astype(F32) * mask[i] for i in cols_f]
        parts += [t_ref[0, col].astype(F32) * mask[col], mask[col]]
        return jnp.concatenate(parts, axis=0).astype(BF16)

    west = edge((0, 1), 0)
    east = edge((lon - 2, lon - 1), lon - 1)
    n = west.shape[0]
    e_ref[...] = jnp.where(even, east, west)
    o_ref[0:n, :] = jnp.where(even, west, east)
    rows = []
    for j in (lat - 2, lat - 1):
        rows += [f_ref[0, i].astype(F32)[j : j + 1] * mask[i][j : j + 1] for i in range(lon)]
    rows += [t_ref[0, i].astype(F32)[lat - 1 : lat] * mask[i][lat - 1 : lat] for i in range(lon)]
    rows += [mask[i][lat - 1 : lat] for i in range(lon)]
    polar = jnp.concatenate(rows, axis=0).astype(BF16)
    p_ref[...] = polar
    if join:
        o_ref[n:, :] = polar


def shift_rows(x, step, fill):
    rows = lax.broadcasted_iota(jnp.int32, x.shape, 0)
    n = x.shape[0]
    moved = pltpu.roll(x, (-step) % n, 0)
    return jnp.where(rows == (n - 1 if step > 0 else 0), fill, moved)


def conv_kernel(
    lon, lat, chans, moff,
    f_ref, t_ref, land_ref, re_ref, ro_ref, rm_ref, r1_ref, r2_ref, own_ref, w_ref,
    first_ref, mask_ref, stat_ref, ss_ref, tt_ref, tx_ref,
):
    even = lax.rem(lax.axis_index("space"), 2) == 0
    mask = column_mask(land_ref, lon, lat, chans)
    recv_e = re_ref[...].astype(F32)
    recv_o = ro_ref[0 : recv_e.shape[0], :].astype(F32)
    west = jnp.where(even, recv_o, recv_e)
    east = jnp.where(even, recv_e, recv_o)
    polar_m = rm_ref[moff : moff + 4 * lon, :].astype(F32)
    if r1_ref is r2_ref:
        other = r1_ref[...].astype(F32)
        own = own_ref[...].astype(F32)
        polar_1 = jnp.where(even, other, own)
        polar_2 = jnp.where(even, own, other)
    else:
        polar_1 = r1_ref[...].astype(F32)
        polar_2 = r2_ref[...].astype(F32)

    def ghost(kind, cols):
        line = jnp.concatenate([p[kind * lon : (kind + 1) * lon] for p in (polar_1, polar_m, polar_2)], axis=0)
        picks = [2 * lon - 1 - i for i in cols]
        return jnp.concatenate([line[k : k + 1] for k in picks], axis=0)

    zero = jnp.zeros((1, chans), F32)
    wide = list(range(-2, lon + 2))
    near = list(range(-1, lon + 1))
    g62, g63 = ghost(0, wide), ghost(1, wide)
    gt, gm = ghost(2, near), ghost(3, near)
    cols = [west[0:lat], west[lat : 2 * lat]]
    cols += [f_ref[0, i].astype(F32) * mask[i] for i in range(lon)]
    cols += [east[0:lat], east[lat : 2 * lat]]
    top = []
    for k, x in enumerate(cols):
        ss_ref[k, :, 0:chans] = shift_rows(x, -1, zero).astype(BF16)
        ss_ref[k, :, chans : 2 * chans] = x.astype(BF16)
        ss_ref[k, :, 2 * chans :] = shift_rows(x, 1, g63[k : k + 1]).astype(BF16)
        top.append(x[lat - 1 : lat])
    top = jnp.concatenate(top, axis=0)
    fold = jnp.concatenate([g62, g63, top], axis=1)
    total = None
    n = lon + 2
    pad = jnp.zeros((16 - n, 3 * chans), F32)
    for a in (-1, 0, 1):
        ghost_rows = jnp.concatenate([fold[1 - a : 1 - a + n], pad], axis=0).astype(BF16)
        piece = jnp.concatenate([ss_ref[a + 1 : a + 1 + n].reshape(n * lat, 3 * chans), ghost_rows], axis=0)
        part = dot(piece, w_ref[3 * (a + 1) : 3 * (a + 2)].reshape(3 * chans, chans))
        total = part if total is None else total + part
    first = total.astype(BF16)
    first_ref[...] = first
    own_first = first[lat : lat + lon * lat].astype(F32)
    own_mask = jnp.concatenate(mask, axis=0)
    kept = own_first * own_mask
    sums = jnp.sum(kept, axis=0, keepdims=True)
    squares = jnp.sum(kept * own_first, axis=0, keepdims=True)
    count = jnp.sum(own_mask, axis=0, keepdims=True)
    stat_ref[...] = jnp.concatenate([sums, squares, count, jnp.zeros((5, chans), F32)], axis=0)
    mask_ref[...] = jnp.concatenate(
        [west[3 * lat :], own_mask, east[3 * lat :], gm, jnp.zeros((16 - n, chans), F32)], axis=0
    ).astype(BF16)
    tcols = [west[2 * lat : 3 * lat]]
    tcols += [t_ref[0, i].astype(F32) * mask[i] for i in range(lon)]
    tcols += [east[2 * lat : 3 * lat]]
    for k, x in enumerate(tcols):
        tt_ref[k, :, 0:chans] = shift_rows(x, 1, zero).astype(BF16)
        tt_ref[k, :, chans : 2 * chans] = x.astype(BF16)
        tt_ref[k, :, 2 * chans :] = shift_rows(x, -1, zero).astype(BF16)
    tx_ref[...] = jnp.concatenate([gt, jnp.zeros((16 - n, chans), F32)], axis=0)


def adjoint_kernel(lon, lat, chans, tt_ref, tx_ref, wt_ref, dact_ref):
    gt = tx_ref[...]
    total = None
    for a in (-1, 0, 1):
        extra = jnp.concatenate([gt[1 + a : 1 + a + lon], jnp.zeros((16 - lon, chans), F32)], axis=0)
        extra = jnp.concatenate([jnp.zeros((16, 2 * chans), F32), extra], axis=1).astype(BF16)
        piece = jnp.concatenate([tt_ref[1 - a : 1 - a + lon].reshape(lon * lat, 3 * chans), extra], axis=0)
        part = dot(piece, wt_ref[a + 1])
        total = part if total is None else total + part
    rows = lax.broadcasted_iota(jnp.int32, (lat, chans), 0)
    for i in range(lon):
        add = total[lon * lat + i : lon * lat + i + 1]
        dact_ref[i * lat : (i + 1) * lat, :] = total[i * lat : (i + 1) * lat] + jnp.where(rows == lat - 1, add, 0.0)


def moments(stat_ref):
    count = stat_ref[2:3, :]
    mean = stat_ref[0:1, :] / count
    var = stat_ref[1:2, :] / count - mean * mean
    return count, mean, lax.rsqrt(var + 1e-05)


def act_kernel(lon, lat, chans, first_ref, mask_ref, stat_ref, gain_ref, offset_ref, dact_ref, gsum_ref, dpre_ref, aa_ref):
    count, mean, rstd = moments(stat_ref)
    gain, offset = gain_ref[...], offset_ref[...]

    def forward(lo, hi):
        xhat = (first_ref[lo:hi].astype(F32) - mean) * rstd
        u = gain * xhat + offset
        hyper = jnp.tanh(0.7978845608 * (u + 0.044715 * u * u * u))
        m = mask_ref[lo:hi].astype(F32)
        return xhat, u, hyper, m, 0.5 * u * (1.0 + hyper) * m

    n = lon + 2
    zero = jnp.zeros((1, chans), F32)
    ghost = forward(n * lat, n * lat + 16)[4]
    scale = lax.rsqrt(count)
    goff = jnp.zeros((1, chans), F32)
    ggain = jnp.zeros((1, chans), F32)
    for k in range(n):
        xhat, u, hyper, m, act = forward(k * lat, (k + 1) * lat)
        aa_ref[k, :, 0:chans] = shift_rows(act, -1, zero).astype(BF16)
        aa_ref[k, :, chans : 2 * chans] = act.astype(BF16)
        aa_ref[k, :, 2 * chans :] = shift_rows(act, 1, ghost[k : k + 1]).astype(BF16)
        if 0 < k <= lon:
            slope = 0.5 * (1.0 + hyper) + 0.5 * u * (1.0 - hyper * hyper) * 0.7978845608 * (
                1.0 + 3.0 * 0.044715 * u * u
            )
            rows = slice((k - 1) * lat, k * lat)
            dpre = dact_ref[rows] * scale * m * slope
            dpre_ref[rows] = dpre
            goff = goff + jnp.sum(dpre, axis=0, keepdims=True)
            ggain = ggain + jnp.sum(dpre * xhat, axis=0, keepdims=True)
    gsum_ref[...] = jnp.concatenate([goff, ggain, jnp.zeros((6, chans), F32)], axis=0)


def put_taps(grad_ref, grad, shifted_ref, base, lon, lat, chans):
    chunks, width = grad_ref.shape[0], grad_ref.shape[2]
    for a in (-1, 0, 1):
        piece = shifted_ref[base + a : base + a + lon].reshape(lon * lat, 3 * chans)
        part = lax.dot_general(grad, piece, (((0,), (0,)), ((), ())), preferred_element_type=F32).astype(BF16)
        for b in range(3):
            for c in range(chunks):
                grad_ref[c, 3 * (a + 1) + b] = part[c * width : (c + 1) * width, b * chans : (b + 1) * chans]


def out_kernel(lon, lat, chans, aa_ref, mask_ref, t_ref, stat_ref, w_ref, out_ref, grad_ref):
    total = None
    for a in (-1, 0, 1):
        piece = aa_ref[a + 1 : a + 1 + lon].reshape(lon * lat, 3 * chans)
        part = dot(piece, w_ref[3 * (a + 1) : 3 * (a + 2)].reshape(3 * chans, chans))
        total = part if total is None else total + part
    own_mask = mask_ref[lat : lat + lon * lat].astype(F32)
    out_ref[...] = (total * own_mask).astype(BF16).reshape(1, lon, lat, chans)
    scale = lax.rsqrt(stat_ref[2:3, :])
    dout = (t_ref[...].reshape(lon * lat, chans).astype(F32) * own_mask * scale).astype(BF16)
    put_taps(grad_ref, dout, aa_ref, 1, lon, lat, chans)


def in_kernel(lon, lat, chans, first_ref, mask_ref, stat_ref, gain_ref, dpre_ref, gsum_ref, ss_ref, grad_ref):
    count, mean, rstd = moments(stat_ref)
    goff, ggain = gsum_ref[0:1, :], gsum_ref[1:2, :]
    own = slice(lat, lat + lon * lat)
    xhat = (first_ref[own].astype(F32) - mean) * rstd
    dfirst = mask_ref[own].astype(F32) * (gain_ref[...] * rstd) * (dpre_ref[...] - (goff + xhat * ggain) / count)
    put_taps(grad_ref, dfirst.astype(BF16), ss_ref, 2, lon, lat, chans)


def xor_pairs(size, k):
    return [(i, i ^ k) for i in range(size)]


def all_sum(x, axis):
    size = lax.axis_size(axis)
    bit = 1
    while bit < size:
        other = lax.ppermute(x, axis, xor_pairs(size, bit))
        if 2 * bit < size:
            far = lax.ppermute(x, axis, xor_pairs(size, 2 * bit))
            both = lax.ppermute(x, axis, xor_pairs(size, 3 * bit))
            x = (x + other) + (far + both)
        else:
            x = x + other
        bit *= 4
    return x


def scatter_sum(x, axis):
    size = lax.axis_size(axis)
    me = lax.axis_index(axis)
    bit = 1
    while bit < size:
        mine = (me // bit) % 2
        split = x.reshape(x.shape[0] // 2, 2, *x.shape[1:])
        keep = lax.dynamic_index_in_dim(split, mine, 1, keepdims=False)
        send = lax.dynamic_index_in_dim(split, 1 - mine, 1, keepdims=False)
        got = lax.ppermute(send, axis, xor_pairs(size, bit))
        x = (keep.astype(F32) + got.astype(F32)).astype(BF16)
        bit *= 2
    return x[0]


def space_sum(x):
    size = lax.axis_size("space")
    bit = 1
    while bit < size:
        got = lax.ppermute(x, "space", xor_pairs(size, bit))
        x = x.astype(F32) + got.astype(F32)
        bit *= 2
        if bit < size:
            x = x.astype(BF16)
    return jnp.swapaxes(x, 1, 2)


def body(fields, land, conv_in, conv_out, batchnorm_gain, batchnorm_offset, target_grad):
    lon, lat, chans = fields.shape[1:]
    tiles = lax.axis_size("space")
    sizes = (lon, lat, chans)
    cells = lon * lat
    gain, offset = batchnorm_gain[None, :], batchnorm_offset[None, :]
    n = lon + 2
    join = tiles == 4
    edge = 4 * lat
    shares = lax.axis_size("batch")
    taps = sds((shares, 9, chans // shares, chans), BF16)
    pay_e, pay_o, polar = run(
        functools.partial(pack_kernel, *sizes, join),
        [sds((edge, chans), BF16), sds((edge + (4 * lon if join else 0), chans), BF16), sds((4 * lon, chans), BF16)],
        [fields, target_grad, land],
        name="pack",
    )
    mirror = [(i, tiles - 1 - i) for i in range(tiles)]
    got_o = lax.ppermute(pay_o, "space", [(i, (i - 1 if i % 2 == 0 else i + 1) % tiles) for i in range(tiles)])
    got_e = lax.ppermute(pay_e, "space", xor_pairs(tiles, 1))
    if join:
        got_x = lax.ppermute(polar, "space", xor_pairs(tiles, 2))
        poles = [got_o, got_x, got_x, polar]
    else:
        poles = [
            lax.ppermute(polar, "space", mirror),
            lax.ppermute(polar, "space", [(i, (tiles - 2 - i) % tiles) for i in range(tiles)]),
            lax.ppermute(polar, "space", [(i, (tiles - i) % tiles) for i in range(tiles)]),
            polar,
        ]

    def conv_body(*refs):
        refs = list(refs)
        if join:
            refs[7] = refs[6] = refs[6]
        conv_kernel(*sizes, edge if join else 0, *refs)

    rows = n * lat + 16
    first, mask, stat, ss, tt, tx = run(
        conv_body,
        [
            sds((rows, chans), BF16), sds((rows, chans), BF16), sds((8, chans), F32),
            sds((lon + 4, lat, 3 * chans), BF16), sds((n, lat, 3 * chans), BF16), sds((16, chans), F32),
        ],
        [fields, target_grad, land, got_e, got_o, *poles, conv_in],
        flops=2 * rows * 9 * chans * chans,
        name="conv",
    )
    wt = jnp.swapaxes(conv_out, 1, 2).reshape(3, 3 * chans, chans)
    stat = all_sum(all_sum(stat, "batch"), "space")
    dact = run(
        functools.partial(adjoint_kernel, *sizes),
        [sds((cells, chans), F32)],
        [tt, tx, wt],
        flops=2 * cells * 9 * chans * chans,
        name="adjoint",
    )[0]
    gsum, dpre, aa = run(
        functools.partial(act_kernel, *sizes),
        [sds((8, chans), F32), sds((cells, chans), F32), sds((n, lat, 3 * chans), BF16)],
        [first, mask, stat, gain, offset, dact],
        name="act",
    )
    gsum = all_sum(all_sum(gsum, "batch"), "space")
    output, part_out = run(
        functools.partial(out_kernel, *sizes),
        [sds((1, lon, lat, chans), BF16), taps],
        [aa, mask, target_grad, stat, conv_out],
        flops=4 * cells * 9 * chans * chans,
        name="out",
    )
    grad_out = space_sum(scatter_sum(part_out, "batch"))
    part_in = run(
        functools.partial(in_kernel, *sizes),
        [taps],
        [first, mask, stat, gain, dpre, gsum, ss],
        flops=2 * cells * 9 * chans * chans,
        name="grad_in",
    )[0]
    grad_in = space_sum(scatter_sum(part_in, "batch"))
    return (output, grad_in, grad_out, gsum[1], gsum[0])


def solution(mesh):
    in_specs = (
        P(("groups", "batch"), "space", None, None),
        P("space", None),
        P(),
        P(),
        P(),
        P(),
        P(("groups", "batch"), "space", None, None),
    )
    out_specs = (
        P(("groups", "batch"), "space", None, None),
        P("groups", None, "batch"),
        P("groups", None, "batch"),
        P("groups"),
        P("groups"),
    )
    return jax.shard_map(body, mesh=mesh, in_specs=in_specs, out_specs=out_specs, check_vma=False)
```

```python
import functools

import jax
import jax.numpy as jnp
from jax import lax
from jax.experimental import pallas as pl
from jax.experimental.pallas import tpu as pltpu
from jax.sharding import PartitionSpec as P

F32 = jnp.float32
BF16 = jnp.bfloat16
VMEM = pl.BlockSpec(memory_space=pltpu.VMEM)


def run(body, outs, args, scratch=(), flops=0, name=None, space=VMEM, alias=None):
    nbytes = sum(a.size * a.dtype.itemsize for a in args)
    nbytes += sum(o.size * o.dtype.itemsize for o in outs)
    return pl.pallas_call(
        body,
        out_shape=list(outs),
        in_specs=[space] * len(args),
        out_specs=[VMEM] * len(outs),
        scratch_shapes=list(scratch),
        cost_estimate=pl.CostEstimate(flops=flops, bytes_accessed=nbytes, transcendentals=0),
        compiler_params=pltpu.CompilerParams(vmem_limit_bytes=24 << 20),
        input_output_aliases=alias or {},
        name=name,
    )(*args)


def sds(shape, dtype):
    return jax.ShapeDtypeStruct(shape, dtype)


def dot(a, b):
    return jnp.dot(a, b, preferred_element_type=F32)


def spread(line, lat, chans):
    rows = lax.broadcasted_iota(jnp.int32, (lat, lat), 0)
    cols = lax.broadcasted_iota(jnp.int32, (lat, lat), 1)
    col = jnp.sum(jnp.where(rows == cols, jnp.broadcast_to(line, (lat, lat)), 0.0), axis=1, keepdims=True)
    return jnp.broadcast_to(col, (lat, chans))


def pack_kernel(lon, lat, chans, join, f_hbm, t_hbm, land_hbm, e_ref, o_ref, p_ref, fc, fr, tc, tr, land, sems):
    copies = [
        pltpu.make_async_copy(f_hbm.at[0, 0:2], fc.at[0:2], sems.at[0]),
        pltpu.make_async_copy(f_hbm.at[0, lon - 2 : lon], fc.at[2:4], sems.at[1]),
        pltpu.make_async_copy(f_hbm.at[0, :, lat - 8 : lat], fr, sems.at[2]),
        pltpu.make_async_copy(t_hbm.at[0, 0:1], tc.at[0:1], sems.at[3]),
        pltpu.make_async_copy(t_hbm.at[0, lon - 1 : lon], tc.at[1:2], sems.at[4]),
        pltpu.make_async_copy(t_hbm.at[0, :, lat - 8 : lat], tr, sems.at[5]),
        pltpu.make_async_copy(land_hbm, land, sems.at[6]),
    ]
    for c in copies:
        c.start()
    even = lax.rem(lax.axis_index("space"), 2) == 0
    for c in copies:
        c.wait()
    lines = land[...].astype(F32)

    def edge(k, cols_f, side):
        masks = [spread(lines[i : i + 1], lat, chans) for i in cols_f]
        parts = [fc[k + n].astype(F32) * m for n, m in enumerate(masks)]
        col = cols_f[0] if side == 0 else cols_f[1]
        parts.append(tc[side].astype(F32) * masks[0 if side == 0 else 1])
        line = jnp.concatenate([lines[col : col + 1], jnp.zeros((1, chans - lat), F32)], axis=1)
        parts += [line, jnp.zeros((15, chans), F32)]
        return jnp.concatenate(parts, axis=0).astype(BF16)

    west = edge(0, (0, 1), 0)
    east = edge(2, (lon - 2, lon - 1), 1)
    n = west.shape[0]
    e_ref[...] = jnp.where(even, east, west)
    o_ref[0:n, :] = jnp.where(even, west, east)
    lane = lax.broadcasted_iota(jnp.int32, (lon, lat), 1)
    last = {}
    for j in (lat - 2, lat - 1):
        col = jnp.sum(jnp.where(lane == j, lines, 0.0), axis=1, keepdims=True)
        last[j] = jnp.broadcast_to(col, (lon, chans))
    rows = []
    for j, ref in ((lat - 2, fr), (lat - 1, fr), (lat - 1, tr)):
        k = j - (lat - 8)
        line = jnp.concatenate([ref[i].astype(F32)[k : k + 1] for i in range(lon)], axis=0)
        rows.append(line * last[j])
    rows.append(last[lat - 1])
    polar = jnp.concatenate(rows, axis=0).astype(BF16)
    p_ref[...] = polar
    if join:
        o_ref[n:, :] = polar


def shift_rows(x, step, fill):
    rows = lax.broadcasted_iota(jnp.int32, x.shape, 0)
    n = x.shape[0]
    moved = pltpu.roll(x, (-step) % n, 0)
    return jnp.where(rows == (n - 1 if step > 0 else 0), fill, moved)


def prep_kernel(
    lon, lat, chans,
    f_hbm, t_hbm, land_hbm, win_hbm, wout_hbm, gain_hbm, offset_hbm,
    ss_ref, tt_ref, mask_ref, win_ref, wout_ref, wt_ref, bn_ref,
    f_ref, t_ref, land_ref, sems,
):
    pairs = [
        (land_hbm, land_ref), (f_hbm, f_ref), (t_hbm, t_ref), (wout_hbm, wout_ref), (win_hbm, win_ref),
        (gain_hbm, bn_ref.at[0:1]), (offset_hbm, bn_ref.at[1:2]),
    ]
    copies = [pltpu.make_async_copy(src, dst, sems.at[i]) for i, (src, dst) in enumerate(pairs)]
    for c in copies:
        c.start()
    for c in copies[:3]:
        c.wait()
    lines = land_ref[...].astype(F32)
    zero = jnp.zeros((1, chans), F32)
    for i in range(lon):
        mask = spread(lines[i : i + 1], lat, chans)
        mask_ref[i * lat : (i + 1) * lat] = mask.astype(BF16)
        x = f_ref[0, i].astype(F32) * mask
        ss_ref[i + 2, :, 0:chans] = shift_rows(x, -1, zero).astype(BF16)
        ss_ref[i + 2, :, chans : 2 * chans] = x.astype(BF16)
        ss_ref[i + 2, :, 2 * chans :] = shift_rows(x, 1, zero).astype(BF16)
        x = t_ref[0, i].astype(F32) * mask
        tt_ref[i + 1, :, 0:chans] = shift_rows(x, 1, zero).astype(BF16)
        tt_ref[i + 1, :, chans : 2 * chans] = x.astype(BF16)
        tt_ref[i + 1, :, 2 * chans :] = shift_rows(x, -1, zero).astype(BF16)
    for c in copies[3:]:
        c.wait()
    for a in range(3):
        for b in range(3):
            wt_ref[a, b * chans : (b + 1) * chans] = wout_ref[3 * a + b].T


def conv_kernel(
    lon, lat, chans, moff,
    re_ref, ro_ref, rm_ref, r1_ref, r2_ref, own_ref, ss_in, tt_in, om_ref, w_ref,
    ss_ref, tt_ref, first_ref, mask_ref, stat_ref, tx_ref,
):
    even = lax.rem(lax.axis_index("space"), 2) == 0
    recv_e = re_ref[...].astype(F32)
    recv_o = ro_ref[0 : recv_e.shape[0], :].astype(F32)
    west = jnp.where(even, recv_o, recv_e)
    east = jnp.where(even, recv_e, recv_o)
    polar_m = rm_ref[moff : moff + 4 * lon, :].astype(F32)
    if r1_ref is r2_ref:
        other = r1_ref[...].astype(F32)
        own = own_ref[...].astype(F32)
        polar_1 = jnp.where(even, other, own)
        polar_2 = jnp.where(even, own, other)
    else:
        polar_1 = r1_ref[...].astype(F32)
        polar_2 = r2_ref[...].astype(F32)

    def ghost(kind, cols):
        line = jnp.concatenate([p[kind * lon : (kind + 1) * lon] for p in (polar_1, polar_m, polar_2)], axis=0)
        picks = [2 * lon - 1 - i for i in cols]
        return jnp.concatenate([line[k : k + 1] for k in picks], axis=0)

    zero = jnp.zeros((1, chans), F32)
    wide = list(range(-2, lon + 2))
    near = list(range(-1, lon + 1))
    g62, g63 = ghost(0, wide), ghost(1, wide)
    gt, gm = ghost(2, near), ghost(3, near)
    halo = {0: west[0:lat], 1: west[lat : 2 * lat], lon + 2: east[0:lat], lon + 3: east[lat : 2 * lat]}
    rows8 = lax.broadcasted_iota(jnp.int32, (8, chans), 0)
    top = []
    for k in range(lon + 4):
        fill = g63[k : k + 1]
        if k in halo:
            x = halo[k]
            ss_ref[k, :, 0:chans] = shift_rows(x, -1, zero).astype(BF16)
            ss_ref[k, :, chans : 2 * chans] = x.astype(BF16)
            ss_ref[k, :, 2 * chans :] = shift_rows(x, 1, fill).astype(BF16)
            top.append(x[lat - 1 : lat])
        else:
            tail = ss_ref[k, lat - 8 :, chans : 2 * chans].astype(F32)
            top.append(tail[7:8])
            ss_ref[k, lat - 8 :, 2 * chans :] = shift_rows(tail, 1, fill).astype(BF16)
    top = jnp.concatenate(top, axis=0)
    fold = jnp.concatenate([g62, g63, top], axis=1)
    total = None
    n = lon + 2
    pad = jnp.zeros((16 - n, 3 * chans), F32)
    for a in (-1, 0, 1):
        ghost_rows = jnp.concatenate([fold[1 - a : 1 - a + n], pad], axis=0).astype(BF16)
        piece = jnp.concatenate([ss_ref[a + 1 : a + 1 + n].reshape(n * lat, 3 * chans), ghost_rows], axis=0)
        part = dot(piece, w_ref[3 * (a + 1) : 3 * (a + 2)].reshape(3 * chans, chans))
        total = part if total is None else total + part
    first = total.astype(BF16)
    first_ref[...] = first
    own_first = first[lat : lat + lon * lat].astype(F32)
    own_mask = om_ref[...].astype(F32)
    kept = own_first * own_mask
    sums = jnp.sum(kept, axis=0, keepdims=True)
    squares = jnp.sum(kept * own_first, axis=0, keepdims=True)
    count = jnp.sum(own_mask, axis=0, keepdims=True)
    stat_ref[...] = jnp.concatenate([sums, squares, count, jnp.zeros((5, chans), F32)], axis=0)
    edges = [spread(x[3 * lat : 3 * lat + 1, 0:lat], lat, chans) for x in (west, east)]
    mask_ref[0:lat] = edges[0].astype(BF16)
    mask_ref[lat : lat + lon * lat] = om_ref[...]
    mask_ref[lat + lon * lat : n * lat] = edges[1].astype(BF16)
    mask_ref[n * lat :] = jnp.concatenate([gm, jnp.zeros((16 - n, chans), F32)], axis=0).astype(BF16)
    for k, x in ((0, west[2 * lat : 3 * lat]), (lon + 1, east[2 * lat : 3 * lat])):
        tt_ref[k, :, 0:chans] = shift_rows(x, 1, zero).astype(BF16)
        tt_ref[k, :, chans : 2 * chans] = x.astype(BF16)
        tt_ref[k, :, 2 * chans :] = shift_rows(x, -1, zero).astype(BF16)
    tx_ref[...] = jnp.concatenate([gt, jnp.zeros((16 - n, chans), F32)], axis=0)


def adjoint_kernel(lon, lat, chans, tt_ref, tx_ref, wt_ref, dact_ref):
    gt = tx_ref[...]
    total = None
    for a in (-1, 0, 1):
        extra = jnp.concatenate([gt[1 + a : 1 + a + lon], jnp.zeros((16 - lon, chans), F32)], axis=0)
        extra = jnp.concatenate([jnp.zeros((16, 2 * chans), F32), extra], axis=1).astype(BF16)
        piece = jnp.concatenate([tt_ref[1 - a : 1 - a + lon].reshape(lon * lat, 3 * chans), extra], axis=0)
        part = dot(piece, wt_ref[a + 1])
        total = part if total is None else total + part
    rows = lax.broadcasted_iota(jnp.int32, (lat, chans), 0)
    for i in range(lon):
        add = total[lon * lat + i : lon * lat + i + 1]
        dact_ref[i * lat : (i + 1) * lat, :] = total[i * lat : (i + 1) * lat] + jnp.where(rows == lat - 1, add, 0.0)


def moments(stat_ref):
    count = stat_ref[2:3, :]
    mean = stat_ref[0:1, :] / count
    var = stat_ref[1:2, :] / count - mean * mean
    return count, mean, lax.rsqrt(var + 1e-05)


def act_kernel(lon, lat, chans, first_ref, mask_ref, stat_ref, bn_ref, dact_ref, gsum_ref, dpre_ref, aa_ref):
    count, mean, rstd = moments(stat_ref)
    gain, offset = bn_ref[0:1, :], bn_ref[1:2, :]

    def forward(lo, hi):
        xhat = (first_ref[lo:hi].astype(F32) - mean) * rstd
        u = gain * xhat + offset
        hyper = jnp.tanh(0.7978845608 * (u + 0.044715 * u * u * u))
        m = mask_ref[lo:hi].astype(F32)
        return xhat, u, hyper, m, 0.5 * u * (1.0 + hyper) * m

    n = lon + 2
    zero = jnp.zeros((1, chans), F32)
    ghost = forward(n * lat, n * lat + 16)[4]
    scale = lax.rsqrt(count)
    goff = jnp.zeros((1, chans), F32)
    ggain = jnp.zeros((1, chans), F32)
    for k in range(n):
        xhat, u, hyper, m, act = forward(k * lat, (k + 1) * lat)
        aa_ref[k, :, 0:chans] = shift_rows(act, -1, zero).astype(BF16)
        aa_ref[k, :, chans : 2 * chans] = act.astype(BF16)
        aa_ref[k, :, 2 * chans :] = shift_rows(act, 1, ghost[k : k + 1]).astype(BF16)
        if 0 < k <= lon:
            slope = 0.5 * (1.0 + hyper) + 0.5 * u * (1.0 - hyper * hyper) * 0.7978845608 * (
                1.0 + 3.0 * 0.044715 * u * u
            )
            rows = slice((k - 1) * lat, k * lat)
            dpre = dact_ref[rows] * scale * m * slope
            dpre_ref[rows] = dpre
            goff = goff + jnp.sum(dpre, axis=0, keepdims=True)
            ggain = ggain + jnp.sum(dpre * xhat, axis=0, keepdims=True)
    gsum_ref[...] = jnp.concatenate([goff, ggain, jnp.zeros((6, chans), F32)], axis=0)


def put_taps(grad_ref, grad, shifted_ref, base, lon, lat, chans):
    chunks, width = grad_ref.shape[0], grad_ref.shape[2]
    for a in (-1, 0, 1):
        piece = shifted_ref[base + a : base + a + lon].reshape(lon * lat, 3 * chans)
        part = lax.dot_general(grad, piece, (((0,), (0,)), ((), ())), preferred_element_type=F32).astype(BF16)
        for b in range(3):
            for c in range(chunks):
                grad_ref[c, 3 * (a + 1) + b] = part[c * width : (c + 1) * width, b * chans : (b + 1) * chans]


def out_kernel(lon, lat, chans, aa_ref, mask_ref, tt_ref, stat_ref, w_ref, out_ref, grad_ref):
    total = None
    for a in (-1, 0, 1):
        piece = aa_ref[a + 1 : a + 1 + lon].reshape(lon * lat, 3 * chans)
        part = dot(piece, w_ref[3 * (a + 1) : 3 * (a + 2)].reshape(3 * chans, chans))
        total = part if total is None else total + part
    own_mask = mask_ref[lat : lat + lon * lat].astype(F32)
    out_ref[...] = (total * own_mask).astype(BF16).reshape(1, lon, lat, chans)
    scale = lax.rsqrt(stat_ref[2:3, :])
    target = tt_ref[1 : 1 + lon, :, chans : 2 * chans].reshape(lon * lat, chans).astype(F32)
    dout = (target * scale).astype(BF16)
    put_taps(grad_ref, dout, aa_ref, 1, lon, lat, chans)


def in_kernel(lon, lat, chans, first_ref, mask_ref, stat_ref, bn_ref, dpre_ref, gsum_ref, ss_ref, grad_ref):
    count, mean, rstd = moments(stat_ref)
    goff, ggain = gsum_ref[0:1, :], gsum_ref[1:2, :]
    own = slice(lat, lat + lon * lat)
    xhat = (first_ref[own].astype(F32) - mean) * rstd
    dfirst = mask_ref[own].astype(F32) * (bn_ref[0:1, :] * rstd) * (dpre_ref[...] - (goff + xhat * ggain) / count)
    put_taps(grad_ref, dfirst.astype(BF16), ss_ref, 2, lon, lat, chans)


def xor_pairs(size, k):
    return [(i, i ^ k) for i in range(size)]


def all_sum(x, axis):
    size = lax.axis_size(axis)
    bit = 1
    while bit < size:
        other = lax.ppermute(x, axis, xor_pairs(size, bit))
        if 2 * bit < size:
            far = lax.ppermute(x, axis, xor_pairs(size, 2 * bit))
            both = lax.ppermute(x, axis, xor_pairs(size, 3 * bit))
            x = (x + other) + (far + both)
        else:
            x = x + other
        bit *= 4
    return x


def scatter_sum(x, axis):
    size = lax.axis_size(axis)
    me = lax.axis_index(axis)
    bit = 1
    while bit < size:
        mine = (me // bit) % 2
        split = x.reshape(x.shape[0] // 2, 2, *x.shape[1:])
        keep = lax.dynamic_index_in_dim(split, mine, 1, keepdims=False)
        send = lax.dynamic_index_in_dim(split, 1 - mine, 1, keepdims=False)
        got = lax.ppermute(send, axis, xor_pairs(size, bit))
        x = (keep.astype(F32) + got.astype(F32)).astype(BF16)
        bit *= 2
    return x[0]


def space_sum(x):
    size = lax.axis_size("space")
    bit = 1
    while bit < size:
        got = lax.ppermute(x, "space", xor_pairs(size, bit))
        x = x.astype(F32) + got.astype(F32)
        bit *= 2
        if bit < size:
            x = x.astype(BF16)
    return jnp.swapaxes(x, 1, 2)


def body(fields, land, conv_in, conv_out, batchnorm_gain, batchnorm_offset, target_grad):
    lon, lat, chans = fields.shape[1:]
    tiles = lax.axis_size("space")
    sizes = (lon, lat, chans)
    cells = lon * lat
    gain, offset = batchnorm_gain[None, :], batchnorm_offset[None, :]
    fields, land, conv_in, conv_out, target_grad, gain, offset = (
        pltpu.with_memory_space_constraint(x, pltpu.HBM)
        for x in (fields, land, conv_in, conv_out, target_grad, gain, offset)
    )
    n = lon + 2
    join = tiles == 4
    edge = 3 * lat + 16
    shares = lax.axis_size("batch")
    taps = sds((shares, 9, chans // shares, chans), BF16)
    pay_e, pay_o, polar = run(
        functools.partial(pack_kernel, *sizes, join),
        [sds((edge, chans), BF16), sds((edge + (4 * lon if join else 0), chans), BF16), sds((4 * lon, chans), BF16)],
        [fields, target_grad, land],
        scratch=[
            pltpu.VMEM((4, lat, chans), BF16), pltpu.VMEM((lon, 8, chans), BF16),
            pltpu.VMEM((2, lat, chans), BF16), pltpu.VMEM((lon, 8, chans), BF16),
            pltpu.VMEM((lon, lat), jnp.int32), pltpu.SemaphoreType.DMA((7,)),
        ],
        name="pack",
        space=pl.BlockSpec(memory_space=pltpu.HBM),
    )
    mirror = [(i, tiles - 1 - i) for i in range(tiles)]
    got_o = lax.ppermute(pay_o, "space", [(i, (i - 1 if i % 2 == 0 else i + 1) % tiles) for i in range(tiles)])
    got_e = lax.ppermute(pay_e, "space", xor_pairs(tiles, 1))
    if join:
        got_x = lax.ppermute(polar, "space", xor_pairs(tiles, 2))
        poles = [got_o, got_x, got_x, polar]
    else:
        poles = [
            lax.ppermute(polar, "space", mirror),
            lax.ppermute(polar, "space", [(i, (tiles - 2 - i) % tiles) for i in range(tiles)]),
            lax.ppermute(polar, "space", [(i, (tiles - i) % tiles) for i in range(tiles)]),
            polar,
        ]
    wide = sds((lon + 4, lat, 3 * chans), BF16)
    near = sds((n, lat, 3 * chans), BF16)
    ss, tt, own_mask, win, wout, wt, bn = run(
        functools.partial(prep_kernel, *sizes),
        [
            wide, near, sds((cells, chans), BF16), sds(conv_in.shape, BF16), sds(conv_out.shape, BF16),
            sds((3, 3 * chans, chans), BF16), sds((8, chans), F32),
        ],
        [fields, target_grad, land, conv_in, conv_out, gain, offset],
        scratch=[
            pltpu.VMEM(fields.shape, BF16), pltpu.VMEM(fields.shape, BF16), pltpu.VMEM(land.shape, jnp.int32),
            pltpu.SemaphoreType.DMA((7,)),
        ],
        name="prep",
        space=pl.BlockSpec(memory_space=pltpu.HBM),
    )

    def conv_body(*refs):
        refs = list(refs)
        if join:
            refs[4] = refs[3]
        conv_kernel(*sizes, edge if join else 0, *refs)

    rows = n * lat + 16
    ss, tt, first, mask, stat, tx = run(
        conv_body,
        [wide, near, sds((rows, chans), BF16), sds((rows, chans), BF16), sds((8, chans), F32), sds((16, chans), F32)],
        [got_e, got_o, *poles, ss, tt, own_mask, win],
        flops=2 * rows * 9 * chans * chans,
        name="conv",
        alias={6: 0, 7: 1},
    )
    stat = all_sum(all_sum(stat, "batch"), "space")
    dact = run(
        functools.partial(adjoint_kernel, *sizes),
        [sds((cells, chans), F32)],
        [tt, tx, wt],
        flops=2 * cells * 9 * chans * chans,
        name="adjoint",
    )[0]
    gsum, dpre, aa = run(
        functools.partial(act_kernel, *sizes),
        [sds((8, chans), F32), sds((cells, chans), F32), sds((n, lat, 3 * chans), BF16)],
        [first, mask, stat, bn, dact],
        name="act",
    )
    gsum = all_sum(all_sum(gsum, "batch"), "space")
    output, part_out = run(
        functools.partial(out_kernel, *sizes),
        [sds((1, lon, lat, chans), BF16), taps],
        [aa, mask, tt, stat, wout],
        flops=4 * cells * 9 * chans * chans,
        name="out",
    )
    grad_out = space_sum(scatter_sum(part_out, "batch"))
    part_in = run(
        functools.partial(in_kernel, *sizes),
        [taps],
        [first, mask, stat, bn, dpre, gsum, ss],
        flops=2 * cells * 9 * chans * chans,
        name="grad_in",
    )[0]
    grad_in = space_sum(scatter_sum(part_in, "batch"))
    return (output, grad_in, grad_out, gsum[1], gsum[0])


def solution(mesh):
    in_specs = (
        P(("groups", "batch"), "space", None, None),
        P("space", None),
        P(),
        P(),
        P(),
        P(),
        P(("groups", "batch"), "space", None, None),
    )
    out_specs = (
        P(("groups", "batch"), "space", None, None),
        P("groups", None, "batch"),
        P("groups", None, "batch"),
        P("groups"),
        P("groups"),
    )
    return jax.shard_map(body, mesh=mesh, in_specs=in_specs, out_specs=out_specs, check_vma=False)
```

```python
import functools

import jax
import jax.numpy as jnp
from jax import lax
from jax.experimental import pallas as pl
from jax.experimental.pallas import tpu as pltpu
from jax.sharding import PartitionSpec as P

F32 = jnp.float32
BF16 = jnp.bfloat16
VMEM = pl.BlockSpec(memory_space=pltpu.VMEM)


def run(body, outs, args, scratch=(), flops=0, name=None, space=VMEM, alias=None):
    nbytes = sum(a.size * a.dtype.itemsize for a in args)
    nbytes += sum(o.size * o.dtype.itemsize for o in outs)
    return pl.pallas_call(
        body,
        out_shape=list(outs),
        in_specs=[space] * len(args),
        out_specs=[VMEM] * len(outs),
        scratch_shapes=list(scratch),
        cost_estimate=pl.CostEstimate(flops=flops, bytes_accessed=nbytes, transcendentals=0),
        compiler_params=pltpu.CompilerParams(vmem_limit_bytes=24 << 20),
        input_output_aliases=alias or {},
        name=name,
    )(*args)


def sds(shape, dtype):
    return jax.ShapeDtypeStruct(shape, dtype)


def dot(a, b):
    return jnp.dot(a, b, preferred_element_type=F32)


def spread(line, lat, chans):
    rows = lax.broadcasted_iota(jnp.int32, (lat, lat), 0)
    cols = lax.broadcasted_iota(jnp.int32, (lat, lat), 1)
    col = jnp.sum(jnp.where(rows == cols, jnp.broadcast_to(line, (lat, lat)), 0.0), axis=1, keepdims=True)
    return jnp.broadcast_to(col, (lat, chans))


def pack_kernel(lon, lat, chans, join, f_hbm, t_hbm, land_hbm, e_ref, o_ref, p_ref, fc, fr, tc, tr, land, sems):
    copies = [
        pltpu.make_async_copy(f_hbm.at[0, 0:2], fc.at[0:2], sems.at[0]),
        pltpu.make_async_copy(f_hbm.at[0, lon - 2 : lon], fc.at[2:4], sems.at[1]),
        pltpu.make_async_copy(f_hbm.at[0, :, lat - 8 : lat], fr, sems.at[2]),
        pltpu.make_async_copy(t_hbm.at[0, 0:1], tc.at[0:1], sems.at[3]),
        pltpu.make_async_copy(t_hbm.at[0, lon - 1 : lon], tc.at[1:2], sems.at[4]),
        pltpu.make_async_copy(t_hbm.at[0, :, lat - 8 : lat], tr, sems.at[5]),
        pltpu.make_async_copy(land_hbm, land, sems.at[6]),
    ]
    for c in copies:
        c.start()
    even = lax.rem(lax.axis_index("space"), 2) == 0
    for c in copies:
        c.wait()
    lines = land[...].astype(F32)

    def edge(k, cols_f, side):
        masks = [spread(lines[i : i + 1], lat, chans) for i in cols_f]
        parts = [fc[k + n].astype(F32) * m for n, m in enumerate(masks)]
        col = cols_f[0] if side == 0 else cols_f[1]
        parts.append(tc[side].astype(F32) * masks[0 if side == 0 else 1])
        line = jnp.concatenate([lines[col : col + 1], jnp.zeros((1, chans - lat), F32)], axis=1)
        parts += [line, jnp.zeros((15, chans), F32)]
        return jnp.concatenate(parts, axis=0).astype(BF16)

    west = edge(0, (0, 1), 0)
    east = edge(2, (lon - 2, lon - 1), 1)
    n = west.shape[0]
    e_ref[...] = jnp.where(even, east, west)
    o_ref[0:n, :] = jnp.where(even, west, east)
    lane = lax.broadcasted_iota(jnp.int32, (lon, lat), 1)
    last = {}
    for j in (lat - 2, lat - 1):
        col = jnp.sum(jnp.where(lane == j, lines, 0.0), axis=1, keepdims=True)
        last[j] = jnp.broadcast_to(col, (lon, chans))
    rows = []
    for j, ref in ((lat - 2, fr), (lat - 1, fr), (lat - 1, tr)):
        k = j - (lat - 8)
        line = jnp.concatenate([ref[i].astype(F32)[k : k + 1] for i in range(lon)], axis=0)
        rows.append(line * last[j])
    rows.append(last[lat - 1])
    polar = jnp.concatenate(rows, axis=0).astype(BF16)
    p_ref[...] = polar
    if join:
        o_ref[n:, :] = polar


def shift_rows(x, step, fill):
    rows = lax.broadcasted_iota(jnp.int32, x.shape, 0)
    n = x.shape[0]
    moved = pltpu.roll(x, (-step) % n, 0)
    return jnp.where(rows == (n - 1 if step > 0 else 0), fill, moved)


def prep_kernel(
    lon, lat, chans,
    f_hbm, t_hbm, land_hbm, win_hbm, wout_hbm, gain_hbm, offset_hbm,
    ss_ref, tt_ref, mask_ref, win_ref, wout_ref, wt_ref, bn_ref,
    f_ref, t_ref, land_ref, sems,
):
    pairs = [
        (land_hbm, land_ref), (f_hbm, f_ref), (t_hbm, t_ref), (wout_hbm, wout_ref), (win_hbm, win_ref),
        (gain_hbm, bn_ref.at[0:1]), (offset_hbm, bn_ref.at[1:2]),
    ]
    copies = [pltpu.make_async_copy(src, dst, sems.at[i]) for i, (src, dst) in enumerate(pairs)]
    for c in copies:
        c.start()
    for c in copies[:3]:
        c.wait()
    lines = land_ref[...].astype(F32)
    zero = jnp.zeros((1, chans), F32)
    for i in range(lon):
        mask = spread(lines[i : i + 1], lat, chans)
        mask_ref[i * lat : (i + 1) * lat] = mask.astype(BF16)
        x = f_ref[0, i].astype(F32) * mask
        ss_ref[i + 2, :, 0:chans] = shift_rows(x, -1, zero).astype(BF16)
        ss_ref[i + 2, :, chans : 2 * chans] = x.astype(BF16)
        ss_ref[i + 2, :, 2 * chans :] = shift_rows(x, 1, zero).astype(BF16)
        x = t_ref[0, i].astype(F32) * mask
        tt_ref[i + 1, :, 0:chans] = shift_rows(x, 1, zero).astype(BF16)
        tt_ref[i + 1, :, chans : 2 * chans] = x.astype(BF16)
        tt_ref[i + 1, :, 2 * chans :] = shift_rows(x, -1, zero).astype(BF16)
    for c in copies[3:]:
        c.wait()
    for a in range(3):
        for b in range(3):
            wt_ref[a, b * chans : (b + 1) * chans] = wout_ref[3 * a + b].T


def conv_kernel(
    lon, lat, chans, moff,
    re_ref, ro_ref, rm_ref, r1_ref, r2_ref, own_ref, ss_in, tt_in, om_ref, w_ref,
    ss_ref, tt_ref, first_ref, mask_ref, stat_ref, tx_ref,
):
    even = lax.rem(lax.axis_index("space"), 2) == 0
    recv_e = re_ref[...].astype(F32)
    recv_o = ro_ref[0 : recv_e.shape[0], :].astype(F32)
    west = jnp.where(even, recv_o, recv_e)
    east = jnp.where(even, recv_e, recv_o)
    polar_m = rm_ref[moff : moff + 4 * lon, :].astype(F32)
    if r1_ref is r2_ref:
        other = r1_ref[...].astype(F32)
        own = own_ref[...].astype(F32)
        polar_1 = jnp.where(even, other, own)
        polar_2 = jnp.where(even, own, other)
    else:
        polar_1 = r1_ref[...].astype(F32)
        polar_2 = r2_ref[...].astype(F32)

    def ghost(kind, cols):
        line = jnp.concatenate([p[kind * lon : (kind + 1) * lon] for p in (polar_1, polar_m, polar_2)], axis=0)
        picks = [2 * lon - 1 - i for i in cols]
        return jnp.concatenate([line[k : k + 1] for k in picks], axis=0)

    zero = jnp.zeros((1, chans), F32)
    wide = list(range(-2, lon + 2))
    near = list(range(-1, lon + 1))
    g62, g63 = ghost(0, wide), ghost(1, wide)
    gt, gm = ghost(2, near), ghost(3, near)
    halo = {0: west[0:lat], 1: west[lat : 2 * lat], lon + 2: east[0:lat], lon + 3: east[lat : 2 * lat]}
    rows8 = lax.broadcasted_iota(jnp.int32, (8, chans), 0)
    top = []
    for k in range(lon + 4):
        fill = g63[k : k + 1]
        if k in halo:
            x = halo[k]
            ss_ref[k, :, 0:chans] = shift_rows(x, -1, zero).astype(BF16)
            ss_ref[k, :, chans : 2 * chans] = x.astype(BF16)
            ss_ref[k, :, 2 * chans :] = shift_rows(x, 1, fill).astype(BF16)
            top.append(x[lat - 1 : lat])
        else:
            tail = ss_ref[k, lat - 8 :, chans : 2 * chans].astype(F32)
            top.append(tail[7:8])
            ss_ref[k, lat - 8 :, 2 * chans :] = shift_rows(tail, 1, fill).astype(BF16)
    top = jnp.concatenate(top, axis=0)
    fold = jnp.concatenate([g62, g63, top], axis=1)
    total = None
    n = lon + 2
    pad = jnp.zeros((16 - n, 3 * chans), F32)
    for a in (-1, 0, 1):
        ghost_rows = jnp.concatenate([fold[1 - a : 1 - a + n], pad], axis=0).astype(BF16)
        piece = jnp.concatenate([ss_ref[a + 1 : a + 1 + n].reshape(n * lat, 3 * chans), ghost_rows], axis=0)
        part = dot(piece, w_ref[3 * (a + 1) : 3 * (a + 2)].reshape(3 * chans, chans))
        total = part if total is None else total + part
    first = total.astype(BF16)
    first_ref[...] = first
    own_first = first[lat : lat + lon * lat].astype(F32)
    own_mask = om_ref[...].astype(F32)
    kept = own_first * own_mask
    sums = jnp.sum(kept, axis=0, keepdims=True)
    squares = jnp.sum(kept * own_first, axis=0, keepdims=True)
    count = jnp.sum(own_mask, axis=0, keepdims=True)
    stat_ref[...] = jnp.concatenate([sums, squares, count, jnp.zeros((5, chans), F32)], axis=0)
    edges = [spread(x[3 * lat : 3 * lat + 1, 0:lat], lat, chans) for x in (west, east)]
    mask_ref[0:lat] = edges[0].astype(BF16)
    mask_ref[lat : lat + lon * lat] = om_ref[...]
    mask_ref[lat + lon * lat : n * lat] = edges[1].astype(BF16)
    mask_ref[n * lat :] = jnp.concatenate([gm, jnp.zeros((16 - n, chans), F32)], axis=0).astype(BF16)
    for k, x in ((0, west[2 * lat : 3 * lat]), (lon + 1, east[2 * lat : 3 * lat])):
        tt_ref[k, :, 0:chans] = shift_rows(x, 1, zero).astype(BF16)
        tt_ref[k, :, chans : 2 * chans] = x.astype(BF16)
        tt_ref[k, :, 2 * chans :] = shift_rows(x, -1, zero).astype(BF16)
    tx_ref[...] = jnp.concatenate([gt, jnp.zeros((16 - n, chans), F32)], axis=0)


def adjoint_kernel(lon, lat, chans, tt_ref, tx_ref, wt_ref, dact_ref):
    gt = tx_ref[...]
    total = None
    for a in (-1, 0, 1):
        extra = jnp.concatenate([gt[1 + a : 1 + a + lon], jnp.zeros((16 - lon, chans), F32)], axis=0)
        extra = jnp.concatenate([jnp.zeros((16, 2 * chans), F32), extra], axis=1).astype(BF16)
        piece = jnp.concatenate([tt_ref[1 - a : 1 - a + lon].reshape(lon * lat, 3 * chans), extra], axis=0)
        part = dot(piece, wt_ref[a + 1])
        total = part if total is None else total + part
    rows = lax.broadcasted_iota(jnp.int32, (lat, chans), 0)
    for i in range(lon):
        add = total[lon * lat + i : lon * lat + i + 1]
        dact_ref[i * lat : (i + 1) * lat, :] = total[i * lat : (i + 1) * lat] + jnp.where(rows == lat - 1, add, 0.0)


def moments(stat_ref):
    count = stat_ref[2:3, :]
    mean = stat_ref[0:1, :] / count
    var = stat_ref[1:2, :] / count - mean * mean
    return count, mean, lax.rsqrt(var + 1e-05)


def act_kernel(lon, lat, chans, first_ref, mask_ref, stat_ref, bn_ref, dact_ref, gsum_ref, dpre_ref, aa_ref):
    count, mean, rstd = moments(stat_ref)
    gain, offset = bn_ref[0:1, :], bn_ref[1:2, :]

    def forward(lo, hi):
        xhat = (first_ref[lo:hi].astype(F32) - mean) * rstd
        u = gain * xhat + offset
        hyper = jnp.tanh(0.7978845608 * (u + 0.044715 * u * u * u))
        m = mask_ref[lo:hi].astype(F32)
        return xhat, u, hyper, m, 0.5 * u * (1.0 + hyper) * m

    n = lon + 2
    zero = jnp.zeros((1, chans), F32)
    ghost = forward(n * lat, n * lat + 16)[4]
    scale = lax.rsqrt(count)
    goff = jnp.zeros((1, chans), F32)
    ggain = jnp.zeros((1, chans), F32)
    for k in range(n):
        xhat, u, hyper, m, act = forward(k * lat, (k + 1) * lat)
        aa_ref[k, :, 0:chans] = shift_rows(act, -1, zero).astype(BF16)
        aa_ref[k, :, chans : 2 * chans] = act.astype(BF16)
        aa_ref[k, :, 2 * chans :] = shift_rows(act, 1, ghost[k : k + 1]).astype(BF16)
        if 0 < k <= lon:
            slope = 0.5 * (1.0 + hyper) + 0.5 * u * (1.0 - hyper * hyper) * 0.7978845608 * (
                1.0 + 3.0 * 0.044715 * u * u
            )
            rows = slice((k - 1) * lat, k * lat)
            dpre = dact_ref[rows] * scale * m * slope
            dpre_ref[rows] = dpre
            goff = goff + jnp.sum(dpre, axis=0, keepdims=True)
            ggain = ggain + jnp.sum(dpre * xhat, axis=0, keepdims=True)
    gsum_ref[...] = jnp.concatenate([goff, ggain, jnp.zeros((6, chans), F32)], axis=0)


def put_taps(grad_ref, grad, shifted_ref, base, lon, lat, chans):
    chunks, width = grad_ref.shape[0], grad_ref.shape[2]
    turned = grad.T
    for a in (-1, 0, 1):
        piece = shifted_ref[base + a : base + a + lon].reshape(lon * lat, 3 * chans)
        part = dot(turned, piece).astype(BF16)
        for b in range(3):
            for c in range(chunks):
                grad_ref[c, 3 * (a + 1) + b] = part[c * width : (c + 1) * width, b * chans : (b + 1) * chans]


def out_kernel(lon, lat, chans, aa_ref, mask_ref, tt_ref, stat_ref, w_ref, out_ref, grad_ref):
    total = None
    for a in (-1, 0, 1):
        piece = aa_ref[a + 1 : a + 1 + lon].reshape(lon * lat, 3 * chans)
        part = dot(piece, w_ref[3 * (a + 1) : 3 * (a + 2)].reshape(3 * chans, chans))
        total = part if total is None else total + part
    own_mask = mask_ref[lat : lat + lon * lat].astype(F32)
    out_ref[...] = (total * own_mask).astype(BF16).reshape(1, lon, lat, chans)
    scale = lax.rsqrt(stat_ref[2:3, :])
    target = tt_ref[1 : 1 + lon, :, chans : 2 * chans].reshape(lon * lat, chans).astype(F32)
    dout = (target * scale).astype(BF16)
    put_taps(grad_ref, dout, aa_ref, 1, lon, lat, chans)


def in_kernel(lon, lat, chans, first_ref, mask_ref, stat_ref, bn_ref, dpre_ref, gsum_ref, ss_ref, grad_ref):
    count, mean, rstd = moments(stat_ref)
    goff, ggain = gsum_ref[0:1, :], gsum_ref[1:2, :]
    own = slice(lat, lat + lon * lat)
    xhat = (first_ref[own].astype(F32) - mean) * rstd
    dfirst = mask_ref[own].astype(F32) * (bn_ref[0:1, :] * rstd) * (dpre_ref[...] - (goff + xhat * ggain) / count)
    put_taps(grad_ref, dfirst.astype(BF16), ss_ref, 2, lon, lat, chans)


def xor_pairs(size, k):
    return [(i, i ^ k) for i in range(size)]


def all_sum(x, axis):
    size = lax.axis_size(axis)
    bit = 1
    while bit < size:
        other = lax.ppermute(x, axis, xor_pairs(size, bit))
        if 2 * bit < size:
            far = lax.ppermute(x, axis, xor_pairs(size, 2 * bit))
            both = lax.ppermute(x, axis, xor_pairs(size, 3 * bit))
            x = (x + other) + (far + both)
        else:
            x = x + other
        bit *= 4
    return x


def scatter_sum(x, axis, last=BF16):
    size = lax.axis_size(axis)
    me = lax.axis_index(axis)
    bit = 1
    while bit < size:
        mine = (me // bit) % 2
        split = x.reshape(x.shape[0] // 2, 2, *x.shape[1:])
        keep = lax.dynamic_index_in_dim(split, mine, 1, keepdims=False)
        send = lax.dynamic_index_in_dim(split, 1 - mine, 1, keepdims=False)
        got = lax.ppermute(send, axis, xor_pairs(size, bit))
        bit *= 2
        x = (keep.astype(F32) + got.astype(F32)).astype(BF16 if bit < size else last)
    return x[0]


def space_sum(x):
    size = lax.axis_size("space")
    bit = 1
    while bit < size:
        got = lax.ppermute(x, "space", xor_pairs(size, bit))
        x = x.astype(F32) + got.astype(F32)
        bit *= 2
        if bit < size:
            x = x.astype(BF16)
    return jnp.swapaxes(x, 1, 2)


def put_shifted(ref, k, x, step):
    chans = x.shape[1]
    zero = jnp.zeros((1, chans), F32)
    ref[k, :, 0:chans] = shift_rows(x, -step, zero).astype(BF16)
    ref[k, :, chans : 2 * chans] = x.astype(BF16)
    ref[k, :, 2 * chans :] = shift_rows(x, step, zero).astype(BF16)


def sample_prep(
    lon, lat, chans, tiles,
    f_hbm, t_hbm, land_hbm, win_hbm, wout_hbm, gain_hbm, offset_hbm,
    ss_ref, tt_ref, mask_ref, win_ref, wout_ref, wt_ref, bn_ref,
    f_ref, t_ref, land_ref, sems,
):
    pairs = [
        (land_hbm, land_ref), (f_hbm, f_ref), (t_hbm, t_ref), (wout_hbm, wout_ref), (win_hbm, win_ref),
        (gain_hbm, bn_ref.at[0:1]), (offset_hbm, bn_ref.at[1:2]),
    ]
    copies = [pltpu.make_async_copy(src, dst, sems.at[i]) for i, (src, dst) in enumerate(pairs)]
    for c in copies:
        c.start()
    first = lax.axis_index("space") * lon
    for c in copies[:3]:
        c.wait()
    lines = land_ref[...].astype(F32)
    for i in range(lon):
        mask = spread(lines[i : i + 1], lat, chans)
        mask_ref[first + i] = mask.astype(BF16)
        put_shifted(ss_ref, first + i + 1, f_ref[0, i].astype(F32) * mask, 1)
        put_shifted(tt_ref, first + i + 1, t_ref[0, i].astype(F32) * mask, -1)
    for c in copies[3:]:
        c.wait()
    for a in range(3):
        for b in range(3):
            wt_ref[a, b * chans : (b + 1) * chans] = wout_ref[3 * a + b].T


def sample_build(lon, lat, chans, f1_ref, f2_ref, l1_ref, l2_ref, l3_ref, ss_in, mask_in, ss_ref, mask_ref):
    me = lax.axis_index("space")
    for k, f_ref, land_ref in ((1, f1_ref, l1_ref), (2, f2_ref, l2_ref), (3, None, l3_ref)):
        first = jnp.bitwise_xor(me, k) * lon
        lines = land_ref[...].astype(F32)
        for i in range(lon):
            mask = spread(lines[i : i + 1], lat, chans)
            mask_ref[first + i] = mask.astype(BF16)
            if f_ref is not None:
                put_shifted(ss_ref, first + i + 1, f_ref[0, i].astype(F32) * mask, 1)


def sample_conv(lon, lat, chans, f3_ref, ss_in, mask_ref, w_ref, ss_ref, first_ref, stat_ref):
    nx = mask_ref.shape[0]
    start = jnp.bitwise_xor(lax.axis_index("space"), 3) * lon
    for i in range(lon):
        put_shifted(ss_ref, start + i + 1, f3_ref[0, i].astype(F32) * mask_ref[start + i].astype(F32), 1)
    tails = [ss_ref[i + 1, lat - 8 :, chans : 2 * chans].astype(F32) for i in range(nx)]
    for i in range(nx):
        fill = tails[nx - 1 - i][7:8]
        ss_ref[i + 1, lat - 8 :, 2 * chans :] = shift_rows(tails[i], 1, fill).astype(BF16)
    ss_ref[0] = ss_ref[nx]
    ss_ref[nx + 1] = ss_ref[1]
    sums, squares, count = [jnp.zeros((8, chans), F32)] * 3
    step = 8
    for c in range(0, nx, step):
        total = None
        for a in (-1, 0, 1):
            piece = ss_ref[c + a + 1 : c + a + 1 + step].reshape(step * lat, 3 * chans)
            part = dot(piece, w_ref[3 * (a + 1) : 3 * (a + 2)].reshape(3 * chans, chans))
            total = part if total is None else total + part
        first = total.astype(BF16)
        first_ref[c : c + step] = first.reshape(step, lat, chans)
        x = first.astype(F32)
        m = mask_ref[c : c + step].reshape(step * lat, chans).astype(F32)
        kept = x * m
        fold = lambda v: jnp.sum(v.reshape(-1, 8, chans), axis=0)
        sums, squares, count = sums + fold(kept), squares + fold(kept * x), count + fold(m)
    rows = [jnp.sum(v, axis=0, keepdims=True) for v in (sums, squares, count)]
    stat_ref[...] = jnp.concatenate(rows + [jnp.zeros((5, chans), F32)], axis=0)


def sample_adjoint(lon, lat, chans, t1_ref, t2_ref, t3_ref, mask_ref, wt_ref, tt_in, tt_ref, dact_ref):
    nx = mask_ref.shape[0]
    me = lax.axis_index("space")
    for k, t_ref in ((1, t1_ref), (2, t2_ref), (3, t3_ref)):
        start = jnp.bitwise_xor(me, k) * lon
        for i in range(lon):
            put_shifted(tt_ref, start + i + 1, t_ref[0, i].astype(F32) * mask_ref[start + i].astype(F32), -1)
    tt_ref[0] = tt_ref[nx]
    tt_ref[nx + 1] = tt_ref[1]
    top = [tt_ref[i + 1, lat - 8 :, chans : 2 * chans].astype(F32)[7:8] for i in range(nx)]
    extra = None
    for a in (-1, 0, 1):
        rows = jnp.concatenate([top[nx - 1 - (i + a) % nx] for i in range(nx)], axis=0).astype(BF16)
        part = dot(rows, wt_ref[a + 1, 2 * chans :])
        extra = part if extra is None else extra + part
    last = lax.broadcasted_iota(jnp.int32, (lat, chans), 0) == lat - 1
    step = 8
    for c in range(0, nx, step):
        total = None
        for a in (-1, 0, 1):
            piece = tt_ref[c + 1 - a : c + 1 - a + step].reshape(step * lat, 3 * chans)
            part = dot(piece, wt_ref[a + 1])
            total = part if total is None else total + part
        for i in range(step):
            add = jnp.where(last, extra[c + i : c + i + 1], 0.0)
            dact_ref[c + i] = total[i * lat : (i + 1) * lat] + add


def sample_act(lat, chans, first_ref, mask_ref, stat_ref, bn_ref, dact_ref, gsum_ref, dpre_ref, aa_ref):
    nx = mask_ref.shape[0]
    count, mean, rstd = moments(stat_ref)
    gain, offset = bn_ref[0:1, :], bn_ref[1:2, :]
    scale = lax.rsqrt(count)
    fold = lambda v: jnp.sum(v.reshape(-1, 8, chans), axis=0)
    goff, ggain = [jnp.zeros((8, chans), F32)] * 2
    for i in range(nx // 2):
        acts = []
        for k in (i, nx - 1 - i):
            xhat = (first_ref[k].astype(F32) - mean) * rstd
            u = gain * xhat + offset
            square = u * u
            hyper = jnp.tanh(0.7978845608 * (u + 0.044715 * square * u))
            m = mask_ref[k].astype(F32)
            half = 0.5 * (1.0 + hyper)
            acts.append(u * half * m)
            slope = half + 0.5 * u * (1.0 - hyper * hyper) * 0.7978845608 * (1.0 + 3.0 * 0.044715 * square)
            dpre = dact_ref[k] * scale * m * slope
            dpre_ref[k] = dpre
            goff, ggain = goff + fold(dpre), ggain + fold(dpre * xhat)
        for k, x, other in ((i, acts[0], acts[1]), (nx - 1 - i, acts[1], acts[0])):
            aa_ref[k + 1, :, 0:chans] = shift_rows(x, -1, jnp.zeros((1, chans), F32)).astype(BF16)
            aa_ref[k + 1, :, chans : 2 * chans] = x.astype(BF16)
            aa_ref[k + 1, :, 2 * chans :] = shift_rows(x, 1, other[lat - 1 : lat]).astype(BF16)
    aa_ref[0] = aa_ref[nx]
    aa_ref[nx + 1] = aa_ref[1]
    rows = [jnp.sum(v, axis=0, keepdims=True) for v in (goff, ggain)]
    gsum_ref[...] = jnp.concatenate(rows + [jnp.zeros((6, chans), F32)], axis=0)


def sample_out(lon, lat, chans, aa_ref, mask_ref, tt_ref, stat_ref, w_ref, out_ref, grad_ref):
    nx = mask_ref.shape[0]
    start = lax.axis_index("space") * lon
    scale = lax.rsqrt(stat_ref[2:3, :])
    target = tt_ref[1 : 1 + nx, :, chans : 2 * chans].reshape(nx * lat, chans).astype(F32)
    put_taps(grad_ref, (target * scale).astype(BF16), aa_ref, 1, nx, lat, chans)
    total = None
    for a in (-1, 0, 1):
        piece = aa_ref[pl.ds(start + a + 1, lon)].reshape(lon * lat, 3 * chans)
        part = dot(piece, w_ref[3 * (a + 1) : 3 * (a + 2)].reshape(3 * chans, chans))
        total = part if total is None else total + part
    own_mask = mask_ref[pl.ds(start, lon)].reshape(lon * lat, chans).astype(F32)
    out_ref[...] = (total * own_mask).astype(BF16).reshape(1, lon, lat, chans)


def sample_in(lat, chans, first_ref, mask_ref, stat_ref, bn_ref, dpre_ref, gsum_ref, ss_ref, grad_ref):
    nx = mask_ref.shape[0]
    count, mean, rstd = moments(stat_ref)
    goff, ggain = gsum_ref[0:1, :] / count, gsum_ref[1:2, :] / count
    factor = bn_ref[0:1, :] * rstd
    rows = []
    for k in range(nx):
        xhat = (first_ref[k].astype(F32) - mean) * rstd
        rows.append((mask_ref[k].astype(F32) * factor * (dpre_ref[k] - (goff + xhat * ggain))).astype(BF16))
    put_taps(grad_ref, jnp.concatenate(rows, axis=0), ss_ref, 1, nx, lat, chans)


def tile_body(fields, land, conv_in, conv_out, batchnorm_gain, batchnorm_offset, target_grad):
    lon, lat, chans = fields.shape[1:]
    tiles = lax.axis_size("space")
    sizes = (lon, lat, chans)
    cells = lon * lat
    gain, offset = batchnorm_gain[None, :], batchnorm_offset[None, :]
    fields, land, conv_in, conv_out, target_grad, gain, offset = (
        pltpu.with_memory_space_constraint(x, pltpu.HBM)
        for x in (fields, land, conv_in, conv_out, target_grad, gain, offset)
    )
    n = lon + 2
    join = tiles == 4
    edge = 3 * lat + 16
    shares = lax.axis_size("batch")
    taps = sds((shares, 9, chans // shares, chans), BF16)
    pay_e, pay_o, polar = run(
        functools.partial(pack_kernel, *sizes, join),
        [sds((edge, chans), BF16), sds((edge + (4 * lon if join else 0), chans), BF16), sds((4 * lon, chans), BF16)],
        [fields, target_grad, land],
        scratch=[
            pltpu.VMEM((4, lat, chans), BF16), pltpu.VMEM((lon, 8, chans), BF16),
            pltpu.VMEM((2, lat, chans), BF16), pltpu.VMEM((lon, 8, chans), BF16),
            pltpu.VMEM((lon, lat), jnp.int32), pltpu.SemaphoreType.DMA((7,)),
        ],
        name="pack",
        space=pl.BlockSpec(memory_space=pltpu.HBM),
    )
    mirror = [(i, tiles - 1 - i) for i in range(tiles)]
    got_o = lax.ppermute(pay_o, "space", [(i, (i - 1 if i % 2 == 0 else i + 1) % tiles) for i in range(tiles)])
    got_e = lax.ppermute(pay_e, "space", xor_pairs(tiles, 1))
    if join:
        got_x = lax.ppermute(polar, "space", xor_pairs(tiles, 2))
        poles = [got_o, got_x, got_x, polar]
    else:
        poles = [
            lax.ppermute(polar, "space", mirror),
            lax.ppermute(polar, "space", [(i, (tiles - 2 - i) % tiles) for i in range(tiles)]),
            lax.ppermute(polar, "space", [(i, (tiles - i) % tiles) for i in range(tiles)]),
            polar,
        ]
    wide = sds((lon + 4, lat, 3 * chans), BF16)
    near = sds((n, lat, 3 * chans), BF16)
    ss, tt, own_mask, win, wout, wt, bn = run(
        functools.partial(prep_kernel, *sizes),
        [
            wide, near, sds((cells, chans), BF16), sds(conv_in.shape, BF16), sds(conv_out.shape, BF16),
            sds((3, 3 * chans, chans), BF16), sds((8, chans), F32),
        ],
        [fields, target_grad, land, conv_in, conv_out, gain, offset],
        scratch=[
            pltpu.VMEM(fields.shape, BF16), pltpu.VMEM(fields.shape, BF16), pltpu.VMEM(land.shape, jnp.int32),
            pltpu.SemaphoreType.DMA((7,)),
        ],
        name="prep",
        space=pl.BlockSpec(memory_space=pltpu.HBM),
    )

    def conv_body(*refs):
        refs = list(refs)
        if join:
            refs[4] = refs[3]
        conv_kernel(*sizes, edge if join else 0, *refs)

    rows = n * lat + 16
    ss, tt, first, mask, stat, tx = run(
        conv_body,
        [wide, near, sds((rows, chans), BF16), sds((rows, chans), BF16), sds((8, chans), F32), sds((16, chans), F32)],
        [got_e, got_o, *poles, ss, tt, own_mask, win],
        flops=2 * rows * 9 * chans * chans,
        name="conv",
        alias={6: 0, 7: 1},
    )
    stat = all_sum(all_sum(stat, "batch"), "space")
    dact = run(
        functools.partial(adjoint_kernel, *sizes),
        [sds((cells, chans), F32)],
        [tt, tx, wt],
        flops=2 * cells * 9 * chans * chans,
        name="adjoint",
    )[0]
    gsum, dpre, aa = run(
        functools.partial(act_kernel, *sizes),
        [sds((8, chans), F32), sds((cells, chans), F32), sds((n, lat, 3 * chans), BF16)],
        [first, mask, stat, bn, dact],
        name="act",
    )
    gsum = all_sum(all_sum(gsum, "batch"), "space")
    output, part_out = run(
        functools.partial(out_kernel, *sizes),
        [sds((1, lon, lat, chans), BF16), taps],
        [aa, mask, tt, stat, wout],
        flops=4 * cells * 9 * chans * chans,
        name="out",
    )
    grad_out = space_sum(scatter_sum(part_out, "batch"))
    part_in = run(
        functools.partial(in_kernel, *sizes),
        [taps],
        [first, mask, stat, bn, dpre, gsum, ss],
        flops=2 * cells * 9 * chans * chans,
        name="grad_in",
    )[0]
    grad_in = space_sum(scatter_sum(part_in, "batch"))
    return (output, grad_in, grad_out, gsum[1], gsum[0])


def sample_body(fields, land, conv_in, conv_out, batchnorm_gain, batchnorm_offset, target_grad):
    lon, lat, chans = fields.shape[1:]
    tiles = lax.axis_size("space")
    sizes = (lon, lat, chans)
    nx = tiles * lon
    near, across, both = (xor_pairs(tiles, k) for k in (1, 2, 3))
    f2 = lax.ppermute(fields, "space", across)
    f1 = lax.ppermute(fields, "space", near)
    l1, l2, l3 = (lax.ppermute(land, "space", p) for p in (near, across, both))
    t2 = lax.ppermute(target_grad, "space", across)
    t1 = lax.ppermute(target_grad, "space", near)
    f3 = lax.ppermute(f2, "space", near)
    t3 = lax.ppermute(t2, "space", near)
    gain, offset = batchnorm_gain[None, :], batchnorm_offset[None, :]
    params = [
        pltpu.with_memory_space_constraint(x, pltpu.HBM)
        for x in (fields, target_grad, land, conv_in, conv_out, gain, offset)
    ]
    shares = lax.axis_size("batch")
    taps = sds((shares, 9, chans // shares, chans), BF16)
    shifted = sds((nx + 2, lat, 3 * chans), BF16)
    cells = sds((nx, lat, chans), BF16)
    cells_f = sds((nx, lat, chans), F32)
    sums = sds((8, chans), F32)
    work = 2 * nx * lat * 9 * chans * chans
    ss, tt, mask, win, wout, wt, bn = run(
        functools.partial(sample_prep, *sizes, tiles),
        [shifted, shifted, cells, sds(conv_in.shape, BF16), sds(conv_out.shape, BF16), sds((3, 3 * chans, chans), BF16), sums],
        params,
        scratch=[
            pltpu.VMEM(fields.shape, BF16), pltpu.VMEM(fields.shape, BF16), pltpu.VMEM(land.shape, jnp.int32),
            pltpu.SemaphoreType.DMA((7,)),
        ],
        name="prep",
        space=pl.BlockSpec(memory_space=pltpu.HBM),
    )
    ss, mask = run(
        functools.partial(sample_build, *sizes), [shifted, cells], [f1, f2, l1, l2, l3, ss, mask], name="build", alias={5: 0, 6: 1}
    )
    ss, first, stat = run(
        functools.partial(sample_conv, *sizes), [shifted, cells, sums], [f3, ss, mask, win], flops=work, name="conv", alias={1: 0}
    )
    stat = all_sum(stat, "batch")
    tt, dact = run(
        functools.partial(sample_adjoint, *sizes), [shifted, cells_f], [t1, t2, t3, mask, wt, tt], flops=work, name="adjoint", alias={5: 0}
    )
    gsum, dpre, aa = run(
        functools.partial(sample_act, lat, chans), [sums, cells_f, shifted], [first, mask, stat, bn, dact], name="act"
    )
    gsum = all_sum(gsum, "batch")
    output, part_out = run(
        functools.partial(sample_out, *sizes), [sds(fields.shape, BF16), taps], [aa, mask, tt, stat, wout], flops=work, name="out"
    )
    grad_out = scatter_sum(part_out, "batch", F32)
    (part_in,) = run(
        functools.partial(sample_in, lat, chans), [taps], [first, mask, stat, bn, dpre, gsum, ss], flops=work, name="grad_in"
    )
    grad_in = scatter_sum(part_in, "batch", F32)
    return (output, jnp.swapaxes(grad_in, 1, 2), jnp.swapaxes(grad_out, 1, 2), gsum[1], gsum[0])


def body(*args):
    return (sample_body if lax.axis_size("space") == 4 else tile_body)(*args)


def solution(mesh):
    in_specs = (
        P(("groups", "batch"), "space", None, None),
        P("space", None),
        P(),
        P(),
        P(),
        P(),
        P(("groups", "batch"), "space", None, None),
    )
    out_specs = (
        P(("groups", "batch"), "space", None, None),
        P("groups", None, "batch"),
        P("groups", None, "batch"),
        P("groups"),
        P("groups"),
    )
    return jax.shard_map(body, mesh=mesh, in_specs=in_specs, out_specs=out_specs, check_vma=False)
```

```python
import functools

import jax
import jax.numpy as jnp
from jax import lax
from jax.experimental import pallas as pl
from jax.experimental.pallas import tpu as pltpu
from jax.sharding import PartitionSpec as P


F32 = jnp.float32
BF16 = jnp.bfloat16
VMEM = pl.BlockSpec(memory_space=pltpu.VMEM)


def run(body, outs, args, scratch=(), flops=0, space=VMEM, alias=None):
    nbytes = sum(a.size * a.dtype.itemsize for a in args)
    nbytes += sum(o.size * o.dtype.itemsize for o in outs)
    return pl.pallas_call(
        body,
        out_shape=list(outs),
        in_specs=[space] * len(args),
        out_specs=[VMEM] * len(outs),
        scratch_shapes=list(scratch),
        cost_estimate=pl.CostEstimate(flops=flops, bytes_accessed=nbytes, transcendentals=0),
        compiler_params=pltpu.CompilerParams(vmem_limit_bytes=24 << 20),
        input_output_aliases=alias or {},
    )(*args)


def sds(shape, dtype):
    return jax.ShapeDtypeStruct(shape, dtype)


def dot(a, b):
    return jnp.dot(a, b, preferred_element_type=F32)


def spread(line, lat, chans):
    rows = lax.broadcasted_iota(jnp.int32, (lat, lat), 0)
    cols = lax.broadcasted_iota(jnp.int32, (lat, lat), 1)
    col = jnp.sum(jnp.where(rows == cols, jnp.broadcast_to(line, (lat, lat)), 0.0), axis=1, keepdims=True)
    return jnp.broadcast_to(col, (lat, chans))


def pack_kernel(lon, lat, chans, join, f_hbm, t_hbm, land_hbm, e_ref, o_ref, p_ref, fc, fr, tc, tr, land, sems):
    copies = [
        pltpu.make_async_copy(f_hbm.at[0, 0:2], fc.at[0:2], sems.at[0]),
        pltpu.make_async_copy(f_hbm.at[0, lon - 2 : lon], fc.at[2:4], sems.at[1]),
        pltpu.make_async_copy(f_hbm.at[0, :, lat - 8 : lat], fr, sems.at[2]),
        pltpu.make_async_copy(t_hbm.at[0, 0:1], tc.at[0:1], sems.at[3]),
        pltpu.make_async_copy(t_hbm.at[0, lon - 1 : lon], tc.at[1:2], sems.at[4]),
        pltpu.make_async_copy(t_hbm.at[0, :, lat - 8 : lat], tr, sems.at[5]),
        pltpu.make_async_copy(land_hbm, land, sems.at[6]),
    ]
    for c in copies:
        c.start()
    even = lax.rem(lax.axis_index("space"), 2) == 0
    for c in copies:
        c.wait()
    lines = land[...].astype(F32)

    def edge(k, cols_f, side):
        masks = [spread(lines[i : i + 1], lat, chans) for i in cols_f]
        parts = [fc[k + n].astype(F32) * m for n, m in enumerate(masks)]
        col = cols_f[0] if side == 0 else cols_f[1]
        parts.append(tc[side].astype(F32) * masks[0 if side == 0 else 1])
        line = jnp.concatenate([lines[col : col + 1], jnp.zeros((1, chans - lat), F32)], axis=1)
        parts += [line, jnp.zeros((15, chans), F32)]
        return jnp.concatenate(parts, axis=0).astype(BF16)

    west = edge(0, (0, 1), 0)
    east = edge(2, (lon - 2, lon - 1), 1)
    n = west.shape[0]
    e_ref[...] = jnp.where(even, east, west)
    o_ref[0:n, :] = jnp.where(even, west, east)
    lane = lax.broadcasted_iota(jnp.int32, (lon, lat), 1)
    last = {}
    for j in (lat - 2, lat - 1):
        col = jnp.sum(jnp.where(lane == j, lines, 0.0), axis=1, keepdims=True)
        last[j] = jnp.broadcast_to(col, (lon, chans))
    rows = []
    for j, ref in ((lat - 2, fr), (lat - 1, fr), (lat - 1, tr)):
        k = j - (lat - 8)
        line = jnp.concatenate([ref[i].astype(F32)[k : k + 1] for i in range(lon)], axis=0)
        rows.append(line * last[j])
    rows.append(last[lat - 1])
    polar = jnp.concatenate(rows, axis=0).astype(BF16)
    p_ref[...] = polar
    if join:
        o_ref[n:, :] = polar


def shift_rows(x, step, fill):
    rows = lax.broadcasted_iota(jnp.int32, x.shape, 0)
    n = x.shape[0]
    moved = pltpu.roll(x, (-step) % n, 0)
    return jnp.where(rows == (n - 1 if step > 0 else 0), fill, moved)


def prep_kernel(
    lon, lat, chans,
    f_hbm, t_hbm, land_hbm, win_hbm, wout_hbm, gain_hbm, offset_hbm,
    ss_ref, tt_ref, mask_ref, win_ref, wout_ref, wt_ref, bn_ref,
    f_ref, t_ref, land_ref, sems,
):
    pairs = [
        (land_hbm, land_ref), (f_hbm, f_ref), (t_hbm, t_ref), (wout_hbm, wout_ref), (win_hbm, win_ref),
        (gain_hbm, bn_ref.at[0:1]), (offset_hbm, bn_ref.at[1:2]),
    ]
    copies = [pltpu.make_async_copy(src, dst, sems.at[i]) for i, (src, dst) in enumerate(pairs)]
    for c in copies:
        c.start()
    for c in copies[:3]:
        c.wait()
    lines = land_ref[...].astype(F32)
    zero = jnp.zeros((1, chans), F32)
    for i in range(lon):
        mask = spread(lines[i : i + 1], lat, chans)
        mask_ref[i * lat : (i + 1) * lat] = mask.astype(BF16)
        x = f_ref[0, i].astype(F32) * mask
        ss_ref[i + 2, :, 0:chans] = shift_rows(x, -1, zero).astype(BF16)
        ss_ref[i + 2, :, chans : 2 * chans] = x.astype(BF16)
        ss_ref[i + 2, :, 2 * chans :] = shift_rows(x, 1, zero).astype(BF16)
        x = t_ref[0, i].astype(F32) * mask
        tt_ref[i + 1, :, 0:chans] = shift_rows(x, 1, zero).astype(BF16)
        tt_ref[i + 1, :, chans : 2 * chans] = x.astype(BF16)
        tt_ref[i + 1, :, 2 * chans :] = shift_rows(x, -1, zero).astype(BF16)
    for c in copies[3:]:
        c.wait()
    for a in range(3):
        for b in range(3):
            wt_ref[a, b * chans : (b + 1) * chans] = wout_ref[3 * a + b].T


def conv_kernel(
    lon, lat, chans, moff,
    re_ref, ro_ref, rm_ref, r1_ref, r2_ref, own_ref, ss_in, tt_in, om_ref, w_ref,
    ss_ref, tt_ref, first_ref, mask_ref, stat_ref, tx_ref,
):
    even = lax.rem(lax.axis_index("space"), 2) == 0
    recv_e = re_ref[...].astype(F32)
    recv_o = ro_ref[0 : recv_e.shape[0], :].astype(F32)
    west = jnp.where(even, recv_o, recv_e)
    east = jnp.where(even, recv_e, recv_o)
    polar_m = rm_ref[moff : moff + 4 * lon, :].astype(F32)
    if r1_ref is r2_ref:
        other = r1_ref[...].astype(F32)
        own = own_ref[...].astype(F32)
        polar_1 = jnp.where(even, other, own)
        polar_2 = jnp.where(even, own, other)
    else:
        polar_1 = r1_ref[...].astype(F32)
        polar_2 = r2_ref[...].astype(F32)

    def ghost(kind, cols):
        line = jnp.concatenate([p[kind * lon : (kind + 1) * lon] for p in (polar_1, polar_m, polar_2)], axis=0)
        picks = [2 * lon - 1 - i for i in cols]
        return jnp.concatenate([line[k : k + 1] for k in picks], axis=0)

    zero = jnp.zeros((1, chans), F32)
    wide = list(range(-2, lon + 2))
    near = list(range(-1, lon + 1))
    g62, g63 = ghost(0, wide), ghost(1, wide)
    gt, gm = ghost(2, near), ghost(3, near)
    halo = {0: west[0:lat], 1: west[lat : 2 * lat], lon + 2: east[0:lat], lon + 3: east[lat : 2 * lat]}
    rows8 = lax.broadcasted_iota(jnp.int32, (8, chans), 0)
    top = []
    for k in range(lon + 4):
        fill = g63[k : k + 1]
        if k in halo:
            x = halo[k]
            ss_ref[k, :, 0:chans] = shift_rows(x, -1, zero).astype(BF16)
            ss_ref[k, :, chans : 2 * chans] = x.astype(BF16)
            ss_ref[k, :, 2 * chans :] = shift_rows(x, 1, fill).astype(BF16)
            top.append(x[lat - 1 : lat])
        else:
            tail = ss_ref[k, lat - 8 :, chans : 2 * chans].astype(F32)
            top.append(tail[7:8])
            ss_ref[k, lat - 8 :, 2 * chans :] = shift_rows(tail, 1, fill).astype(BF16)
    top = jnp.concatenate(top, axis=0)
    fold = jnp.concatenate([g62, g63, top], axis=1)
    total = None
    n = lon + 2
    pad = jnp.zeros((16 - n, 3 * chans), F32)
    for a in (-1, 0, 1):
        ghost_rows = jnp.concatenate([fold[1 - a : 1 - a + n], pad], axis=0).astype(BF16)
        piece = jnp.concatenate([ss_ref[a + 1 : a + 1 + n].reshape(n * lat, 3 * chans), ghost_rows], axis=0)
        part = dot(piece, w_ref[3 * (a + 1) : 3 * (a + 2)].reshape(3 * chans, chans))
        total = part if total is None else total + part
    first = total.astype(BF16)
    first_ref[...] = first
    own_first = first[lat : lat + lon * lat].astype(F32)
    own_mask = om_ref[...].astype(F32)
    kept = own_first * own_mask
    sums = jnp.sum(kept, axis=0, keepdims=True)
    squares = jnp.sum(kept * own_first, axis=0, keepdims=True)
    count = jnp.sum(own_mask, axis=0, keepdims=True)
    stat_ref[...] = jnp.concatenate([sums, squares, count, jnp.zeros((5, chans), F32)], axis=0)
    edges = [spread(x[3 * lat : 3 * lat + 1, 0:lat], lat, chans) for x in (west, east)]
    mask_ref[0:lat] = edges[0].astype(BF16)
    mask_ref[lat : lat + lon * lat] = om_ref[...]
    mask_ref[lat + lon * lat : n * lat] = edges[1].astype(BF16)
    mask_ref[n * lat :] = jnp.concatenate([gm, jnp.zeros((16 - n, chans), F32)], axis=0).astype(BF16)
    for k, x in ((0, west[2 * lat : 3 * lat]), (lon + 1, east[2 * lat : 3 * lat])):
        tt_ref[k, :, 0:chans] = shift_rows(x, 1, zero).astype(BF16)
        tt_ref[k, :, chans : 2 * chans] = x.astype(BF16)
        tt_ref[k, :, 2 * chans :] = shift_rows(x, -1, zero).astype(BF16)
    tx_ref[...] = jnp.concatenate([gt, jnp.zeros((16 - n, chans), F32)], axis=0)


def adjoint_kernel(lon, lat, chans, tt_ref, tx_ref, wt_ref, dact_ref):
    gt = tx_ref[...]
    total = None
    for a in (-1, 0, 1):
        extra = jnp.concatenate([gt[1 + a : 1 + a + lon], jnp.zeros((16 - lon, chans), F32)], axis=0)
        extra = jnp.concatenate([jnp.zeros((16, 2 * chans), F32), extra], axis=1).astype(BF16)
        piece = jnp.concatenate([tt_ref[1 - a : 1 - a + lon].reshape(lon * lat, 3 * chans), extra], axis=0)
        part = dot(piece, wt_ref[a + 1])
        total = part if total is None else total + part
    rows = lax.broadcasted_iota(jnp.int32, (lat, chans), 0)
    for i in range(lon):
        add = total[lon * lat + i : lon * lat + i + 1]
        dact_ref[i * lat : (i + 1) * lat, :] = total[i * lat : (i + 1) * lat] + jnp.where(rows == lat - 1, add, 0.0)


def moments(stat_ref):
    count = stat_ref[2:3, :]
    mean = stat_ref[0:1, :] / count
    var = stat_ref[1:2, :] / count - mean * mean
    return count, mean, lax.rsqrt(var + 1e-05)


def act_kernel(lon, lat, chans, first_ref, mask_ref, stat_ref, bn_ref, dact_ref, gsum_ref, dpre_ref, aa_ref):
    count, mean, rstd = moments(stat_ref)
    gain, offset = bn_ref[0:1, :], bn_ref[1:2, :]

    def forward(lo, hi):
        xhat = (first_ref[lo:hi].astype(F32) - mean) * rstd
        u = gain * xhat + offset
        hyper = jnp.tanh(0.7978845608 * (u + 0.044715 * u * u * u))
        m = mask_ref[lo:hi].astype(F32)
        return xhat, u, hyper, m, 0.5 * u * (1.0 + hyper) * m

    n = lon + 2
    zero = jnp.zeros((1, chans), F32)
    ghost = forward(n * lat, n * lat + 16)[4]
    scale = lax.rsqrt(count)
    goff = jnp.zeros((1, chans), F32)
    ggain = jnp.zeros((1, chans), F32)
    for k in range(n):
        xhat, u, hyper, m, act = forward(k * lat, (k + 1) * lat)
        aa_ref[k, :, 0:chans] = shift_rows(act, -1, zero).astype(BF16)
        aa_ref[k, :, chans : 2 * chans] = act.astype(BF16)
        aa_ref[k, :, 2 * chans :] = shift_rows(act, 1, ghost[k : k + 1]).astype(BF16)
        if 0 < k <= lon:
            slope = 0.5 * (1.0 + hyper) + 0.5 * u * (1.0 - hyper * hyper) * 0.7978845608 * (
                1.0 + 3.0 * 0.044715 * u * u
            )
            rows = slice((k - 1) * lat, k * lat)
            dpre = dact_ref[rows] * scale * m * slope
            dpre_ref[rows] = dpre
            goff = goff + jnp.sum(dpre, axis=0, keepdims=True)
            ggain = ggain + jnp.sum(dpre * xhat, axis=0, keepdims=True)
    gsum_ref[...] = jnp.concatenate([goff, ggain, jnp.zeros((6, chans), F32)], axis=0)


def put_taps(grad_ref, grad, shifted_ref, base, lon, lat, chans):
    chunks, width = grad_ref.shape[0], grad_ref.shape[2]
    turned = grad.T
    for a in (-1, 0, 1):
        piece = shifted_ref[base + a : base + a + lon].reshape(lon * lat, 3 * chans)
        part = dot(turned, piece).astype(BF16)
        for b in range(3):
            for c in range(chunks):
                grad_ref[c, 3 * (a + 1) + b] = part[c * width : (c + 1) * width, b * chans : (b + 1) * chans]


def out_kernel(lon, lat, chans, aa_ref, mask_ref, tt_ref, stat_ref, w_ref, out_ref, grad_ref):
    total = None
    for a in (-1, 0, 1):
        piece = aa_ref[a + 1 : a + 1 + lon].reshape(lon * lat, 3 * chans)
        part = dot(piece, w_ref[3 * (a + 1) : 3 * (a + 2)].reshape(3 * chans, chans))
        total = part if total is None else total + part
    own_mask = mask_ref[lat : lat + lon * lat].astype(F32)
    out_ref[...] = (total * own_mask).astype(BF16).reshape(1, lon, lat, chans)
    scale = lax.rsqrt(stat_ref[2:3, :])
    target = tt_ref[1 : 1 + lon, :, chans : 2 * chans].reshape(lon * lat, chans).astype(F32)
    dout = (target * scale).astype(BF16)
    put_taps(grad_ref, dout, aa_ref, 1, lon, lat, chans)


def in_kernel(lon, lat, chans, first_ref, mask_ref, stat_ref, bn_ref, dpre_ref, gsum_ref, ss_ref, grad_ref):
    count, mean, rstd = moments(stat_ref)
    goff, ggain = gsum_ref[0:1, :], gsum_ref[1:2, :]
    own = slice(lat, lat + lon * lat)
    xhat = (first_ref[own].astype(F32) - mean) * rstd
    dfirst = mask_ref[own].astype(F32) * (bn_ref[0:1, :] * rstd) * (dpre_ref[...] - (goff + xhat * ggain) / count)
    put_taps(grad_ref, dfirst.astype(BF16), ss_ref, 2, lon, lat, chans)


def xor_pairs(size, k):
    return [(i, i ^ k) for i in range(size)]


def all_sum(x, axis):
    size = lax.axis_size(axis)
    bit = 1
    while bit < size:
        other = lax.ppermute(x, axis, xor_pairs(size, bit))
        if 2 * bit < size:
            far = lax.ppermute(x, axis, xor_pairs(size, 2 * bit))
            both = lax.ppermute(x, axis, xor_pairs(size, 3 * bit))
            x = (x + other) + (far + both)
        else:
            x = x + other
        bit *= 4
    return x


def scatter_sum(x, axis, last=BF16):
    size = lax.axis_size(axis)
    me = lax.axis_index(axis)
    bit = 1
    while bit < size:
        mine = (me // bit) % 2
        split = x.reshape(x.shape[0] // 2, 2, *x.shape[1:])
        keep = lax.dynamic_index_in_dim(split, mine, 1, keepdims=False)
        send = lax.dynamic_index_in_dim(split, 1 - mine, 1, keepdims=False)
        got = lax.ppermute(send, axis, xor_pairs(size, bit))
        bit *= 2
        x = (keep.astype(F32) + got.astype(F32)).astype(BF16 if bit < size else last)
    return x[0]


def space_sum(x):
    size = lax.axis_size("space")
    bit = 1
    while bit < size:
        got = lax.ppermute(x, "space", xor_pairs(size, bit))
        x = x.astype(F32) + got.astype(F32)
        bit *= 2
        if bit < size:
            x = x.astype(BF16)
    return jnp.swapaxes(x, 1, 2)


def put_shifted(ref, k, x, step):
    chans = x.shape[1]
    zero = jnp.zeros((1, chans), F32)
    ref[k, :, 0:chans] = shift_rows(x, -step, zero).astype(BF16)
    ref[k, :, chans : 2 * chans] = x.astype(BF16)
    ref[k, :, 2 * chans :] = shift_rows(x, step, zero).astype(BF16)


def join_kernel(a_ref, b_ref, out_ref):
    rows = a_ref.shape[0]
    out_ref[0:rows] = a_ref[...]
    out_ref[rows:] = b_ref[...]


def sample_prep(
    lon, lat, chans, tiles,
    f_hbm, t_hbm, land_hbm, win_hbm, wout_hbm, gain_hbm, offset_hbm,
    ss_ref, tt_ref, mask_ref, target_ref, land_ref, win_ref, wout_ref, wt_ref, bn_ref,
    f_ref, t_ref, sems,
):
    pairs = [
        (land_hbm, land_ref), (f_hbm, f_ref), (t_hbm, t_ref), (wout_hbm, wout_ref), (win_hbm, win_ref),
        (gain_hbm, bn_ref.at[0:1]), (offset_hbm, bn_ref.at[1:2]),
    ]
    copies = [pltpu.make_async_copy(src, dst, sems.at[i]) for i, (src, dst) in enumerate(pairs)]
    for c in copies:
        c.start()
    first = lax.axis_index("space") * lon
    for c in copies[:3]:
        c.wait()
    lines = land_ref[...].astype(F32)
    for i in range(lon):
        mask = spread(lines[i : i + 1], lat, chans)
        mask_ref[first + i] = mask.astype(BF16)
        put_shifted(ss_ref, first + i + 1, f_ref[0, i].astype(F32) * mask, 1)
        target = t_ref[0, i].astype(F32) * mask
        target_ref[0, i] = target.astype(BF16)
        put_shifted(tt_ref, first + i + 1, target, -1)
    for c in copies[3:]:
        c.wait()
    for a in range(3):
        for b in range(3):
            wt_ref[a, b * chans : (b + 1) * chans] = wout_ref[3 * a + b].T


def sample_build(lon, lat, chans, f1_ref, f2_ref, l2_ref, l13_ref, ss_in, mask_in, ss_ref, mask_ref):
    me = lax.axis_index("space")
    for k, f_ref, land_ref in ((1, f1_ref, l13_ref), (2, f2_ref, l2_ref), (3, None, l13_ref)):
        first = jnp.bitwise_xor(me, k) * lon
        lines = land_ref[lon if k == 3 else 0 : 2 * lon if k == 3 else lon].astype(F32)
        for i in range(lon):
            mask = spread(lines[i : i + 1], lat, chans)
            mask_ref[first + i] = mask.astype(BF16)
            if f_ref is not None:
                put_shifted(ss_ref, first + i + 1, f_ref[0, i].astype(F32) * mask, 1)


def sample_conv(lon, lat, chans, f3_ref, ss_in, mask_ref, w_ref, ss_ref, first_ref, stat_ref):
    nx = mask_ref.shape[0]
    start = jnp.bitwise_xor(lax.axis_index("space"), 3) * lon
    for i in range(lon):
        put_shifted(ss_ref, start + i + 1, f3_ref[0, i].astype(F32) * mask_ref[start + i].astype(F32), 1)
    tails = [ss_ref[i + 1, lat - 8 :, chans : 2 * chans].astype(F32) for i in range(nx)]
    for i in range(nx):
        fill = tails[nx - 1 - i][7:8]
        ss_ref[i + 1, lat - 8 :, 2 * chans :] = shift_rows(tails[i], 1, fill).astype(BF16)
    ss_ref[0] = ss_ref[nx]
    ss_ref[nx + 1] = ss_ref[1]
    sums, squares, count = [jnp.zeros((8, chans), F32)] * 3
    step = 8
    for c in range(0, nx, step):
        total = None
        for a in (-1, 0, 1):
            piece = ss_ref[c + a + 1 : c + a + 1 + step].reshape(step * lat, 3 * chans)
            part = dot(piece, w_ref[3 * (a + 1) : 3 * (a + 2)].reshape(3 * chans, chans))
            total = part if total is None else total + part
        first = total.astype(BF16)
        first_ref[c : c + step] = first.reshape(step, lat, chans)
        x = first.astype(F32)
        m = mask_ref[c : c + step].reshape(step * lat, chans).astype(F32)
        kept = x * m
        fold = lambda v: jnp.sum(v.reshape(-1, 8, chans), axis=0)
        sums, squares, count = sums + fold(kept), squares + fold(kept * x), count + fold(m)
    rows = [jnp.sum(v, axis=0, keepdims=True) for v in (sums, squares, count)]
    stat_ref[...] = jnp.concatenate(rows + [jnp.zeros((5, chans), F32)], axis=0)


def sample_adjoint(lon, lat, chans, t1_ref, t2_ref, t3_ref, wt_ref, tt_in, tt_ref, dact_ref):
    nx = dact_ref.shape[0]
    me = lax.axis_index("space")
    for k, t_ref in ((1, t1_ref), (2, t2_ref), (3, t3_ref)):
        start = jnp.bitwise_xor(me, k) * lon
        for i in range(lon):
            put_shifted(tt_ref, start + i + 1, t_ref[0, i].astype(F32), -1)
    tt_ref[0] = tt_ref[nx]
    tt_ref[nx + 1] = tt_ref[1]
    top = [tt_ref[i + 1, lat - 8 :, chans : 2 * chans].astype(F32)[7:8] for i in range(nx)]
    extra = None
    for a in (-1, 0, 1):
        rows = jnp.concatenate([top[nx - 1 - (i + a) % nx] for i in range(nx)], axis=0).astype(BF16)
        part = dot(rows, wt_ref[a + 1, 2 * chans :])
        extra = part if extra is None else extra + part
    last = lax.broadcasted_iota(jnp.int32, (lat, chans), 0) == lat - 1
    step = 8
    for c in range(0, nx, step):
        total = None
        for a in (-1, 0, 1):
            piece = tt_ref[c + 1 - a : c + 1 - a + step].reshape(step * lat, 3 * chans)
            part = dot(piece, wt_ref[a + 1])
            total = part if total is None else total + part
        for i in range(step):
            add = jnp.where(last, extra[c + i : c + i + 1], 0.0)
            dact_ref[c + i] = total[i * lat : (i + 1) * lat] + add


def sample_act(lat, chans, first_ref, mask_ref, stat_ref, bn_ref, dact_ref, gsum_ref, dpre_ref, aa_ref):
    nx = mask_ref.shape[0]
    count, mean, rstd = moments(stat_ref)
    gain, offset = bn_ref[0:1, :], bn_ref[1:2, :]
    scale = lax.rsqrt(count)
    fold = lambda v: jnp.sum(v.reshape(-1, 8, chans), axis=0)
    goff, ggain = [jnp.zeros((8, chans), F32)] * 2
    for i in range(nx // 2):
        acts = []
        for k in (i, nx - 1 - i):
            xhat = (first_ref[k].astype(F32) - mean) * rstd
            u = gain * xhat + offset
            square = u * u
            hyper = jnp.tanh(0.7978845608 * (u + 0.044715 * square * u))
            m = mask_ref[k].astype(F32)
            half = 0.5 * (1.0 + hyper)
            acts.append(u * half * m)
            slope = half + 0.5 * u * (1.0 - hyper * hyper) * 0.7978845608 * (1.0 + 3.0 * 0.044715 * square)
            dpre = dact_ref[k] * scale * m * slope
            dpre_ref[k] = dpre
            goff, ggain = goff + fold(dpre), ggain + fold(dpre * xhat)
        for k, x, other in ((i, acts[0], acts[1]), (nx - 1 - i, acts[1], acts[0])):
            aa_ref[k + 1, :, 0:chans] = shift_rows(x, -1, jnp.zeros((1, chans), F32)).astype(BF16)
            aa_ref[k + 1, :, chans : 2 * chans] = x.astype(BF16)
            aa_ref[k + 1, :, 2 * chans :] = shift_rows(x, 1, other[lat - 1 : lat]).astype(BF16)
    aa_ref[0] = aa_ref[nx]
    aa_ref[nx + 1] = aa_ref[1]
    rows = [jnp.sum(v, axis=0, keepdims=True) for v in (goff, ggain)]
    gsum_ref[...] = jnp.concatenate(rows + [jnp.zeros((6, chans), F32)], axis=0)


def halve(get, keep_ref, send_ref, bit):
    mine = lax.rem(lax.div(lax.axis_index("batch"), bit), 2)
    for j in range(keep_ref.shape[0]):
        keep_ref[j] = get(2 * j + mine)
        send_ref[j] = get(2 * j + 1 - mine)


def fold_kernel(bit, a_ref, b_ref, keep_ref, send_ref):
    halve(lambda k: (a_ref[k].astype(F32) + b_ref[k].astype(F32)).astype(BF16), keep_ref, send_ref, bit)


def exchange_sum(keep, send, size):
    bit = 1
    while True:
        got = lax.ppermute(send, "batch", xor_pairs(size, bit))
        bit *= 2
        if bit == size:
            return jnp.swapaxes(keep[0].astype(F32) + got[0].astype(F32), 1, 2), keep
        half = sds((keep.shape[0] // 2,) + keep.shape[1:], BF16)
        keep, send = run(functools.partial(fold_kernel, bit), [half, half], [keep, got])


def sample_grad(lat, chans, aa_ref, tt_ref, stat_ref, keep_ref, send_ref, grad_ref):
    nx = aa_ref.shape[0] - 2
    scale = lax.rsqrt(stat_ref[2:3, :])
    target = tt_ref[1 : 1 + nx, :, chans : 2 * chans].reshape(nx * lat, chans).astype(F32)
    put_taps(grad_ref, (target * scale).astype(BF16), aa_ref, 1, nx, lat, chans)
    halve(lambda k: grad_ref[k], keep_ref, send_ref, 1)


def sample_out(lon, lat, chans, aa_ref, mask_ref, w_ref, after_ref, out_ref):
    start = lax.axis_index("space") * lon
    total = None
    for a in (-1, 0, 1):
        piece = aa_ref[pl.ds(start + a + 1, lon)].reshape(lon * lat, 3 * chans)
        part = dot(piece, w_ref[3 * (a + 1) : 3 * (a + 2)].reshape(3 * chans, chans))
        total = part if total is None else total + part
    own_mask = mask_ref[pl.ds(start, lon)].reshape(lon * lat, chans).astype(F32)
    out_ref[...] = (total * own_mask).astype(BF16).reshape(1, lon, lat, chans)


def sample_in(lat, chans, first_ref, mask_ref, stat_ref, bn_ref, dpre_ref, gsum_ref, ss_ref, keep_ref, send_ref, grad_ref):
    nx = mask_ref.shape[0]
    count, mean, rstd = moments(stat_ref)
    goff, ggain = gsum_ref[0:1, :] / count, gsum_ref[1:2, :] / count
    factor = bn_ref[0:1, :] * rstd
    rows = []
    for k in range(nx):
        xhat = (first_ref[k].astype(F32) - mean) * rstd
        rows.append((mask_ref[k].astype(F32) * factor * (dpre_ref[k] - (goff + xhat * ggain))).astype(BF16))
    put_taps(grad_ref, jnp.concatenate(rows, axis=0), ss_ref, 1, nx, lat, chans)
    halve(lambda k: grad_ref[k], keep_ref, send_ref, 1)


def tile_body(fields, land, conv_in, conv_out, batchnorm_gain, batchnorm_offset, target_grad):
    lon, lat, chans = fields.shape[1:]
    tiles = lax.axis_size("space")
    sizes = (lon, lat, chans)
    cells = lon * lat
    gain, offset = batchnorm_gain[None, :], batchnorm_offset[None, :]
    fields, land, conv_in, conv_out, target_grad, gain, offset = (
        pltpu.with_memory_space_constraint(x, pltpu.HBM)
        for x in (fields, land, conv_in, conv_out, target_grad, gain, offset)
    )
    n = lon + 2
    join = tiles == 4
    edge = 3 * lat + 16
    shares = lax.axis_size("batch")
    taps = sds((shares, 9, chans // shares, chans), BF16)
    pay_e, pay_o, polar = run(
        functools.partial(pack_kernel, *sizes, join),
        [sds((edge, chans), BF16), sds((edge + (4 * lon if join else 0), chans), BF16), sds((4 * lon, chans), BF16)],
        [fields, target_grad, land],
        scratch=[
            pltpu.VMEM((4, lat, chans), BF16), pltpu.VMEM((lon, 8, chans), BF16),
            pltpu.VMEM((2, lat, chans), BF16), pltpu.VMEM((lon, 8, chans), BF16),
            pltpu.VMEM((lon, lat), jnp.int32), pltpu.SemaphoreType.DMA((7,)),
        ],
        space=pl.BlockSpec(memory_space=pltpu.HBM),
    )
    mirror = [(i, tiles - 1 - i) for i in range(tiles)]
    got_o = lax.ppermute(pay_o, "space", [(i, (i - 1 if i % 2 == 0 else i + 1) % tiles) for i in range(tiles)])
    got_e = lax.ppermute(pay_e, "space", xor_pairs(tiles, 1))
    if join:
        got_x = lax.ppermute(polar, "space", xor_pairs(tiles, 2))
        poles = [got_o, got_x, got_x, polar]
    else:
        poles = [
            lax.ppermute(polar, "space", mirror),
            lax.ppermute(polar, "space", [(i, (tiles - 2 - i) % tiles) for i in range(tiles)]),
            lax.ppermute(polar, "space", [(i, (tiles - i) % tiles) for i in range(tiles)]),
            polar,
        ]
    wide = sds((lon + 4, lat, 3 * chans), BF16)
    near = sds((n, lat, 3 * chans), BF16)
    ss, tt, own_mask, win, wout, wt, bn = run(
        functools.partial(prep_kernel, *sizes),
        [
            wide, near, sds((cells, chans), BF16), sds(conv_in.shape, BF16), sds(conv_out.shape, BF16),
            sds((3, 3 * chans, chans), BF16), sds((8, chans), F32),
        ],
        [fields, target_grad, land, conv_in, conv_out, gain, offset],
        scratch=[
            pltpu.VMEM(fields.shape, BF16), pltpu.VMEM(fields.shape, BF16), pltpu.VMEM(land.shape, jnp.int32),
            pltpu.SemaphoreType.DMA((7,)),
        ],
        space=pl.BlockSpec(memory_space=pltpu.HBM),
    )

    def conv_body(*refs):
        refs = list(refs)
        if join:
            refs[4] = refs[3]
        conv_kernel(*sizes, edge if join else 0, *refs)

    rows = n * lat + 16
    ss, tt, first, mask, stat, tx = run(
        conv_body,
        [wide, near, sds((rows, chans), BF16), sds((rows, chans), BF16), sds((8, chans), F32), sds((16, chans), F32)],
        [got_e, got_o, *poles, ss, tt, own_mask, win],
        flops=2 * rows * 9 * chans * chans,
        alias={6: 0, 7: 1},
    )
    stat = all_sum(all_sum(stat, "batch"), "space")
    dact = run(
        functools.partial(adjoint_kernel, *sizes),
        [sds((cells, chans), F32)],
        [tt, tx, wt],
        flops=2 * cells * 9 * chans * chans,
    )[0]
    gsum, dpre, aa = run(
        functools.partial(act_kernel, *sizes),
        [sds((8, chans), F32), sds((cells, chans), F32), sds((n, lat, 3 * chans), BF16)],
        [first, mask, stat, bn, dact],
    )
    gsum = all_sum(all_sum(gsum, "batch"), "space")
    output, part_out = run(
        functools.partial(out_kernel, *sizes),
        [sds((1, lon, lat, chans), BF16), taps],
        [aa, mask, tt, stat, wout],
        flops=4 * cells * 9 * chans * chans,
    )
    grad_out = space_sum(scatter_sum(part_out, "batch"))
    part_in = run(
        functools.partial(in_kernel, *sizes),
        [taps],
        [first, mask, stat, bn, dpre, gsum, ss],
        flops=2 * cells * 9 * chans * chans,
    )[0]
    grad_in = space_sum(scatter_sum(part_in, "batch"))
    return (output, grad_in, grad_out, gsum[1], gsum[0])


def sample_body(fields, land, conv_in, conv_out, batchnorm_gain, batchnorm_offset, target_grad):
    lon, lat, chans = fields.shape[1:]
    tiles = lax.axis_size("space")
    sizes = (lon, lat, chans)
    nx = tiles * lon
    near, across = xor_pairs(tiles, 1), xor_pairs(tiles, 2)
    move = lambda x, pairs: lax.ppermute(x, "space", pairs)
    f2 = move(fields, across)
    l2 = move(land, across)
    f1 = move(fields, near)
    f3 = move(f2, near)
    gain, offset = batchnorm_gain[None, :], batchnorm_offset[None, :]
    params = [
        pltpu.with_memory_space_constraint(x, pltpu.HBM)
        for x in (fields, target_grad, land, conv_in, conv_out, gain, offset)
    ]
    shares = lax.axis_size("batch")
    half = sds((shares // 2, 9, chans // shares, chans), BF16)
    whole = [pltpu.VMEM((shares, 9, chans // shares, chans), BF16)]
    shifted = sds((nx + 2, lat, 3 * chans), BF16)
    cells = sds((nx, lat, chans), BF16)
    cells_f = sds((nx, lat, chans), F32)
    sums = sds((8, chans), F32)
    work = 2 * nx * lat * 9 * chans * chans
    ss, tt, mask, target, land_own, win, wout, wt, bn = run(
        functools.partial(sample_prep, *sizes, tiles),
        [shifted, shifted, cells, sds(target_grad.shape, BF16), sds(land.shape, jnp.int32), sds(conv_in.shape, BF16), sds(conv_out.shape, BF16), sds((3, 3 * chans, chans), BF16), sums],
        params,
        scratch=[
            pltpu.VMEM(fields.shape, BF16), pltpu.VMEM(fields.shape, BF16), pltpu.SemaphoreType.DMA((7,)),
        ],
        space=pl.BlockSpec(memory_space=pltpu.HBM),
    )
    (both,) = run(join_kernel, [sds((2 * lon, lat), jnp.int32)], [land_own, l2])
    l13 = move(both, near)
    ss, mask = run(
        functools.partial(sample_build, *sizes), [shifted, cells], [f1, f2, l2, l13, ss, mask], alias={4: 0, 5: 1}
    )
    t2 = move(target, across)
    t1 = move(target, near)
    t3 = move(t2, near)
    ss, first, stat = run(
        functools.partial(sample_conv, *sizes), [shifted, cells, sums], [f3, ss, mask, win], flops=work, alias={1: 0}
    )
    stat = all_sum(stat, "batch")
    tt, dact = run(
        functools.partial(sample_adjoint, *sizes), [shifted, cells_f], [t1, t2, t3, wt, tt], flops=work, alias={4: 0}
    )
    gsum, dpre, aa = run(
        functools.partial(sample_act, lat, chans), [sums, cells_f, shifted], [first, mask, stat, bn, dact]
    )
    gsum = all_sum(gsum, "batch")
    keep_o, send_o = run(
        functools.partial(sample_grad, lat, chans), [half, half], [aa, tt, stat], scratch=whole, flops=work
    )
    grad_out, _ = exchange_sum(keep_o, send_o, shares)
    keep_i, send_i = run(
        functools.partial(sample_in, lat, chans),
        [half, half], [first, mask, stat, bn, dpre, gsum, ss], scratch=whole, flops=work,
    )
    grad_in, folded = exchange_sum(keep_i, send_i, shares)
    (output,) = run(
        functools.partial(sample_out, *sizes), [sds(fields.shape, BF16)], [aa, mask, wout, folded], flops=work // tiles
    )
    return (output, grad_in, grad_out, gsum[1], gsum[0])


def body(*args):
    if lax.axis_size("space") != 4:
        return tile_body(*args)
    return sample_body(*args)


def solution(mesh):
    in_specs = (
        P(("groups", "batch"), "space", None, None),
        P("space", None),
        P(),
        P(),
        P(),
        P(),
        P(("groups", "batch"), "space", None, None),
    )
    out_specs = (
        P(("groups", "batch"), "space", None, None),
        P("groups", None, "batch"),
        P("groups", None, "batch"),
        P("groups"),
        P("groups"),
    )
    return jax.shard_map(body, mesh=mesh, in_specs=in_specs, out_specs=out_specs, check_vma=False)
```

```python
import functools

import jax
import jax.numpy as jnp
from jax import lax
from jax.experimental import pallas as pl
from jax.experimental.pallas import tpu as pltpu
from jax.sharding import PartitionSpec as P


F32 = jnp.float32
BF16 = jnp.bfloat16
VMEM = pl.BlockSpec(memory_space=pltpu.VMEM)


def run(body, outs, args, scratch=(), flops=0, space=VMEM, alias=None):
    nbytes = sum(a.size * a.dtype.itemsize for a in args)
    nbytes += sum(o.size * o.dtype.itemsize for o in outs)
    return pl.pallas_call(
        body,
        out_shape=list(outs),
        in_specs=[space] * len(args),
        out_specs=[VMEM] * len(outs),
        scratch_shapes=list(scratch),
        cost_estimate=pl.CostEstimate(flops=flops, bytes_accessed=nbytes, transcendentals=0),
        compiler_params=pltpu.CompilerParams(vmem_limit_bytes=24 << 20),
        input_output_aliases=alias or {},
    )(*args)


def sds(shape, dtype):
    return jax.ShapeDtypeStruct(shape, dtype)


def dot(a, b):
    return jnp.dot(a, b, preferred_element_type=F32)


def spread(line, lat, chans):
    rows = lax.broadcasted_iota(jnp.int32, (lat, lat), 0)
    cols = lax.broadcasted_iota(jnp.int32, (lat, lat), 1)
    col = jnp.sum(jnp.where(rows == cols, jnp.broadcast_to(line, (lat, lat)), 0.0), axis=1, keepdims=True)
    return jnp.broadcast_to(col, (lat, chans))


def pack_kernel(lon, lat, chans, join, f_hbm, t_hbm, land_hbm, e_ref, o_ref, p_ref, fc, fr, tc, tr, land, sems):
    copies = [
        pltpu.make_async_copy(f_hbm.at[0, 0:2], fc.at[0:2], sems.at[0]),
        pltpu.make_async_copy(f_hbm.at[0, lon - 2 : lon], fc.at[2:4], sems.at[1]),
        pltpu.make_async_copy(f_hbm.at[0, :, lat - 8 : lat], fr, sems.at[2]),
        pltpu.make_async_copy(t_hbm.at[0, 0:1], tc.at[0:1], sems.at[3]),
        pltpu.make_async_copy(t_hbm.at[0, lon - 1 : lon], tc.at[1:2], sems.at[4]),
        pltpu.make_async_copy(t_hbm.at[0, :, lat - 8 : lat], tr, sems.at[5]),
        pltpu.make_async_copy(land_hbm, land, sems.at[6]),
    ]
    for c in copies:
        c.start()
    even = lax.rem(lax.axis_index("space"), 2) == 0
    for c in copies:
        c.wait()
    lines = land[...].astype(F32)

    def edge(k, cols_f, side):
        masks = [spread(lines[i : i + 1], lat, chans) for i in cols_f]
        parts = [fc[k + n].astype(F32) * m for n, m in enumerate(masks)]
        col = cols_f[0] if side == 0 else cols_f[1]
        parts.append(tc[side].astype(F32) * masks[0 if side == 0 else 1])
        line = jnp.concatenate([lines[col : col + 1], jnp.zeros((1, chans - lat), F32)], axis=1)
        parts += [line, jnp.zeros((15, chans), F32)]
        return jnp.concatenate(parts, axis=0).astype(BF16)

    west = edge(0, (0, 1), 0)
    east = edge(2, (lon - 2, lon - 1), 1)
    n = west.shape[0]
    e_ref[...] = jnp.where(even, east, west)
    o_ref[0:n, :] = jnp.where(even, west, east)
    lane = lax.broadcasted_iota(jnp.int32, (lon, lat), 1)
    last = {}
    for j in (lat - 2, lat - 1):
        col = jnp.sum(jnp.where(lane == j, lines, 0.0), axis=1, keepdims=True)
        last[j] = jnp.broadcast_to(col, (lon, chans))
    rows = []
    for j, ref in ((lat - 2, fr), (lat - 1, fr), (lat - 1, tr)):
        k = j - (lat - 8)
        line = jnp.concatenate([ref[i].astype(F32)[k : k + 1] for i in range(lon)], axis=0)
        rows.append(line * last[j])
    rows.append(last[lat - 1])
    polar = jnp.concatenate(rows, axis=0).astype(BF16)
    p_ref[...] = polar
    if join:
        o_ref[n:, :] = polar


def shift_rows(x, step, fill):
    rows = lax.broadcasted_iota(jnp.int32, x.shape, 0)
    n = x.shape[0]
    moved = pltpu.roll(x, (-step) % n, 0)
    return jnp.where(rows == (n - 1 if step > 0 else 0), fill, moved)


def prep_kernel(
    lon, lat, chans,
    f_hbm, t_hbm, land_hbm, win_hbm, wout_hbm, gain_hbm, offset_hbm,
    ss_ref, tt_ref, mask_ref, win_ref, wout_ref, wt_ref, bn_ref,
    f_ref, t_ref, land_ref, sems,
):
    pairs = [
        (land_hbm, land_ref), (f_hbm, f_ref), (t_hbm, t_ref), (wout_hbm, wout_ref), (win_hbm, win_ref),
        (gain_hbm, bn_ref.at[0:1]), (offset_hbm, bn_ref.at[1:2]),
    ]
    copies = [pltpu.make_async_copy(src, dst, sems.at[i]) for i, (src, dst) in enumerate(pairs)]
    for c in copies:
        c.start()
    for c in copies[:3]:
        c.wait()
    lines = land_ref[...].astype(F32)
    zero = jnp.zeros((1, chans), F32)
    for i in range(lon):
        mask = spread(lines[i : i + 1], lat, chans)
        mask_ref[i * lat : (i + 1) * lat] = mask.astype(BF16)
        x = f_ref[0, i].astype(F32) * mask
        ss_ref[i + 2, :, 0:chans] = shift_rows(x, -1, zero).astype(BF16)
        ss_ref[i + 2, :, chans : 2 * chans] = x.astype(BF16)
        ss_ref[i + 2, :, 2 * chans :] = shift_rows(x, 1, zero).astype(BF16)
        x = t_ref[0, i].astype(F32) * mask
        tt_ref[i + 1, :, 0:chans] = shift_rows(x, 1, zero).astype(BF16)
        tt_ref[i + 1, :, chans : 2 * chans] = x.astype(BF16)
        tt_ref[i + 1, :, 2 * chans :] = shift_rows(x, -1, zero).astype(BF16)
    for c in copies[3:]:
        c.wait()
    for a in range(3):
        for b in range(3):
            wt_ref[a, b * chans : (b + 1) * chans] = wout_ref[3 * a + b].T


def conv_kernel(
    lon, lat, chans, moff,
    re_ref, ro_ref, rm_ref, r1_ref, r2_ref, own_ref, ss_in, tt_in, om_ref, w_ref,
    ss_ref, tt_ref, first_ref, mask_ref, stat_ref, tx_ref,
):
    even = lax.rem(lax.axis_index("space"), 2) == 0
    recv_e = re_ref[...].astype(F32)
    recv_o = ro_ref[0 : recv_e.shape[0], :].astype(F32)
    west = jnp.where(even, recv_o, recv_e)
    east = jnp.where(even, recv_e, recv_o)
    polar_m = rm_ref[moff : moff + 4 * lon, :].astype(F32)
    if r1_ref is r2_ref:
        other = r1_ref[...].astype(F32)
        own = own_ref[...].astype(F32)
        polar_1 = jnp.where(even, other, own)
        polar_2 = jnp.where(even, own, other)
    else:
        polar_1 = r1_ref[...].astype(F32)
        polar_2 = r2_ref[...].astype(F32)

    def ghost(kind, cols):
        line = jnp.concatenate([p[kind * lon : (kind + 1) * lon] for p in (polar_1, polar_m, polar_2)], axis=0)
        picks = [2 * lon - 1 - i for i in cols]
        return jnp.concatenate([line[k : k + 1] for k in picks], axis=0)

    zero = jnp.zeros((1, chans), F32)
    wide = list(range(-2, lon + 2))
    near = list(range(-1, lon + 1))
    g62, g63 = ghost(0, wide), ghost(1, wide)
    gt, gm = ghost(2, near), ghost(3, near)
    halo = {0: west[0:lat], 1: west[lat : 2 * lat], lon + 2: east[0:lat], lon + 3: east[lat : 2 * lat]}
    rows8 = lax.broadcasted_iota(jnp.int32, (8, chans), 0)
    top = []
    for k in range(lon + 4):
        fill = g63[k : k + 1]
        if k in halo:
            x = halo[k]
            ss_ref[k, :, 0:chans] = shift_rows(x, -1, zero).astype(BF16)
            ss_ref[k, :, chans : 2 * chans] = x.astype(BF16)
            ss_ref[k, :, 2 * chans :] = shift_rows(x, 1, fill).astype(BF16)
            top.append(x[lat - 1 : lat])
        else:
            tail = ss_ref[k, lat - 8 :, chans : 2 * chans].astype(F32)
            top.append(tail[7:8])
            ss_ref[k, lat - 8 :, 2 * chans :] = shift_rows(tail, 1, fill).astype(BF16)
    top = jnp.concatenate(top, axis=0)
    fold = jnp.concatenate([g62, g63, top], axis=1)
    total = None
    n = lon + 2
    pad = jnp.zeros((16 - n, 3 * chans), F32)
    for a in (-1, 0, 1):
        ghost_rows = jnp.concatenate([fold[1 - a : 1 - a + n], pad], axis=0).astype(BF16)
        piece = jnp.concatenate([ss_ref[a + 1 : a + 1 + n].reshape(n * lat, 3 * chans), ghost_rows], axis=0)
        part = dot(piece, w_ref[3 * (a + 1) : 3 * (a + 2)].reshape(3 * chans, chans))
        total = part if total is None else total + part
    first = total.astype(BF16)
    first_ref[...] = first
    own_first = first[lat : lat + lon * lat].astype(F32)
    own_mask = om_ref[...].astype(F32)
    kept = own_first * own_mask
    sums = jnp.sum(kept, axis=0, keepdims=True)
    squares = jnp.sum(kept * own_first, axis=0, keepdims=True)
    count = jnp.sum(own_mask, axis=0, keepdims=True)
    stat_ref[...] = jnp.concatenate([sums, squares, count, jnp.zeros((5, chans), F32)], axis=0)
    edges = [spread(x[3 * lat : 3 * lat + 1, 0:lat], lat, chans) for x in (west, east)]
    mask_ref[0:lat] = edges[0].astype(BF16)
    mask_ref[lat : lat + lon * lat] = om_ref[...]
    mask_ref[lat + lon * lat : n * lat] = edges[1].astype(BF16)
    mask_ref[n * lat :] = jnp.concatenate([gm, jnp.zeros((16 - n, chans), F32)], axis=0).astype(BF16)
    for k, x in ((0, west[2 * lat : 3 * lat]), (lon + 1, east[2 * lat : 3 * lat])):
        tt_ref[k, :, 0:chans] = shift_rows(x, 1, zero).astype(BF16)
        tt_ref[k, :, chans : 2 * chans] = x.astype(BF16)
        tt_ref[k, :, 2 * chans :] = shift_rows(x, -1, zero).astype(BF16)
    tx_ref[...] = jnp.concatenate([gt, jnp.zeros((16 - n, chans), F32)], axis=0)


def adjoint_kernel(lon, lat, chans, tt_ref, tx_ref, wt_ref, dact_ref):
    gt = tx_ref[...]
    total = None
    for a in (-1, 0, 1):
        extra = jnp.concatenate([gt[1 + a : 1 + a + lon], jnp.zeros((16 - lon, chans), F32)], axis=0)
        extra = jnp.concatenate([jnp.zeros((16, 2 * chans), F32), extra], axis=1).astype(BF16)
        piece = jnp.concatenate([tt_ref[1 - a : 1 - a + lon].reshape(lon * lat, 3 * chans), extra], axis=0)
        part = dot(piece, wt_ref[a + 1])
        total = part if total is None else total + part
    rows = lax.broadcasted_iota(jnp.int32, (lat, chans), 0)
    for i in range(lon):
        add = total[lon * lat + i : lon * lat + i + 1]
        dact_ref[i * lat : (i + 1) * lat, :] = total[i * lat : (i + 1) * lat] + jnp.where(rows == lat - 1, add, 0.0)


def moments(stat_ref):
    count = stat_ref[2:3, :]
    mean = stat_ref[0:1, :] / count
    var = stat_ref[1:2, :] / count - mean * mean
    return count, mean, lax.rsqrt(var + 1e-05)


def act_kernel(lon, lat, chans, first_ref, mask_ref, stat_ref, bn_ref, dact_ref, gsum_ref, dpre_ref, aa_ref):
    count, mean, rstd = moments(stat_ref)
    gain, offset = bn_ref[0:1, :], bn_ref[1:2, :]

    def forward(lo, hi):
        xhat = (first_ref[lo:hi].astype(F32) - mean) * rstd
        u = gain * xhat + offset
        hyper = jnp.tanh(0.7978845608 * (u + 0.044715 * u * u * u))
        m = mask_ref[lo:hi].astype(F32)
        return xhat, u, hyper, m, 0.5 * u * (1.0 + hyper) * m

    n = lon + 2
    zero = jnp.zeros((1, chans), F32)
    ghost = forward(n * lat, n * lat + 16)[4]
    scale = lax.rsqrt(count)
    goff = jnp.zeros((1, chans), F32)
    ggain = jnp.zeros((1, chans), F32)
    for k in range(n):
        xhat, u, hyper, m, act = forward(k * lat, (k + 1) * lat)
        aa_ref[k, :, 0:chans] = shift_rows(act, -1, zero).astype(BF16)
        aa_ref[k, :, chans : 2 * chans] = act.astype(BF16)
        aa_ref[k, :, 2 * chans :] = shift_rows(act, 1, ghost[k : k + 1]).astype(BF16)
        if 0 < k <= lon:
            slope = 0.5 * (1.0 + hyper) + 0.5 * u * (1.0 - hyper * hyper) * 0.7978845608 * (
                1.0 + 3.0 * 0.044715 * u * u
            )
            rows = slice((k - 1) * lat, k * lat)
            dpre = dact_ref[rows] * scale * m * slope
            dpre_ref[rows] = dpre
            goff = goff + jnp.sum(dpre, axis=0, keepdims=True)
            ggain = ggain + jnp.sum(dpre * xhat, axis=0, keepdims=True)
    gsum_ref[...] = jnp.concatenate([goff, ggain, jnp.zeros((6, chans), F32)], axis=0)


def put_taps(grad_ref, grad, shifted_ref, base, lon, lat, chans):
    chunks, width = grad_ref.shape[0], grad_ref.shape[2]
    pieces = [shifted_ref[base + a : base + a + lon].reshape(lon * lat, 3 * chans) for a in (-1, 0, 1)]
    part = dot(grad.T, jnp.concatenate(pieces, axis=1)).astype(BF16)
    for t in range(9):
        for c in range(chunks):
            grad_ref[c, t] = part[c * width : (c + 1) * width, t * chans : (t + 1) * chans]


def out_kernel(lon, lat, chans, aa_ref, mask_ref, tt_ref, stat_ref, w_ref, out_ref, grad_ref):
    total = None
    for a in (-1, 0, 1):
        piece = aa_ref[a + 1 : a + 1 + lon].reshape(lon * lat, 3 * chans)
        part = dot(piece, w_ref[3 * (a + 1) : 3 * (a + 2)].reshape(3 * chans, chans))
        total = part if total is None else total + part
    own_mask = mask_ref[lat : lat + lon * lat].astype(F32)
    out_ref[...] = (total * own_mask).astype(BF16).reshape(1, lon, lat, chans)
    scale = lax.rsqrt(stat_ref[2:3, :])
    target = tt_ref[1 : 1 + lon, :, chans : 2 * chans].reshape(lon * lat, chans).astype(F32)
    dout = (target * scale).astype(BF16)
    put_taps(grad_ref, dout, aa_ref, 1, lon, lat, chans)


def in_kernel(lon, lat, chans, first_ref, mask_ref, stat_ref, bn_ref, dpre_ref, gsum_ref, ss_ref, grad_ref):
    count, mean, rstd = moments(stat_ref)
    goff, ggain = gsum_ref[0:1, :], gsum_ref[1:2, :]
    own = slice(lat, lat + lon * lat)
    xhat = (first_ref[own].astype(F32) - mean) * rstd
    dfirst = mask_ref[own].astype(F32) * (bn_ref[0:1, :] * rstd) * (dpre_ref[...] - (goff + xhat * ggain) / count)
    put_taps(grad_ref, dfirst.astype(BF16), ss_ref, 2, lon, lat, chans)


def xor_pairs(size, k):
    return [(i, i ^ k) for i in range(size)]


def all_sum(x, axis):
    size = lax.axis_size(axis)
    bit = 1
    while bit < size:
        other = lax.ppermute(x, axis, xor_pairs(size, bit))
        if 2 * bit < size:
            far = lax.ppermute(x, axis, xor_pairs(size, 2 * bit))
            both = lax.ppermute(x, axis, xor_pairs(size, 3 * bit))
            x = (x + other) + (far + both)
        else:
            x = x + other
        bit *= 4
    return x


def scatter_sum(x, axis, last=BF16):
    size = lax.axis_size(axis)
    me = lax.axis_index(axis)
    bit = 1
    while bit < size:
        mine = (me // bit) % 2
        split = x.reshape(x.shape[0] // 2, 2, *x.shape[1:])
        keep = lax.dynamic_index_in_dim(split, mine, 1, keepdims=False)
        send = lax.dynamic_index_in_dim(split, 1 - mine, 1, keepdims=False)
        got = lax.ppermute(send, axis, xor_pairs(size, bit))
        bit *= 2
        x = (keep.astype(F32) + got.astype(F32)).astype(BF16 if bit < size else last)
    return x[0]


def space_sum(x):
    size = lax.axis_size("space")
    bit = 1
    while bit < size:
        got = lax.ppermute(x, "space", xor_pairs(size, bit))
        x = x.astype(F32) + got.astype(F32)
        bit *= 2
        if bit < size:
            x = x.astype(BF16)
    return jnp.swapaxes(x, 1, 2)


def put_shifted(ref, k, x, step):
    chans = x.shape[1]
    zero = jnp.zeros((1, chans), F32)
    ref[k, :, 0:chans] = shift_rows(x, -step, zero).astype(BF16)
    ref[k, :, chans : 2 * chans] = x.astype(BF16)
    ref[k, :, 2 * chans :] = shift_rows(x, step, zero).astype(BF16)


def sample_prep(
    lon, lat, chans, tiles,
    f_hbm, t_hbm, land_hbm, win_hbm, wout_hbm, gain_hbm, offset_hbm,
    ss_ref, tt_ref, mask_ref, target_ref, win_ref, wout_ref, wt_ref, bn_ref,
    f_ref, t_ref, land_ref, wraw_ref, sems,
):
    pairs = [
        (land_hbm, land_ref), (f_hbm, f_ref), (t_hbm, t_ref), (wout_hbm, wout_ref), (win_hbm, wraw_ref),
        (gain_hbm, bn_ref.at[0:1]), (offset_hbm, bn_ref.at[1:2]),
    ]
    copies = [pltpu.make_async_copy(src, dst, sems.at[i]) for i, (src, dst) in enumerate(pairs)]
    for c in copies:
        c.start()
    first = lax.axis_index("space") * lon
    for c in copies[:3]:
        c.wait()
    lines = land_ref[...].astype(F32)
    for i in range(lon):
        mask = spread(lines[i : i + 1], lat, chans)
        mask_ref[first + i] = mask.astype(BF16)
        put_shifted(ss_ref, first + i + 1, f_ref[0, i].astype(F32) * mask, 1)
        target = t_ref[0, i].astype(F32) * mask
        target_ref[0, i] = target.astype(BF16)
        put_shifted(tt_ref, first + i + 1, target, -1)
    for c in copies[3:]:
        c.wait()
    deep = 3 * chans
    zero = jnp.zeros((deep, chans), BF16)
    for q in range(4):
        rows = slice(q * deep, (q + 1) * deep)
        for half in range(2):
            lanes = slice(half * chans, (half + 1) * chans)
            tap = q - half
            inside = 0 <= tap < 3
            win_ref[rows, lanes] = wraw_ref[3 * tap : 3 * tap + 3].reshape(deep, chans) if inside else zero
            turned = [wout_ref[3 * (2 - tap) + b].T for b in range(3)] if inside else [zero]
            wt_ref[rows, lanes] = jnp.concatenate(turned, axis=0)


def paired(ref, start, pairs):
    columns = [jnp.concatenate([ref[start + 2 * m + q] for m in range(pairs)], axis=0) for q in range(4)]
    return jnp.concatenate(columns, axis=1)


def sample_build(lon, lat, chans, f1_ref, f2_ref, l1_ref, l2_ref, l3_ref, ss_in, mask_in, ss_ref, mask_ref):
    me = lax.axis_index("space")
    for k, f_ref, land_ref in ((1, f1_ref, l1_ref), (2, f2_ref, l2_ref), (3, None, l3_ref)):
        first = jnp.bitwise_xor(me, k) * lon
        lines = land_ref[...].astype(F32)
        for i in range(lon):
            mask = spread(lines[i : i + 1], lat, chans)
            mask_ref[first + i] = mask.astype(BF16)
            if f_ref is not None:
                put_shifted(ss_ref, first + i + 1, f_ref[0, i].astype(F32) * mask, 1)


def sample_conv(lon, lat, chans, f3_ref, ss_in, mask_ref, w_ref, ss_ref, first_ref, stat_ref):
    nx = mask_ref.shape[0]
    start = jnp.bitwise_xor(lax.axis_index("space"), 3) * lon
    for i in range(lon):
        put_shifted(ss_ref, start + i + 1, f3_ref[0, i].astype(F32) * mask_ref[start + i].astype(F32), 1)
    tails = [ss_ref[i + 1, lat - 8 :, chans : 2 * chans].astype(F32) for i in range(nx)]
    for i in range(nx):
        fill = tails[nx - 1 - i][7:8]
        ss_ref[i + 1, lat - 8 :, 2 * chans :] = shift_rows(tails[i], 1, fill).astype(BF16)
    ss_ref[0] = ss_ref[nx]
    ss_ref[nx + 1] = ss_ref[1]
    sums, squares, count = [jnp.zeros((8, chans), F32)] * 3
    fold = lambda v: jnp.sum(v.reshape(-1, 8, chans), axis=0)
    pairs = lon
    for c in range(0, nx, 2 * pairs):
        total = dot(paired(ss_ref, c, pairs), w_ref[...])
        for m in range(pairs):
            for half in range(2):
                k = c + 2 * m + half
                first = total[m * lat : (m + 1) * lat, half * chans : (half + 1) * chans].astype(BF16)
                first_ref[k] = first
                x = first.astype(F32)
                mask = mask_ref[k].astype(F32)
                kept = x * mask
                sums, squares, count = sums + fold(kept), squares + fold(kept * x), count + fold(mask)
    rows = [jnp.sum(v, axis=0, keepdims=True) for v in (sums, squares, count)]
    stat_ref[...] = jnp.concatenate(rows + [jnp.zeros((5, chans), F32)], axis=0)


def sample_adjoint(lon, lat, chans, t1_ref, t2_ref, t3_ref, wt_ref, tt_in, tt_ref, dact_ref):
    nx = dact_ref.shape[0]
    me = lax.axis_index("space")
    for k, t_ref in ((1, t1_ref), (2, t2_ref), (3, t3_ref)):
        start = jnp.bitwise_xor(me, k) * lon
        for i in range(lon):
            put_shifted(tt_ref, start + i + 1, t_ref[0, i].astype(F32), -1)
    tt_ref[0] = tt_ref[nx]
    tt_ref[nx + 1] = tt_ref[1]
    top = [tt_ref[i + 1, lat - 8 :, chans : 2 * chans].astype(F32)[7:8] for i in range(nx)]
    extra = None
    for a in (-1, 0, 1):
        rows = jnp.concatenate([top[nx - 1 - (i + a) % nx] for i in range(nx)], axis=0).astype(BF16)
        part = dot(rows, wt_ref[(1 - a) * 3 * chans + 2 * chans : (2 - a) * 3 * chans, 0:chans])
        extra = part if extra is None else extra + part
    last = lax.broadcasted_iota(jnp.int32, (lat, chans), 0) == lat - 1
    pairs = lon
    for c in range(0, nx, 2 * pairs):
        total = dot(paired(tt_ref, c, pairs), wt_ref[...])
        for m in range(pairs):
            for half in range(2):
                k = c + 2 * m + half
                own = total[m * lat : (m + 1) * lat, half * chans : (half + 1) * chans]
                dact_ref[k] = own + jnp.where(last, extra[k : k + 1], 0.0)


def sample_act(lat, chans, first_ref, mask_ref, stat_ref, bn_ref, dact_ref, gsum_ref, dpre_ref, aa_ref):
    nx = mask_ref.shape[0]
    count, mean, rstd = moments(stat_ref)
    gain, offset = bn_ref[0:1, :], bn_ref[1:2, :]
    scale = lax.rsqrt(count)
    fold = lambda v: jnp.sum(v.reshape(-1, 8, chans), axis=0)
    goff, ggain = [jnp.zeros((8, chans), F32)] * 2
    for i in range(nx // 2):
        acts = []
        for k in (i, nx - 1 - i):
            xhat = (first_ref[k].astype(F32) - mean) * rstd
            u = gain * xhat + offset
            square = u * u
            hyper = jnp.tanh(0.7978845608 * (u + 0.044715 * square * u))
            m = mask_ref[k].astype(F32)
            half = 0.5 * (1.0 + hyper)
            acts.append(u * half * m)
            slope = half + 0.5 * u * (1.0 - hyper * hyper) * 0.7978845608 * (1.0 + 3.0 * 0.044715 * square)
            dpre = dact_ref[k] * scale * m * slope
            dpre_ref[k] = dpre
            goff, ggain = goff + fold(dpre), ggain + fold(dpre * xhat)
        for k, x, other in ((i, acts[0], acts[1]), (nx - 1 - i, acts[1], acts[0])):
            aa_ref[k + 1, :, 0:chans] = shift_rows(x, -1, jnp.zeros((1, chans), F32)).astype(BF16)
            aa_ref[k + 1, :, chans : 2 * chans] = x.astype(BF16)
            aa_ref[k + 1, :, 2 * chans :] = shift_rows(x, 1, other[lat - 1 : lat]).astype(BF16)
    aa_ref[0] = aa_ref[nx]
    aa_ref[nx + 1] = aa_ref[1]
    rows = [jnp.sum(v, axis=0, keepdims=True) for v in (goff, ggain)]
    gsum_ref[...] = jnp.concatenate(rows + [jnp.zeros((6, chans), F32)], axis=0)


def halve(get, keep_ref, send_ref, bit):
    mine = lax.rem(lax.div(lax.axis_index("batch"), bit), 2)
    for j in range(keep_ref.shape[0]):
        keep_ref[j] = get(2 * j + mine)
        send_ref[j] = get(2 * j + 1 - mine)


def fold_kernel(bit, a_ref, b_ref, keep_ref, send_ref):
    halve(lambda k: (a_ref[k].astype(F32) + b_ref[k].astype(F32)).astype(BF16), keep_ref, send_ref, bit)


def exchange_sum(keep, send, size):
    bit = 1
    while True:
        got = lax.ppermute(send, "batch", xor_pairs(size, bit))
        bit *= 2
        if bit == size:
            return jnp.swapaxes(keep[0].astype(F32) + got[0].astype(F32), 1, 2), keep
        half = sds((keep.shape[0] // 2,) + keep.shape[1:], BF16)
        keep, send = run(functools.partial(fold_kernel, bit), [half, half], [keep, got])


def sample_grad(lat, chans, aa_ref, tt_ref, stat_ref, keep_ref, send_ref, grad_ref):
    nx = aa_ref.shape[0] - 2
    scale = lax.rsqrt(stat_ref[2:3, :])
    target = tt_ref[1 : 1 + nx, :, chans : 2 * chans].reshape(nx * lat, chans).astype(F32)
    put_taps(grad_ref, (target * scale).astype(BF16), aa_ref, 1, nx, lat, chans)
    halve(lambda k: grad_ref[k], keep_ref, send_ref, 1)


def sample_out(lon, lat, chans, aa_ref, mask_ref, w_ref, gsum_ref, after_ref, out_ref, gain_ref, offset_ref):
    offset_ref[...] = gsum_ref[0:1, :]
    gain_ref[...] = gsum_ref[1:2, :]
    start = lax.axis_index("space") * lon
    total = None
    for a in (-1, 0, 1):
        piece = aa_ref[pl.ds(start + a + 1, lon)].reshape(lon * lat, 3 * chans)
        part = dot(piece, w_ref[3 * (a + 1) : 3 * (a + 2)].reshape(3 * chans, chans))
        total = part if total is None else total + part
    own_mask = mask_ref[pl.ds(start, lon)].reshape(lon * lat, chans).astype(F32)
    out_ref[...] = (total * own_mask).astype(BF16).reshape(1, lon, lat, chans)


def sample_in(lat, chans, first_ref, mask_ref, stat_ref, bn_ref, dpre_ref, gsum_ref, ss_ref, keep_ref, send_ref, grad_ref):
    nx = mask_ref.shape[0]
    count, mean, rstd = moments(stat_ref)
    goff, ggain = gsum_ref[0:1, :] / count, gsum_ref[1:2, :] / count
    factor = bn_ref[0:1, :] * rstd
    rows = []
    for k in range(nx):
        xhat = (first_ref[k].astype(F32) - mean) * rstd
        rows.append((mask_ref[k].astype(F32) * factor * (dpre_ref[k] - (goff + xhat * ggain))).astype(BF16))
    put_taps(grad_ref, jnp.concatenate(rows, axis=0), ss_ref, 1, nx, lat, chans)
    halve(lambda k: grad_ref[k], keep_ref, send_ref, 1)


def tile_body(fields, land, conv_in, conv_out, batchnorm_gain, batchnorm_offset, target_grad):
    lon, lat, chans = fields.shape[1:]
    tiles = lax.axis_size("space")
    sizes = (lon, lat, chans)
    cells = lon * lat
    gain, offset = batchnorm_gain[None, :], batchnorm_offset[None, :]
    fields, land, conv_in, conv_out, target_grad, gain, offset = (
        pltpu.with_memory_space_constraint(x, pltpu.HBM)
        for x in (fields, land, conv_in, conv_out, target_grad, gain, offset)
    )
    n = lon + 2
    join = tiles == 4
    edge = 3 * lat + 16
    shares = lax.axis_size("batch")
    taps = sds((shares, 9, chans // shares, chans), BF16)
    pay_e, pay_o, polar = run(
        functools.partial(pack_kernel, *sizes, join),
        [sds((edge, chans), BF16), sds((edge + (4 * lon if join else 0), chans), BF16), sds((4 * lon, chans), BF16)],
        [fields, target_grad, land],
        scratch=[
            pltpu.VMEM((4, lat, chans), BF16), pltpu.VMEM((lon, 8, chans), BF16),
            pltpu.VMEM((2, lat, chans), BF16), pltpu.VMEM((lon, 8, chans), BF16),
            pltpu.VMEM((lon, lat), jnp.int32), pltpu.SemaphoreType.DMA((7,)),
        ],
        space=pl.BlockSpec(memory_space=pltpu.HBM),
    )
    mirror = [(i, tiles - 1 - i) for i in range(tiles)]
    got_o = lax.ppermute(pay_o, "space", [(i, (i - 1 if i % 2 == 0 else i + 1) % tiles) for i in range(tiles)])
    got_e = lax.ppermute(pay_e, "space", xor_pairs(tiles, 1))
    if join:
        got_x = lax.ppermute(polar, "space", xor_pairs(tiles, 2))
        poles = [got_o, got_x, got_x, polar]
    else:
        poles = [
            lax.ppermute(polar, "space", mirror),
            lax.ppermute(polar, "space", [(i, (tiles - 2 - i) % tiles) for i in range(tiles)]),
            lax.ppermute(polar, "space", [(i, (tiles - i) % tiles) for i in range(tiles)]),
            polar,
        ]
    wide = sds((lon + 4, lat, 3 * chans), BF16)
    near = sds((n, lat, 3 * chans), BF16)
    ss, tt, own_mask, win, wout, wt, bn = run(
        functools.partial(prep_kernel, *sizes),
        [
            wide, near, sds((cells, chans), BF16), sds(conv_in.shape, BF16), sds(conv_out.shape, BF16),
            sds((3, 3 * chans, chans), BF16), sds((8, chans), F32),
        ],
        [fields, target_grad, land, conv_in, conv_out, gain, offset],
        scratch=[
            pltpu.VMEM(fields.shape, BF16), pltpu.VMEM(fields.shape, BF16), pltpu.VMEM(land.shape, jnp.int32),
            pltpu.SemaphoreType.DMA((7,)),
        ],
        space=pl.BlockSpec(memory_space=pltpu.HBM),
    )

    def conv_body(*refs):
        refs = list(refs)
        if join:
            refs[4] = refs[3]
        conv_kernel(*sizes, edge if join else 0, *refs)

    rows = n * lat + 16
    ss, tt, first, mask, stat, tx = run(
        conv_body,
        [wide, near, sds((rows, chans), BF16), sds((rows, chans), BF16), sds((8, chans), F32), sds((16, chans), F32)],
        [got_e, got_o, *poles, ss, tt, own_mask, win],
        flops=2 * rows * 9 * chans * chans,
        alias={6: 0, 7: 1},
    )
    stat = all_sum(all_sum(stat, "batch"), "space")
    dact = run(
        functools.partial(adjoint_kernel, *sizes),
        [sds((cells, chans), F32)],
        [tt, tx, wt],
        flops=2 * cells * 9 * chans * chans,
    )[0]
    gsum, dpre, aa = run(
        functools.partial(act_kernel, *sizes),
        [sds((8, chans), F32), sds((cells, chans), F32), sds((n, lat, 3 * chans), BF16)],
        [first, mask, stat, bn, dact],
    )
    gsum = all_sum(all_sum(gsum, "batch"), "space")
    output, part_out = run(
        functools.partial(out_kernel, *sizes),
        [sds((1, lon, lat, chans), BF16), taps],
        [aa, mask, tt, stat, wout],
        flops=4 * cells * 9 * chans * chans,
    )
    grad_out = space_sum(scatter_sum(part_out, "batch"))
    part_in = run(
        functools.partial(in_kernel, *sizes),
        [taps],
        [first, mask, stat, bn, dpre, gsum, ss],
        flops=2 * cells * 9 * chans * chans,
    )[0]
    grad_in = space_sum(scatter_sum(part_in, "batch"))
    return (output, grad_in, grad_out, gsum[1], gsum[0])


def sample_body(fields, land, conv_in, conv_out, batchnorm_gain, batchnorm_offset, target_grad):
    lon, lat, chans = fields.shape[1:]
    tiles = lax.axis_size("space")
    sizes = (lon, lat, chans)
    nx = tiles * lon
    near, across = xor_pairs(tiles, 1), xor_pairs(tiles, 2)
    move = lambda x, pairs: lax.ppermute(x, "space", pairs)
    f2 = move(fields, across)
    l2 = move(land, across)
    f1 = move(fields, near)
    l1 = move(land, near)
    l3 = move(land, xor_pairs(tiles, 3))
    f3 = move(f2, near)
    gain, offset = batchnorm_gain[None, :], batchnorm_offset[None, :]
    params = [
        pltpu.with_memory_space_constraint(x, pltpu.HBM)
        for x in (fields, target_grad, land, conv_in, conv_out, gain, offset)
    ]
    shares = lax.axis_size("batch")
    half = sds((shares // 2, 9, chans // shares, chans), BF16)
    whole = [pltpu.VMEM((shares, 9, chans // shares, chans), BF16)]
    shifted = sds((nx + 2, lat, 3 * chans), BF16)
    cells = sds((nx, lat, chans), BF16)
    cells_f = sds((nx, lat, chans), F32)
    sums = sds((8, chans), F32)
    work = 2 * nx * lat * 9 * chans * chans
    double = sds((12 * chans, 2 * chans), BF16)
    ss, tt, mask, target, win, wout, wt, bn = run(
        functools.partial(sample_prep, *sizes, tiles),
        [shifted, shifted, cells, sds(target_grad.shape, BF16), double, sds(conv_out.shape, BF16), double, sums],
        params,
        scratch=[
            pltpu.VMEM(fields.shape, BF16), pltpu.VMEM(fields.shape, BF16), pltpu.VMEM(land.shape, jnp.int32),
            pltpu.VMEM(conv_in.shape, BF16), pltpu.SemaphoreType.DMA((7,)),
        ],
        space=pl.BlockSpec(memory_space=pltpu.HBM),
    )
    ss, mask = run(
        functools.partial(sample_build, *sizes), [shifted, cells], [f1, f2, l1, l2, l3, ss, mask], alias={5: 0, 6: 1}
    )
    t2 = move(target, across)
    t1 = move(target, near)
    t3 = move(t2, near)
    ss, first, stat = run(
        functools.partial(sample_conv, *sizes), [shifted, cells, sums], [f3, ss, mask, win], flops=work, alias={1: 0}
    )
    stat = all_sum(stat, "batch")
    tt, dact = run(
        functools.partial(sample_adjoint, *sizes), [shifted, cells_f], [t1, t2, t3, wt, tt], flops=work, alias={4: 0}
    )
    gsum, dpre, aa = run(
        functools.partial(sample_act, lat, chans), [sums, cells_f, shifted], [first, mask, stat, bn, dact]
    )
    gsum = all_sum(gsum, "batch")
    keep_o, send_o = run(
        functools.partial(sample_grad, lat, chans), [half, half], [aa, tt, stat], scratch=whole, flops=work
    )
    grad_out, _ = exchange_sum(keep_o, send_o, shares)
    keep_i, send_i = run(
        functools.partial(sample_in, lat, chans),
        [half, half], [first, mask, stat, bn, dpre, gsum, ss], scratch=whole, flops=work,
    )
    grad_in, folded = exchange_sum(keep_i, send_i, shares)
    output, grad_gain, grad_offset = run(
        functools.partial(sample_out, *sizes),
        [sds(fields.shape, BF16), sds((1, chans), F32), sds((1, chans), F32)],
        [aa, mask, wout, gsum, folded], flops=work // tiles,
    )
    return (output, grad_in, grad_out, grad_gain[0], grad_offset[0])


def body(*args):
    if lax.axis_size("space") != 4:
        return tile_body(*args)
    return sample_body(*args)


def solution(mesh):
    in_specs = (
        P(("groups", "batch"), "space", None, None),
        P("space", None),
        P(),
        P(),
        P(),
        P(),
        P(("groups", "batch"), "space", None, None),
    )
    out_specs = (
        P(("groups", "batch"), "space", None, None),
        P("groups", None, "batch"),
        P("groups", None, "batch"),
        P("groups"),
        P("groups"),
    )
    return jax.shard_map(body, mesh=mesh, in_specs=in_specs, out_specs=out_specs, check_vma=False)
```

```python
import functools

import jax
import jax.numpy as jnp
from jax import lax
from jax.experimental import pallas as pl
from jax.experimental.pallas import tpu as pltpu
from jax.sharding import PartitionSpec as P


F32 = jnp.float32
BF16 = jnp.bfloat16
VMEM = pl.BlockSpec(memory_space=pltpu.VMEM)


def run(body, outs, args, scratch=(), flops=0, space=VMEM, alias=None):
    nbytes = sum(a.size * a.dtype.itemsize for a in args)
    nbytes += sum(o.size * o.dtype.itemsize for o in outs)
    return pl.pallas_call(
        body,
        out_shape=list(outs),
        in_specs=[space] * len(args),
        out_specs=[VMEM] * len(outs),
        scratch_shapes=list(scratch),
        cost_estimate=pl.CostEstimate(flops=flops, bytes_accessed=nbytes, transcendentals=0),
        compiler_params=pltpu.CompilerParams(vmem_limit_bytes=24 << 20),
        input_output_aliases=alias or {},
    )(*args)


def sds(shape, dtype):
    return jax.ShapeDtypeStruct(shape, dtype)


def dot(a, b):
    return jnp.dot(a, b, preferred_element_type=F32)


def spread(line, lat, chans):
    rows = lax.broadcasted_iota(jnp.int32, (lat, lat), 0)
    cols = lax.broadcasted_iota(jnp.int32, (lat, lat), 1)
    col = jnp.sum(jnp.where(rows == cols, jnp.broadcast_to(line, (lat, lat)), 0.0), axis=1, keepdims=True)
    return jnp.broadcast_to(col, (lat, chans))


def pack_kernel(lon, lat, chans, join, f_hbm, t_hbm, land_hbm, e_ref, o_ref, p_ref, fc, fr, tc, tr, land, sems):
    copies = [
        pltpu.make_async_copy(f_hbm.at[0, 0:2], fc.at[0:2], sems.at[0]),
        pltpu.make_async_copy(f_hbm.at[0, lon - 2 : lon], fc.at[2:4], sems.at[1]),
        pltpu.make_async_copy(f_hbm.at[0, :, lat - 8 : lat], fr, sems.at[2]),
        pltpu.make_async_copy(t_hbm.at[0, 0:1], tc.at[0:1], sems.at[3]),
        pltpu.make_async_copy(t_hbm.at[0, lon - 1 : lon], tc.at[1:2], sems.at[4]),
        pltpu.make_async_copy(t_hbm.at[0, :, lat - 8 : lat], tr, sems.at[5]),
        pltpu.make_async_copy(land_hbm, land, sems.at[6]),
    ]
    for c in copies:
        c.start()
    even = lax.rem(lax.axis_index("space"), 2) == 0
    for c in copies:
        c.wait()
    lines = land[...].astype(F32)

    def edge(k, cols_f, side):
        masks = [spread(lines[i : i + 1], lat, chans) for i in cols_f]
        parts = [fc[k + n].astype(F32) * m for n, m in enumerate(masks)]
        col = cols_f[0] if side == 0 else cols_f[1]
        parts.append(tc[side].astype(F32) * masks[0 if side == 0 else 1])
        line = jnp.concatenate([lines[col : col + 1], jnp.zeros((1, chans - lat), F32)], axis=1)
        parts += [line, jnp.zeros((15, chans), F32)]
        return jnp.concatenate(parts, axis=0).astype(BF16)

    west = edge(0, (0, 1), 0)
    east = edge(2, (lon - 2, lon - 1), 1)
    n = west.shape[0]
    e_ref[...] = jnp.where(even, east, west)
    o_ref[0:n, :] = jnp.where(even, west, east)
    lane = lax.broadcasted_iota(jnp.int32, (lon, lat), 1)
    last = {}
    for j in (lat - 2, lat - 1):
        col = jnp.sum(jnp.where(lane == j, lines, 0.0), axis=1, keepdims=True)
        last[j] = jnp.broadcast_to(col, (lon, chans))
    rows = []
    for j, ref in ((lat - 2, fr), (lat - 1, fr), (lat - 1, tr)):
        k = j - (lat - 8)
        line = jnp.concatenate([ref[i].astype(F32)[k : k + 1] for i in range(lon)], axis=0)
        rows.append(line * last[j])
    rows.append(last[lat - 1])
    polar = jnp.concatenate(rows, axis=0).astype(BF16)
    p_ref[...] = polar
    if join:
        o_ref[n:, :] = polar


def shift_rows(x, step, fill):
    rows = lax.broadcasted_iota(jnp.int32, x.shape, 0)
    n = x.shape[0]
    moved = pltpu.roll(x, (-step) % n, 0)
    return jnp.where(rows == (n - 1 if step > 0 else 0), fill, moved)


def prep_kernel(
    lon, lat, chans,
    f_hbm, t_hbm, land_hbm, win_hbm, wout_hbm, gain_hbm, offset_hbm,
    ss_ref, tt_ref, mask_ref, win_ref, wout_ref, wt_ref, bn_ref,
    f_ref, t_ref, land_ref, sems,
):
    pairs = [
        (land_hbm, land_ref), (f_hbm, f_ref), (t_hbm, t_ref), (wout_hbm, wout_ref), (win_hbm, win_ref),
        (gain_hbm, bn_ref.at[0:1]), (offset_hbm, bn_ref.at[1:2]),
    ]
    copies = [pltpu.make_async_copy(src, dst, sems.at[i]) for i, (src, dst) in enumerate(pairs)]
    for c in copies:
        c.start()
    for c in copies[:3]:
        c.wait()
    lines = land_ref[...].astype(F32)
    zero = jnp.zeros((1, chans), F32)
    for i in range(lon):
        mask = spread(lines[i : i + 1], lat, chans)
        mask_ref[i * lat : (i + 1) * lat] = mask.astype(BF16)
        x = f_ref[0, i].astype(F32) * mask
        ss_ref[i + 2, :, 0:chans] = shift_rows(x, -1, zero).astype(BF16)
        ss_ref[i + 2, :, chans : 2 * chans] = x.astype(BF16)
        ss_ref[i + 2, :, 2 * chans :] = shift_rows(x, 1, zero).astype(BF16)
        x = t_ref[0, i].astype(F32) * mask
        tt_ref[i + 1, :, 0:chans] = shift_rows(x, 1, zero).astype(BF16)
        tt_ref[i + 1, :, chans : 2 * chans] = x.astype(BF16)
        tt_ref[i + 1, :, 2 * chans :] = shift_rows(x, -1, zero).astype(BF16)
    for c in copies[3:]:
        c.wait()
    for a in range(3):
        for b in range(3):
            wt_ref[a, b * chans : (b + 1) * chans] = wout_ref[3 * a + b].T


def conv_kernel(
    lon, lat, chans, moff,
    re_ref, ro_ref, rm_ref, r1_ref, r2_ref, own_ref, ss_in, tt_in, om_ref, w_ref,
    ss_ref, tt_ref, first_ref, mask_ref, stat_ref, tx_ref,
):
    even = lax.rem(lax.axis_index("space"), 2) == 0
    recv_e = re_ref[...].astype(F32)
    recv_o = ro_ref[0 : recv_e.shape[0], :].astype(F32)
    west = jnp.where(even, recv_o, recv_e)
    east = jnp.where(even, recv_e, recv_o)
    polar_m = rm_ref[moff : moff + 4 * lon, :].astype(F32)
    if r1_ref is r2_ref:
        other = r1_ref[...].astype(F32)
        own = own_ref[...].astype(F32)
        polar_1 = jnp.where(even, other, own)
        polar_2 = jnp.where(even, own, other)
    else:
        polar_1 = r1_ref[...].astype(F32)
        polar_2 = r2_ref[...].astype(F32)

    def ghost(kind, cols):
        line = jnp.concatenate([p[kind * lon : (kind + 1) * lon] for p in (polar_1, polar_m, polar_2)], axis=0)
        picks = [2 * lon - 1 - i for i in cols]
        return jnp.concatenate([line[k : k + 1] for k in picks], axis=0)

    zero = jnp.zeros((1, chans), F32)
    wide = list(range(-2, lon + 2))
    near = list(range(-1, lon + 1))
    g62, g63 = ghost(0, wide), ghost(1, wide)
    gt, gm = ghost(2, near), ghost(3, near)
    halo = {0: west[0:lat], 1: west[lat : 2 * lat], lon + 2: east[0:lat], lon + 3: east[lat : 2 * lat]}
    rows8 = lax.broadcasted_iota(jnp.int32, (8, chans), 0)
    top = []
    for k in range(lon + 4):
        fill = g63[k : k + 1]
        if k in halo:
            x = halo[k]
            ss_ref[k, :, 0:chans] = shift_rows(x, -1, zero).astype(BF16)
            ss_ref[k, :, chans : 2 * chans] = x.astype(BF16)
            ss_ref[k, :, 2 * chans :] = shift_rows(x, 1, fill).astype(BF16)
            top.append(x[lat - 1 : lat])
        else:
            tail = ss_ref[k, lat - 8 :, chans : 2 * chans].astype(F32)
            top.append(tail[7:8])
            ss_ref[k, lat - 8 :, 2 * chans :] = shift_rows(tail, 1, fill).astype(BF16)
    top = jnp.concatenate(top, axis=0)
    fold = jnp.concatenate([g62, g63, top], axis=1)
    total = None
    n = lon + 2
    pad = jnp.zeros((16 - n, 3 * chans), F32)
    for a in (-1, 0, 1):
        ghost_rows = jnp.concatenate([fold[1 - a : 1 - a + n], pad], axis=0).astype(BF16)
        piece = jnp.concatenate([ss_ref[a + 1 : a + 1 + n].reshape(n * lat, 3 * chans), ghost_rows], axis=0)
        part = dot(piece, w_ref[3 * (a + 1) : 3 * (a + 2)].reshape(3 * chans, chans))
        total = part if total is None else total + part
    first = total.astype(BF16)
    first_ref[...] = first
    own_first = first[lat : lat + lon * lat].astype(F32)
    own_mask = om_ref[...].astype(F32)
    kept = own_first * own_mask
    sums = jnp.sum(kept, axis=0, keepdims=True)
    squares = jnp.sum(kept * own_first, axis=0, keepdims=True)
    count = jnp.sum(own_mask, axis=0, keepdims=True)
    stat_ref[...] = jnp.concatenate([sums, squares, count, jnp.zeros((5, chans), F32)], axis=0)
    edges = [spread(x[3 * lat : 3 * lat + 1, 0:lat], lat, chans) for x in (west, east)]
    mask_ref[0:lat] = edges[0].astype(BF16)
    mask_ref[lat : lat + lon * lat] = om_ref[...]
    mask_ref[lat + lon * lat : n * lat] = edges[1].astype(BF16)
    mask_ref[n * lat :] = jnp.concatenate([gm, jnp.zeros((16 - n, chans), F32)], axis=0).astype(BF16)
    for k, x in ((0, west[2 * lat : 3 * lat]), (lon + 1, east[2 * lat : 3 * lat])):
        tt_ref[k, :, 0:chans] = shift_rows(x, 1, zero).astype(BF16)
        tt_ref[k, :, chans : 2 * chans] = x.astype(BF16)
        tt_ref[k, :, 2 * chans :] = shift_rows(x, -1, zero).astype(BF16)
    tx_ref[...] = jnp.concatenate([gt, jnp.zeros((16 - n, chans), F32)], axis=0)


def adjoint_kernel(lon, lat, chans, tt_ref, tx_ref, wt_ref, dact_ref):
    gt = tx_ref[...]
    total = None
    for a in (-1, 0, 1):
        extra = jnp.concatenate([gt[1 + a : 1 + a + lon], jnp.zeros((16 - lon, chans), F32)], axis=0)
        extra = jnp.concatenate([jnp.zeros((16, 2 * chans), F32), extra], axis=1).astype(BF16)
        piece = jnp.concatenate([tt_ref[1 - a : 1 - a + lon].reshape(lon * lat, 3 * chans), extra], axis=0)
        part = dot(piece, wt_ref[a + 1])
        total = part if total is None else total + part
    rows = lax.broadcasted_iota(jnp.int32, (lat, chans), 0)
    for i in range(lon):
        add = total[lon * lat + i : lon * lat + i + 1]
        dact_ref[i * lat : (i + 1) * lat, :] = total[i * lat : (i + 1) * lat] + jnp.where(rows == lat - 1, add, 0.0)


def moments(stat_ref):
    count = stat_ref[2:3, :]
    mean = stat_ref[0:1, :] / count
    var = stat_ref[1:2, :] / count - mean * mean
    return count, mean, lax.rsqrt(var + 1e-05)


def act_kernel(lon, lat, chans, first_ref, mask_ref, stat_ref, bn_ref, dact_ref, gsum_ref, dpre_ref, aa_ref):
    count, mean, rstd = moments(stat_ref)
    gain, offset = bn_ref[0:1, :], bn_ref[1:2, :]

    def forward(lo, hi):
        xhat = (first_ref[lo:hi].astype(F32) - mean) * rstd
        u = gain * xhat + offset
        hyper = jnp.tanh(0.7978845608 * (u + 0.044715 * u * u * u))
        m = mask_ref[lo:hi].astype(F32)
        return xhat, u, hyper, m, 0.5 * u * (1.0 + hyper) * m

    n = lon + 2
    zero = jnp.zeros((1, chans), F32)
    ghost = forward(n * lat, n * lat + 16)[4]
    scale = lax.rsqrt(count)
    goff = jnp.zeros((1, chans), F32)
    ggain = jnp.zeros((1, chans), F32)
    for k in range(n):
        xhat, u, hyper, m, act = forward(k * lat, (k + 1) * lat)
        aa_ref[k, :, 0:chans] = shift_rows(act, -1, zero).astype(BF16)
        aa_ref[k, :, chans : 2 * chans] = act.astype(BF16)
        aa_ref[k, :, 2 * chans :] = shift_rows(act, 1, ghost[k : k + 1]).astype(BF16)
        if 0 < k <= lon:
            slope = 0.5 * (1.0 + hyper) + 0.5 * u * (1.0 - hyper * hyper) * 0.7978845608 * (
                1.0 + 3.0 * 0.044715 * u * u
            )
            rows = slice((k - 1) * lat, k * lat)
            dpre = dact_ref[rows] * scale * m * slope
            dpre_ref[rows] = dpre
            goff = goff + jnp.sum(dpre, axis=0, keepdims=True)
            ggain = ggain + jnp.sum(dpre * xhat, axis=0, keepdims=True)
    gsum_ref[...] = jnp.concatenate([goff, ggain, jnp.zeros((6, chans), F32)], axis=0)


def put_taps(grad_ref, grad, shifted_ref, base, lon, lat, chans):
    chunks, width = grad_ref.shape[0], grad_ref.shape[2]
    pieces = [shifted_ref[base + a : base + a + lon].reshape(lon * lat, 3 * chans) for a in (-1, 0, 1)]
    part = dot(grad.T, jnp.concatenate(pieces, axis=1)).astype(BF16)
    for t in range(9):
        for c in range(chunks):
            grad_ref[c, t] = part[c * width : (c + 1) * width, t * chans : (t + 1) * chans]


def out_kernel(lon, lat, chans, aa_ref, mask_ref, tt_ref, stat_ref, w_ref, out_ref, grad_ref):
    total = None
    for a in (-1, 0, 1):
        piece = aa_ref[a + 1 : a + 1 + lon].reshape(lon * lat, 3 * chans)
        part = dot(piece, w_ref[3 * (a + 1) : 3 * (a + 2)].reshape(3 * chans, chans))
        total = part if total is None else total + part
    own_mask = mask_ref[lat : lat + lon * lat].astype(F32)
    out_ref[...] = (total * own_mask).astype(BF16).reshape(1, lon, lat, chans)
    scale = lax.rsqrt(stat_ref[2:3, :])
    target = tt_ref[1 : 1 + lon, :, chans : 2 * chans].reshape(lon * lat, chans).astype(F32)
    dout = (target * scale).astype(BF16)
    put_taps(grad_ref, dout, aa_ref, 1, lon, lat, chans)


def in_kernel(lon, lat, chans, first_ref, mask_ref, stat_ref, bn_ref, dpre_ref, gsum_ref, ss_ref, grad_ref):
    count, mean, rstd = moments(stat_ref)
    goff, ggain = gsum_ref[0:1, :], gsum_ref[1:2, :]
    own = slice(lat, lat + lon * lat)
    xhat = (first_ref[own].astype(F32) - mean) * rstd
    dfirst = mask_ref[own].astype(F32) * (bn_ref[0:1, :] * rstd) * (dpre_ref[...] - (goff + xhat * ggain) / count)
    put_taps(grad_ref, dfirst.astype(BF16), ss_ref, 2, lon, lat, chans)


def xor_pairs(size, k):
    return [(i, i ^ k) for i in range(size)]


def all_sum(x, axis):
    size = lax.axis_size(axis)
    bit = 1
    while bit < size:
        other = lax.ppermute(x, axis, xor_pairs(size, bit))
        if 2 * bit < size:
            far = lax.ppermute(x, axis, xor_pairs(size, 2 * bit))
            both = lax.ppermute(x, axis, xor_pairs(size, 3 * bit))
            x = (x + other) + (far + both)
        else:
            x = x + other
        bit *= 4
    return x


def scatter_sum(x, axis, last=BF16):
    size = lax.axis_size(axis)
    me = lax.axis_index(axis)
    bit = 1
    while bit < size:
        mine = (me // bit) % 2
        split = x.reshape(x.shape[0] // 2, 2, *x.shape[1:])
        keep = lax.dynamic_index_in_dim(split, mine, 1, keepdims=False)
        send = lax.dynamic_index_in_dim(split, 1 - mine, 1, keepdims=False)
        got = lax.ppermute(send, axis, xor_pairs(size, bit))
        bit *= 2
        x = (keep.astype(F32) + got.astype(F32)).astype(BF16 if bit < size else last)
    return x[0]


def space_sum(x):
    size = lax.axis_size("space")
    bit = 1
    while bit < size:
        got = lax.ppermute(x, "space", xor_pairs(size, bit))
        x = x.astype(F32) + got.astype(F32)
        bit *= 2
        if bit < size:
            x = x.astype(BF16)
    return jnp.swapaxes(x, 1, 2)


def put_shifted(ref, k, x, step):
    chans = x.shape[1]
    zero = jnp.zeros((1, chans), F32)
    ref[k, :, 0:chans] = shift_rows(x, -step, zero).astype(BF16)
    ref[k, :, chans : 2 * chans] = x.astype(BF16)
    ref[k, :, 2 * chans :] = shift_rows(x, step, zero).astype(BF16)


def join_kernel(a_ref, b_ref, out_ref):
    rows = a_ref.shape[0]
    out_ref[0:rows] = a_ref[...]
    out_ref[rows:] = b_ref[...]


def sample_prep(
    lon, lat, chans, tiles,
    f_hbm, t_hbm, land_hbm, win_hbm, wout_hbm, gain_hbm, offset_hbm,
    ss_ref, tt_ref, mask_ref, target_ref, land_ref, win_ref, wout_ref, wt_ref, bn_ref,
    f_ref, t_ref, wraw_ref, sems,
):
    pairs = [
        (land_hbm, land_ref), (f_hbm, f_ref), (t_hbm, t_ref), (wout_hbm, wout_ref), (win_hbm, wraw_ref),
        (gain_hbm, bn_ref.at[0:1]), (offset_hbm, bn_ref.at[1:2]),
    ]
    copies = [pltpu.make_async_copy(src, dst, sems.at[i]) for i, (src, dst) in enumerate(pairs)]
    for c in copies:
        c.start()
    first = lax.axis_index("space") * lon
    for c in copies[:3]:
        c.wait()
    lines = land_ref[...].astype(F32)
    for i in range(lon):
        mask = spread(lines[i : i + 1], lat, chans)
        mask_ref[first + i] = mask.astype(BF16)
        put_shifted(ss_ref, first + i + 1, f_ref[0, i].astype(F32) * mask, 1)
        target = t_ref[0, i].astype(F32) * mask
        target_ref[0, i] = target.astype(BF16)
        put_shifted(tt_ref, first + i + 1, target, -1)
    for c in copies[3:]:
        c.wait()
    deep = 3 * chans
    zero = jnp.zeros((deep, chans), BF16)
    for q in range(4):
        rows = slice(q * deep, (q + 1) * deep)
        for half in range(2):
            lanes = slice(half * chans, (half + 1) * chans)
            tap = q - half
            inside = 0 <= tap < 3
            win_ref[rows, lanes] = wraw_ref[3 * tap : 3 * tap + 3].reshape(deep, chans) if inside else zero
            turned = [wout_ref[3 * (2 - tap) + b].T for b in range(3)] if inside else [zero]
            wt_ref[rows, lanes] = jnp.concatenate(turned, axis=0)


def paired(ref, start, pairs):
    columns = [jnp.concatenate([ref[start + 2 * m + q] for m in range(pairs)], axis=0) for q in range(4)]
    return jnp.concatenate(columns, axis=1)


def sample_build(lon, lat, chans, f1_ref, f2_ref, l2_ref, l13_ref, ss_in, mask_in, ss_ref, mask_ref):
    me = lax.axis_index("space")
    for k, f_ref, land_ref in ((1, f1_ref, l13_ref), (2, f2_ref, l2_ref), (3, None, l13_ref)):
        first = jnp.bitwise_xor(me, k) * lon
        lines = land_ref[lon if k == 3 else 0 : 2 * lon if k == 3 else lon].astype(F32)
        for i in range(lon):
            mask = spread(lines[i : i + 1], lat, chans)
            mask_ref[first + i] = mask.astype(BF16)
            if f_ref is not None:
                put_shifted(ss_ref, first + i + 1, f_ref[0, i].astype(F32) * mask, 1)


def sample_conv(lon, lat, chans, f3_ref, ss_in, mask_ref, w_ref, ss_ref, first_ref, stat_ref):
    nx = mask_ref.shape[0]
    start = jnp.bitwise_xor(lax.axis_index("space"), 3) * lon
    for i in range(lon):
        put_shifted(ss_ref, start + i + 1, f3_ref[0, i].astype(F32) * mask_ref[start + i].astype(F32), 1)
    tails = [ss_ref[i + 1, lat - 8 :, chans : 2 * chans].astype(F32) for i in range(nx)]
    for i in range(nx):
        fill = tails[nx - 1 - i][7:8]
        ss_ref[i + 1, lat - 8 :, 2 * chans :] = shift_rows(tails[i], 1, fill).astype(BF16)
    ss_ref[0] = ss_ref[nx]
    ss_ref[nx + 1] = ss_ref[1]
    sums, squares, count = [jnp.zeros((8, chans), F32)] * 3
    fold = lambda v: jnp.sum(v.reshape(-1, 8, chans), axis=0)
    pairs = lon
    for c in range(0, nx, 2 * pairs):
        total = dot(paired(ss_ref, c, pairs), w_ref[...])
        for m in range(pairs):
            for half in range(2):
                k = c + 2 * m + half
                first = total[m * lat : (m + 1) * lat, half * chans : (half + 1) * chans].astype(BF16)
                first_ref[k] = first
                x = first.astype(F32)
                mask = mask_ref[k].astype(F32)
                kept = x * mask
                sums, squares, count = sums + fold(kept), squares + fold(kept * x), count + fold(mask)
    rows = [jnp.sum(v, axis=0, keepdims=True) for v in (sums, squares, count)]
    stat_ref[...] = jnp.concatenate(rows + [jnp.zeros((5, chans), F32)], axis=0)


def sample_adjoint(lon, lat, chans, t1_ref, t2_ref, t3_ref, wt_ref, tt_in, tt_ref, dact_ref):
    nx = dact_ref.shape[0]
    me = lax.axis_index("space")
    for k, t_ref in ((1, t1_ref), (2, t2_ref), (3, t3_ref)):
        start = jnp.bitwise_xor(me, k) * lon
        for i in range(lon):
            put_shifted(tt_ref, start + i + 1, t_ref[0, i].astype(F32), -1)
    tt_ref[0] = tt_ref[nx]
    tt_ref[nx + 1] = tt_ref[1]
    top = [tt_ref[i + 1, lat - 8 :, chans : 2 * chans].astype(F32)[7:8] for i in range(nx)]
    extra = None
    for a in (-1, 0, 1):
        rows = jnp.concatenate([top[nx - 1 - (i + a) % nx] for i in range(nx)], axis=0).astype(BF16)
        part = dot(rows, wt_ref[(1 - a) * 3 * chans + 2 * chans : (2 - a) * 3 * chans, 0:chans])
        extra = part if extra is None else extra + part
    last = lax.broadcasted_iota(jnp.int32, (lat, chans), 0) == lat - 1
    pairs = lon
    for c in range(0, nx, 2 * pairs):
        total = dot(paired(tt_ref, c, pairs), wt_ref[...])
        for m in range(pairs):
            for half in range(2):
                k = c + 2 * m + half
                own = total[m * lat : (m + 1) * lat, half * chans : (half + 1) * chans]
                dact_ref[k] = own + jnp.where(last, extra[k : k + 1], 0.0)


def sample_act(lat, chans, first_ref, mask_ref, stat_ref, bn_ref, dact_ref, gsum_ref, dpre_ref, aa_ref):
    nx = mask_ref.shape[0]
    count, mean, rstd = moments(stat_ref)
    gain, offset = bn_ref[0:1, :], bn_ref[1:2, :]
    scale = lax.rsqrt(count)
    fold = lambda v: jnp.sum(v.reshape(-1, 8, chans), axis=0)
    goff, ggain = [jnp.zeros((8, chans), F32)] * 2
    for i in range(nx // 2):
        acts = []
        for k in (i, nx - 1 - i):
            xhat = (first_ref[k].astype(F32) - mean) * rstd
            u = gain * xhat + offset
            square = u * u
            hyper = jnp.tanh(0.7978845608 * (u + 0.044715 * square * u))
            m = mask_ref[k].astype(F32)
            half = 0.5 * (1.0 + hyper)
            acts.append(u * half * m)
            slope = half + 0.5 * u * (1.0 - hyper * hyper) * 0.7978845608 * (1.0 + 3.0 * 0.044715 * square)
            dpre = dact_ref[k] * scale * m * slope
            dpre_ref[k] = dpre.astype(BF16)
            goff, ggain = goff + fold(dpre), ggain + fold(dpre * xhat)
        for k, x, other in ((i, acts[0], acts[1]), (nx - 1 - i, acts[1], acts[0])):
            aa_ref[k + 1, :, 0:chans] = shift_rows(x, -1, jnp.zeros((1, chans), F32)).astype(BF16)
            aa_ref[k + 1, :, chans : 2 * chans] = x.astype(BF16)
            aa_ref[k + 1, :, 2 * chans :] = shift_rows(x, 1, other[lat - 1 : lat]).astype(BF16)
    aa_ref[0] = aa_ref[nx]
    aa_ref[nx + 1] = aa_ref[1]
    rows = [jnp.sum(v, axis=0, keepdims=True) for v in (goff, ggain)]
    gsum_ref[...] = jnp.concatenate(rows + [jnp.zeros((6, chans), F32)], axis=0)


def halve(get, keep_ref, send_ref, bit):
    mine = lax.rem(lax.div(lax.axis_index("batch"), bit), 2)
    for j in range(keep_ref.shape[0]):
        keep_ref[j] = get(2 * j + mine)
        send_ref[j] = get(2 * j + 1 - mine)


def fold_kernel(bit, a_ref, b_ref, keep_ref, send_ref):
    halve(lambda k: (a_ref[k].astype(F32) + b_ref[k].astype(F32)).astype(BF16), keep_ref, send_ref, bit)


def exchange_sum(keep, send, size):
    bit = 1
    while True:
        got = lax.ppermute(send, "batch", xor_pairs(size, bit))
        bit *= 2
        if bit == size:
            return jnp.swapaxes(keep[0].astype(F32) + got[0].astype(F32), 1, 2), keep
        half = sds((keep.shape[0] // 2,) + keep.shape[1:], BF16)
        keep, send = run(functools.partial(fold_kernel, bit), [half, half], [keep, got])


def sample_grad(lat, chans, aa_ref, tt_ref, stat_ref, keep_ref, send_ref, grad_ref):
    nx = aa_ref.shape[0] - 2
    scale = lax.rsqrt(stat_ref[2:3, :])
    target = tt_ref[1 : 1 + nx, :, chans : 2 * chans].reshape(nx * lat, chans).astype(F32)
    put_taps(grad_ref, (target * scale).astype(BF16), aa_ref, 1, nx, lat, chans)
    halve(lambda k: grad_ref[k], keep_ref, send_ref, 1)


def sample_out(lon, lat, chans, aa_ref, mask_ref, w_ref, gsum_ref, after_ref, out_ref, gain_ref, offset_ref):
    offset_ref[...] = gsum_ref[0:1, :]
    gain_ref[...] = gsum_ref[1:2, :]
    start = lax.axis_index("space") * lon
    total = None
    for a in (-1, 0, 1):
        piece = aa_ref[pl.ds(start + a + 1, lon)].reshape(lon * lat, 3 * chans)
        part = dot(piece, w_ref[3 * (a + 1) : 3 * (a + 2)].reshape(3 * chans, chans))
        total = part if total is None else total + part
    own_mask = mask_ref[pl.ds(start, lon)].reshape(lon * lat, chans).astype(F32)
    out_ref[...] = (total * own_mask).astype(BF16).reshape(1, lon, lat, chans)


def side_by_side(ref, nx, lat, chans):
    return jnp.concatenate([ref[1 + a : 1 + a + nx].reshape(nx * lat, 3 * chans) for a in (-1, 0, 1)], axis=1)


def sample_static(lat, chans, first_ref, mask_ref, ss_ref, d_ref):
    nx = mask_ref.shape[0]
    mask = mask_ref[...].reshape(nx * lat, chans)
    kept = first_ref[...].reshape(nx * lat, chans) * mask
    d_ref[...] = dot(jnp.concatenate([kept.T, mask.T[0:16]], axis=0), side_by_side(ss_ref, nx, lat, chans))


def sample_inner(lat, chans, dpre_ref, ss_ref, a_ref):
    nx = dpre_ref.shape[0]
    a_ref[...] = dot(dpre_ref[...].reshape(nx * lat, chans).T, side_by_side(ss_ref, nx, lat, chans))


def sample_in(chans, a_ref, d_ref, stat_ref, bn_ref, gsum_ref, keep_ref, send_ref, grad_ref):
    count, mean, rstd = moments(stat_ref)
    factor = bn_ref[0:1, :] * rstd
    slope = factor * rstd * gsum_ref[1:2, :] / count
    shift = slope * mean - factor * gsum_ref[0:1, :] / count
    diagonal = lax.broadcasted_iota(jnp.int32, (chans, chans), 0) == lax.broadcasted_iota(jnp.int32, (chans, chans), 1)
    factor, slope, shift = (
        jnp.sum(jnp.where(diagonal, jnp.broadcast_to(v, (chans, chans)), 0.0), axis=1, keepdims=True)
        for v in (factor, slope, shift)
    )
    width = grad_ref.shape[2]
    for t in range(9):
        lanes = slice(t * chans, (t + 1) * chans)
        part = factor * a_ref[:, lanes] + (shift * d_ref[chans : chans + 1, lanes] - slope * d_ref[0:chans, lanes])
        for c in range(grad_ref.shape[0]):
            grad_ref[c, t] = part[c * width : (c + 1) * width].astype(BF16)
    halve(lambda k: grad_ref[k], keep_ref, send_ref, 1)


def tile_body(fields, land, conv_in, conv_out, batchnorm_gain, batchnorm_offset, target_grad):
    lon, lat, chans = fields.shape[1:]
    tiles = lax.axis_size("space")
    sizes = (lon, lat, chans)
    cells = lon * lat
    gain, offset = batchnorm_gain[None, :], batchnorm_offset[None, :]
    fields, land, conv_in, conv_out, target_grad, gain, offset = (
        pltpu.with_memory_space_constraint(x, pltpu.HBM)
        for x in (fields, land, conv_in, conv_out, target_grad, gain, offset)
    )
    n = lon + 2
    join = tiles == 4
    edge = 3 * lat + 16
    shares = lax.axis_size("batch")
    taps = sds((shares, 9, chans // shares, chans), BF16)
    pay_e, pay_o, polar = run(
        functools.partial(pack_kernel, *sizes, join),
        [sds((edge, chans), BF16), sds((edge + (4 * lon if join else 0), chans), BF16), sds((4 * lon, chans), BF16)],
        [fields, target_grad, land],
        scratch=[
            pltpu.VMEM((4, lat, chans), BF16), pltpu.VMEM((lon, 8, chans), BF16),
            pltpu.VMEM((2, lat, chans), BF16), pltpu.VMEM((lon, 8, chans), BF16),
            pltpu.VMEM((lon, lat), jnp.int32), pltpu.SemaphoreType.DMA((7,)),
        ],
        space=pl.BlockSpec(memory_space=pltpu.HBM),
    )
    mirror = [(i, tiles - 1 - i) for i in range(tiles)]
    got_o = lax.ppermute(pay_o, "space", [(i, (i - 1 if i % 2 == 0 else i + 1) % tiles) for i in range(tiles)])
    got_e = lax.ppermute(pay_e, "space", xor_pairs(tiles, 1))
    if join:
        got_x = lax.ppermute(polar, "space", xor_pairs(tiles, 2))
        poles = [got_o, got_x, got_x, polar]
    else:
        poles = [
            lax.ppermute(polar, "space", mirror),
            lax.ppermute(polar, "space", [(i, (tiles - 2 - i) % tiles) for i in range(tiles)]),
            lax.ppermute(polar, "space", [(i, (tiles - i) % tiles) for i in range(tiles)]),
            polar,
        ]
    wide = sds((lon + 4, lat, 3 * chans), BF16)
    near = sds((n, lat, 3 * chans), BF16)
    ss, tt, own_mask, win, wout, wt, bn = run(
        functools.partial(prep_kernel, *sizes),
        [
            wide, near, sds((cells, chans), BF16), sds(conv_in.shape, BF16), sds(conv_out.shape, BF16),
            sds((3, 3 * chans, chans), BF16), sds((8, chans), F32),
        ],
        [fields, target_grad, land, conv_in, conv_out, gain, offset],
        scratch=[
            pltpu.VMEM(fields.shape, BF16), pltpu.VMEM(fields.shape, BF16), pltpu.VMEM(land.shape, jnp.int32),
            pltpu.SemaphoreType.DMA((7,)),
        ],
        space=pl.BlockSpec(memory_space=pltpu.HBM),
    )

    def conv_body(*refs):
        refs = list(refs)
        if join:
            refs[4] = refs[3]
        conv_kernel(*sizes, edge if join else 0, *refs)

    rows = n * lat + 16
    ss, tt, first, mask, stat, tx = run(
        conv_body,
        [wide, near, sds((rows, chans), BF16), sds((rows, chans), BF16), sds((8, chans), F32), sds((16, chans), F32)],
        [got_e, got_o, *poles, ss, tt, own_mask, win],
        flops=2 * rows * 9 * chans * chans,
        alias={6: 0, 7: 1},
    )
    stat = all_sum(all_sum(stat, "batch"), "space")
    dact = run(
        functools.partial(adjoint_kernel, *sizes),
        [sds((cells, chans), F32)],
        [tt, tx, wt],
        flops=2 * cells * 9 * chans * chans,
    )[0]
    gsum, dpre, aa = run(
        functools.partial(act_kernel, *sizes),
        [sds((8, chans), F32), sds((cells, chans), F32), sds((n, lat, 3 * chans), BF16)],
        [first, mask, stat, bn, dact],
    )
    gsum = all_sum(all_sum(gsum, "batch"), "space")
    output, part_out = run(
        functools.partial(out_kernel, *sizes),
        [sds((1, lon, lat, chans), BF16), taps],
        [aa, mask, tt, stat, wout],
        flops=4 * cells * 9 * chans * chans,
    )
    grad_out = space_sum(scatter_sum(part_out, "batch"))
    part_in = run(
        functools.partial(in_kernel, *sizes),
        [taps],
        [first, mask, stat, bn, dpre, gsum, ss],
        flops=2 * cells * 9 * chans * chans,
    )[0]
    grad_in = space_sum(scatter_sum(part_in, "batch"))
    return (output, grad_in, grad_out, gsum[1], gsum[0])


def sample_body(fields, land, conv_in, conv_out, batchnorm_gain, batchnorm_offset, target_grad):
    lon, lat, chans = fields.shape[1:]
    tiles = lax.axis_size("space")
    sizes = (lon, lat, chans)
    nx = tiles * lon
    near, across = xor_pairs(tiles, 1), xor_pairs(tiles, 2)
    move = lambda x, pairs: lax.ppermute(x, "space", pairs)
    f2 = move(fields, across)
    l2 = move(land, across)
    f1 = move(fields, near)
    f3 = move(f2, near)
    gain, offset = batchnorm_gain[None, :], batchnorm_offset[None, :]
    params = [
        pltpu.with_memory_space_constraint(x, pltpu.HBM)
        for x in (fields, target_grad, land, conv_in, conv_out, gain, offset)
    ]
    shares = lax.axis_size("batch")
    half = sds((shares // 2, 9, chans // shares, chans), BF16)
    whole = [pltpu.VMEM((shares, 9, chans // shares, chans), BF16)]
    shifted = sds((nx + 2, lat, 3 * chans), BF16)
    cells = sds((nx, lat, chans), BF16)
    cells_f = sds((nx, lat, chans), F32)
    sums = sds((8, chans), F32)
    work = 2 * nx * lat * 9 * chans * chans
    double = sds((12 * chans, 2 * chans), BF16)
    ss, tt, mask, target, land_own, win, wout, wt, bn = run(
        functools.partial(sample_prep, *sizes, tiles),
        [shifted, shifted, cells, sds(target_grad.shape, BF16), sds(land.shape, jnp.int32), double, sds(conv_out.shape, BF16), double, sums],
        params,
        scratch=[
            pltpu.VMEM(fields.shape, BF16), pltpu.VMEM(fields.shape, BF16), pltpu.VMEM(conv_in.shape, BF16), pltpu.SemaphoreType.DMA((7,)),
        ],
        space=pl.BlockSpec(memory_space=pltpu.HBM),
    )
    (both,) = run(join_kernel, [sds((2 * lon, lat), jnp.int32)], [land_own, l2])
    l13 = move(both, near)
    ss, mask = run(
        functools.partial(sample_build, *sizes), [shifted, cells], [f1, f2, l2, l13, ss, mask], alias={4: 0, 5: 1}
    )
    t2 = move(target, across)
    t1 = move(target, near)
    t3 = move(t2, near)
    ss, first, stat = run(
        functools.partial(sample_conv, *sizes), [shifted, cells, sums], [f3, ss, mask, win], flops=work, alias={1: 0}
    )
    stat = all_sum(stat, "batch")
    tt, dact = run(
        functools.partial(sample_adjoint, *sizes), [shifted, cells_f], [t1, t2, t3, wt, tt], flops=work, alias={4: 0}
    )
    (static,) = run(
        functools.partial(sample_static, lat, chans), [sds((chans + 16, 9 * chans), F32)], [first, mask, ss], flops=work
    )
    gsum, dpre, aa = run(
        functools.partial(sample_act, lat, chans), [sums, cells, shifted], [first, mask, stat, bn, dact]
    )
    gsum = all_sum(gsum, "batch")
    (inner,) = run(functools.partial(sample_inner, lat, chans), [sds((chans, 9 * chans), F32)], [dpre, ss], flops=work)
    keep_o, send_o = run(
        functools.partial(sample_grad, lat, chans), [half, half], [aa, tt, stat], scratch=whole, flops=work
    )
    grad_out, _ = exchange_sum(keep_o, send_o, shares)
    keep_i, send_i = run(
        functools.partial(sample_in, chans), [half, half], [inner, static, stat, bn, gsum], scratch=whole
    )
    grad_in, folded = exchange_sum(keep_i, send_i, shares)
    output, grad_gain, grad_offset = run(
        functools.partial(sample_out, *sizes),
        [sds(fields.shape, BF16), sds((1, chans), F32), sds((1, chans), F32)],
        [aa, mask, wout, gsum, folded], flops=work // tiles,
    )
    return (output, grad_in, grad_out, grad_gain[0], grad_offset[0])


def body(*args):
    if lax.axis_size("space") != 4:
        return tile_body(*args)
    return sample_body(*args)


def solution(mesh):
    in_specs = (
        P(("groups", "batch"), "space", None, None),
        P("space", None),
        P(),
        P(),
        P(),
        P(),
        P(("groups", "batch"), "space", None, None),
    )
    out_specs = (
        P(("groups", "batch"), "space", None, None),
        P("groups", None, "batch"),
        P("groups", None, "batch"),
        P("groups"),
        P("groups"),
    )
    return jax.shard_map(body, mesh=mesh, in_specs=in_specs, out_specs=out_specs, check_vma=False)
```

```python
import functools

import jax
import jax.numpy as jnp
from jax import lax
from jax.experimental import pallas as pl
from jax.experimental.pallas import tpu as pltpu
from jax.sharding import PartitionSpec as P


F32 = jnp.float32
BF16 = jnp.bfloat16
VMEM = pl.BlockSpec(memory_space=pltpu.VMEM)


def run(body, outs, args, scratch=(), flops=0, space=VMEM, alias=None):
    nbytes = sum(a.size * a.dtype.itemsize for a in args)
    nbytes += sum(o.size * o.dtype.itemsize for o in outs)
    return pl.pallas_call(
        body,
        out_shape=list(outs),
        in_specs=[space] * len(args),
        out_specs=[VMEM] * len(outs),
        scratch_shapes=list(scratch),
        cost_estimate=pl.CostEstimate(flops=flops, bytes_accessed=nbytes, transcendentals=0),
        compiler_params=pltpu.CompilerParams(vmem_limit_bytes=24 << 20),
        input_output_aliases=alias or {},
    )(*args)


def sds(shape, dtype):
    return jax.ShapeDtypeStruct(shape, dtype)


def dot(a, b):
    return jnp.dot(a, b, preferred_element_type=F32)


def spread(line, lat, chans):
    rows = lax.broadcasted_iota(jnp.int32, (lat, lat), 0)
    cols = lax.broadcasted_iota(jnp.int32, (lat, lat), 1)
    col = jnp.sum(jnp.where(rows == cols, jnp.broadcast_to(line, (lat, lat)), 0.0), axis=1, keepdims=True)
    return jnp.broadcast_to(col, (lat, chans))


def pack_kernel(lon, lat, chans, join, f_hbm, t_hbm, land_hbm, e_ref, o_ref, p_ref, fc, fr, tc, tr, land, sems):
    copies = [
        pltpu.make_async_copy(f_hbm.at[0, 0:2], fc.at[0:2], sems.at[0]),
        pltpu.make_async_copy(f_hbm.at[0, lon - 2 : lon], fc.at[2:4], sems.at[1]),
        pltpu.make_async_copy(f_hbm.at[0, :, lat - 8 : lat], fr, sems.at[2]),
        pltpu.make_async_copy(t_hbm.at[0, 0:1], tc.at[0:1], sems.at[3]),
        pltpu.make_async_copy(t_hbm.at[0, lon - 1 : lon], tc.at[1:2], sems.at[4]),
        pltpu.make_async_copy(t_hbm.at[0, :, lat - 8 : lat], tr, sems.at[5]),
        pltpu.make_async_copy(land_hbm, land, sems.at[6]),
    ]
    for c in copies:
        c.start()
    even = lax.rem(lax.axis_index("space"), 2) == 0
    for c in copies:
        c.wait()
    lines = land[...].astype(F32)

    def edge(k, cols_f, side):
        masks = [spread(lines[i : i + 1], lat, chans) for i in cols_f]
        parts = [fc[k + n].astype(F32) * m for n, m in enumerate(masks)]
        col = cols_f[0] if side == 0 else cols_f[1]
        parts.append(tc[side].astype(F32) * masks[0 if side == 0 else 1])
        line = jnp.concatenate([lines[col : col + 1], jnp.zeros((1, chans - lat), F32)], axis=1)
        parts += [line, jnp.zeros((15, chans), F32)]
        return jnp.concatenate(parts, axis=0).astype(BF16)

    west = edge(0, (0, 1), 0)
    east = edge(2, (lon - 2, lon - 1), 1)
    n = west.shape[0]
    e_ref[...] = jnp.where(even, east, west)
    o_ref[0:n, :] = jnp.where(even, west, east)
    lane = lax.broadcasted_iota(jnp.int32, (lon, lat), 1)
    last = {}
    for j in (lat - 2, lat - 1):
        col = jnp.sum(jnp.where(lane == j, lines, 0.0), axis=1, keepdims=True)
        last[j] = jnp.broadcast_to(col, (lon, chans))
    rows = []
    for j, ref in ((lat - 2, fr), (lat - 1, fr), (lat - 1, tr)):
        k = j - (lat - 8)
        line = jnp.concatenate([ref[i].astype(F32)[k : k + 1] for i in range(lon)], axis=0)
        rows.append(line * last[j])
    rows.append(last[lat - 1])
    polar = jnp.concatenate(rows, axis=0).astype(BF16)
    p_ref[...] = polar
    if join:
        o_ref[n:, :] = polar


def shift_rows(x, step, fill):
    rows = lax.broadcasted_iota(jnp.int32, x.shape, 0)
    n = x.shape[0]
    moved = pltpu.roll(x, (-step) % n, 0)
    return jnp.where(rows == (n - 1 if step > 0 else 0), fill, moved)


def prep_kernel(
    lon, lat, chans,
    f_hbm, t_hbm, land_hbm, win_hbm, wout_hbm, gain_hbm, offset_hbm,
    ss_ref, tt_ref, mask_ref, win_ref, wout_ref, wt_ref, bn_ref,
    f_ref, t_ref, land_ref, sems,
):
    pairs = [
        (land_hbm, land_ref), (f_hbm, f_ref), (t_hbm, t_ref), (wout_hbm, wout_ref), (win_hbm, win_ref),
        (gain_hbm, bn_ref.at[0:1]), (offset_hbm, bn_ref.at[1:2]),
    ]
    copies = [pltpu.make_async_copy(src, dst, sems.at[i]) for i, (src, dst) in enumerate(pairs)]
    for c in copies:
        c.start()
    for c in copies[:3]:
        c.wait()
    lines = land_ref[...].astype(F32)
    zero = jnp.zeros((1, chans), F32)
    for i in range(lon):
        mask = spread(lines[i : i + 1], lat, chans)
        mask_ref[i * lat : (i + 1) * lat] = mask.astype(BF16)
        x = f_ref[0, i].astype(F32) * mask
        ss_ref[i + 2, :, 0:chans] = shift_rows(x, -1, zero).astype(BF16)
        ss_ref[i + 2, :, chans : 2 * chans] = x.astype(BF16)
        ss_ref[i + 2, :, 2 * chans :] = shift_rows(x, 1, zero).astype(BF16)
        x = t_ref[0, i].astype(F32) * mask
        tt_ref[i + 1, :, 0:chans] = shift_rows(x, 1, zero).astype(BF16)
        tt_ref[i + 1, :, chans : 2 * chans] = x.astype(BF16)
        tt_ref[i + 1, :, 2 * chans :] = shift_rows(x, -1, zero).astype(BF16)
    for c in copies[3:]:
        c.wait()
    for a in range(3):
        for b in range(3):
            wt_ref[a, b * chans : (b + 1) * chans] = wout_ref[3 * a + b].T


def conv_kernel(
    lon, lat, chans, moff,
    re_ref, ro_ref, rm_ref, r1_ref, r2_ref, own_ref, ss_in, tt_in, om_ref, w_ref,
    ss_ref, tt_ref, first_ref, mask_ref, stat_ref, tx_ref,
):
    even = lax.rem(lax.axis_index("space"), 2) == 0
    recv_e = re_ref[...].astype(F32)
    recv_o = ro_ref[0 : recv_e.shape[0], :].astype(F32)
    west = jnp.where(even, recv_o, recv_e)
    east = jnp.where(even, recv_e, recv_o)
    polar_m = rm_ref[moff : moff + 4 * lon, :].astype(F32)
    if r1_ref is r2_ref:
        other = r1_ref[...].astype(F32)
        own = own_ref[...].astype(F32)
        polar_1 = jnp.where(even, other, own)
        polar_2 = jnp.where(even, own, other)
    else:
        polar_1 = r1_ref[...].astype(F32)
        polar_2 = r2_ref[...].astype(F32)

    def ghost(kind, cols):
        line = jnp.concatenate([p[kind * lon : (kind + 1) * lon] for p in (polar_1, polar_m, polar_2)], axis=0)
        picks = [2 * lon - 1 - i for i in cols]
        return jnp.concatenate([line[k : k + 1] for k in picks], axis=0)

    zero = jnp.zeros((1, chans), F32)
    wide = list(range(-2, lon + 2))
    near = list(range(-1, lon + 1))
    g62, g63 = ghost(0, wide), ghost(1, wide)
    gt, gm = ghost(2, near), ghost(3, near)
    halo = {0: west[0:lat], 1: west[lat : 2 * lat], lon + 2: east[0:lat], lon + 3: east[lat : 2 * lat]}
    rows8 = lax.broadcasted_iota(jnp.int32, (8, chans), 0)
    top = []
    for k in range(lon + 4):
        fill = g63[k : k + 1]
        if k in halo:
            x = halo[k]
            ss_ref[k, :, 0:chans] = shift_rows(x, -1, zero).astype(BF16)
            ss_ref[k, :, chans : 2 * chans] = x.astype(BF16)
            ss_ref[k, :, 2 * chans :] = shift_rows(x, 1, fill).astype(BF16)
            top.append(x[lat - 1 : lat])
        else:
            tail = ss_ref[k, lat - 8 :, chans : 2 * chans].astype(F32)
            top.append(tail[7:8])
            ss_ref[k, lat - 8 :, 2 * chans :] = shift_rows(tail, 1, fill).astype(BF16)
    top = jnp.concatenate(top, axis=0)
    fold = jnp.concatenate([g62, g63, top], axis=1)
    total = None
    n = lon + 2
    pad = jnp.zeros((16 - n, 3 * chans), F32)
    for a in (-1, 0, 1):
        ghost_rows = jnp.concatenate([fold[1 - a : 1 - a + n], pad], axis=0).astype(BF16)
        piece = jnp.concatenate([ss_ref[a + 1 : a + 1 + n].reshape(n * lat, 3 * chans), ghost_rows], axis=0)
        part = dot(piece, w_ref[3 * (a + 1) : 3 * (a + 2)].reshape(3 * chans, chans))
        total = part if total is None else total + part
    first = total.astype(BF16)
    first_ref[...] = first
    own_first = first[lat : lat + lon * lat].astype(F32)
    own_mask = om_ref[...].astype(F32)
    kept = own_first * own_mask
    sums = jnp.sum(kept, axis=0, keepdims=True)
    squares = jnp.sum(kept * own_first, axis=0, keepdims=True)
    count = jnp.sum(own_mask, axis=0, keepdims=True)
    stat_ref[...] = jnp.concatenate([sums, squares, count, jnp.zeros((5, chans), F32)], axis=0)
    edges = [spread(x[3 * lat : 3 * lat + 1, 0:lat], lat, chans) for x in (west, east)]
    mask_ref[0:lat] = edges[0].astype(BF16)
    mask_ref[lat : lat + lon * lat] = om_ref[...]
    mask_ref[lat + lon * lat : n * lat] = edges[1].astype(BF16)
    mask_ref[n * lat :] = jnp.concatenate([gm, jnp.zeros((16 - n, chans), F32)], axis=0).astype(BF16)
    for k, x in ((0, west[2 * lat : 3 * lat]), (lon + 1, east[2 * lat : 3 * lat])):
        tt_ref[k, :, 0:chans] = shift_rows(x, 1, zero).astype(BF16)
        tt_ref[k, :, chans : 2 * chans] = x.astype(BF16)
        tt_ref[k, :, 2 * chans :] = shift_rows(x, -1, zero).astype(BF16)
    tx_ref[...] = jnp.concatenate([gt, jnp.zeros((16 - n, chans), F32)], axis=0)


def adjoint_kernel(lon, lat, chans, tt_ref, tx_ref, wt_ref, dact_ref):
    gt = tx_ref[...]
    total = None
    for a in (-1, 0, 1):
        extra = jnp.concatenate([gt[1 + a : 1 + a + lon], jnp.zeros((16 - lon, chans), F32)], axis=0)
        extra = jnp.concatenate([jnp.zeros((16, 2 * chans), F32), extra], axis=1).astype(BF16)
        piece = jnp.concatenate([tt_ref[1 - a : 1 - a + lon].reshape(lon * lat, 3 * chans), extra], axis=0)
        part = dot(piece, wt_ref[a + 1])
        total = part if total is None else total + part
    rows = lax.broadcasted_iota(jnp.int32, (lat, chans), 0)
    for i in range(lon):
        add = total[lon * lat + i : lon * lat + i + 1]
        dact_ref[i * lat : (i + 1) * lat, :] = total[i * lat : (i + 1) * lat] + jnp.where(rows == lat - 1, add, 0.0)


def moments(stat_ref):
    count = stat_ref[2:3, :]
    mean = stat_ref[0:1, :] / count
    var = stat_ref[1:2, :] / count - mean * mean
    return count, mean, lax.rsqrt(var + 1e-05)


def act_kernel(lon, lat, chans, first_ref, mask_ref, stat_ref, bn_ref, dact_ref, gsum_ref, dpre_ref, aa_ref):
    count, mean, rstd = moments(stat_ref)
    gain, offset = bn_ref[0:1, :], bn_ref[1:2, :]

    def forward(lo, hi):
        xhat = (first_ref[lo:hi].astype(F32) - mean) * rstd
        u = gain * xhat + offset
        hyper = jnp.tanh(0.7978845608 * (u + 0.044715 * u * u * u))
        m = mask_ref[lo:hi].astype(F32)
        return xhat, u, hyper, m, 0.5 * u * (1.0 + hyper) * m

    n = lon + 2
    zero = jnp.zeros((1, chans), F32)
    ghost = forward(n * lat, n * lat + 16)[4]
    scale = lax.rsqrt(count)
    goff = jnp.zeros((1, chans), F32)
    ggain = jnp.zeros((1, chans), F32)
    for k in range(n):
        xhat, u, hyper, m, act = forward(k * lat, (k + 1) * lat)
        aa_ref[k, :, 0:chans] = shift_rows(act, -1, zero).astype(BF16)
        aa_ref[k, :, chans : 2 * chans] = act.astype(BF16)
        aa_ref[k, :, 2 * chans :] = shift_rows(act, 1, ghost[k : k + 1]).astype(BF16)
        if 0 < k <= lon:
            slope = 0.5 * (1.0 + hyper) + 0.5 * u * (1.0 - hyper * hyper) * 0.7978845608 * (
                1.0 + 3.0 * 0.044715 * u * u
            )
            rows = slice((k - 1) * lat, k * lat)
            dpre = dact_ref[rows] * scale * m * slope
            dpre_ref[rows] = dpre
            goff = goff + jnp.sum(dpre, axis=0, keepdims=True)
            ggain = ggain + jnp.sum(dpre * xhat, axis=0, keepdims=True)
    gsum_ref[...] = jnp.concatenate([goff, ggain, jnp.zeros((6, chans), F32)], axis=0)


def put_taps(grad_ref, grad, shifted_ref, base, lon, lat, chans):
    chunks, width = grad_ref.shape[0], grad_ref.shape[2]
    pieces = [shifted_ref[base + a : base + a + lon].reshape(lon * lat, 3 * chans) for a in (-1, 0, 1)]
    part = dot(grad.T, jnp.concatenate(pieces, axis=1)).astype(BF16)
    for t in range(9):
        for c in range(chunks):
            grad_ref[c, t] = part[c * width : (c + 1) * width, t * chans : (t + 1) * chans]


def out_kernel(lon, lat, chans, aa_ref, mask_ref, tt_ref, stat_ref, w_ref, out_ref, grad_ref):
    total = None
    for a in (-1, 0, 1):
        piece = aa_ref[a + 1 : a + 1 + lon].reshape(lon * lat, 3 * chans)
        part = dot(piece, w_ref[3 * (a + 1) : 3 * (a + 2)].reshape(3 * chans, chans))
        total = part if total is None else total + part
    own_mask = mask_ref[lat : lat + lon * lat].astype(F32)
    out_ref[...] = (total * own_mask).astype(BF16).reshape(1, lon, lat, chans)
    scale = lax.rsqrt(stat_ref[2:3, :])
    target = tt_ref[1 : 1 + lon, :, chans : 2 * chans].reshape(lon * lat, chans).astype(F32)
    dout = (target * scale).astype(BF16)
    put_taps(grad_ref, dout, aa_ref, 1, lon, lat, chans)


def in_kernel(lon, lat, chans, first_ref, mask_ref, stat_ref, bn_ref, dpre_ref, gsum_ref, ss_ref, grad_ref):
    count, mean, rstd = moments(stat_ref)
    goff, ggain = gsum_ref[0:1, :], gsum_ref[1:2, :]
    own = slice(lat, lat + lon * lat)
    xhat = (first_ref[own].astype(F32) - mean) * rstd
    dfirst = mask_ref[own].astype(F32) * (bn_ref[0:1, :] * rstd) * (dpre_ref[...] - (goff + xhat * ggain) / count)
    put_taps(grad_ref, dfirst.astype(BF16), ss_ref, 2, lon, lat, chans)


def xor_pairs(size, k):
    return [(i, i ^ k) for i in range(size)]


def all_sum(x, axis):
    size = lax.axis_size(axis)
    bit = 1
    while bit < size:
        other = lax.ppermute(x, axis, xor_pairs(size, bit))
        if 2 * bit < size:
            far = lax.ppermute(x, axis, xor_pairs(size, 2 * bit))
            both = lax.ppermute(x, axis, xor_pairs(size, 3 * bit))
            x = (x + other) + (far + both)
        else:
            x = x + other
        bit *= 4
    return x


def scatter_sum(x, axis, last=BF16):
    size = lax.axis_size(axis)
    me = lax.axis_index(axis)
    bit = 1
    while bit < size:
        mine = (me // bit) % 2
        split = x.reshape(x.shape[0] // 2, 2, *x.shape[1:])
        keep = lax.dynamic_index_in_dim(split, mine, 1, keepdims=False)
        send = lax.dynamic_index_in_dim(split, 1 - mine, 1, keepdims=False)
        got = lax.ppermute(send, axis, xor_pairs(size, bit))
        bit *= 2
        x = (keep.astype(F32) + got.astype(F32)).astype(BF16 if bit < size else last)
    return x[0]


def space_sum(x):
    size = lax.axis_size("space")
    bit = 1
    while bit < size:
        got = lax.ppermute(x, "space", xor_pairs(size, bit))
        x = x.astype(F32) + got.astype(F32)
        bit *= 2
        if bit < size:
            x = x.astype(BF16)
    return jnp.swapaxes(x, 1, 2)


def put_shifted(ref, k, x, step):
    chans = x.shape[1]
    zero = jnp.zeros((1, chans), F32)
    ref[k, :, 0:chans] = shift_rows(x, -step, zero).astype(BF16)
    ref[k, :, chans : 2 * chans] = x.astype(BF16)
    ref[k, :, 2 * chans :] = shift_rows(x, step, zero).astype(BF16)


def join_kernel(a_ref, b_ref, out_ref):
    rows = a_ref.shape[0]
    out_ref[0:rows] = a_ref[...]
    out_ref[rows:] = b_ref[...]


def sample_prep(
    lon, lat, chans, tiles,
    f_hbm, t_hbm, land_hbm, win_hbm, wout_hbm, gain_hbm, offset_hbm,
    ss_ref, tt_ref, mask_ref, target_ref, land_ref, win_ref, wout_ref, wt_ref, bn_ref,
    f_ref, t_ref, wraw_ref, sems,
):
    pairs = [
        (land_hbm, land_ref), (f_hbm, f_ref), (t_hbm, t_ref), (wout_hbm, wout_ref), (win_hbm, wraw_ref),
        (gain_hbm, bn_ref.at[0:1]), (offset_hbm, bn_ref.at[1:2]),
    ]
    copies = [pltpu.make_async_copy(src, dst, sems.at[i]) for i, (src, dst) in enumerate(pairs)]
    for c in copies:
        c.start()
    first = lax.axis_index("space") * lon
    for c in copies[:3]:
        c.wait()
    lines = land_ref[...].astype(F32)
    for i in range(lon):
        mask = spread(lines[i : i + 1], lat, chans)
        mask_ref[first + i] = mask.astype(BF16)
        put_shifted(ss_ref, first + i + 1, f_ref[0, i].astype(F32) * mask, 1)
        target = t_ref[0, i].astype(F32) * mask
        target_ref[0, i] = target.astype(BF16)
        put_shifted(tt_ref, first + i + 1, target, -1)
    for c in copies[3:]:
        c.wait()
    deep = 3 * chans
    zero = jnp.zeros((deep, chans), BF16)
    for q in range(4):
        rows = slice(q * deep, (q + 1) * deep)
        for half in range(2):
            lanes = slice(half * chans, (half + 1) * chans)
            tap = q - half
            inside = 0 <= tap < 3
            win_ref[rows, lanes] = wraw_ref[3 * tap : 3 * tap + 3].reshape(deep, chans) if inside else zero
            turned = [wout_ref[3 * (2 - tap) + b].T for b in range(3)] if inside else [zero]
            wt_ref[rows, lanes] = jnp.concatenate(turned, axis=0)


def paired(ref, start, pairs):
    columns = [jnp.concatenate([ref[start + 2 * m + q] for m in range(pairs)], axis=0) for q in range(4)]
    return jnp.concatenate(columns, axis=1)


def sample_build(lon, lat, chans, f1_ref, f2_ref, l2_ref, l13_ref, ss_in, mask_in, ss_ref, mask_ref):
    me = lax.axis_index("space")
    for k, f_ref, land_ref in ((1, f1_ref, l13_ref), (2, f2_ref, l2_ref), (3, None, l13_ref)):
        first = jnp.bitwise_xor(me, k) * lon
        lines = land_ref[lon if k == 3 else 0 : 2 * lon if k == 3 else lon].astype(F32)
        for i in range(lon):
            mask = spread(lines[i : i + 1], lat, chans)
            mask_ref[first + i] = mask.astype(BF16)
            if f_ref is not None:
                put_shifted(ss_ref, first + i + 1, f_ref[0, i].astype(F32) * mask, 1)


def sample_conv(lon, lat, chans, f3_ref, ss_in, mask_ref, w_ref, ss_ref, first_ref, stat_ref):
    nx = mask_ref.shape[0]
    start = jnp.bitwise_xor(lax.axis_index("space"), 3) * lon
    for i in range(lon):
        put_shifted(ss_ref, start + i + 1, f3_ref[0, i].astype(F32) * mask_ref[start + i].astype(F32), 1)
    tails = [ss_ref[i + 1, lat - 8 :, chans : 2 * chans].astype(F32) for i in range(nx)]
    for i in range(nx):
        fill = tails[nx - 1 - i][7:8]
        ss_ref[i + 1, lat - 8 :, 2 * chans :] = shift_rows(tails[i], 1, fill).astype(BF16)
    ss_ref[0] = ss_ref[nx]
    ss_ref[nx + 1] = ss_ref[1]
    sums, squares, count = [jnp.zeros((8, chans), F32)] * 3
    fold = lambda v: jnp.sum(v.reshape(-1, 8, chans), axis=0)
    pairs = lon
    for c in range(0, nx, 2 * pairs):
        total = dot(paired(ss_ref, c, pairs), w_ref[...])
        for m in range(pairs):
            for half in range(2):
                k = c + 2 * m + half
                first = total[m * lat : (m + 1) * lat, half * chans : (half + 1) * chans].astype(BF16)
                first_ref[k] = first
                x = first.astype(F32)
                mask = mask_ref[k].astype(F32)
                kept = x * mask
                sums, squares, count = sums + fold(kept), squares + fold(kept * x), count + fold(mask)
    rows = [jnp.sum(v, axis=0, keepdims=True) for v in (sums, squares, count)]
    stat_ref[...] = jnp.concatenate(rows + [jnp.zeros((5, chans), F32)], axis=0)


def sample_place(lon, t1_ref, t2_ref, tt_in, tt_ref):
    me = lax.axis_index("space")
    for k, t_ref in ((1, t1_ref), (2, t2_ref)):
        start = jnp.bitwise_xor(me, k) * lon
        for i in range(lon):
            put_shifted(tt_ref, start + i + 1, t_ref[0, i].astype(F32), -1)


def sample_adjoint(lon, lat, chans, t3_ref, wt_ref, tt_in, tt_ref, dact_ref):
    nx = dact_ref.shape[0]
    me = lax.axis_index("space")
    for k, t_ref in ((3, t3_ref),):
        start = jnp.bitwise_xor(me, k) * lon
        for i in range(lon):
            put_shifted(tt_ref, start + i + 1, t_ref[0, i].astype(F32), -1)
    tt_ref[0] = tt_ref[nx]
    tt_ref[nx + 1] = tt_ref[1]
    top = [tt_ref[i + 1, lat - 8 :, chans : 2 * chans].astype(F32)[7:8] for i in range(nx)]
    extra = None
    for a in (-1, 0, 1):
        rows = jnp.concatenate([top[nx - 1 - (i + a) % nx] for i in range(nx)], axis=0).astype(BF16)
        part = dot(rows, wt_ref[(1 - a) * 3 * chans + 2 * chans : (2 - a) * 3 * chans, 0:chans])
        extra = part if extra is None else extra + part
    last = lax.broadcasted_iota(jnp.int32, (lat, chans), 0) == lat - 1
    pairs = lon
    for c in range(0, nx, 2 * pairs):
        total = dot(paired(tt_ref, c, pairs), wt_ref[...])
        for m in range(pairs):
            for half in range(2):
                k = c + 2 * m + half
                own = total[m * lat : (m + 1) * lat, half * chans : (half + 1) * chans]
                dact_ref[k] = own + jnp.where(last, extra[k : k + 1], 0.0)


def sample_act(lat, chans, first_ref, mask_ref, stat_ref, bn_ref, dact_ref, gsum_ref, dpre_ref, aa_ref):
    nx = mask_ref.shape[0]
    count, mean, rstd = moments(stat_ref)
    gain, offset = bn_ref[0:1, :], bn_ref[1:2, :]
    scale = lax.rsqrt(count)
    fold = lambda v: jnp.sum(v.reshape(-1, 8, chans), axis=0)
    goff, ggain = [jnp.zeros((8, chans), F32)] * 2
    for i in range(nx // 2):
        acts = []
        for k in (i, nx - 1 - i):
            xhat = (first_ref[k].astype(F32) - mean) * rstd
            u = gain * xhat + offset
            square = u * u
            hyper = jnp.tanh(0.7978845608 * (u + 0.044715 * square * u))
            m = mask_ref[k].astype(F32)
            half = 0.5 * (1.0 + hyper)
            acts.append(u * half * m)
            slope = half + 0.5 * u * (1.0 - hyper * hyper) * 0.7978845608 * (1.0 + 3.0 * 0.044715 * square)
            dpre = dact_ref[k] * scale * m * slope
            dpre_ref[k] = dpre.astype(BF16)
            goff, ggain = goff + fold(dpre), ggain + fold(dpre * xhat)
        for k, x, other in ((i, acts[0], acts[1]), (nx - 1 - i, acts[1], acts[0])):
            aa_ref[k + 1, :, 0:chans] = shift_rows(x, -1, jnp.zeros((1, chans), F32)).astype(BF16)
            aa_ref[k + 1, :, chans : 2 * chans] = x.astype(BF16)
            aa_ref[k + 1, :, 2 * chans :] = shift_rows(x, 1, other[lat - 1 : lat]).astype(BF16)
    aa_ref[0] = aa_ref[nx]
    aa_ref[nx + 1] = aa_ref[1]
    rows = [jnp.sum(v, axis=0, keepdims=True) for v in (goff, ggain)]
    gsum_ref[...] = jnp.concatenate(rows + [jnp.zeros((6, chans), F32)], axis=0)


def halve(get, keep_ref, send_ref, bit):
    mine = lax.rem(lax.div(lax.axis_index("batch"), bit), 2)
    for j in range(keep_ref.shape[0]):
        keep_ref[j] = get(2 * j + mine)
        send_ref[j] = get(2 * j + 1 - mine)


def fold_kernel(bit, a_ref, b_ref, keep_ref, send_ref):
    halve(lambda k: (a_ref[k].astype(F32) + b_ref[k].astype(F32)).astype(BF16), keep_ref, send_ref, bit)


def exchange_sum(keep, send, size):
    bit = 1
    while True:
        got = lax.ppermute(send, "batch", xor_pairs(size, bit))
        bit *= 2
        if bit == size:
            return jnp.swapaxes(keep[0].astype(F32) + got[0].astype(F32), 1, 2), keep
        half = sds((keep.shape[0] // 2,) + keep.shape[1:], BF16)
        keep, send = run(functools.partial(fold_kernel, bit), [half, half], [keep, got])


def sample_grad(lat, chans, aa_ref, tt_ref, stat_ref, keep_ref, send_ref, grad_ref):
    nx = aa_ref.shape[0] - 2
    scale = lax.rsqrt(stat_ref[2:3, :])
    target = tt_ref[1 : 1 + nx, :, chans : 2 * chans].reshape(nx * lat, chans).astype(F32)
    put_taps(grad_ref, (target * scale).astype(BF16), aa_ref, 1, nx, lat, chans)
    halve(lambda k: grad_ref[k], keep_ref, send_ref, 1)


def sample_out(lon, lat, chans, aa_ref, mask_ref, w_ref, gsum_ref, after_ref, out_ref, gain_ref, offset_ref):
    offset_ref[...] = gsum_ref[0:1, :]
    gain_ref[...] = gsum_ref[1:2, :]
    start = lax.axis_index("space") * lon
    total = None
    for a in (-1, 0, 1):
        piece = aa_ref[pl.ds(start + a + 1, lon)].reshape(lon * lat, 3 * chans)
        part = dot(piece, w_ref[3 * (a + 1) : 3 * (a + 2)].reshape(3 * chans, chans))
        total = part if total is None else total + part
    own_mask = mask_ref[pl.ds(start, lon)].reshape(lon * lat, chans).astype(F32)
    out_ref[...] = (total * own_mask).astype(BF16).reshape(1, lon, lat, chans)


def side_by_side(ref, nx, lat, chans):
    return jnp.concatenate([ref[1 + a : 1 + a + nx].reshape(nx * lat, 3 * chans) for a in (-1, 0, 1)], axis=1)


def sample_static(lat, chans, first_ref, mask_ref, ss_ref, d_ref):
    nx = mask_ref.shape[0]
    mask = mask_ref[...].reshape(nx * lat, chans)
    kept = first_ref[...].reshape(nx * lat, chans) * mask
    d_ref[...] = dot(jnp.concatenate([kept.T, mask.T[0:16]], axis=0), side_by_side(ss_ref, nx, lat, chans))


def sample_inner(lat, chans, dpre_ref, ss_ref, a_ref):
    nx = dpre_ref.shape[0]
    a_ref[...] = dot(dpre_ref[...].reshape(nx * lat, chans).T, side_by_side(ss_ref, nx, lat, chans))


def sample_in(chans, a_ref, d_ref, stat_ref, bn_ref, gsum_ref, keep_ref, send_ref, grad_ref):
    count, mean, rstd = moments(stat_ref)
    factor = bn_ref[0:1, :] * rstd
    slope = factor * rstd * gsum_ref[1:2, :] / count
    shift = slope * mean - factor * gsum_ref[0:1, :] / count
    diagonal = lax.broadcasted_iota(jnp.int32, (chans, chans), 0) == lax.broadcasted_iota(jnp.int32, (chans, chans), 1)
    factor, slope, shift = (
        jnp.sum(jnp.where(diagonal, jnp.broadcast_to(v, (chans, chans)), 0.0), axis=1, keepdims=True)
        for v in (factor, slope, shift)
    )
    width = grad_ref.shape[2]
    for t in range(9):
        lanes = slice(t * chans, (t + 1) * chans)
        part = factor * a_ref[:, lanes] + (shift * d_ref[chans : chans + 1, lanes] - slope * d_ref[0:chans, lanes])
        for c in range(grad_ref.shape[0]):
            grad_ref[c, t] = part[c * width : (c + 1) * width].astype(BF16)
    halve(lambda k: grad_ref[k], keep_ref, send_ref, 1)


def tile_body(fields, land, conv_in, conv_out, batchnorm_gain, batchnorm_offset, target_grad):
    lon, lat, chans = fields.shape[1:]
    tiles = lax.axis_size("space")
    sizes = (lon, lat, chans)
    cells = lon * lat
    gain, offset = batchnorm_gain[None, :], batchnorm_offset[None, :]
    fields, land, conv_in, conv_out, target_grad, gain, offset = (
        pltpu.with_memory_space_constraint(x, pltpu.HBM)
        for x in (fields, land, conv_in, conv_out, target_grad, gain, offset)
    )
    n = lon + 2
    join = tiles == 4
    edge = 3 * lat + 16
    shares = lax.axis_size("batch")
    taps = sds((shares, 9, chans // shares, chans), BF16)
    pay_e, pay_o, polar = run(
        functools.partial(pack_kernel, *sizes, join),
        [sds((edge, chans), BF16), sds((edge + (4 * lon if join else 0), chans), BF16), sds((4 * lon, chans), BF16)],
        [fields, target_grad, land],
        scratch=[
            pltpu.VMEM((4, lat, chans), BF16), pltpu.VMEM((lon, 8, chans), BF16),
            pltpu.VMEM((2, lat, chans), BF16), pltpu.VMEM((lon, 8, chans), BF16),
            pltpu.VMEM((lon, lat), jnp.int32), pltpu.SemaphoreType.DMA((7,)),
        ],
        space=pl.BlockSpec(memory_space=pltpu.HBM),
    )
    mirror = [(i, tiles - 1 - i) for i in range(tiles)]
    got_o = lax.ppermute(pay_o, "space", [(i, (i - 1 if i % 2 == 0 else i + 1) % tiles) for i in range(tiles)])
    got_e = lax.ppermute(pay_e, "space", xor_pairs(tiles, 1))
    if join:
        got_x = lax.ppermute(polar, "space", xor_pairs(tiles, 2))
        poles = [got_o, got_x, got_x, polar]
    else:
        poles = [
            lax.ppermute(polar, "space", mirror),
            lax.ppermute(polar, "space", [(i, (tiles - 2 - i) % tiles) for i in range(tiles)]),
            lax.ppermute(polar, "space", [(i, (tiles - i) % tiles) for i in range(tiles)]),
            polar,
        ]
    wide = sds((lon + 4, lat, 3 * chans), BF16)
    near = sds((n, lat, 3 * chans), BF16)
    ss, tt, own_mask, win, wout, wt, bn = run(
        functools.partial(prep_kernel, *sizes),
        [
            wide, near, sds((cells, chans), BF16), sds(conv_in.shape, BF16), sds(conv_out.shape, BF16),
            sds((3, 3 * chans, chans), BF16), sds((8, chans), F32),
        ],
        [fields, target_grad, land, conv_in, conv_out, gain, offset],
        scratch=[
            pltpu.VMEM(fields.shape, BF16), pltpu.VMEM(fields.shape, BF16), pltpu.VMEM(land.shape, jnp.int32),
            pltpu.SemaphoreType.DMA((7,)),
        ],
        space=pl.BlockSpec(memory_space=pltpu.HBM),
    )

    def conv_body(*refs):
        refs = list(refs)
        if join:
            refs[4] = refs[3]
        conv_kernel(*sizes, edge if join else 0, *refs)

    rows = n * lat + 16
    ss, tt, first, mask, stat, tx = run(
        conv_body,
        [wide, near, sds((rows, chans), BF16), sds((rows, chans), BF16), sds((8, chans), F32), sds((16, chans), F32)],
        [got_e, got_o, *poles, ss, tt, own_mask, win],
        flops=2 * rows * 9 * chans * chans,
        alias={6: 0, 7: 1},
    )
    stat = all_sum(all_sum(stat, "batch"), "space")
    dact = run(
        functools.partial(adjoint_kernel, *sizes),
        [sds((cells, chans), F32)],
        [tt, tx, wt],
        flops=2 * cells * 9 * chans * chans,
    )[0]
    gsum, dpre, aa = run(
        functools.partial(act_kernel, *sizes),
        [sds((8, chans), F32), sds((cells, chans), F32), sds((n, lat, 3 * chans), BF16)],
        [first, mask, stat, bn, dact],
    )
    gsum = all_sum(all_sum(gsum, "batch"), "space")
    output, part_out = run(
        functools.partial(out_kernel, *sizes),
        [sds((1, lon, lat, chans), BF16), taps],
        [aa, mask, tt, stat, wout],
        flops=4 * cells * 9 * chans * chans,
    )
    grad_out = space_sum(scatter_sum(part_out, "batch"))
    part_in = run(
        functools.partial(in_kernel, *sizes),
        [taps],
        [first, mask, stat, bn, dpre, gsum, ss],
        flops=2 * cells * 9 * chans * chans,
    )[0]
    grad_in = space_sum(scatter_sum(part_in, "batch"))
    return (output, grad_in, grad_out, gsum[1], gsum[0])


def sample_body(fields, land, conv_in, conv_out, batchnorm_gain, batchnorm_offset, target_grad):
    lon, lat, chans = fields.shape[1:]
    tiles = lax.axis_size("space")
    sizes = (lon, lat, chans)
    nx = tiles * lon
    near, across = xor_pairs(tiles, 1), xor_pairs(tiles, 2)
    move = lambda x, pairs: lax.ppermute(x, "space", pairs)
    f2 = move(fields, across)
    l2 = move(land, across)
    f1 = move(fields, near)
    f3 = move(f2, near)
    gain, offset = batchnorm_gain[None, :], batchnorm_offset[None, :]
    params = [
        pltpu.with_memory_space_constraint(x, pltpu.HBM)
        for x in (fields, target_grad, land, conv_in, conv_out, gain, offset)
    ]
    shares = lax.axis_size("batch")
    half = sds((shares // 2, 9, chans // shares, chans), BF16)
    whole = [pltpu.VMEM((shares, 9, chans // shares, chans), BF16)]
    shifted = sds((nx + 2, lat, 3 * chans), BF16)
    cells = sds((nx, lat, chans), BF16)
    cells_f = sds((nx, lat, chans), F32)
    sums = sds((8, chans), F32)
    work = 2 * nx * lat * 9 * chans * chans
    double = sds((12 * chans, 2 * chans), BF16)
    ss, tt, mask, target, land_own, win, wout, wt, bn = run(
        functools.partial(sample_prep, *sizes, tiles),
        [shifted, shifted, cells, sds(target_grad.shape, BF16), sds(land.shape, jnp.int32), double, sds(conv_out.shape, BF16), double, sums],
        params,
        scratch=[
            pltpu.VMEM(fields.shape, BF16), pltpu.VMEM(fields.shape, BF16), pltpu.VMEM(conv_in.shape, BF16), pltpu.SemaphoreType.DMA((7,)),
        ],
        space=pl.BlockSpec(memory_space=pltpu.HBM),
    )
    (both,) = run(join_kernel, [sds((2 * lon, lat), jnp.int32)], [land_own, l2])
    l13 = move(both, near)
    ss, mask = run(
        functools.partial(sample_build, *sizes), [shifted, cells], [f1, f2, l2, l13, ss, mask], alias={4: 0, 5: 1}
    )
    t2 = move(target, across)
    t1 = move(target, near)
    t3 = move(t2, near)
    ss, first, stat = run(
        functools.partial(sample_conv, *sizes), [shifted, cells, sums], [f3, ss, mask, win], flops=work, alias={1: 0}
    )
    stat = all_sum(stat, "batch")
    (tt,) = run(functools.partial(sample_place, lon), [shifted], [t1, t2, tt], alias={2: 0})
    tt, dact = run(
        functools.partial(sample_adjoint, *sizes), [shifted, cells_f], [t3, wt, tt], flops=work, alias={2: 0}
    )
    (static,) = run(
        functools.partial(sample_static, lat, chans), [sds((chans + 16, 9 * chans), F32)], [first, mask, ss], flops=work
    )
    gsum, dpre, aa = run(
        functools.partial(sample_act, lat, chans), [sums, cells, shifted], [first, mask, stat, bn, dact]
    )
    gsum = all_sum(gsum, "batch")
    (inner,) = run(functools.partial(sample_inner, lat, chans), [sds((chans, 9 * chans), F32)], [dpre, ss], flops=work)
    keep_o, send_o = run(
        functools.partial(sample_grad, lat, chans), [half, half], [aa, tt, stat], scratch=whole, flops=work
    )
    grad_out, _ = exchange_sum(keep_o, send_o, shares)
    keep_i, send_i = run(
        functools.partial(sample_in, chans), [half, half], [inner, static, stat, bn, gsum], scratch=whole
    )
    grad_in, folded = exchange_sum(keep_i, send_i, shares)
    output, grad_gain, grad_offset = run(
        functools.partial(sample_out, *sizes),
        [sds(fields.shape, BF16), sds((1, chans), F32), sds((1, chans), F32)],
        [aa, mask, wout, gsum, folded], flops=work // tiles,
    )
    return (output, grad_in, grad_out, grad_gain[0], grad_offset[0])


def body(*args):
    if lax.axis_size("space") != 4:
        return tile_body(*args)
    return sample_body(*args)


def solution(mesh):
    in_specs = (
        P(("groups", "batch"), "space", None, None),
        P("space", None),
        P(),
        P(),
        P(),
        P(),
        P(("groups", "batch"), "space", None, None),
    )
    out_specs = (
        P(("groups", "batch"), "space", None, None),
        P("groups", None, "batch"),
        P("groups", None, "batch"),
        P("groups"),
        P("groups"),
    )
    return jax.shard_map(body, mesh=mesh, in_specs=in_specs, out_specs=out_specs, check_vma=False)
```

```python
import functools

import jax
import jax.numpy as jnp
from jax import lax
from jax.experimental import pallas as pl
from jax.experimental.pallas import tpu as pltpu
from jax.sharding import PartitionSpec as P


F32 = jnp.float32
BF16 = jnp.bfloat16
VMEM = pl.BlockSpec(memory_space=pltpu.VMEM)


def run(body, outs, args, scratch=(), flops=0, space=VMEM, alias=None):
    nbytes = sum(a.size * a.dtype.itemsize for a in args)
    nbytes += sum(o.size * o.dtype.itemsize for o in outs)
    return pl.pallas_call(
        body,
        out_shape=list(outs),
        in_specs=[space] * len(args),
        out_specs=[VMEM] * len(outs),
        scratch_shapes=list(scratch),
        cost_estimate=pl.CostEstimate(flops=flops, bytes_accessed=nbytes, transcendentals=0),
        compiler_params=pltpu.CompilerParams(vmem_limit_bytes=24 << 20),
        input_output_aliases=alias or {},
    )(*args)


def sds(shape, dtype):
    return jax.ShapeDtypeStruct(shape, dtype)


def dot(a, b):
    return jnp.dot(a, b, preferred_element_type=F32)


def spread(line, lat, chans):
    rows = lax.broadcasted_iota(jnp.int32, (lat, lat), 0)
    cols = lax.broadcasted_iota(jnp.int32, (lat, lat), 1)
    col = jnp.sum(jnp.where(rows == cols, jnp.broadcast_to(line, (lat, lat)), 0.0), axis=1, keepdims=True)
    return jnp.broadcast_to(col, (lat, chans))


def pack_kernel(lon, lat, chans, join, f_hbm, t_hbm, land_hbm, e_ref, o_ref, p_ref, fc, fr, tc, tr, land, sems):
    copies = [
        pltpu.make_async_copy(f_hbm.at[0, 0:2], fc.at[0:2], sems.at[0]),
        pltpu.make_async_copy(f_hbm.at[0, lon - 2 : lon], fc.at[2:4], sems.at[1]),
        pltpu.make_async_copy(f_hbm.at[0, :, lat - 8 : lat], fr, sems.at[2]),
        pltpu.make_async_copy(t_hbm.at[0, 0:1], tc.at[0:1], sems.at[3]),
        pltpu.make_async_copy(t_hbm.at[0, lon - 1 : lon], tc.at[1:2], sems.at[4]),
        pltpu.make_async_copy(t_hbm.at[0, :, lat - 8 : lat], tr, sems.at[5]),
        pltpu.make_async_copy(land_hbm, land, sems.at[6]),
    ]
    for c in copies:
        c.start()
    even = lax.rem(lax.axis_index("space"), 2) == 0
    for c in copies:
        c.wait()
    lines = land[...].astype(F32)

    def edge(k, cols_f, side):
        masks = [spread(lines[i : i + 1], lat, chans) for i in cols_f]
        parts = [fc[k + n].astype(F32) * m for n, m in enumerate(masks)]
        col = cols_f[0] if side == 0 else cols_f[1]
        parts.append(tc[side].astype(F32) * masks[0 if side == 0 else 1])
        line = jnp.concatenate([lines[col : col + 1], jnp.zeros((1, chans - lat), F32)], axis=1)
        parts += [line, jnp.zeros((15, chans), F32)]
        return jnp.concatenate(parts, axis=0).astype(BF16)

    west = edge(0, (0, 1), 0)
    east = edge(2, (lon - 2, lon - 1), 1)
    n = west.shape[0]
    e_ref[...] = jnp.where(even, east, west)
    o_ref[0:n, :] = jnp.where(even, west, east)
    lane = lax.broadcasted_iota(jnp.int32, (lon, lat), 1)
    last = {}
    for j in (lat - 2, lat - 1):
        col = jnp.sum(jnp.where(lane == j, lines, 0.0), axis=1, keepdims=True)
        last[j] = jnp.broadcast_to(col, (lon, chans))
    rows = []
    for j, ref in ((lat - 2, fr), (lat - 1, fr), (lat - 1, tr)):
        k = j - (lat - 8)
        line = jnp.concatenate([ref[i].astype(F32)[k : k + 1] for i in range(lon)], axis=0)
        rows.append(line * last[j])
    rows.append(last[lat - 1])
    polar = jnp.concatenate(rows, axis=0).astype(BF16)
    p_ref[...] = polar
    if join:
        o_ref[n:, :] = polar


def shift_rows(x, step, fill):
    rows = lax.broadcasted_iota(jnp.int32, x.shape, 0)
    n = x.shape[0]
    moved = pltpu.roll(x, (-step) % n, 0)
    return jnp.where(rows == (n - 1 if step > 0 else 0), fill, moved)


def prep_kernel(
    lon, lat, chans,
    f_hbm, t_hbm, land_hbm, win_hbm, wout_hbm, gain_hbm, offset_hbm,
    ss_ref, tt_ref, mask_ref, win_ref, wout_ref, wt_ref, bn_ref,
    f_ref, t_ref, land_ref, sems,
):
    pairs = [
        (land_hbm, land_ref), (f_hbm, f_ref), (t_hbm, t_ref), (wout_hbm, wout_ref), (win_hbm, win_ref),
        (gain_hbm, bn_ref.at[0:1]), (offset_hbm, bn_ref.at[1:2]),
    ]
    copies = [pltpu.make_async_copy(src, dst, sems.at[i]) for i, (src, dst) in enumerate(pairs)]
    for c in copies:
        c.start()
    for c in copies[:3]:
        c.wait()
    lines = land_ref[...].astype(F32)
    zero = jnp.zeros((1, chans), F32)
    for i in range(lon):
        mask = spread(lines[i : i + 1], lat, chans)
        mask_ref[i * lat : (i + 1) * lat] = mask.astype(BF16)
        x = f_ref[0, i].astype(F32) * mask
        ss_ref[i + 2, :, 0:chans] = shift_rows(x, -1, zero).astype(BF16)
        ss_ref[i + 2, :, chans : 2 * chans] = x.astype(BF16)
        ss_ref[i + 2, :, 2 * chans :] = shift_rows(x, 1, zero).astype(BF16)
        x = t_ref[0, i].astype(F32) * mask
        tt_ref[i + 1, :, 0:chans] = shift_rows(x, 1, zero).astype(BF16)
        tt_ref[i + 1, :, chans : 2 * chans] = x.astype(BF16)
        tt_ref[i + 1, :, 2 * chans :] = shift_rows(x, -1, zero).astype(BF16)
    for c in copies[3:]:
        c.wait()
    for a in range(3):
        for b in range(3):
            wt_ref[a, b * chans : (b + 1) * chans] = wout_ref[3 * a + b].T


def conv_kernel(
    lon, lat, chans, moff,
    re_ref, ro_ref, rm_ref, r1_ref, r2_ref, own_ref, ss_in, tt_in, om_ref, w_ref,
    ss_ref, tt_ref, first_ref, mask_ref, stat_ref, tx_ref,
):
    even = lax.rem(lax.axis_index("space"), 2) == 0
    recv_e = re_ref[...].astype(F32)
    recv_o = ro_ref[0 : recv_e.shape[0], :].astype(F32)
    west = jnp.where(even, recv_o, recv_e)
    east = jnp.where(even, recv_e, recv_o)
    polar_m = rm_ref[moff : moff + 4 * lon, :].astype(F32)
    if r1_ref is r2_ref:
        other = r1_ref[...].astype(F32)
        own = own_ref[...].astype(F32)
        polar_1 = jnp.where(even, other, own)
        polar_2 = jnp.where(even, own, other)
    else:
        polar_1 = r1_ref[...].astype(F32)
        polar_2 = r2_ref[...].astype(F32)

    def ghost(kind, cols):
        line = jnp.concatenate([p[kind * lon : (kind + 1) * lon] for p in (polar_1, polar_m, polar_2)], axis=0)
        picks = [2 * lon - 1 - i for i in cols]
        return jnp.concatenate([line[k : k + 1] for k in picks], axis=0)

    zero = jnp.zeros((1, chans), F32)
    wide = list(range(-2, lon + 2))
    near = list(range(-1, lon + 1))
    g62, g63 = ghost(0, wide), ghost(1, wide)
    gt, gm = ghost(2, near), ghost(3, near)
    halo = {0: west[0:lat], 1: west[lat : 2 * lat], lon + 2: east[0:lat], lon + 3: east[lat : 2 * lat]}
    rows8 = lax.broadcasted_iota(jnp.int32, (8, chans), 0)
    top = []
    for k in range(lon + 4):
        fill = g63[k : k + 1]
        if k in halo:
            x = halo[k]
            ss_ref[k, :, 0:chans] = shift_rows(x, -1, zero).astype(BF16)
            ss_ref[k, :, chans : 2 * chans] = x.astype(BF16)
            ss_ref[k, :, 2 * chans :] = shift_rows(x, 1, fill).astype(BF16)
            top.append(x[lat - 1 : lat])
        else:
            tail = ss_ref[k, lat - 8 :, chans : 2 * chans].astype(F32)
            top.append(tail[7:8])
            ss_ref[k, lat - 8 :, 2 * chans :] = shift_rows(tail, 1, fill).astype(BF16)
    top = jnp.concatenate(top, axis=0)
    fold = jnp.concatenate([g62, g63, top], axis=1)
    total = None
    n = lon + 2
    pad = jnp.zeros((16 - n, 3 * chans), F32)
    for a in (-1, 0, 1):
        ghost_rows = jnp.concatenate([fold[1 - a : 1 - a + n], pad], axis=0).astype(BF16)
        piece = jnp.concatenate([ss_ref[a + 1 : a + 1 + n].reshape(n * lat, 3 * chans), ghost_rows], axis=0)
        part = dot(piece, w_ref[3 * (a + 1) : 3 * (a + 2)].reshape(3 * chans, chans))
        total = part if total is None else total + part
    first = total.astype(BF16)
    first_ref[...] = first
    own_first = first[lat : lat + lon * lat].astype(F32)
    own_mask = om_ref[...].astype(F32)
    kept = own_first * own_mask
    sums = jnp.sum(kept, axis=0, keepdims=True)
    squares = jnp.sum(kept * own_first, axis=0, keepdims=True)
    count = jnp.sum(own_mask, axis=0, keepdims=True)
    stat_ref[...] = jnp.concatenate([sums, squares, count, jnp.zeros((5, chans), F32)], axis=0)
    edges = [spread(x[3 * lat : 3 * lat + 1, 0:lat], lat, chans) for x in (west, east)]
    mask_ref[0:lat] = edges[0].astype(BF16)
    mask_ref[lat : lat + lon * lat] = om_ref[...]
    mask_ref[lat + lon * lat : n * lat] = edges[1].astype(BF16)
    mask_ref[n * lat :] = jnp.concatenate([gm, jnp.zeros((16 - n, chans), F32)], axis=0).astype(BF16)
    for k, x in ((0, west[2 * lat : 3 * lat]), (lon + 1, east[2 * lat : 3 * lat])):
        tt_ref[k, :, 0:chans] = shift_rows(x, 1, zero).astype(BF16)
        tt_ref[k, :, chans : 2 * chans] = x.astype(BF16)
        tt_ref[k, :, 2 * chans :] = shift_rows(x, -1, zero).astype(BF16)
    tx_ref[...] = jnp.concatenate([gt, jnp.zeros((16 - n, chans), F32)], axis=0)


def adjoint_kernel(lon, lat, chans, tt_ref, tx_ref, wt_ref, dact_ref):
    gt = tx_ref[...]
    total = None
    for a in (-1, 0, 1):
        extra = jnp.concatenate([gt[1 + a : 1 + a + lon], jnp.zeros((16 - lon, chans), F32)], axis=0)
        extra = jnp.concatenate([jnp.zeros((16, 2 * chans), F32), extra], axis=1).astype(BF16)
        piece = jnp.concatenate([tt_ref[1 - a : 1 - a + lon].reshape(lon * lat, 3 * chans), extra], axis=0)
        part = dot(piece, wt_ref[a + 1])
        total = part if total is None else total + part
    rows = lax.broadcasted_iota(jnp.int32, (lat, chans), 0)
    for i in range(lon):
        add = total[lon * lat + i : lon * lat + i + 1]
        dact_ref[i * lat : (i + 1) * lat, :] = total[i * lat : (i + 1) * lat] + jnp.where(rows == lat - 1, add, 0.0)


def moments(stat_ref):
    count = stat_ref[2:3, :]
    mean = stat_ref[0:1, :] / count
    var = stat_ref[1:2, :] / count - mean * mean
    return count, mean, lax.rsqrt(var + 1e-05)


def act_kernel(lon, lat, chans, first_ref, mask_ref, stat_ref, bn_ref, dact_ref, gsum_ref, dpre_ref, aa_ref):
    count, mean, rstd = moments(stat_ref)
    gain, offset = bn_ref[0:1, :], bn_ref[1:2, :]

    def forward(lo, hi):
        xhat = (first_ref[lo:hi].astype(F32) - mean) * rstd
        u = gain * xhat + offset
        hyper = jnp.tanh(0.7978845608 * (u + 0.044715 * u * u * u))
        m = mask_ref[lo:hi].astype(F32)
        return xhat, u, hyper, m, 0.5 * u * (1.0 + hyper) * m

    n = lon + 2
    zero = jnp.zeros((1, chans), F32)
    ghost = forward(n * lat, n * lat + 16)[4]
    scale = lax.rsqrt(count)
    goff = jnp.zeros((1, chans), F32)
    ggain = jnp.zeros((1, chans), F32)
    for k in range(n):
        xhat, u, hyper, m, act = forward(k * lat, (k + 1) * lat)
        aa_ref[k, :, 0:chans] = shift_rows(act, -1, zero).astype(BF16)
        aa_ref[k, :, chans : 2 * chans] = act.astype(BF16)
        aa_ref[k, :, 2 * chans :] = shift_rows(act, 1, ghost[k : k + 1]).astype(BF16)
        if 0 < k <= lon:
            slope = 0.5 * (1.0 + hyper) + 0.5 * u * (1.0 - hyper * hyper) * 0.7978845608 * (
                1.0 + 3.0 * 0.044715 * u * u
            )
            rows = slice((k - 1) * lat, k * lat)
            dpre = dact_ref[rows] * scale * m * slope
            dpre_ref[rows] = dpre
            goff = goff + jnp.sum(dpre, axis=0, keepdims=True)
            ggain = ggain + jnp.sum(dpre * xhat, axis=0, keepdims=True)
    gsum_ref[...] = jnp.concatenate([goff, ggain, jnp.zeros((6, chans), F32)], axis=0)


def put_taps(grad_ref, grad, shifted_ref, base, lon, lat, chans):
    chunks, width = grad_ref.shape[0], grad_ref.shape[2]
    pieces = [shifted_ref[base + a : base + a + lon].reshape(lon * lat, 3 * chans) for a in (-1, 0, 1)]
    part = dot(grad.T, jnp.concatenate(pieces, axis=1)).astype(BF16)
    for t in range(9):
        for c in range(chunks):
            grad_ref[c, t] = part[c * width : (c + 1) * width, t * chans : (t + 1) * chans]


def out_kernel(lon, lat, chans, aa_ref, mask_ref, tt_ref, stat_ref, w_ref, out_ref, grad_ref):
    total = None
    for a in (-1, 0, 1):
        piece = aa_ref[a + 1 : a + 1 + lon].reshape(lon * lat, 3 * chans)
        part = dot(piece, w_ref[3 * (a + 1) : 3 * (a + 2)].reshape(3 * chans, chans))
        total = part if total is None else total + part
    own_mask = mask_ref[lat : lat + lon * lat].astype(F32)
    out_ref[...] = (total * own_mask).astype(BF16).reshape(1, lon, lat, chans)
    scale = lax.rsqrt(stat_ref[2:3, :])
    target = tt_ref[1 : 1 + lon, :, chans : 2 * chans].reshape(lon * lat, chans).astype(F32)
    dout = (target * scale).astype(BF16)
    put_taps(grad_ref, dout, aa_ref, 1, lon, lat, chans)


def in_kernel(lon, lat, chans, first_ref, mask_ref, stat_ref, bn_ref, dpre_ref, gsum_ref, ss_ref, grad_ref):
    count, mean, rstd = moments(stat_ref)
    goff, ggain = gsum_ref[0:1, :], gsum_ref[1:2, :]
    own = slice(lat, lat + lon * lat)
    xhat = (first_ref[own].astype(F32) - mean) * rstd
    dfirst = mask_ref[own].astype(F32) * (bn_ref[0:1, :] * rstd) * (dpre_ref[...] - (goff + xhat * ggain) / count)
    put_taps(grad_ref, dfirst.astype(BF16), ss_ref, 2, lon, lat, chans)


def xor_pairs(size, k):
    return [(i, i ^ k) for i in range(size)]


def all_sum(x, axis):
    size = lax.axis_size(axis)
    bit = 1
    while bit < size:
        other = lax.ppermute(x, axis, xor_pairs(size, bit))
        if 2 * bit < size:
            far = lax.ppermute(x, axis, xor_pairs(size, 2 * bit))
            both = lax.ppermute(x, axis, xor_pairs(size, 3 * bit))
            x = (x + other) + (far + both)
        else:
            x = x + other
        bit *= 4
    return x


def scatter_sum(x, axis, last=BF16):
    size = lax.axis_size(axis)
    me = lax.axis_index(axis)
    bit = 1
    while bit < size:
        mine = (me // bit) % 2
        split = x.reshape(x.shape[0] // 2, 2, *x.shape[1:])
        keep = lax.dynamic_index_in_dim(split, mine, 1, keepdims=False)
        send = lax.dynamic_index_in_dim(split, 1 - mine, 1, keepdims=False)
        got = lax.ppermute(send, axis, xor_pairs(size, bit))
        bit *= 2
        x = (keep.astype(F32) + got.astype(F32)).astype(BF16 if bit < size else last)
    return x[0]


def space_sum(x):
    size = lax.axis_size("space")
    bit = 1
    while bit < size:
        got = lax.ppermute(x, "space", xor_pairs(size, bit))
        x = x.astype(F32) + got.astype(F32)
        bit *= 2
        if bit < size:
            x = x.astype(BF16)
    return jnp.swapaxes(x, 1, 2)


def put_shifted(ref, k, x, step):
    chans = x.shape[1]
    zero = jnp.zeros((1, chans), F32)
    ref[k, :, 0:chans] = shift_rows(x, -step, zero).astype(BF16)
    ref[k, :, chans : 2 * chans] = x.astype(BF16)
    ref[k, :, 2 * chans :] = shift_rows(x, step, zero).astype(BF16)


def join_kernel(a_ref, b_ref, out_ref):
    rows = a_ref.shape[0]
    out_ref[0:rows] = a_ref[...]
    out_ref[rows:] = b_ref[...]


def sample_prep(
    lon, lat, chans, tiles,
    f_hbm, t_hbm, land_hbm, win_hbm, wout_hbm, gain_hbm, offset_hbm,
    ss_ref, tt_ref, mask_ref, target_ref, land_ref, win_ref, wout_ref, wt_ref, bn_ref,
    f_ref, t_ref, wraw_ref, sems,
):
    pairs = [
        (land_hbm, land_ref), (f_hbm, f_ref), (t_hbm, t_ref), (wout_hbm, wout_ref), (win_hbm, wraw_ref),
        (gain_hbm, bn_ref.at[0:1]), (offset_hbm, bn_ref.at[1:2]),
    ]
    copies = [pltpu.make_async_copy(src, dst, sems.at[i]) for i, (src, dst) in enumerate(pairs)]
    for c in copies:
        c.start()
    first = lax.axis_index("space") * lon
    for c in copies[:3]:
        c.wait()
    lines = land_ref[...].astype(F32)
    for i in range(lon):
        mask = spread(lines[i : i + 1], lat, chans)
        mask_ref[first + i] = mask.astype(BF16)
        put_shifted(ss_ref, first + i + 1, f_ref[0, i].astype(F32) * mask, 1)
        target = t_ref[0, i].astype(F32) * mask
        target_ref[0, i] = target.astype(BF16)
        put_shifted(tt_ref, first + i + 1, target, -1)
    for c in copies[3:]:
        c.wait()
    deep = 3 * chans
    zero = jnp.zeros((deep, chans), BF16)
    for q in range(4):
        rows = slice(q * deep, (q + 1) * deep)
        for half in range(2):
            lanes = slice(half * chans, (half + 1) * chans)
            tap = q - half
            inside = 0 <= tap < 3
            win_ref[rows, lanes] = wraw_ref[3 * tap : 3 * tap + 3].reshape(deep, chans) if inside else zero
            turned = [wout_ref[3 * (2 - tap) + b].T for b in range(3)] if inside else [zero]
            wt_ref[rows, lanes] = jnp.concatenate(turned, axis=0)


def paired(ref, start, pairs):
    columns = [jnp.concatenate([ref[start + 2 * m + q] for m in range(pairs)], axis=0) for q in range(4)]
    return jnp.concatenate(columns, axis=1)


def sample_build(lon, lat, chans, f1_ref, f2_ref, l2_ref, l13_ref, ss_in, mask_in, ss_ref, mask_ref):
    me = lax.axis_index("space")
    for k, f_ref, land_ref in ((1, f1_ref, l13_ref), (2, f2_ref, l2_ref), (3, None, l13_ref)):
        first = jnp.bitwise_xor(me, k) * lon
        lines = land_ref[lon if k == 3 else 0 : 2 * lon if k == 3 else lon].astype(F32)
        for i in range(lon):
            mask = spread(lines[i : i + 1], lat, chans)
            mask_ref[first + i] = mask.astype(BF16)
            if f_ref is not None:
                put_shifted(ss_ref, first + i + 1, f_ref[0, i].astype(F32) * mask, 1)


def sample_conv(lon, lat, chans, f3_ref, ss_in, mask_ref, w_ref, ss_ref, first_ref, stat_ref):
    nx = mask_ref.shape[0]
    start = jnp.bitwise_xor(lax.axis_index("space"), 3) * lon
    for i in range(lon):
        put_shifted(ss_ref, start + i + 1, f3_ref[0, i].astype(F32) * mask_ref[start + i].astype(F32), 1)
    tails = [ss_ref[i + 1, lat - 8 :, chans : 2 * chans].astype(F32) for i in range(nx)]
    for i in range(nx):
        fill = tails[nx - 1 - i][7:8]
        ss_ref[i + 1, lat - 8 :, 2 * chans :] = shift_rows(tails[i], 1, fill).astype(BF16)
    ss_ref[0] = ss_ref[nx]
    ss_ref[nx + 1] = ss_ref[1]
    sums, squares, count = [jnp.zeros((8, chans), F32)] * 3
    fold = lambda v: jnp.sum(v.reshape(-1, 8, chans), axis=0)
    pairs = lon
    for c in range(0, nx, 2 * pairs):
        total = dot(paired(ss_ref, c, pairs), w_ref[...])
        for m in range(pairs):
            for half in range(2):
                k = c + 2 * m + half
                first = total[m * lat : (m + 1) * lat, half * chans : (half + 1) * chans].astype(BF16)
                first_ref[k] = first
                x = first.astype(F32)
                mask = mask_ref[k].astype(F32)
                kept = x * mask
                sums, squares, count = sums + fold(kept), squares + fold(kept * x), count + fold(mask)
    rows = [jnp.sum(v, axis=0, keepdims=True) for v in (sums, squares, count)]
    stat_ref[...] = jnp.concatenate(rows + [jnp.zeros((5, chans), F32)], axis=0)


def sample_place(lon, t1_ref, t2_ref, tt_in, tt_ref):
    me = lax.axis_index("space")
    for k, t_ref in ((1, t1_ref), (2, t2_ref)):
        start = jnp.bitwise_xor(me, k) * lon
        for i in range(lon):
            put_shifted(tt_ref, start + i + 1, t_ref[0, i].astype(F32), -1)


def sample_adjoint(lon, lat, chans, t3_ref, mask_ref, wt_ref, tt_in, tt_ref, dact_ref):
    nx = dact_ref.shape[0]
    me = lax.axis_index("space")
    for k, t_ref in ((3, t3_ref),):
        start = jnp.bitwise_xor(me, k) * lon
        for i in range(lon):
            put_shifted(tt_ref, start + i + 1, t_ref[0, i].astype(F32), -1)
    tt_ref[0] = tt_ref[nx]
    tt_ref[nx + 1] = tt_ref[1]
    top = [tt_ref[i + 1, lat - 8 :, chans : 2 * chans].astype(F32)[7:8] for i in range(nx)]
    extra = None
    for a in (-1, 0, 1):
        rows = jnp.concatenate([top[nx - 1 - (i + a) % nx] for i in range(nx)], axis=0).astype(BF16)
        part = dot(rows, wt_ref[(1 - a) * 3 * chans + 2 * chans : (2 - a) * 3 * chans, 0:chans])
        extra = part if extra is None else extra + part
    last = lax.broadcasted_iota(jnp.int32, (lat, chans), 0) == lat - 1
    pairs = lon
    for c in range(0, nx, 2 * pairs):
        total = dot(paired(tt_ref, c, pairs), wt_ref[...])
        for m in range(pairs):
            for half in range(2):
                k = c + 2 * m + half
                own = total[m * lat : (m + 1) * lat, half * chans : (half + 1) * chans]
                dact_ref[k] = (own + jnp.where(last, extra[k : k + 1], 0.0)) * mask_ref[k].astype(F32)


def sample_act(lat, chans, first_ref, mask_ref, stat_ref, bn_ref, dact_ref, gsum_ref, dpre_ref, aa_ref):
    nx = mask_ref.shape[0]
    count, mean, rstd = moments(stat_ref)
    gain, offset = bn_ref[0:1, :] * rstd, bn_ref[1:2, :]
    scale = lax.rsqrt(count)
    fold = lambda v: jnp.sum(v.reshape(-1, 8, chans), axis=0)
    goff, ggain = [jnp.zeros((8, chans), F32)] * 2
    for i in range(nx // 2):
        acts = []
        for k in (i, nx - 1 - i):
            centred = first_ref[k].astype(F32) - mean
            u = centred * gain + offset
            square = u * u
            half = 0.5 * jnp.tanh(u * (square * (0.7978845608 * 0.044715) + 0.7978845608)) + 0.5
            acts.append(u * half * mask_ref[k].astype(F32))
            bend = square * (6.0 * 0.7978845608 * 0.044715) + 2.0 * 0.7978845608
            slope = half + (half - half * half) * u * bend
            dpre = dact_ref[k] * scale * slope
            dpre_ref[k] = dpre
            goff, ggain = goff + fold(dpre), ggain + fold(dpre * centred)
        for k, x, other in ((i, acts[0], acts[1]), (nx - 1 - i, acts[1], acts[0])):
            aa_ref[k + 1, :, 0:chans] = shift_rows(x, -1, jnp.zeros((1, chans), F32)).astype(BF16)
            aa_ref[k + 1, :, chans : 2 * chans] = x.astype(BF16)
            aa_ref[k + 1, :, 2 * chans :] = shift_rows(x, 1, other[lat - 1 : lat]).astype(BF16)
    aa_ref[0] = aa_ref[nx]
    aa_ref[nx + 1] = aa_ref[1]
    rows = [jnp.sum(v, axis=0, keepdims=True) for v in (goff, ggain * rstd)]
    gsum_ref[...] = jnp.concatenate(rows + [jnp.zeros((6, chans), F32)], axis=0)


def halve(get, keep_ref, send_ref, bit):
    mine = lax.rem(lax.div(lax.axis_index("batch"), bit), 2)
    for j in range(keep_ref.shape[0]):
        keep_ref[j] = get(2 * j + mine)
        send_ref[j] = get(2 * j + 1 - mine)


def fold_kernel(bit, a_ref, b_ref, keep_ref, send_ref):
    halve(lambda k: (a_ref[k].astype(F32) + b_ref[k].astype(F32)).astype(BF16), keep_ref, send_ref, bit)


def exchange_sum(keep, send, size):
    bit = 1
    while True:
        got = lax.ppermute(send, "batch", xor_pairs(size, bit))
        bit *= 2
        if bit == size:
            return jnp.swapaxes(keep[0].astype(F32) + got[0].astype(F32), 1, 2), keep
        half = sds((keep.shape[0] // 2,) + keep.shape[1:], BF16)
        keep, send = run(functools.partial(fold_kernel, bit), [half, half], [keep, got])


def sample_grad(lat, chans, aa_ref, tt_ref, stat_ref, keep_ref, send_ref, grad_ref):
    nx = aa_ref.shape[0] - 2
    scale = lax.rsqrt(stat_ref[2:3, :])
    target = tt_ref[1 : 1 + nx, :, chans : 2 * chans].reshape(nx * lat, chans).astype(F32)
    put_taps(grad_ref, (target * scale).astype(BF16), aa_ref, 1, nx, lat, chans)
    halve(lambda k: grad_ref[k], keep_ref, send_ref, 1)


def sample_out(lon, lat, chans, aa_ref, mask_ref, w_ref, gsum_ref, after_ref, out_ref, gain_ref, offset_ref):
    offset_ref[...] = gsum_ref[0:1, :]
    gain_ref[...] = gsum_ref[1:2, :]
    start = lax.axis_index("space") * lon
    total = None
    for a in (-1, 0, 1):
        piece = aa_ref[pl.ds(start + a + 1, lon)].reshape(lon * lat, 3 * chans)
        part = dot(piece, w_ref[3 * (a + 1) : 3 * (a + 2)].reshape(3 * chans, chans))
        total = part if total is None else total + part
    own_mask = mask_ref[pl.ds(start, lon)].reshape(lon * lat, chans).astype(F32)
    out_ref[...] = (total * own_mask).astype(BF16).reshape(1, lon, lat, chans)


def sample_in(lat, chans, first_ref, mask_ref, stat_ref, bn_ref, dpre_ref, gsum_ref, ss_ref, keep_ref, send_ref, grad_ref):
    nx = mask_ref.shape[0]
    count, mean, rstd = moments(stat_ref)
    goff, ggain = gsum_ref[0:1, :] / count, gsum_ref[1:2, :] / count
    factor = bn_ref[0:1, :] * rstd
    rows = []
    for k in range(nx):
        xhat = (first_ref[k].astype(F32) - mean) * rstd
        rows.append((mask_ref[k].astype(F32) * factor * (dpre_ref[k] - (goff + xhat * ggain))).astype(BF16))
    put_taps(grad_ref, jnp.concatenate(rows, axis=0), ss_ref, 1, nx, lat, chans)
    halve(lambda k: grad_ref[k], keep_ref, send_ref, 1)


def tile_body(fields, land, conv_in, conv_out, batchnorm_gain, batchnorm_offset, target_grad):
    lon, lat, chans = fields.shape[1:]
    tiles = lax.axis_size("space")
    sizes = (lon, lat, chans)
    cells = lon * lat
    gain, offset = batchnorm_gain[None, :], batchnorm_offset[None, :]
    fields, land, conv_in, conv_out, target_grad, gain, offset = (
        pltpu.with_memory_space_constraint(x, pltpu.HBM)
        for x in (fields, land, conv_in, conv_out, target_grad, gain, offset)
    )
    n = lon + 2
    join = tiles == 4
    edge = 3 * lat + 16
    shares = lax.axis_size("batch")
    taps = sds((shares, 9, chans // shares, chans), BF16)
    pay_e, pay_o, polar = run(
        functools.partial(pack_kernel, *sizes, join),
        [sds((edge, chans), BF16), sds((edge + (4 * lon if join else 0), chans), BF16), sds((4 * lon, chans), BF16)],
        [fields, target_grad, land],
        scratch=[
            pltpu.VMEM((4, lat, chans), BF16), pltpu.VMEM((lon, 8, chans), BF16),
            pltpu.VMEM((2, lat, chans), BF16), pltpu.VMEM((lon, 8, chans), BF16),
            pltpu.VMEM((lon, lat), jnp.int32), pltpu.SemaphoreType.DMA((7,)),
        ],
        space=pl.BlockSpec(memory_space=pltpu.HBM),
    )
    mirror = [(i, tiles - 1 - i) for i in range(tiles)]
    got_o = lax.ppermute(pay_o, "space", [(i, (i - 1 if i % 2 == 0 else i + 1) % tiles) for i in range(tiles)])
    got_e = lax.ppermute(pay_e, "space", xor_pairs(tiles, 1))
    if join:
        got_x = lax.ppermute(polar, "space", xor_pairs(tiles, 2))
        poles = [got_o, got_x, got_x, polar]
    else:
        poles = [
            lax.ppermute(polar, "space", mirror),
            lax.ppermute(polar, "space", [(i, (tiles - 2 - i) % tiles) for i in range(tiles)]),
            lax.ppermute(polar, "space", [(i, (tiles - i) % tiles) for i in range(tiles)]),
            polar,
        ]
    wide = sds((lon + 4, lat, 3 * chans), BF16)
    near = sds((n, lat, 3 * chans), BF16)
    ss, tt, own_mask, win, wout, wt, bn = run(
        functools.partial(prep_kernel, *sizes),
        [
            wide, near, sds((cells, chans), BF16), sds(conv_in.shape, BF16), sds(conv_out.shape, BF16),
            sds((3, 3 * chans, chans), BF16), sds((8, chans), F32),
        ],
        [fields, target_grad, land, conv_in, conv_out, gain, offset],
        scratch=[
            pltpu.VMEM(fields.shape, BF16), pltpu.VMEM(fields.shape, BF16), pltpu.VMEM(land.shape, jnp.int32),
            pltpu.SemaphoreType.DMA((7,)),
        ],
        space=pl.BlockSpec(memory_space=pltpu.HBM),
    )

    def conv_body(*refs):
        refs = list(refs)
        if join:
            refs[4] = refs[3]
        conv_kernel(*sizes, edge if join else 0, *refs)

    rows = n * lat + 16
    ss, tt, first, mask, stat, tx = run(
        conv_body,
        [wide, near, sds((rows, chans), BF16), sds((rows, chans), BF16), sds((8, chans), F32), sds((16, chans), F32)],
        [got_e, got_o, *poles, ss, tt, own_mask, win],
        flops=2 * rows * 9 * chans * chans,
        alias={6: 0, 7: 1},
    )
    stat = all_sum(all_sum(stat, "batch"), "space")
    dact = run(
        functools.partial(adjoint_kernel, *sizes),
        [sds((cells, chans), F32)],
        [tt, tx, wt],
        flops=2 * cells * 9 * chans * chans,
    )[0]
    gsum, dpre, aa = run(
        functools.partial(act_kernel, *sizes),
        [sds((8, chans), F32), sds((cells, chans), F32), sds((n, lat, 3 * chans), BF16)],
        [first, mask, stat, bn, dact],
    )
    gsum = all_sum(all_sum(gsum, "batch"), "space")
    output, part_out = run(
        functools.partial(out_kernel, *sizes),
        [sds((1, lon, lat, chans), BF16), taps],
        [aa, mask, tt, stat, wout],
        flops=4 * cells * 9 * chans * chans,
    )
    grad_out = space_sum(scatter_sum(part_out, "batch"))
    part_in = run(
        functools.partial(in_kernel, *sizes),
        [taps],
        [first, mask, stat, bn, dpre, gsum, ss],
        flops=2 * cells * 9 * chans * chans,
    )[0]
    grad_in = space_sum(scatter_sum(part_in, "batch"))
    return (output, grad_in, grad_out, gsum[1], gsum[0])


def sample_body(fields, land, conv_in, conv_out, batchnorm_gain, batchnorm_offset, target_grad):
    lon, lat, chans = fields.shape[1:]
    tiles = lax.axis_size("space")
    sizes = (lon, lat, chans)
    nx = tiles * lon
    near, across = xor_pairs(tiles, 1), xor_pairs(tiles, 2)
    move = lambda x, pairs: lax.ppermute(x, "space", pairs)
    f2 = move(fields, across)
    l2 = move(land, across)
    f1 = move(fields, near)
    f3 = move(f2, near)
    gain, offset = batchnorm_gain[None, :], batchnorm_offset[None, :]
    params = [
        pltpu.with_memory_space_constraint(x, pltpu.HBM)
        for x in (fields, target_grad, land, conv_in, conv_out, gain, offset)
    ]
    shares = lax.axis_size("batch")
    half = sds((shares // 2, 9, chans // shares, chans), BF16)
    whole = [pltpu.VMEM((shares, 9, chans // shares, chans), BF16)]
    shifted = sds((nx + 2, lat, 3 * chans), BF16)
    cells = sds((nx, lat, chans), BF16)
    cells_f = sds((nx, lat, chans), F32)
    sums = sds((8, chans), F32)
    work = 2 * nx * lat * 9 * chans * chans
    double = sds((12 * chans, 2 * chans), BF16)
    ss, tt, mask, target, land_own, win, wout, wt, bn = run(
        functools.partial(sample_prep, *sizes, tiles),
        [shifted, shifted, cells, sds(target_grad.shape, BF16), sds(land.shape, jnp.int32), double, sds(conv_out.shape, BF16), double, sums],
        params,
        scratch=[
            pltpu.VMEM(fields.shape, BF16), pltpu.VMEM(fields.shape, BF16), pltpu.VMEM(conv_in.shape, BF16), pltpu.SemaphoreType.DMA((7,)),
        ],
        space=pl.BlockSpec(memory_space=pltpu.HBM),
    )
    (both,) = run(join_kernel, [sds((2 * lon, lat), jnp.int32)], [land_own, l2])
    l13 = move(both, near)
    ss, mask = run(
        functools.partial(sample_build, *sizes), [shifted, cells], [f1, f2, l2, l13, ss, mask], alias={4: 0, 5: 1}
    )
    t2 = move(target, across)
    t1 = move(target, near)
    t3 = move(t2, near)
    ss, first, stat = run(
        functools.partial(sample_conv, *sizes), [shifted, cells, sums], [f3, ss, mask, win], flops=work, alias={1: 0}
    )
    stat = all_sum(stat, "batch")
    (tt,) = run(functools.partial(sample_place, lon), [shifted], [t1, t2, tt], alias={2: 0})
    tt, dact = run(
        functools.partial(sample_adjoint, *sizes), [shifted, cells_f], [t3, mask, wt, tt], flops=work, alias={3: 0}
    )
    gsum, dpre, aa = run(
        functools.partial(sample_act, lat, chans), [sums, cells_f, shifted], [first, mask, stat, bn, dact]
    )
    gsum = all_sum(gsum, "batch")
    keep_o, send_o = run(
        functools.partial(sample_grad, lat, chans), [half, half], [aa, tt, stat], scratch=whole, flops=work
    )
    grad_out, _ = exchange_sum(keep_o, send_o, shares)
    keep_i, send_i = run(
        functools.partial(sample_in, lat, chans),
        [half, half], [first, mask, stat, bn, dpre, gsum, ss], scratch=whole, flops=work,
    )
    grad_in, folded = exchange_sum(keep_i, send_i, shares)
    output, grad_gain, grad_offset = run(
        functools.partial(sample_out, *sizes),
        [sds(fields.shape, BF16), sds((1, chans), F32), sds((1, chans), F32)],
        [aa, mask, wout, gsum, folded], flops=work // tiles,
    )
    return (output, grad_in, grad_out, grad_gain[0], grad_offset[0])


def body(*args):
    if lax.axis_size("space") != 4:
        return tile_body(*args)
    return sample_body(*args)


def solution(mesh):
    in_specs = (
        P(("groups", "batch"), "space", None, None),
        P("space", None),
        P(),
        P(),
        P(),
        P(),
        P(("groups", "batch"), "space", None, None),
    )
    out_specs = (
        P(("groups", "batch"), "space", None, None),
        P("groups", None, "batch"),
        P("groups", None, "batch"),
        P("groups"),
        P("groups"),
    )
    return jax.shard_map(body, mesh=mesh, in_specs=in_specs, out_specs=out_specs, check_vma=False)
```

```python
import functools

import jax
import jax.numpy as jnp
from jax import lax
from jax.experimental import pallas as pl
from jax.experimental.pallas import tpu as pltpu
from jax.sharding import PartitionSpec as P


F32 = jnp.float32
BF16 = jnp.bfloat16
VMEM = pl.BlockSpec(memory_space=pltpu.VMEM)


def run(body, outs, args, scratch=(), flops=0, space=VMEM, alias=None):
    nbytes = sum(a.size * a.dtype.itemsize for a in args)
    nbytes += sum(o.size * o.dtype.itemsize for o in outs)
    return pl.pallas_call(
        body,
        out_shape=list(outs),
        in_specs=[space] * len(args),
        out_specs=[VMEM] * len(outs),
        scratch_shapes=list(scratch),
        cost_estimate=pl.CostEstimate(flops=flops, bytes_accessed=nbytes, transcendentals=0),
        compiler_params=pltpu.CompilerParams(vmem_limit_bytes=24 << 20),
        input_output_aliases=alias or {},
    )(*args)


def sds(shape, dtype):
    return jax.ShapeDtypeStruct(shape, dtype)


def dot(a, b):
    return jnp.dot(a, b, preferred_element_type=F32)


def spread(line, lat, chans):
    rows = lax.broadcasted_iota(jnp.int32, (lat, lat), 0)
    cols = lax.broadcasted_iota(jnp.int32, (lat, lat), 1)
    col = jnp.sum(jnp.where(rows == cols, jnp.broadcast_to(line, (lat, lat)), 0.0), axis=1, keepdims=True)
    return jnp.broadcast_to(col, (lat, chans))


def pack_kernel(lon, lat, chans, join, f_hbm, t_hbm, land_hbm, e_ref, o_ref, p_ref, fc, fr, tc, tr, land, sems):
    copies = [
        pltpu.make_async_copy(f_hbm.at[0, 0:2], fc.at[0:2], sems.at[0]),
        pltpu.make_async_copy(f_hbm.at[0, lon - 2 : lon], fc.at[2:4], sems.at[1]),
        pltpu.make_async_copy(f_hbm.at[0, :, lat - 8 : lat], fr, sems.at[2]),
        pltpu.make_async_copy(t_hbm.at[0, 0:1], tc.at[0:1], sems.at[3]),
        pltpu.make_async_copy(t_hbm.at[0, lon - 1 : lon], tc.at[1:2], sems.at[4]),
        pltpu.make_async_copy(t_hbm.at[0, :, lat - 8 : lat], tr, sems.at[5]),
        pltpu.make_async_copy(land_hbm, land, sems.at[6]),
    ]
    for c in copies:
        c.start()
    even = lax.rem(lax.axis_index("space"), 2) == 0
    for c in copies:
        c.wait()
    lines = land[...].astype(F32)

    def edge(k, cols_f, side):
        masks = [spread(lines[i : i + 1], lat, chans) for i in cols_f]
        parts = [fc[k + n].astype(F32) * m for n, m in enumerate(masks)]
        col = cols_f[0] if side == 0 else cols_f[1]
        parts.append(tc[side].astype(F32) * masks[0 if side == 0 else 1])
        line = jnp.concatenate([lines[col : col + 1], jnp.zeros((1, chans - lat), F32)], axis=1)
        parts += [line, jnp.zeros((15, chans), F32)]
        return jnp.concatenate(parts, axis=0).astype(BF16)

    west = edge(0, (0, 1), 0)
    east = edge(2, (lon - 2, lon - 1), 1)
    n = west.shape[0]
    e_ref[...] = jnp.where(even, east, west)
    o_ref[0:n, :] = jnp.where(even, west, east)
    lane = lax.broadcasted_iota(jnp.int32, (lon, lat), 1)
    last = {}
    for j in (lat - 2, lat - 1):
        col = jnp.sum(jnp.where(lane == j, lines, 0.0), axis=1, keepdims=True)
        last[j] = jnp.broadcast_to(col, (lon, chans))
    rows = []
    for j, ref in ((lat - 2, fr), (lat - 1, fr), (lat - 1, tr)):
        k = j - (lat - 8)
        line = jnp.concatenate([ref[i].astype(F32)[k : k + 1] for i in range(lon)], axis=0)
        rows.append(line * last[j])
    rows.append(last[lat - 1])
    polar = jnp.concatenate(rows, axis=0).astype(BF16)
    p_ref[...] = polar
    if join:
        o_ref[n:, :] = polar


def shift_rows(x, step, fill):
    rows = lax.broadcasted_iota(jnp.int32, x.shape, 0)
    n = x.shape[0]
    moved = pltpu.roll(x, (-step) % n, 0)
    return jnp.where(rows == (n - 1 if step > 0 else 0), fill, moved)


def prep_kernel(
    lon, lat, chans,
    f_hbm, t_hbm, land_hbm, win_hbm, wout_hbm, gain_hbm, offset_hbm,
    ss_ref, tt_ref, mask_ref, win_ref, wout_ref, wt_ref, bn_ref,
    f_ref, t_ref, land_ref, sems,
):
    pairs = [
        (land_hbm, land_ref), (f_hbm, f_ref), (t_hbm, t_ref), (wout_hbm, wout_ref), (win_hbm, win_ref),
        (gain_hbm, bn_ref.at[0:1]), (offset_hbm, bn_ref.at[1:2]),
    ]
    copies = [pltpu.make_async_copy(src, dst, sems.at[i]) for i, (src, dst) in enumerate(pairs)]
    for c in copies:
        c.start()
    for c in copies[:3]:
        c.wait()
    lines = land_ref[...].astype(F32)
    zero = jnp.zeros((1, chans), F32)
    for i in range(lon):
        mask = spread(lines[i : i + 1], lat, chans)
        mask_ref[i * lat : (i + 1) * lat] = mask.astype(BF16)
        x = f_ref[0, i].astype(F32) * mask
        ss_ref[i + 2, :, 0:chans] = shift_rows(x, -1, zero).astype(BF16)
        ss_ref[i + 2, :, chans : 2 * chans] = x.astype(BF16)
        ss_ref[i + 2, :, 2 * chans :] = shift_rows(x, 1, zero).astype(BF16)
        x = t_ref[0, i].astype(F32) * mask
        tt_ref[i + 1, :, 0:chans] = shift_rows(x, 1, zero).astype(BF16)
        tt_ref[i + 1, :, chans : 2 * chans] = x.astype(BF16)
        tt_ref[i + 1, :, 2 * chans :] = shift_rows(x, -1, zero).astype(BF16)
    for c in copies[3:]:
        c.wait()
    for a in range(3):
        for b in range(3):
            wt_ref[a, b * chans : (b + 1) * chans] = wout_ref[3 * a + b].T


def conv_kernel(
    lon, lat, chans, moff,
    re_ref, ro_ref, rm_ref, r1_ref, r2_ref, own_ref, ss_in, tt_in, om_ref, w_ref,
    ss_ref, tt_ref, first_ref, mask_ref, stat_ref, tx_ref,
):
    even = lax.rem(lax.axis_index("space"), 2) == 0
    recv_e = re_ref[...].astype(F32)
    recv_o = ro_ref[0 : recv_e.shape[0], :].astype(F32)
    west = jnp.where(even, recv_o, recv_e)
    east = jnp.where(even, recv_e, recv_o)
    polar_m = rm_ref[moff : moff + 4 * lon, :].astype(F32)
    if r1_ref is r2_ref:
        other = r1_ref[...].astype(F32)
        own = own_ref[...].astype(F32)
        polar_1 = jnp.where(even, other, own)
        polar_2 = jnp.where(even, own, other)
    else:
        polar_1 = r1_ref[...].astype(F32)
        polar_2 = r2_ref[...].astype(F32)

    def ghost(kind, cols):
        line = jnp.concatenate([p[kind * lon : (kind + 1) * lon] for p in (polar_1, polar_m, polar_2)], axis=0)
        picks = [2 * lon - 1 - i for i in cols]
        return jnp.concatenate([line[k : k + 1] for k in picks], axis=0)

    zero = jnp.zeros((1, chans), F32)
    wide = list(range(-2, lon + 2))
    near = list(range(-1, lon + 1))
    g62, g63 = ghost(0, wide), ghost(1, wide)
    gt, gm = ghost(2, near), ghost(3, near)
    halo = {0: west[0:lat], 1: west[lat : 2 * lat], lon + 2: east[0:lat], lon + 3: east[lat : 2 * lat]}
    rows8 = lax.broadcasted_iota(jnp.int32, (8, chans), 0)
    top = []
    for k in range(lon + 4):
        fill = g63[k : k + 1]
        if k in halo:
            x = halo[k]
            ss_ref[k, :, 0:chans] = shift_rows(x, -1, zero).astype(BF16)
            ss_ref[k, :, chans : 2 * chans] = x.astype(BF16)
            ss_ref[k, :, 2 * chans :] = shift_rows(x, 1, fill).astype(BF16)
            top.append(x[lat - 1 : lat])
        else:
            tail = ss_ref[k, lat - 8 :, chans : 2 * chans].astype(F32)
            top.append(tail[7:8])
            ss_ref[k, lat - 8 :, 2 * chans :] = shift_rows(tail, 1, fill).astype(BF16)
    top = jnp.concatenate(top, axis=0)
    fold = jnp.concatenate([g62, g63, top], axis=1)
    total = None
    n = lon + 2
    pad = jnp.zeros((16 - n, 3 * chans), F32)
    for a in (-1, 0, 1):
        ghost_rows = jnp.concatenate([fold[1 - a : 1 - a + n], pad], axis=0).astype(BF16)
        piece = jnp.concatenate([ss_ref[a + 1 : a + 1 + n].reshape(n * lat, 3 * chans), ghost_rows], axis=0)
        part = dot(piece, w_ref[3 * (a + 1) : 3 * (a + 2)].reshape(3 * chans, chans))
        total = part if total is None else total + part
    first = total.astype(BF16)
    first_ref[...] = first
    own_first = first[lat : lat + lon * lat].astype(F32)
    own_mask = om_ref[...].astype(F32)
    kept = own_first * own_mask
    sums = jnp.sum(kept, axis=0, keepdims=True)
    squares = jnp.sum(kept * own_first, axis=0, keepdims=True)
    count = jnp.sum(own_mask, axis=0, keepdims=True)
    stat_ref[...] = jnp.concatenate([sums, squares, count, jnp.zeros((5, chans), F32)], axis=0)
    edges = [spread(x[3 * lat : 3 * lat + 1, 0:lat], lat, chans) for x in (west, east)]
    mask_ref[0:lat] = edges[0].astype(BF16)
    mask_ref[lat : lat + lon * lat] = om_ref[...]
    mask_ref[lat + lon * lat : n * lat] = edges[1].astype(BF16)
    mask_ref[n * lat :] = jnp.concatenate([gm, jnp.zeros((16 - n, chans), F32)], axis=0).astype(BF16)
    for k, x in ((0, west[2 * lat : 3 * lat]), (lon + 1, east[2 * lat : 3 * lat])):
        tt_ref[k, :, 0:chans] = shift_rows(x, 1, zero).astype(BF16)
        tt_ref[k, :, chans : 2 * chans] = x.astype(BF16)
        tt_ref[k, :, 2 * chans :] = shift_rows(x, -1, zero).astype(BF16)
    tx_ref[...] = jnp.concatenate([gt, jnp.zeros((16 - n, chans), F32)], axis=0)


def adjoint_kernel(lon, lat, chans, tt_ref, tx_ref, wt_ref, dact_ref):
    gt = tx_ref[...]
    total = None
    for a in (-1, 0, 1):
        extra = jnp.concatenate([gt[1 + a : 1 + a + lon], jnp.zeros((16 - lon, chans), F32)], axis=0)
        extra = jnp.concatenate([jnp.zeros((16, 2 * chans), F32), extra], axis=1).astype(BF16)
        piece = jnp.concatenate([tt_ref[1 - a : 1 - a + lon].reshape(lon * lat, 3 * chans), extra], axis=0)
        part = dot(piece, wt_ref[a + 1])
        total = part if total is None else total + part
    rows = lax.broadcasted_iota(jnp.int32, (lat, chans), 0)
    for i in range(lon):
        add = total[lon * lat + i : lon * lat + i + 1]
        dact_ref[i * lat : (i + 1) * lat, :] = total[i * lat : (i + 1) * lat] + jnp.where(rows == lat - 1, add, 0.0)


def moments(stat_ref):
    count = stat_ref[2:3, :]
    mean = stat_ref[0:1, :] / count
    var = stat_ref[1:2, :] / count - mean * mean
    return count, mean, lax.rsqrt(var + 1e-05)


def act_kernel(lon, lat, chans, first_ref, mask_ref, stat_ref, bn_ref, dact_ref, gsum_ref, dpre_ref, aa_ref):
    count, mean, rstd = moments(stat_ref)
    gain, offset = bn_ref[0:1, :], bn_ref[1:2, :]

    def forward(lo, hi):
        xhat = (first_ref[lo:hi].astype(F32) - mean) * rstd
        u = gain * xhat + offset
        hyper = jnp.tanh(0.7978845608 * (u + 0.044715 * u * u * u))
        m = mask_ref[lo:hi].astype(F32)
        return xhat, u, hyper, m, 0.5 * u * (1.0 + hyper) * m

    n = lon + 2
    zero = jnp.zeros((1, chans), F32)
    ghost = forward(n * lat, n * lat + 16)[4]
    scale = lax.rsqrt(count)
    goff = jnp.zeros((1, chans), F32)
    ggain = jnp.zeros((1, chans), F32)
    for k in range(n):
        xhat, u, hyper, m, act = forward(k * lat, (k + 1) * lat)
        aa_ref[k, :, 0:chans] = shift_rows(act, -1, zero).astype(BF16)
        aa_ref[k, :, chans : 2 * chans] = act.astype(BF16)
        aa_ref[k, :, 2 * chans :] = shift_rows(act, 1, ghost[k : k + 1]).astype(BF16)
        if 0 < k <= lon:
            slope = 0.5 * (1.0 + hyper) + 0.5 * u * (1.0 - hyper * hyper) * 0.7978845608 * (
                1.0 + 3.0 * 0.044715 * u * u
            )
            rows = slice((k - 1) * lat, k * lat)
            dpre = dact_ref[rows] * scale * m * slope
            dpre_ref[rows] = dpre
            goff = goff + jnp.sum(dpre, axis=0, keepdims=True)
            ggain = ggain + jnp.sum(dpre * xhat, axis=0, keepdims=True)
    gsum_ref[...] = jnp.concatenate([goff, ggain, jnp.zeros((6, chans), F32)], axis=0)


def put_taps(grad_ref, grad, shifted_ref, base, lon, lat, chans):
    chunks, width = grad_ref.shape[0], grad_ref.shape[2]
    pieces = [shifted_ref[base + a : base + a + lon].reshape(lon * lat, 3 * chans) for a in (-1, 0, 1)]
    part = dot(grad.T, jnp.concatenate(pieces, axis=1)).astype(BF16)
    for t in range(9):
        for c in range(chunks):
            grad_ref[c, t] = part[c * width : (c + 1) * width, t * chans : (t + 1) * chans]


def out_kernel(lon, lat, chans, aa_ref, mask_ref, tt_ref, stat_ref, w_ref, out_ref, grad_ref):
    total = None
    for a in (-1, 0, 1):
        piece = aa_ref[a + 1 : a + 1 + lon].reshape(lon * lat, 3 * chans)
        part = dot(piece, w_ref[3 * (a + 1) : 3 * (a + 2)].reshape(3 * chans, chans))
        total = part if total is None else total + part
    own_mask = mask_ref[lat : lat + lon * lat].astype(F32)
    out_ref[...] = (total * own_mask).astype(BF16).reshape(1, lon, lat, chans)
    scale = lax.rsqrt(stat_ref[2:3, :])
    target = tt_ref[1 : 1 + lon, :, chans : 2 * chans].reshape(lon * lat, chans).astype(F32)
    dout = (target * scale).astype(BF16)
    put_taps(grad_ref, dout, aa_ref, 1, lon, lat, chans)


def in_kernel(lon, lat, chans, first_ref, mask_ref, stat_ref, bn_ref, dpre_ref, gsum_ref, ss_ref, grad_ref):
    count, mean, rstd = moments(stat_ref)
    goff, ggain = gsum_ref[0:1, :], gsum_ref[1:2, :]
    own = slice(lat, lat + lon * lat)
    xhat = (first_ref[own].astype(F32) - mean) * rstd
    dfirst = mask_ref[own].astype(F32) * (bn_ref[0:1, :] * rstd) * (dpre_ref[...] - (goff + xhat * ggain) / count)
    put_taps(grad_ref, dfirst.astype(BF16), ss_ref, 2, lon, lat, chans)


def xor_pairs(size, k):
    return [(i, i ^ k) for i in range(size)]


def all_sum(x, axis):
    size = lax.axis_size(axis)
    bit = 1
    while bit < size:
        other = lax.ppermute(x, axis, xor_pairs(size, bit))
        if 2 * bit < size:
            far = lax.ppermute(x, axis, xor_pairs(size, 2 * bit))
            both = lax.ppermute(x, axis, xor_pairs(size, 3 * bit))
            x = (x + other) + (far + both)
        else:
            x = x + other
        bit *= 4
    return x


def scatter_sum(x, axis, last=BF16):
    size = lax.axis_size(axis)
    me = lax.axis_index(axis)
    bit = 1
    while bit < size:
        mine = (me // bit) % 2
        split = x.reshape(x.shape[0] // 2, 2, *x.shape[1:])
        keep = lax.dynamic_index_in_dim(split, mine, 1, keepdims=False)
        send = lax.dynamic_index_in_dim(split, 1 - mine, 1, keepdims=False)
        got = lax.ppermute(send, axis, xor_pairs(size, bit))
        bit *= 2
        x = (keep.astype(F32) + got.astype(F32)).astype(BF16 if bit < size else last)
    return x[0]


def space_sum(x):
    size = lax.axis_size("space")
    bit = 1
    while bit < size:
        got = lax.ppermute(x, "space", xor_pairs(size, bit))
        x = x.astype(F32) + got.astype(F32)
        bit *= 2
        if bit < size:
            x = x.astype(BF16)
    return jnp.swapaxes(x, 1, 2)


def put_shifted(ref, k, x, step):
    chans = x.shape[1]
    zero = jnp.zeros((1, chans), F32)
    ref[k, :, 0:chans] = shift_rows(x, -step, zero).astype(BF16)
    ref[k, :, chans : 2 * chans] = x.astype(BF16)
    ref[k, :, 2 * chans :] = shift_rows(x, step, zero).astype(BF16)


def join_kernel(a_ref, b_ref, out_ref):
    rows = a_ref.shape[0]
    out_ref[0:rows] = a_ref[...]
    out_ref[rows:] = b_ref[...]


def sample_prep(
    lon, lat, chans, tiles,
    f_hbm, t_hbm, land_hbm, win_hbm, wout_hbm, gain_hbm, offset_hbm,
    ss_ref, tt_ref, mask_ref, land_ref, win_ref, wout_ref, wt_ref, bn_ref,
    f_ref, t_ref, wraw_ref, sems,
):
    pairs = [
        (land_hbm, land_ref), (f_hbm, f_ref), (t_hbm, t_ref), (wout_hbm, wout_ref), (win_hbm, wraw_ref),
        (gain_hbm, bn_ref.at[0:1]), (offset_hbm, bn_ref.at[1:2]),
    ]
    copies = [pltpu.make_async_copy(src, dst, sems.at[i]) for i, (src, dst) in enumerate(pairs)]
    for c in copies:
        c.start()
    first = lax.axis_index("space") * lon
    for c in copies[:3]:
        c.wait()
    lines = land_ref[...].astype(F32)
    for i in range(lon):
        mask = spread(lines[i : i + 1], lat, chans)
        mask_ref[first + i] = mask.astype(BF16)
        put_shifted(ss_ref, first + i + 1, f_ref[0, i].astype(F32) * mask, 1)
        target = t_ref[0, i].astype(F32) * mask
        put_shifted(tt_ref, first + i + 1, target, -1)
    for c in copies[3:]:
        c.wait()
    deep = 3 * chans
    zero = jnp.zeros((deep, chans), BF16)
    for q in range(4):
        rows = slice(q * deep, (q + 1) * deep)
        for half in range(2):
            lanes = slice(half * chans, (half + 1) * chans)
            tap = q - half
            inside = 0 <= tap < 3
            win_ref[rows, lanes] = wraw_ref[3 * tap : 3 * tap + 3].reshape(deep, chans) if inside else zero
            turned = [wout_ref[3 * (2 - tap) + b].T for b in range(3)] if inside else [zero]
            wt_ref[rows, lanes] = jnp.concatenate(turned, axis=0)


def paired(ref, start, pairs):
    columns = [jnp.concatenate([ref[start + 2 * m + q] for m in range(pairs)], axis=0) for q in range(4)]
    return jnp.concatenate(columns, axis=1)


def sample_build(lon, lat, chans, f1_ref, f2_ref, l2_ref, l13_ref, ss_in, mask_in, ss_ref, mask_ref):
    me = lax.axis_index("space")
    for k, f_ref, land_ref in ((1, f1_ref, l13_ref), (2, f2_ref, l2_ref), (3, None, l13_ref)):
        first = jnp.bitwise_xor(me, k) * lon
        lines = land_ref[lon if k == 3 else 0 : 2 * lon if k == 3 else lon].astype(F32)
        for i in range(lon):
            mask = spread(lines[i : i + 1], lat, chans)
            mask_ref[first + i] = mask.astype(BF16)
            if f_ref is not None:
                put_shifted(ss_ref, first + i + 1, f_ref[0, i].astype(F32) * mask, 1)


def sample_conv(lon, lat, chans, f3_ref, ss_in, mask_ref, w_ref, ss_ref, first_ref, stat_ref):
    nx = mask_ref.shape[0]
    start = jnp.bitwise_xor(lax.axis_index("space"), 3) * lon
    for i in range(lon):
        put_shifted(ss_ref, start + i + 1, f3_ref[0, i].astype(F32) * mask_ref[start + i].astype(F32), 1)
    tails = [ss_ref[i + 1, lat - 8 :, chans : 2 * chans].astype(F32) for i in range(nx)]
    for i in range(nx):
        fill = tails[nx - 1 - i][7:8]
        ss_ref[i + 1, lat - 8 :, 2 * chans :] = shift_rows(tails[i], 1, fill).astype(BF16)
    ss_ref[0] = ss_ref[nx]
    ss_ref[nx + 1] = ss_ref[1]
    sums, squares, count = [jnp.zeros((8, chans), F32)] * 3
    fold = lambda v: jnp.sum(v.reshape(-1, 8, chans), axis=0)
    pairs = lon
    for c in range(0, nx, 2 * pairs):
        total = dot(paired(ss_ref, c, pairs), w_ref[...])
        for m in range(pairs):
            for half in range(2):
                k = c + 2 * m + half
                first = total[m * lat : (m + 1) * lat, half * chans : (half + 1) * chans].astype(BF16)
                first_ref[k] = first
                x = first.astype(F32)
                mask = mask_ref[k].astype(F32)
                kept = x * mask
                sums, squares, count = sums + fold(kept), squares + fold(kept * x), count + fold(mask)
    rows = [jnp.sum(v, axis=0, keepdims=True) for v in (sums, squares, count)]
    stat_ref[...] = jnp.concatenate(rows + [jnp.zeros((5, chans), F32)], axis=0)


def sample_place(lon, t1_ref, t2_ref, mask_ref, tt_in, tt_ref):
    me = lax.axis_index("space")
    for k, t_ref in ((1, t1_ref), (2, t2_ref)):
        start = jnp.bitwise_xor(me, k) * lon
        for i in range(lon):
            put_shifted(tt_ref, start + i + 1, t_ref[0, i].astype(F32) * mask_ref[start + i].astype(F32), -1)


def sample_adjoint(lon, lat, chans, t3_ref, mask_ref, wt_ref, tt_in, tt_ref, dact_ref):
    nx = dact_ref.shape[0]
    me = lax.axis_index("space")
    for k, t_ref in ((3, t3_ref),):
        start = jnp.bitwise_xor(me, k) * lon
        for i in range(lon):
            put_shifted(tt_ref, start + i + 1, t_ref[0, i].astype(F32) * mask_ref[start + i].astype(F32), -1)
    tt_ref[0] = tt_ref[nx]
    tt_ref[nx + 1] = tt_ref[1]
    top = [tt_ref[i + 1, lat - 8 :, chans : 2 * chans].astype(F32)[7:8] for i in range(nx)]
    extra = None
    for a in (-1, 0, 1):
        rows = jnp.concatenate([top[nx - 1 - (i + a) % nx] for i in range(nx)], axis=0).astype(BF16)
        part = dot(rows, wt_ref[(1 - a) * 3 * chans + 2 * chans : (2 - a) * 3 * chans, 0:chans])
        extra = part if extra is None else extra + part
    last = lax.broadcasted_iota(jnp.int32, (lat, chans), 0) == lat - 1
    pairs = lon
    for c in range(0, nx, 2 * pairs):
        total = dot(paired(tt_ref, c, pairs), wt_ref[...])
        for m in range(pairs):
            for half in range(2):
                k = c + 2 * m + half
                own = total[m * lat : (m + 1) * lat, half * chans : (half + 1) * chans]
                dact_ref[k] = (own + jnp.where(last, extra[k : k + 1], 0.0)) * mask_ref[k].astype(F32)


def sample_act(lat, chans, first_ref, mask_ref, stat_ref, bn_ref, dact_ref, gsum_ref, dpre_ref, aa_ref):
    nx = mask_ref.shape[0]
    count, mean, rstd = moments(stat_ref)
    gain, offset = bn_ref[0:1, :] * rstd, bn_ref[1:2, :]
    scale = lax.rsqrt(count)
    fold = lambda v: jnp.sum(v.reshape(-1, 8, chans), axis=0)
    goff, ggain = [jnp.zeros((8, chans), F32)] * 2
    for i in range(nx // 2):
        acts = []
        for k in (i, nx - 1 - i):
            centred = first_ref[k].astype(F32) - mean
            u = centred * gain + offset
            square = u * u
            half = 0.5 * jnp.tanh(u * (square * (0.7978845608 * 0.044715) + 0.7978845608)) + 0.5
            acts.append(u * half * mask_ref[k].astype(F32))
            bend = square * (6.0 * 0.7978845608 * 0.044715) + 2.0 * 0.7978845608
            slope = half + (half - half * half) * u * bend
            dpre = dact_ref[k] * scale * slope
            dpre_ref[k] = dpre
            goff, ggain = goff + fold(dpre), ggain + fold(dpre * centred)
        for k, x, other in ((i, acts[0], acts[1]), (nx - 1 - i, acts[1], acts[0])):
            aa_ref[k + 1, :, 0:chans] = shift_rows(x, -1, jnp.zeros((1, chans), F32)).astype(BF16)
            aa_ref[k + 1, :, chans : 2 * chans] = x.astype(BF16)
            aa_ref[k + 1, :, 2 * chans :] = shift_rows(x, 1, other[lat - 1 : lat]).astype(BF16)
    aa_ref[0] = aa_ref[nx]
    aa_ref[nx + 1] = aa_ref[1]
    rows = [jnp.sum(v, axis=0, keepdims=True) for v in (goff, ggain * rstd)]
    gsum_ref[...] = jnp.concatenate(rows + [jnp.zeros((6, chans), F32)], axis=0)


def halve(get, keep_ref, send_ref, bit):
    mine = lax.rem(lax.div(lax.axis_index("batch"), bit), 2)
    for j in range(keep_ref.shape[0]):
        keep_ref[j] = get(2 * j + mine)
        send_ref[j] = get(2 * j + 1 - mine)


def fold_kernel(bit, a_ref, b_ref, keep_ref, send_ref):
    halve(lambda k: (a_ref[k].astype(F32) + b_ref[k].astype(F32)).astype(BF16), keep_ref, send_ref, bit)


def exchange_sum(keep, send, size):
    bit = 1
    while True:
        got = lax.ppermute(send, "batch", xor_pairs(size, bit))
        bit *= 2
        if bit == size:
            return jnp.swapaxes(keep[0].astype(F32) + got[0].astype(F32), 1, 2), keep
        half = sds((keep.shape[0] // 2,) + keep.shape[1:], BF16)
        keep, send = run(functools.partial(fold_kernel, bit), [half, half], [keep, got])


def sample_grad(lat, chans, aa_ref, tt_ref, stat_ref, keep_ref, send_ref, grad_ref):
    nx = aa_ref.shape[0] - 2
    scale = lax.rsqrt(stat_ref[2:3, :])
    target = tt_ref[1 : 1 + nx, :, chans : 2 * chans].reshape(nx * lat, chans).astype(F32)
    put_taps(grad_ref, (target * scale).astype(BF16), aa_ref, 1, nx, lat, chans)
    halve(lambda k: grad_ref[k], keep_ref, send_ref, 1)


def sample_out(lon, lat, chans, aa_ref, mask_ref, w_ref, gsum_ref, after_ref, out_ref, gain_ref, offset_ref):
    offset_ref[...] = gsum_ref[0:1, :]
    gain_ref[...] = gsum_ref[1:2, :]
    start = lax.axis_index("space") * lon
    total = None
    for a in (-1, 0, 1):
        piece = aa_ref[pl.ds(start + a + 1, lon)].reshape(lon * lat, 3 * chans)
        part = dot(piece, w_ref[3 * (a + 1) : 3 * (a + 2)].reshape(3 * chans, chans))
        total = part if total is None else total + part
    own_mask = mask_ref[pl.ds(start, lon)].reshape(lon * lat, chans).astype(F32)
    out_ref[...] = (total * own_mask).astype(BF16).reshape(1, lon, lat, chans)


def sample_in(lat, chans, first_ref, mask_ref, stat_ref, bn_ref, dpre_ref, gsum_ref, ss_ref, keep_ref, send_ref, grad_ref):
    nx = mask_ref.shape[0]
    count, mean, rstd = moments(stat_ref)
    goff, ggain = gsum_ref[0:1, :] / count, gsum_ref[1:2, :] / count
    factor = bn_ref[0:1, :] * rstd
    rows = []
    for k in range(nx):
        xhat = (first_ref[k].astype(F32) - mean) * rstd
        rows.append((mask_ref[k].astype(F32) * factor * (dpre_ref[k] - (goff + xhat * ggain))).astype(BF16))
    put_taps(grad_ref, jnp.concatenate(rows, axis=0), ss_ref, 1, nx, lat, chans)
    halve(lambda k: grad_ref[k], keep_ref, send_ref, 1)


def tile_body(fields, land, conv_in, conv_out, batchnorm_gain, batchnorm_offset, target_grad):
    lon, lat, chans = fields.shape[1:]
    tiles = lax.axis_size("space")
    sizes = (lon, lat, chans)
    cells = lon * lat
    gain, offset = batchnorm_gain[None, :], batchnorm_offset[None, :]
    fields, land, conv_in, conv_out, target_grad, gain, offset = (
        pltpu.with_memory_space_constraint(x, pltpu.HBM)
        for x in (fields, land, conv_in, conv_out, target_grad, gain, offset)
    )
    n = lon + 2
    join = tiles == 4
    edge = 3 * lat + 16
    shares = lax.axis_size("batch")
    taps = sds((shares, 9, chans // shares, chans), BF16)
    pay_e, pay_o, polar = run(
        functools.partial(pack_kernel, *sizes, join),
        [sds((edge, chans), BF16), sds((edge + (4 * lon if join else 0), chans), BF16), sds((4 * lon, chans), BF16)],
        [fields, target_grad, land],
        scratch=[
            pltpu.VMEM((4, lat, chans), BF16), pltpu.VMEM((lon, 8, chans), BF16),
            pltpu.VMEM((2, lat, chans), BF16), pltpu.VMEM((lon, 8, chans), BF16),
            pltpu.VMEM((lon, lat), jnp.int32), pltpu.SemaphoreType.DMA((7,)),
        ],
        space=pl.BlockSpec(memory_space=pltpu.HBM),
    )
    mirror = [(i, tiles - 1 - i) for i in range(tiles)]
    got_o = lax.ppermute(pay_o, "space", [(i, (i - 1 if i % 2 == 0 else i + 1) % tiles) for i in range(tiles)])
    got_e = lax.ppermute(pay_e, "space", xor_pairs(tiles, 1))
    if join:
        got_x = lax.ppermute(polar, "space", xor_pairs(tiles, 2))
        poles = [got_o, got_x, got_x, polar]
    else:
        poles = [
            lax.ppermute(polar, "space", mirror),
            lax.ppermute(polar, "space", [(i, (tiles - 2 - i) % tiles) for i in range(tiles)]),
            lax.ppermute(polar, "space", [(i, (tiles - i) % tiles) for i in range(tiles)]),
            polar,
        ]
    wide = sds((lon + 4, lat, 3 * chans), BF16)
    near = sds((n, lat, 3 * chans), BF16)
    ss, tt, own_mask, win, wout, wt, bn = run(
        functools.partial(prep_kernel, *sizes),
        [
            wide, near, sds((cells, chans), BF16), sds(conv_in.shape, BF16), sds(conv_out.shape, BF16),
            sds((3, 3 * chans, chans), BF16), sds((8, chans), F32),
        ],
        [fields, target_grad, land, conv_in, conv_out, gain, offset],
        scratch=[
            pltpu.VMEM(fields.shape, BF16), pltpu.VMEM(fields.shape, BF16), pltpu.VMEM(land.shape, jnp.int32),
            pltpu.SemaphoreType.DMA((7,)),
        ],
        space=pl.BlockSpec(memory_space=pltpu.HBM),
    )

    def conv_body(*refs):
        refs = list(refs)
        if join:
            refs[4] = refs[3]
        conv_kernel(*sizes, edge if join else 0, *refs)

    rows = n * lat + 16
    ss, tt, first, mask, stat, tx = run(
        conv_body,
        [wide, near, sds((rows, chans), BF16), sds((rows, chans), BF16), sds((8, chans), F32), sds((16, chans), F32)],
        [got_e, got_o, *poles, ss, tt, own_mask, win],
        flops=2 * rows * 9 * chans * chans,
        alias={6: 0, 7: 1},
    )
    stat = all_sum(all_sum(stat, "batch"), "space")
    dact = run(
        functools.partial(adjoint_kernel, *sizes),
        [sds((cells, chans), F32)],
        [tt, tx, wt],
        flops=2 * cells * 9 * chans * chans,
    )[0]
    gsum, dpre, aa = run(
        functools.partial(act_kernel, *sizes),
        [sds((8, chans), F32), sds((cells, chans), F32), sds((n, lat, 3 * chans), BF16)],
        [first, mask, stat, bn, dact],
    )
    gsum = all_sum(all_sum(gsum, "batch"), "space")
    output, part_out = run(
        functools.partial(out_kernel, *sizes),
        [sds((1, lon, lat, chans), BF16), taps],
        [aa, mask, tt, stat, wout],
        flops=4 * cells * 9 * chans * chans,
    )
    grad_out = space_sum(scatter_sum(part_out, "batch"))
    part_in = run(
        functools.partial(in_kernel, *sizes),
        [taps],
        [first, mask, stat, bn, dpre, gsum, ss],
        flops=2 * cells * 9 * chans * chans,
    )[0]
    grad_in = space_sum(scatter_sum(part_in, "batch"))
    return (output, grad_in, grad_out, gsum[1], gsum[0])


def sample_body(fields, land, conv_in, conv_out, batchnorm_gain, batchnorm_offset, target_grad):
    lon, lat, chans = fields.shape[1:]
    tiles = lax.axis_size("space")
    sizes = (lon, lat, chans)
    nx = tiles * lon
    near, across = xor_pairs(tiles, 1), xor_pairs(tiles, 2)
    move = lambda x, pairs: lax.ppermute(x, "space", pairs)
    f2 = move(fields, across)
    l2 = move(land, across)
    f1 = move(fields, near)
    f3 = move(f2, near)
    gain, offset = batchnorm_gain[None, :], batchnorm_offset[None, :]
    params = [
        pltpu.with_memory_space_constraint(x, pltpu.HBM)
        for x in (fields, target_grad, land, conv_in, conv_out, gain, offset)
    ]
    shares = lax.axis_size("batch")
    half = sds((shares // 2, 9, chans // shares, chans), BF16)
    whole = [pltpu.VMEM((shares, 9, chans // shares, chans), BF16)]
    shifted = sds((nx + 2, lat, 3 * chans), BF16)
    cells = sds((nx, lat, chans), BF16)
    cells_f = sds((nx, lat, chans), F32)
    sums = sds((8, chans), F32)
    work = 2 * nx * lat * 9 * chans * chans
    double = sds((12 * chans, 2 * chans), BF16)
    ss, tt, mask, land_own, win, wout, wt, bn = run(
        functools.partial(sample_prep, *sizes, tiles),
        [shifted, shifted, cells, sds(land.shape, jnp.int32), double, sds(conv_out.shape, BF16), double, sums],
        params,
        scratch=[
            pltpu.VMEM(fields.shape, BF16), pltpu.VMEM(fields.shape, BF16), pltpu.VMEM(conv_in.shape, BF16), pltpu.SemaphoreType.DMA((7,)),
        ],
        space=pl.BlockSpec(memory_space=pltpu.HBM),
    )
    (both,) = run(join_kernel, [sds((2 * lon, lat), jnp.int32)], [land_own, l2])
    l13 = move(both, near)
    ss, mask = run(
        functools.partial(sample_build, *sizes), [shifted, cells], [f1, f2, l2, l13, ss, mask], alias={4: 0, 5: 1}
    )
    t2 = move(target_grad, across)
    t1 = move(target_grad, near)
    t3 = move(t2, near)
    ss, first, stat = run(
        functools.partial(sample_conv, *sizes), [shifted, cells, sums], [f3, ss, mask, win], flops=work, alias={1: 0}
    )
    stat = all_sum(stat, "batch")
    (tt,) = run(functools.partial(sample_place, lon), [shifted], [t1, t2, mask, tt], alias={3: 0})
    tt, dact = run(
        functools.partial(sample_adjoint, *sizes), [shifted, cells_f], [t3, mask, wt, tt], flops=work, alias={3: 0}
    )
    gsum, dpre, aa = run(
        functools.partial(sample_act, lat, chans), [sums, cells_f, shifted], [first, mask, stat, bn, dact]
    )
    gsum = all_sum(gsum, "batch")
    keep_o, send_o = run(
        functools.partial(sample_grad, lat, chans), [half, half], [aa, tt, stat], scratch=whole, flops=work
    )
    grad_out, _ = exchange_sum(keep_o, send_o, shares)
    keep_i, send_i = run(
        functools.partial(sample_in, lat, chans),
        [half, half], [first, mask, stat, bn, dpre, gsum, ss], scratch=whole, flops=work,
    )
    grad_in, folded = exchange_sum(keep_i, send_i, shares)
    output, grad_gain, grad_offset = run(
        functools.partial(sample_out, *sizes),
        [sds(fields.shape, BF16), sds((1, chans), F32), sds((1, chans), F32)],
        [aa, mask, wout, gsum, folded], flops=work // tiles,
    )
    return (output, grad_in, grad_out, grad_gain[0], grad_offset[0])


def body(*args):
    if lax.axis_size("space") != 4:
        return tile_body(*args)
    return sample_body(*args)


def solution(mesh):
    in_specs = (
        P(("groups", "batch"), "space", None, None),
        P("space", None),
        P(),
        P(),
        P(),
        P(),
        P(("groups", "batch"), "space", None, None),
    )
    out_specs = (
        P(("groups", "batch"), "space", None, None),
        P("groups", None, "batch"),
        P("groups", None, "batch"),
        P("groups"),
        P("groups"),
    )
    return jax.shard_map(body, mesh=mesh, in_specs=in_specs, out_specs=out_specs, check_vma=False)
```

```python
import functools

import jax
import jax.numpy as jnp
from jax import lax
from jax.experimental import pallas as pl
from jax.experimental.pallas import tpu as pltpu
from jax.sharding import PartitionSpec as P


F32 = jnp.float32
BF16 = jnp.bfloat16
VMEM = pl.BlockSpec(memory_space=pltpu.VMEM)


def run(body, outs, args, scratch=(), flops=0, space=VMEM, alias=None):
    nbytes = sum(a.size * a.dtype.itemsize for a in args)
    nbytes += sum(o.size * o.dtype.itemsize for o in outs)
    return pl.pallas_call(
        body,
        out_shape=list(outs),
        in_specs=[space] * len(args),
        out_specs=[VMEM] * len(outs),
        scratch_shapes=list(scratch),
        cost_estimate=pl.CostEstimate(flops=flops, bytes_accessed=nbytes, transcendentals=0),
        compiler_params=pltpu.CompilerParams(vmem_limit_bytes=24 << 20),
        input_output_aliases=alias or {},
    )(*args)


def sds(shape, dtype):
    return jax.ShapeDtypeStruct(shape, dtype)


def dot(a, b):
    return jnp.dot(a, b, preferred_element_type=F32)


def spread(line, lat, chans):
    rows = lax.broadcasted_iota(jnp.int32, (lat, lat), 0)
    cols = lax.broadcasted_iota(jnp.int32, (lat, lat), 1)
    col = jnp.sum(jnp.where(rows == cols, jnp.broadcast_to(line, (lat, lat)), 0.0), axis=1, keepdims=True)
    return jnp.broadcast_to(col, (lat, chans))


def pack_kernel(lon, lat, chans, join, f_hbm, t_hbm, land_hbm, e_ref, o_ref, p_ref, fc, fr, tc, tr, land, sems):
    copies = [
        pltpu.make_async_copy(f_hbm.at[0, 0:2], fc.at[0:2], sems.at[0]),
        pltpu.make_async_copy(f_hbm.at[0, lon - 2 : lon], fc.at[2:4], sems.at[1]),
        pltpu.make_async_copy(f_hbm.at[0, :, lat - 8 : lat], fr, sems.at[2]),
        pltpu.make_async_copy(t_hbm.at[0, 0:1], tc.at[0:1], sems.at[3]),
        pltpu.make_async_copy(t_hbm.at[0, lon - 1 : lon], tc.at[1:2], sems.at[4]),
        pltpu.make_async_copy(t_hbm.at[0, :, lat - 8 : lat], tr, sems.at[5]),
        pltpu.make_async_copy(land_hbm, land, sems.at[6]),
    ]
    for c in copies:
        c.start()
    even = lax.rem(lax.axis_index("space"), 2) == 0
    for c in copies:
        c.wait()
    lines = land[...].astype(F32)

    def edge(k, cols_f, side):
        masks = [spread(lines[i : i + 1], lat, chans) for i in cols_f]
        parts = [fc[k + n].astype(F32) * m for n, m in enumerate(masks)]
        col = cols_f[0] if side == 0 else cols_f[1]
        parts.append(tc[side].astype(F32) * masks[0 if side == 0 else 1])
        line = jnp.concatenate([lines[col : col + 1], jnp.zeros((1, chans - lat), F32)], axis=1)
        parts += [line, jnp.zeros((15, chans), F32)]
        return jnp.concatenate(parts, axis=0).astype(BF16)

    west = edge(0, (0, 1), 0)
    east = edge(2, (lon - 2, lon - 1), 1)
    n = west.shape[0]
    e_ref[...] = jnp.where(even, east, west)
    o_ref[0:n, :] = jnp.where(even, west, east)
    lane = lax.broadcasted_iota(jnp.int32, (lon, lat), 1)
    last = {}
    for j in (lat - 2, lat - 1):
        col = jnp.sum(jnp.where(lane == j, lines, 0.0), axis=1, keepdims=True)
        last[j] = jnp.broadcast_to(col, (lon, chans))
    rows = []
    for j, ref in ((lat - 2, fr), (lat - 1, fr), (lat - 1, tr)):
        k = j - (lat - 8)
        line = jnp.concatenate([ref[i].astype(F32)[k : k + 1] for i in range(lon)], axis=0)
        rows.append(line * last[j])
    rows.append(last[lat - 1])
    polar = jnp.concatenate(rows, axis=0).astype(BF16)
    p_ref[...] = polar
    if join:
        o_ref[n:, :] = polar


def shift_rows(x, step, fill):
    rows = lax.broadcasted_iota(jnp.int32, x.shape, 0)
    n = x.shape[0]
    moved = pltpu.roll(x, (-step) % n, 0)
    return jnp.where(rows == (n - 1 if step > 0 else 0), fill, moved)


def prep_kernel(
    lon, lat, chans,
    f_hbm, t_hbm, land_hbm, win_hbm, wout_hbm, gain_hbm, offset_hbm,
    ss_ref, tt_ref, mask_ref, win_ref, wout_ref, wt_ref, bn_ref,
    f_ref, t_ref, land_ref, sems,
):
    pairs = [
        (land_hbm, land_ref), (f_hbm, f_ref), (t_hbm, t_ref), (wout_hbm, wout_ref), (win_hbm, win_ref),
        (gain_hbm, bn_ref.at[0:1]), (offset_hbm, bn_ref.at[1:2]),
    ]
    copies = [pltpu.make_async_copy(src, dst, sems.at[i]) for i, (src, dst) in enumerate(pairs)]
    for c in copies:
        c.start()
    for c in copies[:3]:
        c.wait()
    lines = land_ref[...].astype(F32)
    zero = jnp.zeros((1, chans), F32)
    for i in range(lon):
        mask = spread(lines[i : i + 1], lat, chans)
        mask_ref[i * lat : (i + 1) * lat] = mask.astype(BF16)
        x = f_ref[0, i].astype(F32) * mask
        ss_ref[i + 2, :, 0:chans] = shift_rows(x, -1, zero).astype(BF16)
        ss_ref[i + 2, :, chans : 2 * chans] = x.astype(BF16)
        ss_ref[i + 2, :, 2 * chans :] = shift_rows(x, 1, zero).astype(BF16)
        x = t_ref[0, i].astype(F32) * mask
        tt_ref[i + 1, :, 0:chans] = shift_rows(x, 1, zero).astype(BF16)
        tt_ref[i + 1, :, chans : 2 * chans] = x.astype(BF16)
        tt_ref[i + 1, :, 2 * chans :] = shift_rows(x, -1, zero).astype(BF16)
    for c in copies[3:]:
        c.wait()
    for a in range(3):
        for b in range(3):
            wt_ref[a, b * chans : (b + 1) * chans] = wout_ref[3 * a + b].T


def conv_kernel(
    lon, lat, chans, moff,
    re_ref, ro_ref, rm_ref, r1_ref, r2_ref, own_ref, ss_in, tt_in, om_ref, w_ref,
    ss_ref, tt_ref, first_ref, mask_ref, stat_ref, tx_ref,
):
    even = lax.rem(lax.axis_index("space"), 2) == 0
    recv_e = re_ref[...].astype(F32)
    recv_o = ro_ref[0 : recv_e.shape[0], :].astype(F32)
    west = jnp.where(even, recv_o, recv_e)
    east = jnp.where(even, recv_e, recv_o)
    polar_m = rm_ref[moff : moff + 4 * lon, :].astype(F32)
    if r1_ref is r2_ref:
        other = r1_ref[...].astype(F32)
        own = own_ref[...].astype(F32)
        polar_1 = jnp.where(even, other, own)
        polar_2 = jnp.where(even, own, other)
    else:
        polar_1 = r1_ref[...].astype(F32)
        polar_2 = r2_ref[...].astype(F32)

    def ghost(kind, cols):
        line = jnp.concatenate([p[kind * lon : (kind + 1) * lon] for p in (polar_1, polar_m, polar_2)], axis=0)
        picks = [2 * lon - 1 - i for i in cols]
        return jnp.concatenate([line[k : k + 1] for k in picks], axis=0)

    zero = jnp.zeros((1, chans), F32)
    wide = list(range(-2, lon + 2))
    near = list(range(-1, lon + 1))
    g62, g63 = ghost(0, wide), ghost(1, wide)
    gt, gm = ghost(2, near), ghost(3, near)
    halo = {0: west[0:lat], 1: west[lat : 2 * lat], lon + 2: east[0:lat], lon + 3: east[lat : 2 * lat]}
    rows8 = lax.broadcasted_iota(jnp.int32, (8, chans), 0)
    top = []
    for k in range(lon + 4):
        fill = g63[k : k + 1]
        if k in halo:
            x = halo[k]
            ss_ref[k, :, 0:chans] = shift_rows(x, -1, zero).astype(BF16)
            ss_ref[k, :, chans : 2 * chans] = x.astype(BF16)
            ss_ref[k, :, 2 * chans :] = shift_rows(x, 1, fill).astype(BF16)
            top.append(x[lat - 1 : lat])
        else:
            tail = ss_ref[k, lat - 8 :, chans : 2 * chans].astype(F32)
            top.append(tail[7:8])
            ss_ref[k, lat - 8 :, 2 * chans :] = shift_rows(tail, 1, fill).astype(BF16)
    top = jnp.concatenate(top, axis=0)
    fold = jnp.concatenate([g62, g63, top], axis=1)
    total = None
    n = lon + 2
    pad = jnp.zeros((16 - n, 3 * chans), F32)
    for a in (-1, 0, 1):
        ghost_rows = jnp.concatenate([fold[1 - a : 1 - a + n], pad], axis=0).astype(BF16)
        piece = jnp.concatenate([ss_ref[a + 1 : a + 1 + n].reshape(n * lat, 3 * chans), ghost_rows], axis=0)
        part = dot(piece, w_ref[3 * (a + 1) : 3 * (a + 2)].reshape(3 * chans, chans))
        total = part if total is None else total + part
    first = total.astype(BF16)
    first_ref[...] = first
    own_first = first[lat : lat + lon * lat].astype(F32)
    own_mask = om_ref[...].astype(F32)
    kept = own_first * own_mask
    sums = jnp.sum(kept, axis=0, keepdims=True)
    squares = jnp.sum(kept * own_first, axis=0, keepdims=True)
    count = jnp.sum(own_mask, axis=0, keepdims=True)
    stat_ref[...] = jnp.concatenate([sums, squares, count, jnp.zeros((5, chans), F32)], axis=0)
    edges = [spread(x[3 * lat : 3 * lat + 1, 0:lat], lat, chans) for x in (west, east)]
    mask_ref[0:lat] = edges[0].astype(BF16)
    mask_ref[lat : lat + lon * lat] = om_ref[...]
    mask_ref[lat + lon * lat : n * lat] = edges[1].astype(BF16)
    mask_ref[n * lat :] = jnp.concatenate([gm, jnp.zeros((16 - n, chans), F32)], axis=0).astype(BF16)
    for k, x in ((0, west[2 * lat : 3 * lat]), (lon + 1, east[2 * lat : 3 * lat])):
        tt_ref[k, :, 0:chans] = shift_rows(x, 1, zero).astype(BF16)
        tt_ref[k, :, chans : 2 * chans] = x.astype(BF16)
        tt_ref[k, :, 2 * chans :] = shift_rows(x, -1, zero).astype(BF16)
    tx_ref[...] = jnp.concatenate([gt, jnp.zeros((16 - n, chans), F32)], axis=0)


def adjoint_kernel(lon, lat, chans, tt_ref, tx_ref, wt_ref, dact_ref):
    gt = tx_ref[...]
    total = None
    for a in (-1, 0, 1):
        extra = jnp.concatenate([gt[1 + a : 1 + a + lon], jnp.zeros((16 - lon, chans), F32)], axis=0)
        extra = jnp.concatenate([jnp.zeros((16, 2 * chans), F32), extra], axis=1).astype(BF16)
        piece = jnp.concatenate([tt_ref[1 - a : 1 - a + lon].reshape(lon * lat, 3 * chans), extra], axis=0)
        part = dot(piece, wt_ref[a + 1])
        total = part if total is None else total + part
    rows = lax.broadcasted_iota(jnp.int32, (lat, chans), 0)
    for i in range(lon):
        add = total[lon * lat + i : lon * lat + i + 1]
        dact_ref[i * lat : (i + 1) * lat, :] = total[i * lat : (i + 1) * lat] + jnp.where(rows == lat - 1, add, 0.0)


def moments(stat_ref):
    count = stat_ref[2:3, :]
    mean = stat_ref[0:1, :] / count
    var = stat_ref[1:2, :] / count - mean * mean
    return count, mean, lax.rsqrt(var + 1e-05)


def act_kernel(lon, lat, chans, first_ref, mask_ref, stat_ref, bn_ref, dact_ref, gsum_ref, dpre_ref, aa_ref):
    count, mean, rstd = moments(stat_ref)
    gain, offset = bn_ref[0:1, :], bn_ref[1:2, :]

    def forward(lo, hi):
        xhat = (first_ref[lo:hi].astype(F32) - mean) * rstd
        u = gain * xhat + offset
        hyper = jnp.tanh(0.7978845608 * (u + 0.044715 * u * u * u))
        m = mask_ref[lo:hi].astype(F32)
        return xhat, u, hyper, m, 0.5 * u * (1.0 + hyper) * m

    n = lon + 2
    zero = jnp.zeros((1, chans), F32)
    ghost = forward(n * lat, n * lat + 16)[4]
    scale = lax.rsqrt(count)
    goff = jnp.zeros((1, chans), F32)
    ggain = jnp.zeros((1, chans), F32)
    for k in range(n):
        xhat, u, hyper, m, act = forward(k * lat, (k + 1) * lat)
        aa_ref[k, :, 0:chans] = shift_rows(act, -1, zero).astype(BF16)
        aa_ref[k, :, chans : 2 * chans] = act.astype(BF16)
        aa_ref[k, :, 2 * chans :] = shift_rows(act, 1, ghost[k : k + 1]).astype(BF16)
        if 0 < k <= lon:
            slope = 0.5 * (1.0 + hyper) + 0.5 * u * (1.0 - hyper * hyper) * 0.7978845608 * (
                1.0 + 3.0 * 0.044715 * u * u
            )
            rows = slice((k - 1) * lat, k * lat)
            dpre = dact_ref[rows] * scale * m * slope
            dpre_ref[rows] = dpre
            goff = goff + jnp.sum(dpre, axis=0, keepdims=True)
            ggain = ggain + jnp.sum(dpre * xhat, axis=0, keepdims=True)
    gsum_ref[...] = jnp.concatenate([goff, ggain, jnp.zeros((6, chans), F32)], axis=0)


def put_taps(grad_ref, grad, shifted_ref, base, lon, lat, chans):
    chunks, width = grad_ref.shape[0], grad_ref.shape[2]
    pieces = [shifted_ref[base + a : base + a + lon].reshape(lon * lat, 3 * chans) for a in (-1, 0, 1)]
    part = dot(grad.T, jnp.concatenate(pieces, axis=1)).astype(BF16)
    for t in range(9):
        for c in range(chunks):
            grad_ref[c, t] = part[c * width : (c + 1) * width, t * chans : (t + 1) * chans]


def out_kernel(lon, lat, chans, aa_ref, mask_ref, tt_ref, stat_ref, w_ref, out_ref, grad_ref):
    total = None
    for a in (-1, 0, 1):
        piece = aa_ref[a + 1 : a + 1 + lon].reshape(lon * lat, 3 * chans)
        part = dot(piece, w_ref[3 * (a + 1) : 3 * (a + 2)].reshape(3 * chans, chans))
        total = part if total is None else total + part
    own_mask = mask_ref[lat : lat + lon * lat].astype(F32)
    out_ref[...] = (total * own_mask).astype(BF16).reshape(1, lon, lat, chans)
    scale = lax.rsqrt(stat_ref[2:3, :])
    target = tt_ref[1 : 1 + lon, :, chans : 2 * chans].reshape(lon * lat, chans).astype(F32)
    dout = (target * scale).astype(BF16)
    put_taps(grad_ref, dout, aa_ref, 1, lon, lat, chans)


def in_kernel(lon, lat, chans, first_ref, mask_ref, stat_ref, bn_ref, dpre_ref, gsum_ref, ss_ref, grad_ref):
    count, mean, rstd = moments(stat_ref)
    goff, ggain = gsum_ref[0:1, :], gsum_ref[1:2, :]
    own = slice(lat, lat + lon * lat)
    xhat = (first_ref[own].astype(F32) - mean) * rstd
    dfirst = mask_ref[own].astype(F32) * (bn_ref[0:1, :] * rstd) * (dpre_ref[...] - (goff + xhat * ggain) / count)
    put_taps(grad_ref, dfirst.astype(BF16), ss_ref, 2, lon, lat, chans)


def xor_pairs(size, k):
    return [(i, i ^ k) for i in range(size)]


def all_sum(x, axis):
    size = lax.axis_size(axis)
    bit = 1
    while bit < size:
        other = lax.ppermute(x, axis, xor_pairs(size, bit))
        if 2 * bit < size:
            far = lax.ppermute(x, axis, xor_pairs(size, 2 * bit))
            both = lax.ppermute(x, axis, xor_pairs(size, 3 * bit))
            x = (x + other) + (far + both)
        else:
            x = x + other
        bit *= 4
    return x


def scatter_sum(x, axis, last=BF16):
    size = lax.axis_size(axis)
    me = lax.axis_index(axis)
    bit = 1
    while bit < size:
        mine = (me // bit) % 2
        split = x.reshape(x.shape[0] // 2, 2, *x.shape[1:])
        keep = lax.dynamic_index_in_dim(split, mine, 1, keepdims=False)
        send = lax.dynamic_index_in_dim(split, 1 - mine, 1, keepdims=False)
        got = lax.ppermute(send, axis, xor_pairs(size, bit))
        bit *= 2
        x = (keep.astype(F32) + got.astype(F32)).astype(BF16 if bit < size else last)
    return x[0]


def space_sum(x):
    size = lax.axis_size("space")
    bit = 1
    while bit < size:
        got = lax.ppermute(x, "space", xor_pairs(size, bit))
        x = x.astype(F32) + got.astype(F32)
        bit *= 2
        if bit < size:
            x = x.astype(BF16)
    return jnp.swapaxes(x, 1, 2)


def put_shifted(ref, k, x, step):
    chans = x.shape[1]
    zero = jnp.zeros((1, chans), F32)
    ref[k, :, 0:chans] = shift_rows(x, -step, zero).astype(BF16)
    ref[k, :, chans : 2 * chans] = x.astype(BF16)
    ref[k, :, 2 * chans :] = shift_rows(x, step, zero).astype(BF16)


def sample_prep(
    lon, lat, chans, tiles,
    f_hbm, t_hbm, land_hbm, win_hbm, wout_hbm, gain_hbm, offset_hbm,
    ss_ref, tt_ref, mask_ref, target_ref, win_ref, wout_ref, wt_ref, bn_ref,
    f_ref, t_ref, land_ref, wraw_ref, sems,
):
    pairs = [
        (land_hbm, land_ref), (f_hbm, f_ref), (t_hbm, t_ref), (wout_hbm, wout_ref), (win_hbm, wraw_ref),
        (gain_hbm, bn_ref.at[0:1]), (offset_hbm, bn_ref.at[1:2]),
    ]
    copies = [pltpu.make_async_copy(src, dst, sems.at[i]) for i, (src, dst) in enumerate(pairs)]
    for c in copies:
        c.start()
    first = lax.axis_index("space") * lon
    for c in copies[:3]:
        c.wait()
    lines = land_ref[...].astype(F32)
    for i in range(lon):
        mask = spread(lines[i : i + 1], lat, chans)
        mask_ref[first + i] = mask.astype(BF16)
        put_shifted(ss_ref, first + i + 1, f_ref[0, i].astype(F32) * mask, 1)
        target = t_ref[0, i].astype(F32) * mask
        target_ref[0, i] = target.astype(BF16)
        put_shifted(tt_ref, first + i + 1, target, -1)
    for c in copies[3:]:
        c.wait()
    deep = 3 * chans
    zero = jnp.zeros((deep, chans), BF16)
    for q in range(4):
        rows = slice(q * deep, (q + 1) * deep)
        for half in range(2):
            lanes = slice(half * chans, (half + 1) * chans)
            tap = q - half
            inside = 0 <= tap < 3
            win_ref[rows, lanes] = wraw_ref[3 * tap : 3 * tap + 3].reshape(deep, chans) if inside else zero
            turned = [wout_ref[3 * (2 - tap) + b].T for b in range(3)] if inside else [zero]
            wt_ref[rows, lanes] = jnp.concatenate(turned, axis=0)


def paired(ref, start, pairs):
    columns = [jnp.concatenate([ref[start + 2 * m + q] for m in range(pairs)], axis=0) for q in range(4)]
    return jnp.concatenate(columns, axis=1)


def sample_build(lon, lat, chans, f1_ref, f2_ref, l1_ref, l2_ref, l3_ref, ss_in, mask_in, ss_ref, mask_ref):
    me = lax.axis_index("space")
    for k, f_ref, land_ref in ((1, f1_ref, l1_ref), (2, f2_ref, l2_ref), (3, None, l3_ref)):
        first = jnp.bitwise_xor(me, k) * lon
        lines = land_ref[...].astype(F32)
        for i in range(lon):
            mask = spread(lines[i : i + 1], lat, chans)
            mask_ref[first + i] = mask.astype(BF16)
            if f_ref is not None:
                put_shifted(ss_ref, first + i + 1, f_ref[0, i].astype(F32) * mask, 1)


def sample_conv(lon, lat, chans, f3_ref, ss_in, mask_ref, w_ref, ss_ref, first_ref, stat_ref):
    nx = mask_ref.shape[0]
    start = jnp.bitwise_xor(lax.axis_index("space"), 3) * lon
    for i in range(lon):
        put_shifted(ss_ref, start + i + 1, f3_ref[0, i].astype(F32) * mask_ref[start + i].astype(F32), 1)
    tails = [ss_ref[i + 1, lat - 8 :, chans : 2 * chans].astype(F32) for i in range(nx)]
    for i in range(nx):
        fill = tails[nx - 1 - i][7:8]
        ss_ref[i + 1, lat - 8 :, 2 * chans :] = shift_rows(tails[i], 1, fill).astype(BF16)
    ss_ref[0] = ss_ref[nx]
    ss_ref[nx + 1] = ss_ref[1]
    sums, squares, count = [jnp.zeros((8, chans), F32)] * 3
    fold = lambda v: jnp.sum(v.reshape(-1, 8, chans), axis=0)
    pairs = lon
    for c in range(0, nx, 2 * pairs):
        total = dot(paired(ss_ref, c, pairs), w_ref[...])
        for m in range(pairs):
            for half in range(2):
                k = c + 2 * m + half
                first = total[m * lat : (m + 1) * lat, half * chans : (half + 1) * chans].astype(BF16)
                first_ref[k] = first
                x = first.astype(F32)
                mask = mask_ref[k].astype(F32)
                kept = x * mask
                sums, squares, count = sums + fold(kept), squares + fold(kept * x), count + fold(mask)
    rows = [jnp.sum(v, axis=0, keepdims=True) for v in (sums, squares, count)]
    stat_ref[...] = jnp.concatenate(rows + [jnp.zeros((5, chans), F32)], axis=0)


def sample_place(lon, t1_ref, t2_ref, tt_in, tt_ref):
    me = lax.axis_index("space")
    for k, t_ref in ((1, t1_ref), (2, t2_ref)):
        start = jnp.bitwise_xor(me, k) * lon
        for i in range(lon):
            put_shifted(tt_ref, start + i + 1, t_ref[0, i].astype(F32), -1)


def sample_adjoint(lon, lat, chans, t3_ref, mask_ref, wt_ref, tt_in, tt_ref, dact_ref):
    nx = dact_ref.shape[0]
    me = lax.axis_index("space")
    for k, t_ref in ((3, t3_ref),):
        start = jnp.bitwise_xor(me, k) * lon
        for i in range(lon):
            put_shifted(tt_ref, start + i + 1, t_ref[0, i].astype(F32), -1)
    tt_ref[0] = tt_ref[nx]
    tt_ref[nx + 1] = tt_ref[1]
    top = [tt_ref[i + 1, lat - 8 :, chans : 2 * chans].astype(F32)[7:8] for i in range(nx)]
    extra = None
    for a in (-1, 0, 1):
        rows = jnp.concatenate([top[nx - 1 - (i + a) % nx] for i in range(nx)], axis=0).astype(BF16)
        part = dot(rows, wt_ref[(1 - a) * 3 * chans + 2 * chans : (2 - a) * 3 * chans, 0:chans])
        extra = part if extra is None else extra + part
    last = lax.broadcasted_iota(jnp.int32, (lat, chans), 0) == lat - 1
    pairs = lon
    for c in range(0, nx, 2 * pairs):
        total = dot(paired(tt_ref, c, pairs), wt_ref[...])
        for m in range(pairs):
            for half in range(2):
                k = c + 2 * m + half
                own = total[m * lat : (m + 1) * lat, half * chans : (half + 1) * chans]
                dact_ref[k] = (own + jnp.where(last, extra[k : k + 1], 0.0)) * mask_ref[k].astype(F32)


def sample_act(lat, chans, first_ref, mask_ref, stat_ref, bn_ref, dact_ref, gsum_ref, dpre_ref, aa_ref):
    nx = mask_ref.shape[0]
    count, mean, rstd = moments(stat_ref)
    gain, offset = bn_ref[0:1, :] * rstd, bn_ref[1:2, :]
    scale = lax.rsqrt(count)
    fold = lambda v: jnp.sum(v.reshape(-1, 8, chans), axis=0)
    goff, ggain = [jnp.zeros((8, chans), F32)] * 2
    for i in range(nx // 2):
        acts = []
        for k in (i, nx - 1 - i):
            centred = first_ref[k].astype(F32) - mean
            u = centred * gain + offset
            square = u * u
            half = 0.5 * jnp.tanh(u * (square * (0.7978845608 * 0.044715) + 0.7978845608)) + 0.5
            acts.append(u * half * mask_ref[k].astype(F32))
            bend = square * (6.0 * 0.7978845608 * 0.044715) + 2.0 * 0.7978845608
            slope = half + (half - half * half) * u * bend
            dpre = dact_ref[k] * scale * slope
            dpre_ref[k] = dpre
            goff, ggain = goff + fold(dpre), ggain + fold(dpre * centred)
        for k, x, other in ((i, acts[0], acts[1]), (nx - 1 - i, acts[1], acts[0])):
            aa_ref[k + 1, :, 0:chans] = shift_rows(x, -1, jnp.zeros((1, chans), F32)).astype(BF16)
            aa_ref[k + 1, :, chans : 2 * chans] = x.astype(BF16)
            aa_ref[k + 1, :, 2 * chans :] = shift_rows(x, 1, other[lat - 1 : lat]).astype(BF16)
    aa_ref[0] = aa_ref[nx]
    aa_ref[nx + 1] = aa_ref[1]
    rows = [jnp.sum(v, axis=0, keepdims=True) for v in (goff, ggain * rstd)]
    gsum_ref[...] = jnp.concatenate(rows + [jnp.zeros((6, chans), F32)], axis=0)


def halve(get, keep_ref, send_ref, bit):
    mine = lax.rem(lax.div(lax.axis_index("batch"), bit), 2)
    for j in range(keep_ref.shape[0]):
        keep_ref[j] = get(2 * j + mine)
        send_ref[j] = get(2 * j + 1 - mine)


def fold_kernel(bit, a_ref, b_ref, keep_ref, send_ref):
    halve(lambda k: (a_ref[k].astype(F32) + b_ref[k].astype(F32)).astype(BF16), keep_ref, send_ref, bit)


def exchange_sum(keep, send, size):
    bit = 1
    while True:
        got = lax.ppermute(send, "batch", xor_pairs(size, bit))
        bit *= 2
        if bit == size:
            return jnp.swapaxes(keep[0].astype(F32) + got[0].astype(F32), 1, 2), keep
        half = sds((keep.shape[0] // 2,) + keep.shape[1:], BF16)
        keep, send = run(functools.partial(fold_kernel, bit), [half, half], [keep, got])


def sample_grad(lat, chans, aa_ref, tt_ref, stat_ref, keep_ref, send_ref, grad_ref):
    nx = aa_ref.shape[0] - 2
    scale = lax.rsqrt(stat_ref[2:3, :])
    target = tt_ref[1 : 1 + nx, :, chans : 2 * chans].reshape(nx * lat, chans).astype(F32)
    put_taps(grad_ref, (target * scale).astype(BF16), aa_ref, 1, nx, lat, chans)
    halve(lambda k: grad_ref[k], keep_ref, send_ref, 1)


def sample_out(lon, lat, chans, aa_ref, mask_ref, w_ref, gsum_ref, after_ref, out_ref, gain_ref, offset_ref):
    offset_ref[...] = gsum_ref[0:1, :]
    gain_ref[...] = gsum_ref[1:2, :]
    start = lax.axis_index("space") * lon
    total = None
    for a in (-1, 0, 1):
        piece = aa_ref[pl.ds(start + a + 1, lon)].reshape(lon * lat, 3 * chans)
        part = dot(piece, w_ref[3 * (a + 1) : 3 * (a + 2)].reshape(3 * chans, chans))
        total = part if total is None else total + part
    own_mask = mask_ref[pl.ds(start, lon)].reshape(lon * lat, chans).astype(F32)
    out_ref[...] = (total * own_mask).astype(BF16).reshape(1, lon, lat, chans)


def sample_in(lat, chans, first_ref, mask_ref, stat_ref, bn_ref, dpre_ref, gsum_ref, ss_ref, keep_ref, send_ref, grad_ref):
    nx = mask_ref.shape[0]
    count, mean, rstd = moments(stat_ref)
    goff, ggain = gsum_ref[0:1, :] / count, gsum_ref[1:2, :] / count
    factor = bn_ref[0:1, :] * rstd
    rows = []
    for k in range(nx):
        xhat = (first_ref[k].astype(F32) - mean) * rstd
        rows.append((mask_ref[k].astype(F32) * factor * (dpre_ref[k] - (goff + xhat * ggain))).astype(BF16))
    put_taps(grad_ref, jnp.concatenate(rows, axis=0), ss_ref, 1, nx, lat, chans)
    halve(lambda k: grad_ref[k], keep_ref, send_ref, 1)


def tile_body(fields, land, conv_in, conv_out, batchnorm_gain, batchnorm_offset, target_grad):
    lon, lat, chans = fields.shape[1:]
    tiles = lax.axis_size("space")
    sizes = (lon, lat, chans)
    cells = lon * lat
    gain, offset = batchnorm_gain[None, :], batchnorm_offset[None, :]
    fields, land, conv_in, conv_out, target_grad, gain, offset = (
        pltpu.with_memory_space_constraint(x, pltpu.HBM)
        for x in (fields, land, conv_in, conv_out, target_grad, gain, offset)
    )
    n = lon + 2
    join = tiles == 4
    edge = 3 * lat + 16
    shares = lax.axis_size("batch")
    taps = sds((shares, 9, chans // shares, chans), BF16)
    pay_e, pay_o, polar = run(
        functools.partial(pack_kernel, *sizes, join),
        [sds((edge, chans), BF16), sds((edge + (4 * lon if join else 0), chans), BF16), sds((4 * lon, chans), BF16)],
        [fields, target_grad, land],
        scratch=[
            pltpu.VMEM((4, lat, chans), BF16), pltpu.VMEM((lon, 8, chans), BF16),
            pltpu.VMEM((2, lat, chans), BF16), pltpu.VMEM((lon, 8, chans), BF16),
            pltpu.VMEM((lon, lat), jnp.int32), pltpu.SemaphoreType.DMA((7,)),
        ],
        space=pl.BlockSpec(memory_space=pltpu.HBM),
    )
    mirror = [(i, tiles - 1 - i) for i in range(tiles)]
    got_o = lax.ppermute(pay_o, "space", [(i, (i - 1 if i % 2 == 0 else i + 1) % tiles) for i in range(tiles)])
    got_e = lax.ppermute(pay_e, "space", xor_pairs(tiles, 1))
    if join:
        got_x = lax.ppermute(polar, "space", xor_pairs(tiles, 2))
        poles = [got_o, got_x, got_x, polar]
    else:
        poles = [
            lax.ppermute(polar, "space", mirror),
            lax.ppermute(polar, "space", [(i, (tiles - 2 - i) % tiles) for i in range(tiles)]),
            lax.ppermute(polar, "space", [(i, (tiles - i) % tiles) for i in range(tiles)]),
            polar,
        ]
    wide = sds((lon + 4, lat, 3 * chans), BF16)
    near = sds((n, lat, 3 * chans), BF16)
    ss, tt, own_mask, win, wout, wt, bn = run(
        functools.partial(prep_kernel, *sizes),
        [
            wide, near, sds((cells, chans), BF16), sds(conv_in.shape, BF16), sds(conv_out.shape, BF16),
            sds((3, 3 * chans, chans), BF16), sds((8, chans), F32),
        ],
        [fields, target_grad, land, conv_in, conv_out, gain, offset],
        scratch=[
            pltpu.VMEM(fields.shape, BF16), pltpu.VMEM(fields.shape, BF16), pltpu.VMEM(land.shape, jnp.int32),
            pltpu.SemaphoreType.DMA((7,)),
        ],
        space=pl.BlockSpec(memory_space=pltpu.HBM),
    )

    def conv_body(*refs):
        refs = list(refs)
        if join:
            refs[4] = refs[3]
        conv_kernel(*sizes, edge if join else 0, *refs)

    rows = n * lat + 16
    ss, tt, first, mask, stat, tx = run(
        conv_body,
        [wide, near, sds((rows, chans), BF16), sds((rows, chans), BF16), sds((8, chans), F32), sds((16, chans), F32)],
        [got_e, got_o, *poles, ss, tt, own_mask, win],
        flops=2 * rows * 9 * chans * chans,
        alias={6: 0, 7: 1},
    )
    stat = all_sum(all_sum(stat, "batch"), "space")
    dact = run(
        functools.partial(adjoint_kernel, *sizes),
        [sds((cells, chans), F32)],
        [tt, tx, wt],
        flops=2 * cells * 9 * chans * chans,
    )[0]
    gsum, dpre, aa = run(
        functools.partial(act_kernel, *sizes),
        [sds((8, chans), F32), sds((cells, chans), F32), sds((n, lat, 3 * chans), BF16)],
        [first, mask, stat, bn, dact],
    )
    gsum = all_sum(all_sum(gsum, "batch"), "space")
    output, part_out = run(
        functools.partial(out_kernel, *sizes),
        [sds((1, lon, lat, chans), BF16), taps],
        [aa, mask, tt, stat, wout],
        flops=4 * cells * 9 * chans * chans,
    )
    grad_out = space_sum(scatter_sum(part_out, "batch"))
    part_in = run(
        functools.partial(in_kernel, *sizes),
        [taps],
        [first, mask, stat, bn, dpre, gsum, ss],
        flops=2 * cells * 9 * chans * chans,
    )[0]
    grad_in = space_sum(scatter_sum(part_in, "batch"))
    return (output, grad_in, grad_out, gsum[1], gsum[0])


def sample_body(fields, land, conv_in, conv_out, batchnorm_gain, batchnorm_offset, target_grad):
    lon, lat, chans = fields.shape[1:]
    tiles = lax.axis_size("space")
    sizes = (lon, lat, chans)
    nx = tiles * lon
    near, across = xor_pairs(tiles, 1), xor_pairs(tiles, 2)
    move = lambda x, pairs: lax.ppermute(x, "space", pairs)
    f2 = move(fields, across)
    l2 = move(land, across)
    f1 = move(fields, near)
    l1 = move(land, near)
    l3 = move(land, xor_pairs(tiles, 3))
    f3 = move(f2, near)
    gain, offset = batchnorm_gain[None, :], batchnorm_offset[None, :]
    params = [
        pltpu.with_memory_space_constraint(x, pltpu.HBM)
        for x in (fields, target_grad, land, conv_in, conv_out, gain, offset)
    ]
    shares = lax.axis_size("batch")
    half = sds((shares // 2, 9, chans // shares, chans), BF16)
    whole = [pltpu.VMEM((shares, 9, chans // shares, chans), BF16)]
    shifted = sds((nx + 2, lat, 3 * chans), BF16)
    cells = sds((nx, lat, chans), BF16)
    cells_f = sds((nx, lat, chans), F32)
    sums = sds((8, chans), F32)
    work = 2 * nx * lat * 9 * chans * chans
    double = sds((12 * chans, 2 * chans), BF16)
    ss, tt, mask, target, win, wout, wt, bn = run(
        functools.partial(sample_prep, *sizes, tiles),
        [shifted, shifted, cells, sds(target_grad.shape, BF16), double, sds(conv_out.shape, BF16), double, sums],
        params,
        scratch=[
            pltpu.VMEM(fields.shape, BF16), pltpu.VMEM(fields.shape, BF16), pltpu.VMEM(land.shape, jnp.int32),
            pltpu.VMEM(conv_in.shape, BF16), pltpu.SemaphoreType.DMA((7,)),
        ],
        space=pl.BlockSpec(memory_space=pltpu.HBM),
    )
    ss, mask = run(
        functools.partial(sample_build, *sizes), [shifted, cells], [f1, f2, l1, l2, l3, ss, mask], alias={5: 0, 6: 1}
    )
    t2 = move(target, across)
    t1 = move(target, near)
    t3 = move(t2, near)
    ss, first, stat = run(
        functools.partial(sample_conv, *sizes), [shifted, cells, sums], [f3, ss, mask, win], flops=work, alias={1: 0}
    )
    stat = all_sum(stat, "batch")
    (tt,) = run(functools.partial(sample_place, lon), [shifted], [t1, t2, tt], alias={2: 0})
    tt, dact = run(
        functools.partial(sample_adjoint, *sizes), [shifted, cells_f], [t3, mask, wt, tt], flops=work, alias={3: 0}
    )
    gsum, dpre, aa = run(
        functools.partial(sample_act, lat, chans), [sums, cells_f, shifted], [first, mask, stat, bn, dact]
    )
    gsum = all_sum(gsum, "batch")
    keep_o, send_o = run(
        functools.partial(sample_grad, lat, chans), [half, half], [aa, tt, stat], scratch=whole, flops=work
    )
    grad_out, _ = exchange_sum(keep_o, send_o, shares)
    keep_i, send_i = run(
        functools.partial(sample_in, lat, chans),
        [half, half], [first, mask, stat, bn, dpre, gsum, ss], scratch=whole, flops=work,
    )
    grad_in, folded = exchange_sum(keep_i, send_i, shares)
    output, grad_gain, grad_offset = run(
        functools.partial(sample_out, *sizes),
        [sds(fields.shape, BF16), sds((1, chans), F32), sds((1, chans), F32)],
        [aa, mask, wout, gsum, folded], flops=work // tiles,
    )
    return (output, grad_in, grad_out, grad_gain[0], grad_offset[0])


def body(*args):
    if lax.axis_size("space") != 4:
        return tile_body(*args)
    return sample_body(*args)


def solution(mesh):
    in_specs = (
        P(("groups", "batch"), "space", None, None),
        P("space", None),
        P(),
        P(),
        P(),
        P(),
        P(("groups", "batch"), "space", None, None),
    )
    out_specs = (
        P(("groups", "batch"), "space", None, None),
        P("groups", None, "batch"),
        P("groups", None, "batch"),
        P("groups"),
        P("groups"),
    )
    return jax.shard_map(body, mesh=mesh, in_specs=in_specs, out_specs=out_specs, check_vma=False)
```

```python
import functools

import jax
import jax.numpy as jnp
from jax import lax
from jax.experimental import pallas as pl
from jax.experimental.pallas import tpu as pltpu
from jax.sharding import PartitionSpec as P


F32 = jnp.float32
BF16 = jnp.bfloat16
VMEM = pl.BlockSpec(memory_space=pltpu.VMEM)


def run(body, outs, args, scratch=(), flops=0, space=VMEM, alias=None):
    nbytes = sum(a.size * a.dtype.itemsize for a in args)
    nbytes += sum(o.size * o.dtype.itemsize for o in outs)
    return pl.pallas_call(
        body,
        out_shape=list(outs),
        in_specs=[space] * len(args),
        out_specs=[VMEM] * len(outs),
        scratch_shapes=list(scratch),
        cost_estimate=pl.CostEstimate(flops=flops, bytes_accessed=nbytes, transcendentals=0),
        compiler_params=pltpu.CompilerParams(vmem_limit_bytes=24 << 20),
        input_output_aliases=alias or {},
    )(*args)


def sds(shape, dtype):
    return jax.ShapeDtypeStruct(shape, dtype)


def dot(a, b):
    return jnp.dot(a, b, preferred_element_type=F32)


def spread(line, lat, chans):
    rows = lax.broadcasted_iota(jnp.int32, (lat, lat), 0)
    cols = lax.broadcasted_iota(jnp.int32, (lat, lat), 1)
    col = jnp.sum(jnp.where(rows == cols, jnp.broadcast_to(line, (lat, lat)), 0.0), axis=1, keepdims=True)
    return jnp.broadcast_to(col, (lat, chans))


def pack_kernel(lon, lat, chans, join, f_hbm, t_hbm, land_hbm, e_ref, o_ref, p_ref, fc, fr, tc, tr, land, sems):
    copies = [
        pltpu.make_async_copy(f_hbm.at[0, 0:2], fc.at[0:2], sems.at[0]),
        pltpu.make_async_copy(f_hbm.at[0, lon - 2 : lon], fc.at[2:4], sems.at[1]),
        pltpu.make_async_copy(f_hbm.at[0, :, lat - 8 : lat], fr, sems.at[2]),
        pltpu.make_async_copy(t_hbm.at[0, 0:1], tc.at[0:1], sems.at[3]),
        pltpu.make_async_copy(t_hbm.at[0, lon - 1 : lon], tc.at[1:2], sems.at[4]),
        pltpu.make_async_copy(t_hbm.at[0, :, lat - 8 : lat], tr, sems.at[5]),
        pltpu.make_async_copy(land_hbm, land, sems.at[6]),
    ]
    for c in copies:
        c.start()
    even = lax.rem(lax.axis_index("space"), 2) == 0
    for c in copies:
        c.wait()
    lines = land[...].astype(F32)

    def edge(k, cols_f, side):
        masks = [spread(lines[i : i + 1], lat, chans) for i in cols_f]
        parts = [fc[k + n].astype(F32) * m for n, m in enumerate(masks)]
        col = cols_f[0] if side == 0 else cols_f[1]
        parts.append(tc[side].astype(F32) * masks[0 if side == 0 else 1])
        line = jnp.concatenate([lines[col : col + 1], jnp.zeros((1, chans - lat), F32)], axis=1)
        parts += [line, jnp.zeros((15, chans), F32)]
        return jnp.concatenate(parts, axis=0).astype(BF16)

    west = edge(0, (0, 1), 0)
    east = edge(2, (lon - 2, lon - 1), 1)
    n = west.shape[0]
    e_ref[...] = jnp.where(even, east, west)
    o_ref[0:n, :] = jnp.where(even, west, east)
    lane = lax.broadcasted_iota(jnp.int32, (lon, lat), 1)
    last = {}
    for j in (lat - 2, lat - 1):
        col = jnp.sum(jnp.where(lane == j, lines, 0.0), axis=1, keepdims=True)
        last[j] = jnp.broadcast_to(col, (lon, chans))
    rows = []
    for j, ref in ((lat - 2, fr), (lat - 1, fr), (lat - 1, tr)):
        k = j - (lat - 8)
        line = jnp.concatenate([ref[i].astype(F32)[k : k + 1] for i in range(lon)], axis=0)
        rows.append(line * last[j])
    rows.append(last[lat - 1])
    polar = jnp.concatenate(rows, axis=0).astype(BF16)
    p_ref[...] = polar
    if join:
        o_ref[n:, :] = polar


def shift_rows(x, step, fill):
    rows = lax.broadcasted_iota(jnp.int32, x.shape, 0)
    n = x.shape[0]
    moved = pltpu.roll(x, (-step) % n, 0)
    return jnp.where(rows == (n - 1 if step > 0 else 0), fill, moved)


def prep_kernel(
    lon, lat, chans,
    f_hbm, t_hbm, land_hbm, win_hbm, wout_hbm, gain_hbm, offset_hbm,
    ss_ref, tt_ref, mask_ref, win_ref, wout_ref, wt_ref, bn_ref,
    f_ref, t_ref, land_ref, sems,
):
    pairs = [
        (land_hbm, land_ref), (f_hbm, f_ref), (t_hbm, t_ref), (wout_hbm, wout_ref), (win_hbm, win_ref),
        (gain_hbm, bn_ref.at[0:1]), (offset_hbm, bn_ref.at[1:2]),
    ]
    copies = [pltpu.make_async_copy(src, dst, sems.at[i]) for i, (src, dst) in enumerate(pairs)]
    for c in copies:
        c.start()
    for c in copies[:3]:
        c.wait()
    lines = land_ref[...].astype(F32)
    zero = jnp.zeros((1, chans), F32)
    for i in range(lon):
        mask = spread(lines[i : i + 1], lat, chans)
        mask_ref[i * lat : (i + 1) * lat] = mask.astype(BF16)
        x = f_ref[0, i].astype(F32) * mask
        ss_ref[i + 2, :, 0:chans] = shift_rows(x, -1, zero).astype(BF16)
        ss_ref[i + 2, :, chans : 2 * chans] = x.astype(BF16)
        ss_ref[i + 2, :, 2 * chans :] = shift_rows(x, 1, zero).astype(BF16)
        x = t_ref[0, i].astype(F32) * mask
        tt_ref[i + 1, :, 0:chans] = shift_rows(x, 1, zero).astype(BF16)
        tt_ref[i + 1, :, chans : 2 * chans] = x.astype(BF16)
        tt_ref[i + 1, :, 2 * chans :] = shift_rows(x, -1, zero).astype(BF16)
    for c in copies[3:]:
        c.wait()
    for a in range(3):
        for b in range(3):
            wt_ref[a, b * chans : (b + 1) * chans] = wout_ref[3 * a + b].T


def conv_kernel(
    lon, lat, chans, moff,
    re_ref, ro_ref, rm_ref, r1_ref, r2_ref, own_ref, ss_in, tt_in, om_ref, w_ref,
    ss_ref, tt_ref, first_ref, mask_ref, stat_ref, tx_ref,
):
    even = lax.rem(lax.axis_index("space"), 2) == 0
    recv_e = re_ref[...].astype(F32)
    recv_o = ro_ref[0 : recv_e.shape[0], :].astype(F32)
    west = jnp.where(even, recv_o, recv_e)
    east = jnp.where(even, recv_e, recv_o)
    polar_m = rm_ref[moff : moff + 4 * lon, :].astype(F32)
    if r1_ref is r2_ref:
        other = r1_ref[...].astype(F32)
        own = own_ref[...].astype(F32)
        polar_1 = jnp.where(even, other, own)
        polar_2 = jnp.where(even, own, other)
    else:
        polar_1 = r1_ref[...].astype(F32)
        polar_2 = r2_ref[...].astype(F32)

    def ghost(kind, cols):
        line = jnp.concatenate([p[kind * lon : (kind + 1) * lon] for p in (polar_1, polar_m, polar_2)], axis=0)
        picks = [2 * lon - 1 - i for i in cols]
        return jnp.concatenate([line[k : k + 1] for k in picks], axis=0)

    zero = jnp.zeros((1, chans), F32)
    wide = list(range(-2, lon + 2))
    near = list(range(-1, lon + 1))
    g62, g63 = ghost(0, wide), ghost(1, wide)
    gt, gm = ghost(2, near), ghost(3, near)
    halo = {0: west[0:lat], 1: west[lat : 2 * lat], lon + 2: east[0:lat], lon + 3: east[lat : 2 * lat]}
    rows8 = lax.broadcasted_iota(jnp.int32, (8, chans), 0)
    top = []
    for k in range(lon + 4):
        fill = g63[k : k + 1]
        if k in halo:
            x = halo[k]
            ss_ref[k, :, 0:chans] = shift_rows(x, -1, zero).astype(BF16)
            ss_ref[k, :, chans : 2 * chans] = x.astype(BF16)
            ss_ref[k, :, 2 * chans :] = shift_rows(x, 1, fill).astype(BF16)
            top.append(x[lat - 1 : lat])
        else:
            tail = ss_ref[k, lat - 8 :, chans : 2 * chans].astype(F32)
            top.append(tail[7:8])
            ss_ref[k, lat - 8 :, 2 * chans :] = shift_rows(tail, 1, fill).astype(BF16)
    top = jnp.concatenate(top, axis=0)
    fold = jnp.concatenate([g62, g63, top], axis=1)
    total = None
    n = lon + 2
    pad = jnp.zeros((16 - n, 3 * chans), F32)
    for a in (-1, 0, 1):
        ghost_rows = jnp.concatenate([fold[1 - a : 1 - a + n], pad], axis=0).astype(BF16)
        piece = jnp.concatenate([ss_ref[a + 1 : a + 1 + n].reshape(n * lat, 3 * chans), ghost_rows], axis=0)
        part = dot(piece, w_ref[3 * (a + 1) : 3 * (a + 2)].reshape(3 * chans, chans))
        total = part if total is None else total + part
    first = total.astype(BF16)
    first_ref[...] = first
    own_first = first[lat : lat + lon * lat].astype(F32)
    own_mask = om_ref[...].astype(F32)
    kept = own_first * own_mask
    sums = jnp.sum(kept, axis=0, keepdims=True)
    squares = jnp.sum(kept * own_first, axis=0, keepdims=True)
    count = jnp.sum(own_mask, axis=0, keepdims=True)
    stat_ref[...] = jnp.concatenate([sums, squares, count, jnp.zeros((5, chans), F32)], axis=0)
    edges = [spread(x[3 * lat : 3 * lat + 1, 0:lat], lat, chans) for x in (west, east)]
    mask_ref[0:lat] = edges[0].astype(BF16)
    mask_ref[lat : lat + lon * lat] = om_ref[...]
    mask_ref[lat + lon * lat : n * lat] = edges[1].astype(BF16)
    mask_ref[n * lat :] = jnp.concatenate([gm, jnp.zeros((16 - n, chans), F32)], axis=0).astype(BF16)
    for k, x in ((0, west[2 * lat : 3 * lat]), (lon + 1, east[2 * lat : 3 * lat])):
        tt_ref[k, :, 0:chans] = shift_rows(x, 1, zero).astype(BF16)
        tt_ref[k, :, chans : 2 * chans] = x.astype(BF16)
        tt_ref[k, :, 2 * chans :] = shift_rows(x, -1, zero).astype(BF16)
    tx_ref[...] = jnp.concatenate([gt, jnp.zeros((16 - n, chans), F32)], axis=0)


def adjoint_kernel(lon, lat, chans, tt_ref, tx_ref, wt_ref, dact_ref):
    gt = tx_ref[...]
    total = None
    for a in (-1, 0, 1):
        extra = jnp.concatenate([gt[1 + a : 1 + a + lon], jnp.zeros((16 - lon, chans), F32)], axis=0)
        extra = jnp.concatenate([jnp.zeros((16, 2 * chans), F32), extra], axis=1).astype(BF16)
        piece = jnp.concatenate([tt_ref[1 - a : 1 - a + lon].reshape(lon * lat, 3 * chans), extra], axis=0)
        part = dot(piece, wt_ref[a + 1])
        total = part if total is None else total + part
    rows = lax.broadcasted_iota(jnp.int32, (lat, chans), 0)
    for i in range(lon):
        add = total[lon * lat + i : lon * lat + i + 1]
        dact_ref[i * lat : (i + 1) * lat, :] = total[i * lat : (i + 1) * lat] + jnp.where(rows == lat - 1, add, 0.0)


def moments(stat_ref):
    count = stat_ref[2:3, :]
    mean = stat_ref[0:1, :] / count
    var = stat_ref[1:2, :] / count - mean * mean
    return count, mean, lax.rsqrt(var + 1e-05)


def act_kernel(lon, lat, chans, first_ref, mask_ref, stat_ref, bn_ref, dact_ref, gsum_ref, dpre_ref, aa_ref):
    count, mean, rstd = moments(stat_ref)
    gain, offset = bn_ref[0:1, :], bn_ref[1:2, :]

    def forward(lo, hi):
        xhat = (first_ref[lo:hi].astype(F32) - mean) * rstd
        u = gain * xhat + offset
        hyper = jnp.tanh(0.7978845608 * (u + 0.044715 * u * u * u))
        m = mask_ref[lo:hi].astype(F32)
        return xhat, u, hyper, m, 0.5 * u * (1.0 + hyper) * m

    n = lon + 2
    zero = jnp.zeros((1, chans), F32)
    ghost = forward(n * lat, n * lat + 16)[4]
    scale = lax.rsqrt(count)
    goff = jnp.zeros((1, chans), F32)
    ggain = jnp.zeros((1, chans), F32)
    for k in range(n):
        xhat, u, hyper, m, act = forward(k * lat, (k + 1) * lat)
        aa_ref[k, :, 0:chans] = shift_rows(act, -1, zero).astype(BF16)
        aa_ref[k, :, chans : 2 * chans] = act.astype(BF16)
        aa_ref[k, :, 2 * chans :] = shift_rows(act, 1, ghost[k : k + 1]).astype(BF16)
        if 0 < k <= lon:
            slope = 0.5 * (1.0 + hyper) + 0.5 * u * (1.0 - hyper * hyper) * 0.7978845608 * (
                1.0 + 3.0 * 0.044715 * u * u
            )
            rows = slice((k - 1) * lat, k * lat)
            dpre = dact_ref[rows] * scale * m * slope
            dpre_ref[rows] = dpre
            goff = goff + jnp.sum(dpre, axis=0, keepdims=True)
            ggain = ggain + jnp.sum(dpre * xhat, axis=0, keepdims=True)
    gsum_ref[...] = jnp.concatenate([goff, ggain, jnp.zeros((6, chans), F32)], axis=0)


def put_taps(grad_ref, grad, shifted_ref, base, lon, lat, chans):
    chunks, width = grad_ref.shape[0], grad_ref.shape[2]
    pieces = [shifted_ref[base + a : base + a + lon].reshape(lon * lat, 3 * chans) for a in (-1, 0, 1)]
    part = dot(grad.T, jnp.concatenate(pieces, axis=1)).astype(BF16)
    for t in range(9):
        for c in range(chunks):
            grad_ref[c, t] = part[c * width : (c + 1) * width, t * chans : (t + 1) * chans]


def out_kernel(lon, lat, chans, aa_ref, mask_ref, tt_ref, stat_ref, w_ref, out_ref, grad_ref):
    total = None
    for a in (-1, 0, 1):
        piece = aa_ref[a + 1 : a + 1 + lon].reshape(lon * lat, 3 * chans)
        part = dot(piece, w_ref[3 * (a + 1) : 3 * (a + 2)].reshape(3 * chans, chans))
        total = part if total is None else total + part
    own_mask = mask_ref[lat : lat + lon * lat].astype(F32)
    out_ref[...] = (total * own_mask).astype(BF16).reshape(1, lon, lat, chans)
    scale = lax.rsqrt(stat_ref[2:3, :])
    target = tt_ref[1 : 1 + lon, :, chans : 2 * chans].reshape(lon * lat, chans).astype(F32)
    dout = (target * scale).astype(BF16)
    put_taps(grad_ref, dout, aa_ref, 1, lon, lat, chans)


def in_kernel(lon, lat, chans, first_ref, mask_ref, stat_ref, bn_ref, dpre_ref, gsum_ref, ss_ref, grad_ref):
    count, mean, rstd = moments(stat_ref)
    goff, ggain = gsum_ref[0:1, :], gsum_ref[1:2, :]
    own = slice(lat, lat + lon * lat)
    xhat = (first_ref[own].astype(F32) - mean) * rstd
    dfirst = mask_ref[own].astype(F32) * (bn_ref[0:1, :] * rstd) * (dpre_ref[...] - (goff + xhat * ggain) / count)
    put_taps(grad_ref, dfirst.astype(BF16), ss_ref, 2, lon, lat, chans)


def xor_pairs(size, k):
    return [(i, i ^ k) for i in range(size)]


def all_sum(x, axis):
    size = lax.axis_size(axis)
    bit = 1
    while bit < size:
        other = lax.ppermute(x, axis, xor_pairs(size, bit))
        if 2 * bit < size:
            far = lax.ppermute(x, axis, xor_pairs(size, 2 * bit))
            both = lax.ppermute(x, axis, xor_pairs(size, 3 * bit))
            x = (x + other) + (far + both)
        else:
            x = x + other
        bit *= 4
    return x


def scatter_sum(x, axis, last=BF16):
    size = lax.axis_size(axis)
    me = lax.axis_index(axis)
    bit = 1
    while bit < size:
        mine = (me // bit) % 2
        split = x.reshape(x.shape[0] // 2, 2, *x.shape[1:])
        keep = lax.dynamic_index_in_dim(split, mine, 1, keepdims=False)
        send = lax.dynamic_index_in_dim(split, 1 - mine, 1, keepdims=False)
        got = lax.ppermute(send, axis, xor_pairs(size, bit))
        bit *= 2
        x = (keep.astype(F32) + got.astype(F32)).astype(BF16 if bit < size else last)
    return x[0]


def space_sum(x):
    size = lax.axis_size("space")
    bit = 1
    while bit < size:
        got = lax.ppermute(x, "space", xor_pairs(size, bit))
        x = x.astype(F32) + got.astype(F32)
        bit *= 2
        if bit < size:
            x = x.astype(BF16)
    return jnp.swapaxes(x, 1, 2)


def put_shifted(ref, k, x, step):
    chans = x.shape[1]
    zero = jnp.zeros((1, chans), F32)
    ref[k, :, 0:chans] = shift_rows(x, -step, zero).astype(BF16)
    ref[k, :, chans : 2 * chans] = x.astype(BF16)
    ref[k, :, 2 * chans :] = shift_rows(x, step, zero).astype(BF16)


def sample_prep(
    lon, lat, chans, tiles,
    f_hbm, t_hbm, land_hbm, win_hbm, wout_hbm, gain_hbm, offset_hbm,
    ss_ref, tt_ref, mask_ref, target_ref, win_ref, wout_ref, wt_ref, bn_ref,
    f_ref, t_ref, land_ref, wraw_ref, sems,
):
    pairs = [
        (land_hbm, land_ref), (f_hbm, f_ref), (t_hbm, t_ref), (wout_hbm, wout_ref), (win_hbm, wraw_ref),
        (gain_hbm, bn_ref.at[0:1]), (offset_hbm, bn_ref.at[1:2]),
    ]
    copies = [pltpu.make_async_copy(src, dst, sems.at[i]) for i, (src, dst) in enumerate(pairs)]
    for c in copies:
        c.start()
    first = lax.axis_index("space") * lon
    for c in copies[:3]:
        c.wait()
    lines = land_ref[...].astype(F32)
    for i in range(lon):
        mask = spread(lines[i : i + 1], lat, chans)
        mask_ref[first + i] = mask.astype(BF16)
        put_shifted(ss_ref, first + i + 1, f_ref[0, i].astype(F32) * mask, 1)
        target = t_ref[0, i].astype(F32) * mask
        target_ref[0, i] = target.astype(BF16)
        put_shifted(tt_ref, first + i + 1, target, -1)
    for c in copies[3:]:
        c.wait()
    deep = 3 * chans
    zero = jnp.zeros((deep, chans), BF16)
    for q in range(4):
        rows = slice(q * deep, (q + 1) * deep)
        for half in range(2):
            lanes = slice(half * chans, (half + 1) * chans)
            tap = q - half
            inside = 0 <= tap < 3
            win_ref[rows, lanes] = wraw_ref[3 * tap : 3 * tap + 3].reshape(deep, chans) if inside else zero
            turned = [wout_ref[3 * (2 - tap) + b].T for b in range(3)] if inside else [zero]
            wt_ref[rows, lanes] = jnp.concatenate(turned, axis=0)


def paired(ref, start, pairs):
    columns = [jnp.concatenate([ref[start + 2 * m + q] for m in range(pairs)], axis=0) for q in range(4)]
    return jnp.concatenate(columns, axis=1)


def sample_build(lon, lat, chans, f1_ref, f2_ref, l1_ref, l2_ref, l3_ref, ss_in, mask_in, ss_ref, mask_ref):
    me = lax.axis_index("space")
    for k, f_ref, land_ref in ((1, f1_ref, l1_ref), (2, f2_ref, l2_ref), (3, None, l3_ref)):
        first = jnp.bitwise_xor(me, k) * lon
        lines = land_ref[...].astype(F32)
        for i in range(lon):
            mask = spread(lines[i : i + 1], lat, chans)
            mask_ref[first + i] = mask.astype(BF16)
            if f_ref is not None:
                put_shifted(ss_ref, first + i + 1, f_ref[0, i].astype(F32) * mask, 1)


def sample_conv(lon, lat, chans, f3_ref, ss_in, mask_ref, w_ref, ss_ref, first_ref, stat_ref):
    nx = mask_ref.shape[0]
    start = jnp.bitwise_xor(lax.axis_index("space"), 3) * lon
    for i in range(lon):
        put_shifted(ss_ref, start + i + 1, f3_ref[0, i].astype(F32) * mask_ref[start + i].astype(F32), 1)
    tails = [ss_ref[i + 1, lat - 8 :, chans : 2 * chans].astype(F32) for i in range(nx)]
    for i in range(nx):
        fill = tails[nx - 1 - i][7:8]
        ss_ref[i + 1, lat - 8 :, 2 * chans :] = shift_rows(tails[i], 1, fill).astype(BF16)
    ss_ref[0] = ss_ref[nx]
    ss_ref[nx + 1] = ss_ref[1]
    sums, squares, count = [jnp.zeros((8, chans), F32)] * 3
    fold = lambda v: jnp.sum(v.reshape(-1, 8, chans), axis=0)
    pairs = lon
    for c in range(0, nx, 2 * pairs):
        total = dot(paired(ss_ref, c, pairs), w_ref[...])
        for m in range(pairs):
            for half in range(2):
                k = c + 2 * m + half
                first = total[m * lat : (m + 1) * lat, half * chans : (half + 1) * chans].astype(BF16)
                first_ref[k] = first
                x = first.astype(F32)
                mask = mask_ref[k].astype(F32)
                kept = x * mask
                sums, squares, count = sums + fold(kept), squares + fold(kept * x), count + fold(mask)
    rows = [jnp.sum(v, axis=0, keepdims=True) for v in (sums, squares, count)]
    stat_ref[...] = jnp.concatenate(rows + [jnp.zeros((5, chans), F32)], axis=0)


def sample_adjoint(lon, lat, chans, t1_ref, t2_ref, t3_ref, mask_ref, wt_ref, tt_in, tt_ref, dact_ref):
    nx = dact_ref.shape[0]
    me = lax.axis_index("space")
    for k, t_ref in ((1, t1_ref), (2, t2_ref), (3, t3_ref)):
        start = jnp.bitwise_xor(me, k) * lon
        for i in range(lon):
            put_shifted(tt_ref, start + i + 1, t_ref[0, i].astype(F32), -1)
    tt_ref[0] = tt_ref[nx]
    tt_ref[nx + 1] = tt_ref[1]
    top = [tt_ref[i + 1, lat - 8 :, chans : 2 * chans].astype(F32)[7:8] for i in range(nx)]
    extra = None
    for a in (-1, 0, 1):
        rows = jnp.concatenate([top[nx - 1 - (i + a) % nx] for i in range(nx)], axis=0).astype(BF16)
        part = dot(rows, wt_ref[(1 - a) * 3 * chans + 2 * chans : (2 - a) * 3 * chans, 0:chans])
        extra = part if extra is None else extra + part
    last = lax.broadcasted_iota(jnp.int32, (lat, chans), 0) == lat - 1
    pairs = lon
    for c in range(0, nx, 2 * pairs):
        total = dot(paired(tt_ref, c, pairs), wt_ref[...])
        for m in range(pairs):
            for half in range(2):
                k = c + 2 * m + half
                own = total[m * lat : (m + 1) * lat, half * chans : (half + 1) * chans]
                dact_ref[k] = (own + jnp.where(last, extra[k : k + 1], 0.0)) * mask_ref[k].astype(F32)


def sample_act(lat, chans, first_ref, mask_ref, stat_ref, bn_ref, dact_ref, gsum_ref, dpre_ref, aa_ref):
    nx = mask_ref.shape[0]
    count, mean, rstd = moments(stat_ref)
    gain, offset = bn_ref[0:1, :] * rstd, bn_ref[1:2, :]
    scale = lax.rsqrt(count)
    fold = lambda v: jnp.sum(v.reshape(-1, 8, chans), axis=0)
    goff, ggain = [jnp.zeros((8, chans), F32)] * 2
    for i in range(nx // 2):
        acts = []
        for k in (i, nx - 1 - i):
            centred = first_ref[k].astype(F32) - mean
            u = centred * gain + offset
            square = u * u
            half = 0.5 * jnp.tanh(u * (square * (0.7978845608 * 0.044715) + 0.7978845608)) + 0.5
            acts.append(u * half * mask_ref[k].astype(F32))
            bend = square * (6.0 * 0.7978845608 * 0.044715) + 2.0 * 0.7978845608
            slope = half + (half - half * half) * u * bend
            dpre = dact_ref[k] * scale * slope
            dpre_ref[k] = dpre
            goff, ggain = goff + fold(dpre), ggain + fold(dpre * centred)
        for k, x, other in ((i, acts[0], acts[1]), (nx - 1 - i, acts[1], acts[0])):
            aa_ref[k + 1, :, 0:chans] = shift_rows(x, -1, jnp.zeros((1, chans), F32)).astype(BF16)
            aa_ref[k + 1, :, chans : 2 * chans] = x.astype(BF16)
            aa_ref[k + 1, :, 2 * chans :] = shift_rows(x, 1, other[lat - 1 : lat]).astype(BF16)
    aa_ref[0] = aa_ref[nx]
    aa_ref[nx + 1] = aa_ref[1]
    rows = [jnp.sum(v, axis=0, keepdims=True) for v in (goff, ggain * rstd)]
    gsum_ref[...] = jnp.concatenate(rows + [jnp.zeros((6, chans), F32)], axis=0)


def halve(get, keep_ref, send_ref, bit):
    mine = lax.rem(lax.div(lax.axis_index("batch"), bit), 2)
    for j in range(keep_ref.shape[0]):
        keep_ref[j] = get(2 * j + mine)
        send_ref[j] = get(2 * j + 1 - mine)


def fold_kernel(bit, a_ref, b_ref, keep_ref, send_ref):
    halve(lambda k: (a_ref[k].astype(F32) + b_ref[k].astype(F32)).astype(BF16), keep_ref, send_ref, bit)


def exchange_sum(keep, send, size):
    bit = 1
    while True:
        got = lax.ppermute(send, "batch", xor_pairs(size, bit))
        bit *= 2
        if bit == size:
            return jnp.swapaxes(keep[0].astype(F32) + got[0].astype(F32), 1, 2), keep
        half = sds((keep.shape[0] // 2,) + keep.shape[1:], BF16)
        keep, send = run(functools.partial(fold_kernel, bit), [half, half], [keep, got])


def sample_grad(lat, chans, aa_ref, tt_ref, stat_ref, keep_ref, send_ref, grad_ref):
    nx = aa_ref.shape[0] - 2
    scale = lax.rsqrt(stat_ref[2:3, :])
    target = tt_ref[1 : 1 + nx, :, chans : 2 * chans].reshape(nx * lat, chans).astype(F32)
    put_taps(grad_ref, (target * scale).astype(BF16), aa_ref, 1, nx, lat, chans)
    halve(lambda k: grad_ref[k], keep_ref, send_ref, 1)


def sample_out(lon, lat, chans, aa_ref, mask_ref, w_ref, gsum_ref, after_ref, out_ref, gain_ref, offset_ref):
    offset_ref[...] = gsum_ref[0:1, :]
    gain_ref[...] = gsum_ref[1:2, :]
    start = lax.axis_index("space") * lon
    total = None
    for a in (-1, 0, 1):
        piece = aa_ref[pl.ds(start + a + 1, lon)].reshape(lon * lat, 3 * chans)
        part = dot(piece, w_ref[3 * (a + 1) : 3 * (a + 2)].reshape(3 * chans, chans))
        total = part if total is None else total + part
    own_mask = mask_ref[pl.ds(start, lon)].reshape(lon * lat, chans).astype(F32)
    out_ref[...] = (total * own_mask).astype(BF16).reshape(1, lon, lat, chans)


def sample_in(lat, chans, first_ref, mask_ref, stat_ref, bn_ref, dpre_ref, gsum_ref, ss_ref, keep_ref, send_ref, grad_ref):
    nx = mask_ref.shape[0]
    count, mean, rstd = moments(stat_ref)
    goff, ggain = gsum_ref[0:1, :] / count, gsum_ref[1:2, :] / count
    factor = bn_ref[0:1, :] * rstd
    rows = []
    for k in range(nx):
        xhat = (first_ref[k].astype(F32) - mean) * rstd
        rows.append((mask_ref[k].astype(F32) * factor * (dpre_ref[k] - (goff + xhat * ggain))).astype(BF16))
    put_taps(grad_ref, jnp.concatenate(rows, axis=0), ss_ref, 1, nx, lat, chans)
    halve(lambda k: grad_ref[k], keep_ref, send_ref, 1)


def tile_body(fields, land, conv_in, conv_out, batchnorm_gain, batchnorm_offset, target_grad):
    lon, lat, chans = fields.shape[1:]
    tiles = lax.axis_size("space")
    sizes = (lon, lat, chans)
    cells = lon * lat
    gain, offset = batchnorm_gain[None, :], batchnorm_offset[None, :]
    fields, land, conv_in, conv_out, target_grad, gain, offset = (
        pltpu.with_memory_space_constraint(x, pltpu.HBM)
        for x in (fields, land, conv_in, conv_out, target_grad, gain, offset)
    )
    n = lon + 2
    join = tiles == 4
    edge = 3 * lat + 16
    shares = lax.axis_size("batch")
    taps = sds((shares, 9, chans // shares, chans), BF16)
    pay_e, pay_o, polar = run(
        functools.partial(pack_kernel, *sizes, join),
        [sds((edge, chans), BF16), sds((edge + (4 * lon if join else 0), chans), BF16), sds((4 * lon, chans), BF16)],
        [fields, target_grad, land],
        scratch=[
            pltpu.VMEM((4, lat, chans), BF16), pltpu.VMEM((lon, 8, chans), BF16),
            pltpu.VMEM((2, lat, chans), BF16), pltpu.VMEM((lon, 8, chans), BF16),
            pltpu.VMEM((lon, lat), jnp.int32), pltpu.SemaphoreType.DMA((7,)),
        ],
        space=pl.BlockSpec(memory_space=pltpu.HBM),
    )
    mirror = [(i, tiles - 1 - i) for i in range(tiles)]
    got_o = lax.ppermute(pay_o, "space", [(i, (i - 1 if i % 2 == 0 else i + 1) % tiles) for i in range(tiles)])
    got_e = lax.ppermute(pay_e, "space", xor_pairs(tiles, 1))
    if join:
        got_x = lax.ppermute(polar, "space", xor_pairs(tiles, 2))
        poles = [got_o, got_x, got_x, polar]
    else:
        poles = [
            lax.ppermute(polar, "space", mirror),
            lax.ppermute(polar, "space", [(i, (tiles - 2 - i) % tiles) for i in range(tiles)]),
            lax.ppermute(polar, "space", [(i, (tiles - i) % tiles) for i in range(tiles)]),
            polar,
        ]
    wide = sds((lon + 4, lat, 3 * chans), BF16)
    near = sds((n, lat, 3 * chans), BF16)
    ss, tt, own_mask, win, wout, wt, bn = run(
        functools.partial(prep_kernel, *sizes),
        [
            wide, near, sds((cells, chans), BF16), sds(conv_in.shape, BF16), sds(conv_out.shape, BF16),
            sds((3, 3 * chans, chans), BF16), sds((8, chans), F32),
        ],
        [fields, target_grad, land, conv_in, conv_out, gain, offset],
        scratch=[
            pltpu.VMEM(fields.shape, BF16), pltpu.VMEM(fields.shape, BF16), pltpu.VMEM(land.shape, jnp.int32),
            pltpu.SemaphoreType.DMA((7,)),
        ],
        space=pl.BlockSpec(memory_space=pltpu.HBM),
    )

    def conv_body(*refs):
        refs = list(refs)
        if join:
            refs[4] = refs[3]
        conv_kernel(*sizes, edge if join else 0, *refs)

    rows = n * lat + 16
    ss, tt, first, mask, stat, tx = run(
        conv_body,
        [wide, near, sds((rows, chans), BF16), sds((rows, chans), BF16), sds((8, chans), F32), sds((16, chans), F32)],
        [got_e, got_o, *poles, ss, tt, own_mask, win],
        flops=2 * rows * 9 * chans * chans,
        alias={6: 0, 7: 1},
    )
    stat = all_sum(all_sum(stat, "batch"), "space")
    dact = run(
        functools.partial(adjoint_kernel, *sizes),
        [sds((cells, chans), F32)],
        [tt, tx, wt],
        flops=2 * cells * 9 * chans * chans,
    )[0]
    gsum, dpre, aa = run(
        functools.partial(act_kernel, *sizes),
        [sds((8, chans), F32), sds((cells, chans), F32), sds((n, lat, 3 * chans), BF16)],
        [first, mask, stat, bn, dact],
    )
    gsum = all_sum(all_sum(gsum, "batch"), "space")
    output, part_out = run(
        functools.partial(out_kernel, *sizes),
        [sds((1, lon, lat, chans), BF16), taps],
        [aa, mask, tt, stat, wout],
        flops=4 * cells * 9 * chans * chans,
    )
    grad_out = space_sum(scatter_sum(part_out, "batch"))
    part_in = run(
        functools.partial(in_kernel, *sizes),
        [taps],
        [first, mask, stat, bn, dpre, gsum, ss],
        flops=2 * cells * 9 * chans * chans,
    )[0]
    grad_in = space_sum(scatter_sum(part_in, "batch"))
    return (output, grad_in, grad_out, gsum[1], gsum[0])


def sample_body(fields, land, conv_in, conv_out, batchnorm_gain, batchnorm_offset, target_grad):
    lon, lat, chans = fields.shape[1:]
    tiles = lax.axis_size("space")
    sizes = (lon, lat, chans)
    nx = tiles * lon
    near, across = xor_pairs(tiles, 1), xor_pairs(tiles, 2)
    move = lambda x, pairs: lax.ppermute(x, "space", pairs)
    f2 = move(fields, across)
    l2 = move(land, across)
    f1 = move(fields, near)
    l1 = move(land, near)
    l3 = move(land, xor_pairs(tiles, 3))
    f3 = move(f2, near)
    gain, offset = batchnorm_gain[None, :], batchnorm_offset[None, :]
    params = [
        pltpu.with_memory_space_constraint(x, pltpu.HBM)
        for x in (fields, target_grad, land, conv_in, conv_out, gain, offset)
    ]
    shares = lax.axis_size("batch")
    half = sds((shares // 2, 9, chans // shares, chans), BF16)
    whole = [pltpu.VMEM((shares, 9, chans // shares, chans), BF16)]
    shifted = sds((nx + 2, lat, 3 * chans), BF16)
    cells = sds((nx, lat, chans), BF16)
    cells_f = sds((nx, lat, chans), F32)
    sums = sds((8, chans), F32)
    work = 2 * nx * lat * 9 * chans * chans
    double = sds((12 * chans, 2 * chans), BF16)
    ss, tt, mask, target, win, wout, wt, bn = run(
        functools.partial(sample_prep, *sizes, tiles),
        [shifted, shifted, cells, sds(target_grad.shape, BF16), double, sds(conv_out.shape, BF16), double, sums],
        params,
        scratch=[
            pltpu.VMEM(fields.shape, BF16), pltpu.VMEM(fields.shape, BF16), pltpu.VMEM(land.shape, jnp.int32),
            pltpu.VMEM(conv_in.shape, BF16), pltpu.SemaphoreType.DMA((7,)),
        ],
        space=pl.BlockSpec(memory_space=pltpu.HBM),
    )
    ss, mask = run(
        functools.partial(sample_build, *sizes), [shifted, cells], [f1, f2, l1, l2, l3, ss, mask], alias={5: 0, 6: 1}
    )
    t2 = move(target, across)
    t1 = move(target, near)
    t3 = move(t2, near)
    ss, first, stat = run(
        functools.partial(sample_conv, *sizes), [shifted, cells, sums], [f3, ss, mask, win], flops=work, alias={1: 0}
    )
    stat = all_sum(stat, "batch")
    tt, dact = run(
        functools.partial(sample_adjoint, *sizes), [shifted, cells_f], [t1, t2, t3, mask, wt, tt], flops=work, alias={5: 0}
    )
    gsum, dpre, aa = run(
        functools.partial(sample_act, lat, chans), [sums, cells_f, shifted], [first, mask, stat, bn, dact]
    )
    gsum = all_sum(gsum, "batch")
    keep_o, send_o = run(
        functools.partial(sample_grad, lat, chans), [half, half], [aa, tt, stat], scratch=whole, flops=work
    )
    grad_out, _ = exchange_sum(keep_o, send_o, shares)
    keep_i, send_i = run(
        functools.partial(sample_in, lat, chans),
        [half, half], [first, mask, stat, bn, dpre, gsum, ss], scratch=whole, flops=work,
    )
    grad_in, folded = exchange_sum(keep_i, send_i, shares)
    output, grad_gain, grad_offset = run(
        functools.partial(sample_out, *sizes),
        [sds(fields.shape, BF16), sds((1, chans), F32), sds((1, chans), F32)],
        [aa, mask, wout, gsum, folded], flops=work // tiles,
    )
    return (output, grad_in, grad_out, grad_gain[0], grad_offset[0])


def body(*args):
    if lax.axis_size("space") != 4:
        return tile_body(*args)
    return sample_body(*args)


def solution(mesh):
    in_specs = (
        P(("groups", "batch"), "space", None, None),
        P("space", None),
        P(),
        P(),
        P(),
        P(),
        P(("groups", "batch"), "space", None, None),
    )
    out_specs = (
        P(("groups", "batch"), "space", None, None),
        P("groups", None, "batch"),
        P("groups", None, "batch"),
        P("groups"),
        P("groups"),
    )
    return jax.shard_map(body, mesh=mesh, in_specs=in_specs, out_specs=out_specs, check_vma=False)
```
